32 devices in a mesh: grp: 8 (over y, x, core), seq: 4 (over z).
Axes of the slice: x: 2, y: 2, z: 4, core: 2. Of those that a mesh axis runs over, the one named last changes fastest.
Arguments:
- tokens: bfloat16 [8192, 2048], P(('grp', 'seq')), may hold values from -6 to 6
- cotangent: bfloat16 [8192, 2048], P(('grp', 'seq')), may hold values from -6 to 6
- segment_ids: int32 [8192], P(('grp', 'seq')), may hold values from 0 to 31, never falling along the last dimension, each value on 1 to 768 neighbouring positions
- tile_owner_slots: int32 [166], replicated, may hold values from 0 to 167, as said below
- weights_low: bfloat16 [168, 2048, 128], P('grp', 'seq')
- master: float32 [168, 2048, 128], P('grp', 'seq')
- moment_one: float32 [168, 2048, 128], P('grp', 'seq')
- moment_two: float32 [168, 2048, 128], P('grp', 'seq'), as said below
- left_basis_set: float32 [168, 2048, 512], P('grp', 'seq'), as said below
- right_basis_set: float32 [168, 512, 128], P('grp', 'seq'), as said below
- gains: float32 [2, 2048], replicated, may hold values from 0.5 to 1.5
- gain_moment_one: float32 [2, 2048], replicated, may hold values from -28 to 28
- gain_moment_two: float32 [2, 2048], replicated, may hold values from 430.8992 to 1720.32
Outputs:
- block_out: bfloat16 [8192, 2048], P(('grp', 'seq'))
- input_grad: float32 [8192, 2048], P(('grp', 'seq'))
- new_master: float32 [168, 2048, 128], P('grp', 'seq')
- new_moment_one: float32 [168, 2048, 128], P('grp', 'seq')
- new_moment_two: float32 [168, 2048, 128], P('grp', 'seq')
- gain_grads: float32 [2, 2048], replicated
- new_gains: float32 [2, 2048], replicated
- new_gain_one: float32 [2, 2048], replicated
- new_gain_two: float32 [2, 2048], replicated
The draws below stay inside these ranges and needn't reach their ends.
Inputs may be any that keep to these rules, and one draw needn't show every extreme that they name: `tile_owner_slots`: the entries are distinct; slot q belongs to data group q // 21. `segment_ids`: never falls along the tokens. `left_basis_set`: each 512 x 512 block is orthogonal. `right_basis_set`: each 128 x 128 block is orthogonal. `moment_two`: positive.
All inputs are finite; a program needn't handle non-finite values.
Results may differ from the reference program's by a relative error of at most 0.015.
Values may be sent and summed in bfloat16 or wider, within the bound.
A program may use at most 704 MiB of HBM per device.

```python
import math
import jax
import jax.numpy as jnp
import numpy as np
from jax import lax

MODEL_WIDTH = 2048
NH = 16
HD = 128
FF = 5632
TILE_COLUMNS = 128
SEQLEN = 1024
TOKENS = 8192
TILE_ROWS = 512
COLS = 21248
COLUMN_TILES = 166
SLOT_COUNT = 168
N_SEQ = 4


def slot_tiles(key):
    slot_picker = jax.random.fold_in(key, 7)
    score_matrix = jax.random.permutation(jax.random.fold_in(slot_picker, 1), SLOT_COUNT).astype(jnp.int32)
    tile_position = jnp.arange(SLOT_COUNT, dtype=jnp.int32)
    score_matrix = jnp.where(tile_position == 0, -2, jnp.where(tile_position == SLOT_COUNT - 1, -1, score_matrix))
    ordering = jnp.argsort(score_matrix, stable=True).astype(jnp.int32)
    chosen = ordering[:COLUMN_TILES]
    shuffle = jax.random.permutation(jax.random.fold_in(slot_picker, 2), COLUMN_TILES).astype(jnp.int32)
    owner_list = chosen[shuffle]
    tile_for_column = jnp.full((SLOT_COUNT,), COLUMN_TILES, jnp.int32).at[owner_list].set(jnp.arange(COLUMN_TILES, dtype=jnp.int32))
    return (owner_list, tile_for_column)


def slot_scales(key):
    owner_list, tile_for_column = slot_tiles(key)
    column = tile_for_column * TILE_COLUMNS
    attn_in = NH * HD + 2 * HD
    attn_out = attn_in + MODEL_WIDTH
    gating = attn_out + 2 * FF
    spread = jnp.where(column < attn_in, MODEL_WIDTH ** (-0.5), jnp.where(column < attn_out, 4.0 * MODEL_WIDTH ** (-0.5), jnp.where(column < gating, MODEL_WIDTH ** (-0.5), jnp.where(column < COLS, FF ** (-0.5), MODEL_WIDTH ** (-0.5)))))
    gradient = jnp.where(column < NH * HD, 0.6, jnp.where(column < attn_in, 2.5, jnp.where(column < attn_out, 0.2, jnp.where(column < gating, 0.35, jnp.where(column < COLS, 0.6, 0.3)))))
    gradient = gradient * TOKENS ** 0.5
    return (spread.astype(jnp.float32), gradient.astype(jnp.float32))


def noise_for_slot(key, shape):
    return jnp.clip(jax.random.normal(key, shape, jnp.float32), -6.0, 6.0)


def orthogonal_basis(key, batch, size):
    bit_count = size.bit_length() - 1
    column = jnp.arange(size, dtype=jnp.int32)
    pairing = column // 2
    is_odd = column % 2 == 1

    def one_matrix(index):
        sub_key = jax.random.fold_in(key, index)
        ordering = jax.random.permutation(jax.random.fold_in(sub_key, 1), size).astype(jnp.int32)
        angles = jax.random.uniform(jax.random.fold_in(sub_key, 2), (size // 2,), jnp.float32, -math.pi, math.pi)
        left_col = ordering[2 * pairing]
        right_col = ordering[2 * pairing + 1]

        def hadamard(picked):
            correlation = jnp.bitwise_and(column[:, None], picked[None, :])
            parity = jnp.zeros_like(correlation)
            for bit_index in range(bit_count):
                parity = parity + jnp.bitwise_and(jnp.right_shift(correlation, bit_index), 1)
            return (1 - 2 * (parity % 2)).astype(jnp.float32) * size ** (-0.5)
        first_part = hadamard(left_col)
        second_part = hadamard(right_col)
        cosine = jnp.cos(angles[pairing])[None, :]
        sine_part = jnp.sin(angles[pairing])[None, :]
        return jnp.where(is_odd[None, :], cosine * second_part - sine_part * first_part, cosine * first_part + sine_part * second_part)
    return lax.map(one_matrix, jnp.arange(batch, dtype=jnp.int32))


def draw_tile_owner_slots(key, part):
    return slot_tiles(key)[0]


def draw_weights_low(key, part):
    spread, gradient = slot_scales(key)
    random_noise = noise_for_slot(jax.random.fold_in(key, 21), (SLOT_COUNT, MODEL_WIDTH, TILE_COLUMNS))
    return (spread[:, None, None] * random_noise).astype(jnp.bfloat16)


def draw_master(key, part):
    spread, gradient = slot_scales(key)
    random_noise = noise_for_slot(jax.random.fold_in(key, 22), (SLOT_COUNT, MODEL_WIDTH, TILE_COLUMNS))
    return spread[:, None, None] * random_noise


def draw_moment_one(key, part):
    spread, gradient = slot_scales(key)
    random_noise = noise_for_slot(jax.random.fold_in(key, 23), (SLOT_COUNT, MODEL_WIDTH, TILE_COLUMNS))
    return gradient[:, None, None] * 0.0526 * random_noise


def draw_moment_two(key, part):
    spread, gradient = slot_scales(key)
    scale_factor = jnp.exp(jax.random.uniform(jax.random.fold_in(key, 24), (SLOT_COUNT, MODEL_WIDTH, TILE_COLUMNS), jnp.float32, 0.0, math.log(4.0)))
    return (gradient * gradient)[:, None, None] * 0.0526 * scale_factor


def draw_left_basis_set(key, part):
    block_list = SLOT_COUNT * (MODEL_WIDTH // TILE_ROWS)
    return orthogonal_basis(jax.random.fold_in(key, 31), block_list, TILE_ROWS).reshape(SLOT_COUNT, MODEL_WIDTH, TILE_ROWS)


def draw_right_basis_set(key, part):
    block_list = SLOT_COUNT * (MODEL_WIDTH // TILE_ROWS)
    return orthogonal_basis(jax.random.fold_in(key, 32), block_list, TILE_COLUMNS).reshape(SLOT_COUNT, MODEL_WIDTH // TILE_ROWS * TILE_COLUMNS, TILE_COLUMNS)


def shard_levels(rng, dims, split, low, top_value):
    def one(axis_at, shards_of):
        heights = jax.random.uniform(jax.random.fold_in(jax.random.fold_in(rng, 6), axis_at), (shards_of,), jnp.float32, low / len(split), top_value / len(split))
        return jnp.repeat(jnp.exp(heights), dims[axis_at] // shards_of).reshape((-1,) + (1,) * (len(dims) - axis_at - 1))

    factor_of = one(*split[0])
    for cut in split[1:]:
        factor_of = factor_of * one(*cut)
    return factor_of


def profile(count, total, reach, skew):
    weights = [(1 << 20) // math.isqrt(standing ** skew) + 1 for standing in range(2, count + 1)]
    rest, holding = total - reach - (count - 1), [1] * (count - 1)
    while rest > 0:
        movable = [i for i in range(count - 1) if holding[i] < reach]
        whole, remaining = sum([weights[i] for i in movable]), rest
        for i in movable:
            more = min(reach - holding[i], max(1, remaining * weights[i] // whole), rest)
            holding[i] = holding[i] + more
            rest = rest - more
    return np.array([reach] + holding)


def uneven(stream_key, amount, total, reach, lean):
    if amount == 2:
        one = jax.random.randint(stream_key, (), max(1, total - reach), min(reach, total - 1) + 1)
        return jnp.stack([one, total - one])
    sizes = jnp.asarray(profile(amount, total, reach, lean), jnp.int32)
    twos = (amount - 1) // 2
    giver, taker = sizes[1:1 + 2 * twos:2], sizes[2:2 + 2 * twos:2]
    room = jnp.minimum(giver - 1, reach - taker)
    shifted = jax.random.randint(jax.random.fold_in(stream_key, 1), (twos,), 0, 1 << 20) % (room + 1)
    sizes = sizes.at[1:1 + 2 * twos:2].set(giver - shifted).at[2:2 + 2 * twos:2].set(taker + shifted)
    return sizes[jax.random.permutation(jax.random.fold_in(stream_key, 2), amount)]


def normal_values(key, extent, scale, bound, shards=(), kind=jnp.bfloat16):
    drawn = jax.random.normal(key, extent, jnp.float32) * scale
    if len(shards) > 0:
        drawn = shard_levels(key, extent, shards, -0.22, 0.18) * drawn
    return jnp.clip(drawn, min=-bound, max=bound).astype(kind)


def setup_inputs(seed: int = 0) -> dict:
    arg_keys = jax.random.split(jax.random.key(seed), 14)
    tokens = normal_values(arg_keys[0], (TOKENS, MODEL_WIDTH), 1.0, 6.0, ((0, 32),))
    cotangent = normal_values(arg_keys[1], (TOKENS, MODEL_WIDTH), 1.0, 6.0, ((0, 32),))
    segment_ids = jnp.searchsorted(jnp.cumsum(uneven(arg_keys[2], TOKENS // SEQLEN * 4, TOKENS, SEQLEN * 3 // 4, 2)), jnp.arange(TOKENS), side="right").astype(jnp.int32)
    tile_owner_slots = draw_tile_owner_slots(jax.random.fold_in(arg_keys[13], 71), 0)
    weights_low = draw_weights_low(jax.random.fold_in(arg_keys[13], 71), 0)
    master = draw_master(jax.random.fold_in(arg_keys[13], 71), 0)
    moment_one = draw_moment_one(jax.random.fold_in(arg_keys[13], 71), 0)
    moment_two = draw_moment_two(jax.random.fold_in(arg_keys[13], 71), 0)
    left_basis_set = draw_left_basis_set(jax.random.fold_in(arg_keys[13], 71), 0)
    right_basis_set = draw_right_basis_set(jax.random.fold_in(arg_keys[13], 71), 0)
    gains = jnp.clip(1.0 + 0.1 * jax.random.normal(arg_keys[10], (2, MODEL_WIDTH), jnp.float32), 0.5, 1.5)
    gain_moment_one = normal_values(arg_keys[11], (2, MODEL_WIDTH), (0.0526 * TOKENS ** 0.5), 28.0, (), jnp.float32)
    gain_moment_two = jnp.clip(jnp.exp(jax.random.uniform(arg_keys[12], (2, MODEL_WIDTH), jnp.float32, math.log(430.8992), math.log(1720.32))), 430.8992, 1720.32)
    return {"tokens": tokens, "cotangent": cotangent, "segment_ids": segment_ids, "tile_owner_slots": tile_owner_slots, "weights_low": weights_low, "master": master, "moment_one": moment_one, "moment_two": moment_two, "left_basis_set": left_basis_set, "right_basis_set": right_basis_set, "gains": gains, "gain_moment_one": gain_moment_one, "gain_moment_two": gain_moment_two}


NORM_EPS = 1e-05
BETA_ONE = 0.95
BETA_TWO = 0.95
ADAM_EPS = 1e-08
WEIGHT_DECAY = 0.01
LEARN_RATE = 0.03
GAIN_RATE = 1.5
ROPE_BASE = 10000.0
MASKED = -1e+30
PRECISE = lax.Precision.HIGHEST

@jax.custom_vjp
def low(v):
    return lax.optimization_barrier(v.astype(jnp.bfloat16)).astype(jnp.float32)

@jax.custom_vjp
def low_back(v):
    return v

def low_keep(v):
    return (low(v), None)

def low_pass(kept, grad):
    return (grad,)

def back_keep(v):
    return (v, None)

def back_low(kept, grad):
    return (low(grad),)
low.defvjp(low_keep, low_pass)
low_back.defvjp(back_keep, back_low)

def rotate(values, positions, direction):
    head_width = values.shape[-1]
    half_width = head_width // 2
    frequency = ROPE_BASE ** (-(jnp.arange(half_width, dtype=jnp.float32) * 2.0) / head_width)
    angles = positions.astype(jnp.float32)[:, None] * frequency[None, :]
    cosine = jnp.cos(angles)[:, None, :]
    sine_part = (jnp.sin(angles) * direction)[:, None, :]
    leading = values[..., :half_width]
    trailing = values[..., half_width:]
    return jnp.concatenate([leading * cosine - trailing * sine_part, trailing * cosine + leading * sine_part], axis=-1)

def visible(query_index, key_index, query_seg, key_seg):
    causal = query_index[:, None] >= key_index[None, :]
    same_seq = query_index[:, None] // SEQLEN == key_index[None, :] // SEQLEN
    same_doc = query_seg[:, None] == key_seg[None, :]
    return causal & same_seq & same_doc

def attend_sequence(inputs):
    queries, key_rows, value_rows, segments = inputs
    length = queries.shape[0]
    places = jnp.arange(length, dtype=jnp.int32)
    allowed = visible(places, places, segments, segments)
    raw_scores = low_back(jnp.einsum('qhd,kd->hqk', queries, key_rows, precision=PRECISE))
    score_matrix = jnp.where(allowed[None], raw_scores * HD ** (-0.5), MASKED)
    weights = low(jax.nn.softmax(score_matrix, axis=-1))
    return jnp.einsum('hqk,kd->qhd', weights, value_rows, precision=PRECISE)

def forward(tok_float, gain_rows, weight_cols, segments):
    rows_here = tok_float.shape[0]
    query_cols = NH * HD
    value_end = query_cols + 2 * HD
    output_end = value_end + MODEL_WIDTH
    gating_end = output_end + 2 * FF
    places = jnp.arange(rows_here, dtype=jnp.int32) % SEQLEN
    inverse_one = lax.rsqrt(lax.optimization_barrier(jnp.mean(tok_float * tok_float, axis=-1, keepdims=True)) + NORM_EPS)
    normed = low(tok_float * inverse_one * gain_rows[0])
    projected = low_back(jnp.dot(normed, weight_cols[:, :value_end], precision=PRECISE))
    queries = low(rotate(projected[:, :query_cols].reshape(rows_here, NH, HD), places, 1.0))
    key_rows = low(rotate(projected[:, query_cols:query_cols + HD].reshape(rows_here, 1, HD), places, 1.0)).reshape(rows_here, HD)
    value_rows = low(projected[:, query_cols + HD:value_end])
    seq_count = rows_here // SEQLEN
    context = lax.map(jax.checkpoint(attend_sequence), (queries.reshape(seq_count, SEQLEN, NH, HD), key_rows.reshape(seq_count, SEQLEN, HD), value_rows.reshape(seq_count, SEQLEN, HD), segments.reshape(seq_count, SEQLEN)))
    context = low(low_back(context.reshape(rows_here, query_cols)))
    branch = low_back(jnp.dot(context, weight_cols[:, value_end:output_end], precision=PRECISE))
    hidden = tok_float + branch
    inverse_two = lax.rsqrt(lax.optimization_barrier(jnp.mean(hidden * hidden, axis=-1, keepdims=True)) + NORM_EPS)
    normed_two = low(hidden * inverse_two * gain_rows[1])
    gate_up = low_back(jnp.dot(normed_two, weight_cols[:, output_end:gating_end], precision=PRECISE))
    activated = low(jax.nn.silu(gate_up[:, :FF]) * gate_up[:, FF:])
    feed_out = low_back(jnp.dot(activated, jnp.transpose(weight_cols[:, gating_end:]), precision=PRECISE))
    return hidden + feed_out

def reference(tokens, cotangent, segment_ids, tile_owner_slots, weights_low, master, moment_one, moment_two, left_basis_set, right_basis_set, gains, gain_moment_one, gain_moment_two):
    weight_cols = jnp.transpose(weights_low[tile_owner_slots], (1, 0, 2)).reshape(MODEL_WIDTH, COLS).astype(jnp.float32)
    seq_total = TOKENS // SEQLEN
    per_block = 1
    for divisor in range(1, seq_total + 1):
        if seq_total % divisor == 0 and divisor * SEQLEN <= 4096:
            per_block = divisor
    block_count = seq_total // per_block
    block_rows = per_block * SEQLEN
    tok_blocks = tokens.reshape(block_count, block_rows, MODEL_WIDTH)
    cot_blocks = cotangent.reshape(block_count, block_rows, MODEL_WIDTH)
    seg_blocks = segment_ids.reshape(block_count, block_rows)

    def one_block(running, inputs):
        tok_block, cot_block, seg_block = inputs

        def closed(tok_float, gain_rows, columns):
            return forward(tok_float, gain_rows, columns, seg_block)
        result, pullback = jax.vjp(closed, tok_block.astype(jnp.float32), gains, weight_cols)
        tok_grad, gain_part, col_part = pullback(cot_block.astype(jnp.float32))
        return ((running[0] + gain_part, running[1] + col_part), (result.astype(jnp.bfloat16), tok_grad))
    (gain_grads, col_grads), (outputs, input_grads) = lax.scan(one_block, (jnp.zeros_like(gains), jnp.zeros_like(weight_cols)), (tok_blocks, cot_blocks, seg_blocks))
    tile_count = tile_owner_slots.shape[0]
    tile_list = jnp.transpose(col_grads.reshape(MODEL_WIDTH, tile_count, TILE_COLUMNS), (1, 0, 2))
    reduced_sum = jnp.zeros((SLOT_COUNT, MODEL_WIDTH, TILE_COLUMNS), jnp.float32).at[tile_owner_slots].set(tile_list)
    row_blocked = (SLOT_COUNT, N_SEQ, TILE_ROWS, TILE_COLUMNS)
    grad_blocks = reduced_sum.reshape(row_blocked)
    left_basis_blocks = left_basis_set.reshape(SLOT_COUNT, N_SEQ, TILE_ROWS, TILE_ROWS)
    right_basis_blocks = right_basis_set.reshape(SLOT_COUNT, N_SEQ, TILE_COLUMNS, TILE_COLUMNS)
    turned = jnp.einsum('zsji,zsjc->zsic', left_basis_blocks, grad_blocks, precision=PRECISE)
    turned = jnp.einsum('zsic,zscd->zsid', turned, right_basis_blocks, precision=PRECISE)
    new_one = BETA_ONE * moment_one.reshape(row_blocked) + (1.0 - BETA_ONE) * turned
    new_two = BETA_TWO * moment_two.reshape(row_blocked) + (1.0 - BETA_TWO) * turned * turned
    scaled = new_one / (jnp.sqrt(new_two) + ADAM_EPS)
    restored = jnp.einsum('zsij,zsjd->zsid', left_basis_blocks, scaled, precision=PRECISE)
    restored = jnp.einsum('zsid,zsed->zsie', restored, right_basis_blocks, precision=PRECISE)
    new_master = master.reshape(row_blocked) * (1.0 - LEARN_RATE * WEIGHT_DECAY) - LEARN_RATE * restored
    gain_one = BETA_ONE * gain_moment_one + (1.0 - BETA_ONE) * gain_grads
    gain_two = BETA_TWO * gain_moment_two + (1.0 - BETA_TWO) * gain_grads * gain_grads
    new_gains = gains - GAIN_RATE * gain_one / (jnp.sqrt(gain_two) + ADAM_EPS)
    slot_dimensions = (SLOT_COUNT, MODEL_WIDTH, TILE_COLUMNS)
    return (outputs.reshape(TOKENS, MODEL_WIDTH), input_grads.reshape(TOKENS, MODEL_WIDTH), new_master.reshape(slot_dimensions), new_one.reshape(slot_dimensions), new_two.reshape(slot_dimensions), gain_grads, new_gains, gain_one, gain_two)
```

```python
import jax
import jax.numpy as jnp
from jax import lax
from jax.sharding import PartitionSpec as P

MODEL_WIDTH = 2048
NH = 16
HD = 128
FF = 5632
SEQLEN = 1024


NORM_EPS = 1e-05
BETA_ONE = 0.95
BETA_TWO = 0.95
ADAM_EPS = 1e-08
WEIGHT_DECAY = 0.01
LEARN_RATE = 0.03
GAIN_RATE = 1.5
ROPE_BASE = 10000.0
MASKED = -1e30
PRECISE = lax.Precision.HIGHEST


def rotate(values, positions, direction):
    head_width = values.shape[-1]
    half_width = head_width // 2
    frequency = ROPE_BASE ** (-(jnp.arange(half_width, dtype=jnp.float32) * 2.0) / head_width)
    angles = positions.astype(jnp.float32)[:, None] * frequency[None, :]
    cosine = jnp.cos(angles)[:, None, :]
    sine_part = (jnp.sin(angles) * direction)[:, None, :]
    leading = values[..., :half_width]
    trailing = values[..., half_width:]
    return jnp.concatenate(
        [leading * cosine - trailing * sine_part, trailing * cosine + leading * sine_part], axis=-1
    )


def visible(query_index, key_index, query_seg, key_seg):
    causal = query_index[:, None] >= key_index[None, :]
    same_seq = query_index[:, None] // SEQLEN == key_index[None, :] // SEQLEN
    same_doc = query_seg[:, None] == key_seg[None, :]
    return causal & same_seq & same_doc


def contract(left_side, right_side):
    return lax.dot_general(
        left_side, right_side, (((0,), (0,)), ((), ())), preferred_element_type=jnp.float32
    )


def times_transpose(left_side, right_side):
    return lax.dot_general(
        left_side, right_side, (((1,), (1,)), ((), ())), preferred_element_type=jnp.float32
    )


def attend(queries, key_rows, value_rows, query_index, query_seg, key_index, key_seg):
    query_total, head_count, head_width = queries.shape
    block_rows = min(512, query_total)
    block_count = query_total // block_rows
    score_scale = head_width ** (-0.5)

    def one_block(inputs):
        block_queries, block_index, block_seg = inputs
        raw_scores = jnp.einsum(
            "qhd,kd->hqk", block_queries, key_rows, preferred_element_type=jnp.float32
        )
        allowed = visible(block_index, key_index, block_seg, key_seg)
        score_matrix = jnp.where(allowed[None], raw_scores * score_scale, MASKED)
        highest = jnp.max(score_matrix, axis=-1, keepdims=True)
        exponent = jnp.exp(score_matrix - highest)
        totals = jnp.sum(exponent, axis=-1, keepdims=True)
        probs_low = (exponent / totals).astype(jnp.bfloat16)
        context = jnp.einsum(
            "hqk,kd->qhd", probs_low, value_rows, preferred_element_type=jnp.float32
        )
        return (context, jnp.transpose((highest + jnp.log(totals))[..., 0]))

    context, log_totals = lax.map(
        one_block,
        (
            queries.reshape(block_count, block_rows, head_count, head_width),
            query_index.reshape(block_count, block_rows),
            query_seg.reshape(block_count, block_rows),
        ),
    )
    return (
        context.reshape(query_total, head_count, head_width),
        log_totals.reshape(query_total, head_count),
    )


def attend_back(
    queries, key_rows, value_rows, grads_low, log_totals, query_index, query_seg, key_index, key_seg
):
    query_total, head_count, head_width = queries.shape
    block_rows = min(512, query_total)
    block_count = query_total // block_rows
    score_scale = head_width ** (-0.5)

    def one_block(running, inputs):
        block_queries, block_grads, block_totals, block_index, block_seg = inputs
        raw_scores = jnp.einsum(
            "qhd,kd->hqk", block_queries, key_rows, preferred_element_type=jnp.float32
        )
        allowed = visible(block_index, key_index, block_seg, key_seg)
        shifted = raw_scores * score_scale - jnp.transpose(block_totals)[:, :, None]
        probs = jnp.where(allowed[None], jnp.exp(shifted), 0.0)
        prob_grad = jnp.einsum(
            "qhd,kd->hqk", block_grads, value_rows, preferred_element_type=jnp.float32
        )
        centre = jnp.sum(probs * prob_grad, axis=-1, keepdims=True)
        score_grad = (probs * (prob_grad - centre) * score_scale).astype(jnp.bfloat16)
        query_part = jnp.einsum(
            "hqk,kd->qhd", score_grad, key_rows, preferred_element_type=jnp.float32
        )
        key_part = running[0] + jnp.einsum(
            "hqk,qhd->kd", score_grad, block_queries, preferred_element_type=jnp.float32
        )
        value_part = running[1] + jnp.einsum(
            "hqk,qhd->kd",
            probs.astype(jnp.bfloat16),
            block_grads,
            preferred_element_type=jnp.float32,
        )
        return ((key_part, value_part), query_part)

    zeros_rows = jnp.zeros(key_rows.shape, jnp.float32)
    (key_grad, value_grad), query_grad = lax.scan(
        one_block,
        (zeros_rows, zeros_rows),
        (
            queries.reshape(block_count, block_rows, head_count, head_width),
            grads_low.reshape(block_count, block_rows, head_count, head_width),
            log_totals.reshape(block_count, block_rows, head_count),
            query_index.reshape(block_count, block_rows),
            query_seg.reshape(block_count, block_rows),
        ),
    )
    return (query_grad.reshape(query_total, head_count, head_width), key_grad, value_grad)


def local(
    tokens,
    cotangent,
    segment_ids,
    tile_owner_slots,
    weights_low,
    master,
    moment_one,
    moment_two,
    left_basis_set,
    right_basis_set,
    gains,
    gain_moment_one,
    gain_moment_two,
):
    grp_count = lax.axis_size("grp")
    seq_count = lax.axis_size("seq")
    grp_here = lax.axis_index("grp")
    rows_here = tokens.shape[0]
    slots_here, rows_block, tile_width = weights_low.shape
    query_cols = NH * HD
    value_end = query_cols + 2 * HD
    output_end = value_end + MODEL_WIDTH
    attn_tiles = output_end // tile_width
    hidden_tiles = FF // tile_width
    share = -(-hidden_tiles // grp_count)
    share_cols = share * tile_width
    sub_rows = rows_block // grp_count
    local_index = lax.axis_index("seq") * rows_here + jnp.arange(rows_here, dtype=jnp.int32)
    local_place = local_index % SEQLEN

    plane_tiles = lax.all_gather(weights_low, "grp", axis=0, tiled=True)
    hidden_ids = grp_here * share + jnp.arange(share, dtype=jnp.int32)
    real = hidden_ids < hidden_tiles
    hidden_ids = jnp.minimum(hidden_ids, hidden_tiles - 1)
    feed_ids = (
        attn_tiles
        + jnp.arange(3, dtype=jnp.int32)[:, None] * hidden_tiles
        + hidden_ids[None, :]
    ).reshape(-1)
    attn_rows = lax.dynamic_slice_in_dim(plane_tiles, grp_here * sub_rows, sub_rows, axis=1)
    attn_rows = jnp.transpose(attn_rows[tile_owner_slots[:attn_tiles]], (1, 0, 2)).reshape(
        sub_rows, output_end
    )
    attn_weights = lax.all_gather(attn_rows, "seq", axis=0, tiled=False)
    attn_weights = lax.all_gather(attn_weights, "grp", axis=1, tiled=True).reshape(
        MODEL_WIDTH, output_end
    )
    feed_tiles = jnp.where(
        jnp.tile(real, 3)[:, None, None], plane_tiles[tile_owner_slots[feed_ids]], 0
    )
    feed_rows = jnp.transpose(feed_tiles, (1, 0, 2)).reshape(rows_block, 3 * share_cols)
    feed_weights = lax.all_gather(feed_rows, "seq", axis=0, tiled=True)
    cot_plane = lax.all_gather(cotangent, "grp", axis=0, tiled=True)

    tok_float = tokens.astype(jnp.float32)
    inverse_one = lax.rsqrt(jnp.mean(tok_float * tok_float, axis=-1, keepdims=True) + NORM_EPS)
    normed = (tok_float * inverse_one * gains[0]).astype(jnp.bfloat16)
    projected = jnp.dot(normed, attn_weights[:, :value_end], preferred_element_type=jnp.float32)
    queries = rotate(projected[:, :query_cols].reshape(rows_here, NH, HD), local_place, 1.0).astype(
        jnp.bfloat16
    )
    key_rows = (
        rotate(
            projected[:, query_cols : query_cols + HD].reshape(rows_here, 1, HD), local_place, 1.0
        )
        .reshape(rows_here, HD)
        .astype(jnp.bfloat16)
    )
    value_rows = projected[:, query_cols + HD : value_end].astype(jnp.bfloat16)
    all_pairs = lax.all_gather(
        jnp.concatenate([key_rows, value_rows], axis=1), "seq", axis=0, tiled=True
    )
    all_keys = all_pairs[:, :HD]
    all_values = all_pairs[:, HD:]
    all_segs = lax.all_gather(segment_ids, "seq", axis=0, tiled=True)
    group_index = jnp.arange(all_keys.shape[0], dtype=jnp.int32)
    group_place = group_index % SEQLEN
    heads_here = NH // seq_count
    head_queries = lax.all_to_all(
        queries.reshape(rows_here, query_cols), "seq", split_axis=1, concat_axis=0, tiled=True
    ).reshape(-1, heads_here, HD)
    head_context, log_totals = attend(
        head_queries, all_keys, all_values, group_index, all_segs, group_index, all_segs
    )
    context = lax.all_to_all(
        head_context.reshape(-1, heads_here * HD).astype(jnp.bfloat16),
        "seq",
        split_axis=0,
        concat_axis=1,
        tiled=True,
    )
    branch = jnp.dot(
        context, attn_weights[:, value_end:], preferred_element_type=jnp.float32
    )
    hidden = tok_float + branch
    inverse_two = lax.rsqrt(jnp.mean(hidden * hidden, axis=-1, keepdims=True) + NORM_EPS)
    normed_two = (hidden * inverse_two * gains[1]).astype(jnp.bfloat16)

    normed_plane = lax.all_gather(normed_two, "grp", axis=0, tiled=True)
    gating_weights = feed_weights[:, : 2 * share_cols]
    down_weights = feed_weights[:, 2 * share_cols :]
    gate_up = jnp.dot(normed_plane, gating_weights, preferred_element_type=jnp.float32)
    gate = gate_up[:, :share_cols]
    upper = gate_up[:, share_cols:]
    sigmoid_gate = jax.nn.sigmoid(gate)
    silu_gate = jax.nn.silu(gate)
    activated = (silu_gate * upper).astype(jnp.bfloat16)
    act_grad = jnp.dot(cot_plane, down_weights, preferred_element_type=jnp.float32)
    gate_grad = (act_grad * upper * sigmoid_gate * (1.0 + gate * (1.0 - sigmoid_gate))).astype(
        jnp.bfloat16
    )
    up_grad = (act_grad * silu_gate).astype(jnp.bfloat16)
    gating_grad = jnp.concatenate([gate_grad, up_grad], axis=1)
    norm_two_grad = lax.psum_scatter(
        times_transpose(gating_grad, gating_weights).astype(jnp.bfloat16),
        "grp",
        scatter_dimension=0,
        tiled=True,
    ).astype(jnp.float32)
    feed_grads = jnp.concatenate(
        [contract(normed_plane, gating_grad), contract(cot_plane, activated)], axis=1
    ).astype(jnp.bfloat16)
    feed_grads = lax.psum_scatter(feed_grads, "seq", scatter_dimension=0, tiled=True)
    feed_grads = jnp.transpose(
        feed_grads.reshape(rows_block, 3 * share, tile_width), (1, 0, 2)
    )
    feed_grads = lax.all_gather(feed_grads, "grp", axis=0, tiled=True)
    feed_out = lax.psum_scatter(
        times_transpose(activated, down_weights).astype(jnp.bfloat16),
        "grp",
        scatter_dimension=0,
        tiled=True,
    ).astype(jnp.float32)
    block_out = (hidden + feed_out).astype(jnp.bfloat16)

    out_grad = cotangent.astype(jnp.float32)
    gain_two_term = jnp.sum(norm_two_grad * hidden * inverse_two, axis=0)
    hidden_grad = (
        out_grad
        + inverse_two * gains[1] * norm_two_grad
        - hidden
        * inverse_two**3
        * jnp.mean(hidden * gains[1] * norm_two_grad, axis=-1, keepdims=True)
    )
    branch_grad = hidden_grad.astype(jnp.bfloat16)
    context_grad = times_transpose(branch_grad, attn_weights[:, value_end:]).astype(jnp.bfloat16)
    head_grads = lax.all_to_all(
        context_grad, "seq", split_axis=1, concat_axis=0, tiled=True
    ).reshape(-1, heads_here, HD)

    def reduce_rows(part):
        cols = part.shape[1]
        blocks = jnp.transpose(
            part.astype(jnp.bfloat16).reshape(seq_count, grp_count, sub_rows, cols), (1, 0, 2, 3)
        ).reshape(grp_count * seq_count * sub_rows, cols)
        summed = lax.psum_scatter(blocks, ("grp", "seq"), scatter_dimension=0, tiled=True)
        return lax.all_gather(summed, "grp", axis=0, tiled=True)

    out_grads = reduce_rows(contract(context, branch_grad))
    head_query_grad, key_part, value_part = attend_back(
        head_queries,
        all_keys,
        all_values,
        head_grads,
        log_totals,
        group_index,
        all_segs,
        group_index,
        all_segs,
    )
    turned_query = (
        rotate(head_query_grad, group_place, -1.0).reshape(-1, heads_here * HD).astype(jnp.bfloat16)
    )
    query_grad = lax.all_to_all(turned_query, "seq", split_axis=0, concat_axis=1, tiled=True)
    key_part = rotate(key_part[:, None, :], group_place, -1.0)[:, 0, :]
    pair_grad = lax.psum_scatter(
        jnp.concatenate([key_part, value_part], axis=1), "seq", scatter_dimension=0, tiled=True
    )
    projected_grad = jnp.concatenate([query_grad, pair_grad.astype(jnp.bfloat16)], axis=1)
    in_grads = reduce_rows(contract(normed, projected_grad))
    norm_one_grad = times_transpose(projected_grad, attn_weights[:, :value_end])
    gain_one_term = jnp.sum(norm_one_grad * tok_float * inverse_one, axis=0)
    input_grad = (
        hidden_grad
        + inverse_one * gains[0] * norm_one_grad
        - tok_float
        * inverse_one**3
        * jnp.mean(tok_float * gains[0] * norm_one_grad, axis=-1, keepdims=True)
    )
    gain_grads = lax.psum(jnp.stack([gain_one_term, gain_two_term]), ("grp", "seq"))

    tile_count = tile_owner_slots.shape[0]
    tile_of_slot = (
        jnp.full((grp_count * slots_here,), tile_count, jnp.int32)
        .at[tile_owner_slots]
        .set(jnp.arange(tile_count, dtype=jnp.int32))
    )
    tiles_here = lax.dynamic_slice_in_dim(tile_of_slot, grp_here * slots_here, slots_here)
    attn_grads = jnp.transpose(
        jnp.concatenate([in_grads, out_grads], axis=1).reshape(rows_block, attn_tiles, tile_width),
        (1, 0, 2),
    )
    feed_at = jnp.clip(tiles_here - attn_tiles, 0, 3 * hidden_tiles - 1)
    which, column = feed_at // hidden_tiles, feed_at % hidden_tiles
    feed_at = (column // share) * (3 * share) + which * share + column % share
    picked = jnp.where(
        (tiles_here < attn_tiles)[:, None, None],
        attn_grads[jnp.minimum(tiles_here, attn_tiles - 1)],
        feed_grads[feed_at],
    )
    reduced_sum = jnp.where((tiles_here < tile_count)[:, None, None], picked, 0).astype(jnp.float32)
    turned = jnp.einsum("zji,zjc->zic", left_basis_set, reduced_sum)
    turned = jnp.einsum("zic,zcd->zid", turned, right_basis_set)
    new_one = BETA_ONE * moment_one + (1.0 - BETA_ONE) * turned
    new_two = BETA_TWO * moment_two + (1.0 - BETA_TWO) * turned * turned
    scaled = new_one / (jnp.sqrt(new_two) + ADAM_EPS)
    restored = jnp.einsum("zij,zjd->zid", left_basis_set, scaled)
    restored = jnp.einsum("zid,zed->zie", restored, right_basis_set)
    new_master = master * (1.0 - LEARN_RATE * WEIGHT_DECAY) - LEARN_RATE * restored
    gain_one = BETA_ONE * gain_moment_one + (1.0 - BETA_ONE) * gain_grads
    gain_two = BETA_TWO * gain_moment_two + (1.0 - BETA_TWO) * gain_grads * gain_grads
    new_gains = gains - GAIN_RATE * gain_one / (jnp.sqrt(gain_two) + ADAM_EPS)
    return (
        block_out,
        input_grad,
        new_master,
        new_one,
        new_two,
        gain_grads,
        new_gains,
        gain_one,
        gain_two,
    )


def solution(mesh):
    return jax.shard_map(
        local,
        mesh=mesh,
        in_specs=(
            P(("grp", "seq"), None),
            P(("grp", "seq"), None),
            P(("grp", "seq")),
            P(),
            P("grp", "seq", None),
            P("grp", "seq", None),
            P("grp", "seq", None),
            P("grp", "seq", None),
            P("grp", "seq", None),
            P("grp", "seq", None),
            P(),
            P(),
            P(),
        ),
        out_specs=(
            P(("grp", "seq"), None),
            P(("grp", "seq"), None),
            P("grp", "seq", None),
            P("grp", "seq", None),
            P("grp", "seq", None),
            P(),
            P(),
            P(),
            P(),
        ),
        check_vma=False,
    )
```

```python
import functools

import jax
import jax.numpy as jnp
from jax import lax
from jax.experimental import pallas as pl
from jax.experimental.pallas import tpu as pltpu
from jax.sharding import PartitionSpec as P

MODEL_WIDTH = 2048
NH = 16
HD = 128
FF = 5632
SEQLEN = 1024


NORM_EPS = 1e-05
BETA_ONE = 0.95
BETA_TWO = 0.95
ADAM_EPS = 1e-08
WEIGHT_DECAY = 0.01
LEARN_RATE = 0.03
GAIN_RATE = 1.5
ROPE_BASE = 10000.0
MASKED = -1e30
PRECISE = lax.Precision.HIGHEST


def rotate(values, positions, direction):
    head_width = values.shape[-1]
    half_width = head_width // 2
    frequency = ROPE_BASE ** (-(jnp.arange(half_width, dtype=jnp.float32) * 2.0) / head_width)
    angles = positions.astype(jnp.float32)[:, None] * frequency[None, :]
    cosine = jnp.cos(angles)[:, None, :]
    sine_part = (jnp.sin(angles) * direction)[:, None, :]
    leading = values[..., :half_width]
    trailing = values[..., half_width:]
    return jnp.concatenate(
        [leading * cosine - trailing * sine_part, trailing * cosine + leading * sine_part], axis=-1
    )


def contract(left_side, right_side):
    return lax.dot_general(
        left_side, right_side, (((0,), (0,)), ((), ())), preferred_element_type=jnp.float32
    )


def times_transpose(left_side, right_side):
    return lax.dot_general(
        left_side, right_side, (((1,), (1,)), ((), ())), preferred_element_type=jnp.float32
    )


def turn_tables(places):
    half_width = HD // 2
    frequency = ROPE_BASE ** (-(jnp.arange(half_width, dtype=jnp.float32) * 2.0) / HD)
    angles = places.astype(jnp.float32)[:, None] * frequency[None, :]
    cosine, sine = jnp.cos(angles), jnp.sin(angles)
    return (
        jnp.concatenate([cosine, cosine], axis=1),
        jnp.concatenate([-sine, sine], axis=1),
    )


ROWS = 256


def score_mask(key_seg_ref, query_seg_ref, block, rows):
    keys = (block + 1) * rows
    same = key_seg_ref[:keys, :] == query_seg_ref[:, block * rows : keys]
    key_at = lax.broadcasted_iota(jnp.int32, (keys, rows), 0)
    query_at = lax.broadcasted_iota(jnp.int32, (keys, rows), 1) + block * rows
    return same & (key_at <= query_at)


def dot_last(left_side, right_side):
    return lax.dot_general(
        left_side, right_side, (((1,), (1,)), ((), ())), preferred_element_type=jnp.float32
    )


def attend_kernel(q_ref, k_ref, v_ref, key_seg_ref, query_seg_ref, context_ref, total_ref):
    scale = HD ** (-0.5)
    values_t = jnp.transpose(v_ref[...].astype(jnp.float32)).astype(jnp.bfloat16)
    for block in range(SEQLEN // ROWS):
        here = slice(block * ROWS, (block + 1) * ROWS)
        keys = (block + 1) * ROWS
        scores = dot_last(k_ref[:keys, :], q_ref[here, :]) * scale
        allowed = score_mask(key_seg_ref, query_seg_ref, block, ROWS)
        scores = jnp.where(allowed, scores, MASKED)
        highest = jnp.max(scores, axis=0, keepdims=True)
        exponent = jnp.exp(scores - highest)
        totals = jnp.sum(exponent, axis=0, keepdims=True)
        probs_low = (exponent * (1.0 / totals)).astype(jnp.bfloat16)
        context_t = jnp.dot(values_t[:, :keys], probs_low, preferred_element_type=jnp.float32)
        context_ref[here, :] = jnp.transpose(context_t).astype(jnp.bfloat16)
        total_ref[0, 0, :, here] = highest + jnp.log(totals)


def attend_back_kernel(
    q_ref,
    k_ref,
    v_ref,
    grad_ref,
    total_ref,
    key_seg_ref,
    query_seg_ref,
    cosine_ref,
    sine_ref,
    query_grad_ref,
    pair_grad_ref,
    key_sum,
    value_sum,
):
    scale = HD ** (-0.5)
    head = pl.program_id(1)

    @pl.when(head == 0)
    def _():
        key_sum[...] = jnp.zeros_like(key_sum)
        value_sum[...] = jnp.zeros_like(value_sum)

    def turn_back(rows, here):
        return rows * cosine_ref[here, :] - pltpu.roll(rows, HD // 2, 1) * sine_ref[here, :]

    keys_t = jnp.transpose(k_ref[...].astype(jnp.float32)).astype(jnp.bfloat16)
    for block in range(SEQLEN // ROWS):
        here = slice(block * ROWS, (block + 1) * ROWS)
        keys = (block + 1) * ROWS
        queries, grads = q_ref[here, :], grad_ref[here, :]
        shifted = dot_last(k_ref[:keys, :], queries) * scale - total_ref[0, 0, :, here]
        allowed = score_mask(key_seg_ref, query_seg_ref, block, ROWS)
        probs = jnp.where(allowed, jnp.exp(shifted), 0.0)
        prob_grad = dot_last(v_ref[:keys, :], grads)
        centre = jnp.sum(probs * prob_grad, axis=0, keepdims=True)
        score_grad = (probs * (prob_grad - centre) * scale).astype(jnp.bfloat16)
        value_sum[:keys, :] += jnp.dot(
            probs.astype(jnp.bfloat16), grads, preferred_element_type=jnp.float32
        )
        key_sum[:keys, :] += jnp.dot(score_grad, queries, preferred_element_type=jnp.float32)
        query_grad = jnp.transpose(
            jnp.dot(keys_t[:, :keys], score_grad, preferred_element_type=jnp.float32)
        )
        query_grad_ref[here, :] = turn_back(query_grad, here).astype(jnp.bfloat16)

    @pl.when(head == pl.num_programs(1) - 1)
    def _():
        for block in range(SEQLEN // ROWS):
            here = slice(block * ROWS, (block + 1) * ROWS)
            pair_grad_ref[here, :HD] = turn_back(key_sum[here, :], here).astype(jnp.bfloat16)
            pair_grad_ref[here, HD:] = value_sum[here, :].astype(jnp.bfloat16)


def attention_specs(kinds):
    specs = {
        "head": pl.BlockSpec((SEQLEN, HD), lambda n, h: (n, h)),
        "keys": pl.BlockSpec((SEQLEN, HD), lambda n, h: (n, 0)),
        "values": pl.BlockSpec((SEQLEN, HD), lambda n, h: (n, 1)),
        "pair": pl.BlockSpec((SEQLEN, 2 * HD), lambda n, h: (n, 0)),
        "total": pl.BlockSpec((1, 1, 1, SEQLEN), lambda n, h: (n, h, 0, 0)),
        "key_seg": pl.BlockSpec((SEQLEN, 1), lambda n, h: (n, 0)),
        "query_seg": pl.BlockSpec((1, SEQLEN), lambda n, h: (0, n)),
        "table": pl.BlockSpec((SEQLEN, HD), lambda n, h: (0, 0)),
    }
    return [specs[kind] for kind in kinds]


def attend(queries, pairs, segments):
    tokens_all, columns = queries.shape
    grid = (tokens_all // SEQLEN, columns // HD)
    return pl.pallas_call(
        attend_kernel,
        grid=grid,
        in_specs=attention_specs(["head", "keys", "values", "key_seg", "query_seg"]),
        out_specs=attention_specs(["head", "total"]),
        out_shape=(
            jax.ShapeDtypeStruct((tokens_all, columns), jnp.bfloat16),
            jax.ShapeDtypeStruct((*grid, 1, SEQLEN), jnp.float32),
        ),
        compiler_params=pltpu.CompilerParams(vmem_limit_bytes=48 * 2**20),
        cost_estimate=pl.CostEstimate(
            flops=4 * tokens_all * SEQLEN * columns,
            bytes_accessed=6 * tokens_all * columns,
            transcendentals=tokens_all * SEQLEN * columns // HD,
        ),
        name="attend",
    )(queries, pairs, pairs, segments[:, None], segments[None, :])


def attend_back(queries, pairs, grads, totals, segments, tables):
    tokens_all, columns = queries.shape
    grid = (tokens_all // SEQLEN, columns // HD)
    return pl.pallas_call(
        attend_back_kernel,
        grid=grid,
        in_specs=attention_specs(
            ["head", "keys", "values", "head", "total", "key_seg", "query_seg", "table", "table"]
        ),
        out_specs=attention_specs(["head", "pair"]),
        out_shape=(
            jax.ShapeDtypeStruct((tokens_all, columns), jnp.bfloat16),
            jax.ShapeDtypeStruct((tokens_all, 2 * HD), jnp.bfloat16),
        ),
        scratch_shapes=[pltpu.VMEM((SEQLEN, HD), jnp.float32)] * 2,
        compiler_params=pltpu.CompilerParams(vmem_limit_bytes=48 * 2**20),
        cost_estimate=pl.CostEstimate(
            flops=10 * tokens_all * SEQLEN * columns,
            bytes_accessed=10 * tokens_all * columns,
            transcendentals=tokens_all * SEQLEN * columns // HD,
        ),
        name="attend_back",
    )(queries, pairs, pairs, grads, totals, segments[:, None], segments[None, :], *tables)


MESH = pl.DeviceIdType.MESH


def remote(source, target, sems, at, device):
    return pltpu.make_async_remote_copy(
        src_ref=source,
        dst_ref=target,
        send_sem=sems[0].at[at],
        recv_sem=sems[1].at[at],
        device_id=device,
        device_id_type=MESH,
    )


def columns_of(ref, index, width):
    return ref.at[:, pl.ds(pl.multiple_of(index * width, width), width)]


def rows_of(ref, index, height):
    return ref.at[pl.ds(pl.multiple_of(index * height, height), height), :]


class Exchange:
    def __init__(self, axis, out_shape, source_view, target_view):
        self.axis, self.out_shape = axis, out_shape
        self.source_view, self.target_view = source_view, target_view
        self.count = lax.axis_size(axis)
        self.sem_count = self.count

    def peers(self, grp, seq):
        me = grp if self.axis == "grp" else seq
        for step in range(1, self.count):
            there = (me + step) % self.count
            yield (there, seq) if self.axis == "grp" else (grp, there)

    def start(self, source, target, sems, grp, seq):
        me = grp if self.axis == "grp" else seq
        self.own = pltpu.make_async_copy(
            self.source_view(source, me), self.target_view(target, me), sems[0].at[0]
        )
        self.own.start()
        self.sent, self.due = [], []
        for step, device in enumerate(self.peers(grp, seq), 1):
            there = (me + step) % self.count
            back = (me + self.count - step) % self.count
            copy = remote(
                self.source_view(source, there), self.target_view(target, me), sems, step, device
            )
            copy.start()
            self.sent.append(copy)
            self.due.append(
                remote(
                    self.source_view(source, back), self.target_view(target, back), sems, step, device
                )
            )

    def forward(self):
        pass

    def finish(self):
        for copy in self.due:
            copy.wait_recv()
        for copy in self.sent:
            copy.wait_send()
        self.own.wait()


class PlaneGather:
    def __init__(self, shape):
        self.out_shape = (lax.axis_size("grp"), *shape)
        self.half = shape[0] // 2
        self.sem_count = 14

    def around(self, grp):
        core, across_x, across_y = grp % 2, (grp // 2) % 2, grp // 4
        return grp + 1 - 2 * core, grp + 2 - 4 * across_x, grp + 4 - 8 * across_y

    def peers(self, grp, seq):
        for other in self.around(grp):
            yield other, seq

    def start(self, source, target, sems, grp, seq):
        core, side_x, side_y = self.around(grp)
        half = self.half

        def part(block, piece):
            if piece == "all":
                return target.at[block]
            return target.at[block, pl.ds(0 if piece == "a" else half, half)]

        def own(piece):
            if piece == "all":
                return source
            return source.at[pl.ds(0 if piece == "a" else half, half)]

        def across(block):
            return self.around(self.around(block)[1])[2]

        def make(at, block, piece, via, first=False):
            view = own(piece) if first else part(block, piece)
            return remote(view, part(block, piece), sems, at, (via, seq))

        self.out = [
            make(1, grp, "a", side_x, True),
            make(2, grp, "b", side_x, True),
            make(3, side_y, "b", side_x),
            make(4, grp, "b", side_y, True),
            make(5, grp, "a", side_y, True),
            make(6, side_x, "a", side_y),
            make(7, grp, "all", core, True),
            make(8, side_x, "a", core),
            make(9, side_x, "b", core),
            make(10, side_y, "b", core),
            make(11, side_y, "a", core),
            make(12, across(grp), "a", core),
            make(13, across(grp), "b", core),
        ]
        self.due = [
            make(1, side_x, "a", side_x),
            make(2, side_x, "b", side_x),
            make(3, across(grp), "b", side_x),
            make(4, side_y, "b", side_y),
            make(5, side_y, "a", side_y),
            make(6, across(grp), "a", side_y),
            make(7, core, "all", core),
            make(8, self.around(core)[1], "a", core),
            make(9, self.around(core)[1], "b", core),
            make(10, self.around(core)[2], "b", core),
            make(11, self.around(core)[2], "a", core),
            make(12, across(core), "a", core),
            make(13, across(core), "b", core),
        ]
        self.kept = pltpu.make_async_copy(source, target.at[grp], sems[0].at[0])
        self.kept.start()
        for at in (1, 4, 2, 5, 7):
            self.out[at - 1].start()

    def forward(self):
        for came, then in ((1, (6, 8)), (4, (3, 10)), (2, (9,)), (5, (11,)), (6, (12,)), (3, (13,))):
            self.due[came - 1].wait_recv()
            for at in then:
                self.out[at - 1].start()

    def finish(self):
        for copy in self.due[6:]:
            copy.wait_recv()
        for copy in self.out:
            copy.wait_send()
        self.kept.wait()


def gather_plane(shape):
    if lax.axis_size("grp") == 8:
        return PlaneGather(shape)
    return Exchange(
        "grp",
        (lax.axis_size("grp"), *shape),
        lambda ref, index: ref,
        lambda ref, index: ref.at[index],
    )


def exchange_kernel(tasks, *refs):
    count = len(tasks)
    sources, targets, sems = refs[:count], refs[count : 2 * count], refs[2 * count :]
    grp, seq = lax.axis_index("grp"), lax.axis_index("seq")
    barrier = pltpu.get_barrier_semaphore()
    axes = {"grp": [], "seq": []}
    for task in tasks:
        axis = task.axis if isinstance(task, Exchange) else "grp"
        devices = list(task.peers(grp, seq))
        if len(devices) > len(axes[axis]):
            axes[axis] = devices
    devices = axes["grp"] + axes["seq"]
    for device in devices:
        pl.semaphore_signal(barrier, inc=1, device_id=device, device_id_type=MESH)
    pl.semaphore_wait(barrier, len(devices))
    for at, task in enumerate(tasks):
        task.start(sources[at], targets[at], sems[2 * at : 2 * at + 2], grp, seq)
    for task in tasks:
        task.forward()
    for task in tasks:
        task.finish()


def exchange(number, work):
    tasks = [task for task, _ in work]
    arrays = [array for _, array in work]
    scratch = []
    for task in tasks:
        scratch += [pltpu.SemaphoreType.DMA((task.sem_count,))] * 2
    return pl.pallas_call(
        functools.partial(exchange_kernel, tasks),
        in_specs=[pl.BlockSpec(memory_space=pl.ANY)] * len(work),
        out_specs=[pl.BlockSpec(memory_space=pl.ANY)] * len(work),
        out_shape=[
            jax.ShapeDtypeStruct(task.out_shape, array.dtype) for task, array in work
        ],
        scratch_shapes=scratch,
        compiler_params=pltpu.CompilerParams(collective_id=number, has_side_effects=True),
        name="exchange",
    )(*arrays)


def to_heads(array):
    count = lax.axis_size("seq")
    rows, columns = array.shape
    width = columns // count
    task = Exchange(
        "seq",
        (rows * count, width),
        lambda ref, index: columns_of(ref, index, width),
        lambda ref, index: rows_of(ref, index, rows),
    )
    return task, array


def to_tokens(array):
    count = lax.axis_size("seq")
    rows_all, width = array.shape
    rows = rows_all // count
    task = Exchange(
        "seq",
        (rows, width * count),
        lambda ref, index: rows_of(ref, index, rows),
        lambda ref, index: columns_of(ref, index, width),
    )
    return task, array


def gather_axis(axis, array):
    task = Exchange(
        axis,
        (lax.axis_size(axis), *array.shape),
        lambda ref, index: ref,
        lambda ref, index: ref.at[index],
    )
    return task, array


def split_rows(axis, array):
    count = lax.axis_size(axis)
    rows, columns = array.shape
    height = rows // count
    task = Exchange(
        axis,
        (count, height, columns),
        lambda ref, index: rows_of(ref, index, height),
        lambda ref, index: ref.at[index],
    )
    return task, array


def split_columns(axis, array):
    count = lax.axis_size(axis)
    rows, columns = array.shape
    width = columns // count
    task = Exchange(
        axis,
        (count, rows, width),
        lambda ref, index: columns_of(ref, index, width),
        lambda ref, index: ref.at[index],
    )
    return task, array


def add_rows(total, first, second):
    step = 32

    def some(at, _):
        rows = pl.ds(pl.multiple_of(at * step, step), step)
        total[rows, :] = (
            first[rows, :].astype(jnp.float32) + second[rows, :].astype(jnp.float32)
        ).astype(total.dtype)
        return 0

    lax.fori_loop(0, total.shape[0] // step, some, 0)


def plane_sum_kernel(
    part_ref, total_ref, core_in, chip, half_x, half_y, whole_x, whole_y, send_sems, recv_sems
):
    grp, seq = lax.axis_index("grp"), lax.axis_index("seq")

    def around(device):
        core, across_x, across_y = device % 2, (device // 2) % 2, device // 4
        return device + 1 - 2 * core, device + 2 - 4 * across_x, device + 4 - 8 * across_y

    def order(device):
        _, side_x, side_y = around(device)
        return around(side_x)[2], side_x, side_y, device

    core, side_x, side_y = around(grp)
    half = total_ref.shape[0] // 2
    low, high = pl.ds(0, half), pl.ds(half, half)
    barrier = pltpu.get_barrier_semaphore()
    for device in (core, side_x, side_y):
        pl.semaphore_signal(barrier, inc=1, device_id=(device, seq), device_id_type=MESH)
    pl.semaphore_wait(barrier, 3)

    sems = (send_sems, recv_sems)
    copies = [
        remote(part_ref.at[block], core_in.at[at], sems, at, (core, seq))
        for at, block in enumerate(order(core))
    ]
    copies += [
        remote(chip.at[0, low], half_x, sems, 4, (side_x, seq)),
        remote(chip.at[0, high], half_y, sems, 5, (side_y, seq)),
        remote(chip.at[1, low], whole_x.at[low], sems, 6, (side_x, seq)),
        remote(chip.at[2, high], whole_y.at[high], sems, 7, (side_y, seq)),
        remote(chip.at[1, high], whole_x.at[high], sems, 8, (side_x, seq)),
        remote(chip.at[2, low], whole_y.at[low], sems, 9, (side_y, seq)),
    ]
    for copy in copies[:4]:
        copy.start()
    blocks = order(grp)
    for at, then in ((0, (4, 5)), (1, (6,)), (2, (7,))):
        copies[at].wait_recv()
        add_rows(chip.at[at], part_ref.at[blocks[at]], core_in.at[at])
        for start in then:
            copies[start].start()
    copies[5].wait_recv()
    add_rows(chip.at[1, high], chip.at[1, high], half_y)
    copies[8].start()
    copies[4].wait_recv()
    add_rows(chip.at[2, low], chip.at[2, low], half_x)
    copies[9].start()
    copies[3].wait_recv()
    add_rows(total_ref, part_ref.at[blocks[3]], core_in.at[3])
    for at, came in ((6, whole_x.at[low]), (7, whole_y.at[high]), (8, whole_x.at[high]), (9, whole_y.at[low])):
        copies[at].wait_recv()
        rows = low if at in (6, 9) else high
        add_rows(total_ref.at[rows], total_ref.at[rows], came)
    for copy in copies:
        copy.wait_send()


def plane_sum(number, part):
    count = lax.axis_size("grp")
    rows_all, columns = part.shape
    rows = rows_all // count
    if count != 8:
        return lax.psum_scatter(part, "grp", scatter_dimension=0, tiled=True).astype(jnp.float32)
    low = jnp.bfloat16
    return pl.pallas_call(
        plane_sum_kernel,
        in_specs=[pl.BlockSpec(memory_space=pltpu.VMEM)],
        out_specs=pl.BlockSpec(memory_space=pltpu.VMEM),
        out_shape=jax.ShapeDtypeStruct((rows, columns), jnp.float32),
        scratch_shapes=[
            pltpu.VMEM((4, rows, columns), low),
            pltpu.VMEM((3, rows, columns), low),
            pltpu.VMEM((rows // 2, columns), low),
            pltpu.VMEM((rows // 2, columns), low),
            pltpu.VMEM((rows, columns), low),
            pltpu.VMEM((rows, columns), low),
            pltpu.SemaphoreType.DMA((10,)),
            pltpu.SemaphoreType.DMA((10,)),
        ],
        compiler_params=pltpu.CompilerParams(
            collective_id=number, has_side_effects=True, vmem_limit_bytes=40 * 2**20
        ),
        name="plane_sum",
    )(part.reshape(count, rows, columns))


def local(
    tokens,
    cotangent,
    segment_ids,
    tile_owner_slots,
    weights_low,
    master,
    moment_one,
    moment_two,
    left_basis_set,
    right_basis_set,
    gains,
    gain_moment_one,
    gain_moment_two,
):
    grp_count = lax.axis_size("grp")
    seq_count = lax.axis_size("seq")
    grp_here = lax.axis_index("grp")
    rows_here = tokens.shape[0]
    slots_here, rows_block, tile_width = weights_low.shape
    query_cols = NH * HD
    value_end = query_cols + 2 * HD
    output_end = value_end + MODEL_WIDTH
    attn_tiles = output_end // tile_width
    hidden_tiles = FF // tile_width
    share = -(-hidden_tiles // grp_count)
    share_cols = share * tile_width
    sub_rows = rows_block // grp_count
    local_index = lax.axis_index("seq") * rows_here + jnp.arange(rows_here, dtype=jnp.int32)
    local_place = local_index % SEQLEN

    plane_tiles = lax.all_gather(weights_low, "grp", axis=0, tiled=True)
    hidden_ids = grp_here * share + jnp.arange(share, dtype=jnp.int32)
    real = hidden_ids < hidden_tiles
    hidden_ids = jnp.minimum(hidden_ids, hidden_tiles - 1)
    feed_ids = (
        attn_tiles
        + jnp.arange(3, dtype=jnp.int32)[:, None] * hidden_tiles
        + hidden_ids[None, :]
    ).reshape(-1)
    attn_rows = lax.dynamic_slice_in_dim(plane_tiles, grp_here * sub_rows, sub_rows, axis=1)
    attn_rows = jnp.transpose(attn_rows[tile_owner_slots[:attn_tiles]], (1, 0, 2)).reshape(
        sub_rows, output_end
    )
    attn_weights = lax.all_gather(attn_rows, "seq", axis=0, tiled=False)
    attn_weights = lax.all_gather(attn_weights, "grp", axis=1, tiled=True).reshape(
        MODEL_WIDTH, output_end
    )
    feed_tiles = jnp.where(
        jnp.tile(real, 3)[:, None, None], plane_tiles[tile_owner_slots[feed_ids]], 0
    )
    feed_rows = jnp.transpose(feed_tiles, (1, 0, 2)).reshape(rows_block, 3 * share_cols)
    feed_weights = lax.all_gather(feed_rows, "seq", axis=0, tiled=True)

    tok_float = tokens.astype(jnp.float32)
    inverse_one = lax.rsqrt(jnp.mean(tok_float * tok_float, axis=-1, keepdims=True) + NORM_EPS)
    normed = (tok_float * inverse_one * gains[0]).astype(jnp.bfloat16)
    projected = jnp.dot(normed, attn_weights[:, :value_end], preferred_element_type=jnp.float32)
    queries = rotate(projected[:, :query_cols].reshape(rows_here, NH, HD), local_place, 1.0).astype(
        jnp.bfloat16
    )
    key_rows = (
        rotate(
            projected[:, query_cols : query_cols + HD].reshape(rows_here, 1, HD), local_place, 1.0
        )
        .reshape(rows_here, HD)
        .astype(jnp.bfloat16)
    )
    value_rows = projected[:, query_cols + HD : value_end].astype(jnp.bfloat16)
    queries, pairs, segments, normed_plane = exchange(
        0,
        [
            to_heads(queries.reshape(rows_here, query_cols)),
            gather_axis("seq", jnp.concatenate([key_rows, value_rows], axis=1)),
            gather_axis("seq", segment_ids.reshape(-1, tile_width)),
            (gather_plane(normed.shape), normed),
        ],
    )
    pairs = pairs.reshape(-1, 2 * HD)
    segments = segments.reshape(-1).astype(jnp.float32)
    head_context, log_totals = attend(queries, pairs, segments)
    context, cot_plane = exchange(
        1, [to_tokens(head_context), (gather_plane(cotangent.shape), cotangent)]
    )
    normed_plane = normed_plane.reshape(-1, MODEL_WIDTH)
    cot_plane = cot_plane.reshape(-1, MODEL_WIDTH)
    branch = jnp.dot(
        context, attn_weights[:, value_end:], preferred_element_type=jnp.float32
    )
    hidden = tok_float + branch
    inverse_two = lax.rsqrt(jnp.mean(hidden * hidden, axis=-1, keepdims=True) + NORM_EPS)
    normed_two = (hidden * inverse_two * gains[1]).astype(jnp.bfloat16)

    (second_plane,) = exchange(2, [(gather_plane(normed_two.shape), normed_two)])
    second_plane = second_plane.reshape(-1, MODEL_WIDTH)
    gating_weights = feed_weights[:, : 2 * share_cols]
    down_weights = feed_weights[:, 2 * share_cols :]
    gate_up = jnp.dot(second_plane, gating_weights, preferred_element_type=jnp.float32)
    gate = gate_up[:, :share_cols]
    upper = gate_up[:, share_cols:]
    sigmoid_gate = jax.nn.sigmoid(gate)
    silu_gate = jax.nn.silu(gate)
    activated = (silu_gate * upper).astype(jnp.bfloat16)
    feed_part = times_transpose(activated, down_weights).astype(jnp.bfloat16)
    feed_part, cot_plane = lax.optimization_barrier((feed_part, cot_plane))
    feed_out = lax.psum_scatter(feed_part, "grp", scatter_dimension=0, tiled=True)
    act_grad = jnp.dot(cot_plane, down_weights, preferred_element_type=jnp.float32)
    gate_grad = (act_grad * upper * sigmoid_gate * (1.0 + gate * (1.0 - sigmoid_gate))).astype(
        jnp.bfloat16
    )
    up_grad = (act_grad * silu_gate).astype(jnp.bfloat16)
    gating_grad = jnp.concatenate([gate_grad, up_grad], axis=1)
    two_part = times_transpose(gating_grad, gating_weights).astype(jnp.bfloat16)
    feed_grads = jnp.concatenate(
        [contract(second_plane, gating_grad), contract(cot_plane, activated)], axis=1
    ).astype(jnp.bfloat16)
    two_part, feed_grads = lax.optimization_barrier((two_part, feed_grads))
    feed_grads = lax.psum_scatter(feed_grads, "seq", scatter_dimension=0, tiled=True)
    norm_two_grad = plane_sum(3, two_part)

    out_grad = cotangent.astype(jnp.float32)
    gain_two_term = jnp.sum(norm_two_grad * hidden * inverse_two, axis=0)
    hidden_grad = (
        out_grad
        + inverse_two * gains[1] * norm_two_grad
        - hidden
        * inverse_two**3
        * jnp.mean(hidden * gains[1] * norm_two_grad, axis=-1, keepdims=True)
    )
    branch_grad = hidden_grad.astype(jnp.bfloat16)
    context_grad = times_transpose(branch_grad, attn_weights[:, value_end:]).astype(jnp.bfloat16)
    head_grads, context_plane = exchange(
        4, [to_heads(context_grad), (gather_plane(context.shape), context)]
    )
    head_query_grad, pair_part = attend_back(
        queries,
        pairs,
        head_grads,
        log_totals,
        segments,
        turn_tables(jnp.arange(SEQLEN, dtype=jnp.int32)),
    )
    query_grad, pair_parts, branch_share = exchange(
        5,
        [
            to_tokens(head_query_grad),
            split_rows("seq", pair_part),
            split_columns("grp", branch_grad),
        ],
    )
    query_grad, feed_grads, feed_out = lax.optimization_barrier((query_grad, feed_grads, feed_out))
    block_out = (hidden + feed_out.astype(jnp.float32)).astype(jnp.bfloat16)
    feed_grads = jnp.transpose(
        feed_grads.reshape(rows_block, 3 * share, tile_width), (1, 0, 2)
    )
    feed_grads = lax.all_gather(feed_grads, "grp", axis=0, tiled=True)
    pair_grad = jnp.sum(pair_parts.astype(jnp.float32), axis=0).astype(jnp.bfloat16)
    projected_grad = jnp.concatenate([query_grad, pair_grad], axis=1)
    norm_one_grad = times_transpose(projected_grad, attn_weights[:, :value_end])
    gain_one_term = jnp.sum(norm_one_grad * tok_float * inverse_one, axis=0)
    input_grad = (
        hidden_grad
        + inverse_one * gains[0] * norm_one_grad
        - tok_float
        * inverse_one**3
        * jnp.mean(tok_float * gains[0] * norm_one_grad, axis=-1, keepdims=True)
    )
    query_share, pair_plane, gain_parts = exchange(
        6,
        [
            split_columns("grp", query_grad),
            gather_axis("grp", pair_grad),
            gather_axis("grp", jnp.stack([gain_one_term, gain_two_term])),
        ],
    )
    gain_plane = jnp.sum(gain_parts, axis=0)
    share_width = MODEL_WIDTH // grp_count
    normed_rows = lax.dynamic_slice_in_dim(
        normed_plane.reshape(-1, seq_count, grp_count, sub_rows), grp_here, 1, axis=2
    ).reshape(-1, seq_count * sub_rows)
    query_weight_grad = contract(normed_plane, query_share.reshape(-1, share_width))
    out_weight_grad = contract(
        context_plane.reshape(-1, MODEL_WIDTH), branch_share.reshape(-1, share_width)
    )
    pair_weight_grad = contract(normed_rows, pair_plane.reshape(-1, 2 * HD))
    shares = jnp.concatenate([query_weight_grad, out_weight_grad], axis=1).astype(jnp.bfloat16)
    share_parts, pair_parts, gain_parts = exchange(
        7,
        [
            split_rows("seq", shares),
            split_rows("seq", pair_weight_grad.astype(jnp.bfloat16)),
            gather_axis("seq", gain_plane),
        ],
    )
    gain_grads = jnp.sum(gain_parts, axis=0)
    shares = jnp.sum(share_parts.astype(jnp.float32), axis=0).astype(jnp.bfloat16)
    pair_rows = jnp.sum(pair_parts.astype(jnp.float32), axis=0).astype(jnp.bfloat16)
    share_plane, pair_weight = exchange(
        8,
        [(gather_plane(shares.shape), shares), (gather_plane(pair_rows.shape), pair_rows)],
    )
    query_tiles, out_tiles = [
        jnp.transpose(
            half.reshape(grp_count, rows_block, share_width // tile_width, tile_width),
            (0, 2, 1, 3),
        ).reshape(-1, rows_block, tile_width)
        for half in (share_plane[:, :, :share_width], share_plane[:, :, share_width:])
    ]
    pair_tiles = jnp.transpose(pair_weight.reshape(rows_block, 2, tile_width), (1, 0, 2))
    attn_grads = jnp.concatenate([query_tiles, pair_tiles, out_tiles], axis=0)

    tile_count = tile_owner_slots.shape[0]
    tile_of_slot = (
        jnp.full((grp_count * slots_here,), tile_count, jnp.int32)
        .at[tile_owner_slots]
        .set(jnp.arange(tile_count, dtype=jnp.int32))
    )
    tiles_here = lax.dynamic_slice_in_dim(tile_of_slot, grp_here * slots_here, slots_here)
    feed_at = jnp.clip(tiles_here - attn_tiles, 0, 3 * hidden_tiles - 1)
    which, column = feed_at // hidden_tiles, feed_at % hidden_tiles
    feed_at = (column // share) * (3 * share) + which * share + column % share
    picked = jnp.where(
        (tiles_here < attn_tiles)[:, None, None],
        attn_grads[jnp.minimum(tiles_here, attn_tiles - 1)],
        feed_grads[feed_at],
    )
    reduced_sum = jnp.where((tiles_here < tile_count)[:, None, None], picked, 0).astype(jnp.float32)
    turned = jnp.einsum("zji,zjc->zic", left_basis_set, reduced_sum)
    turned = jnp.einsum("zic,zcd->zid", turned, right_basis_set)
    new_one = BETA_ONE * moment_one + (1.0 - BETA_ONE) * turned
    new_two = BETA_TWO * moment_two + (1.0 - BETA_TWO) * turned * turned
    scaled = new_one / (jnp.sqrt(new_two) + ADAM_EPS)
    restored = jnp.einsum("zij,zjd->zid", left_basis_set, scaled)
    restored = jnp.einsum("zid,zed->zie", restored, right_basis_set)
    new_master = master * (1.0 - LEARN_RATE * WEIGHT_DECAY) - LEARN_RATE * restored
    gain_one = BETA_ONE * gain_moment_one + (1.0 - BETA_ONE) * gain_grads
    gain_two = BETA_TWO * gain_moment_two + (1.0 - BETA_TWO) * gain_grads * gain_grads
    new_gains = gains - GAIN_RATE * gain_one / (jnp.sqrt(gain_two) + ADAM_EPS)
    return (
        block_out,
        input_grad,
        new_master,
        new_one,
        new_two,
        gain_grads,
        new_gains,
        gain_one,
        gain_two,
    )


def solution(mesh):
    return jax.shard_map(
        local,
        mesh=mesh,
        in_specs=(
            P(("grp", "seq"), None),
            P(("grp", "seq"), None),
            P(("grp", "seq")),
            P(),
            P("grp", "seq", None),
            P("grp", "seq", None),
            P("grp", "seq", None),
            P("grp", "seq", None),
            P("grp", "seq", None),
            P("grp", "seq", None),
            P(),
            P(),
            P(),
        ),
        out_specs=(
            P(("grp", "seq"), None),
            P(("grp", "seq"), None),
            P("grp", "seq", None),
            P("grp", "seq", None),
            P("grp", "seq", None),
            P(),
            P(),
            P(),
            P(),
        ),
        check_vma=False,
    )
```

```python
import functools

import jax
import jax.numpy as jnp
from jax import lax
from jax.experimental import pallas as pl
from jax.experimental.pallas import tpu as pltpu
from jax.sharding import PartitionSpec as P

MODEL_WIDTH = 2048
NH = 16
HD = 128
FF = 5632
SEQLEN = 1024


NORM_EPS = 1e-05
BETA_ONE = 0.95
BETA_TWO = 0.95
ADAM_EPS = 1e-08
WEIGHT_DECAY = 0.01
LEARN_RATE = 0.03
GAIN_RATE = 1.5
ROPE_BASE = 10000.0
MASKED = -1e30
PRECISE = lax.Precision.HIGHEST


def contract(left_side, right_side):
    return lax.dot_general(
        left_side, right_side, (((0,), (0,)), ((), ())), preferred_element_type=jnp.float32
    )


def times_transpose(left_side, right_side):
    return lax.dot_general(
        left_side, right_side, (((1,), (1,)), ((), ())), preferred_element_type=jnp.float32
    )


def turn_tables(places):
    half_width = HD // 2
    frequency = ROPE_BASE ** (-(jnp.arange(half_width, dtype=jnp.float32) * 2.0) / HD)
    angles = places.astype(jnp.float32)[:, None] * frequency[None, :]
    cosine, sine = jnp.cos(angles), jnp.sin(angles)
    return (
        jnp.concatenate([cosine, cosine], axis=1),
        jnp.concatenate([-sine, sine], axis=1),
    )


def turn(rows, cosine, sine):
    return rows * cosine + pltpu.roll(rows, HD // 2, 1) * sine


def turn_back(rows, cosine, sine):
    return rows * cosine - pltpu.roll(rows, HD // 2, 1) * sine


def dot_last(left_side, right_side):
    return lax.dot_general(
        left_side, right_side, (((1,), (1,)), ((), ())), preferred_element_type=jnp.float32
    )


def dot_first(left_side, right_side):
    return lax.dot_general(
        left_side, right_side, (((0,), (0,)), ((), ())), preferred_element_type=jnp.float32
    )


def project_kernel(x_ref, w_ref, cosine_ref, sine_ref, out_ref):
    made = jnp.dot(x_ref[...], w_ref[...], preferred_element_type=jnp.float32)
    cosine, sine = cosine_ref[...], sine_ref[...]
    first, second = made[:, :HD], made[:, HD:]
    last = pl.program_id(0) == pl.num_programs(0) - 1
    out_ref[:, :HD] = turn(first, cosine, sine).astype(out_ref.dtype)
    out_ref[:, HD:] = jnp.where(last, second, turn(second, cosine, sine)).astype(out_ref.dtype)


def project(normed, weights, tables):
    rows, width = normed.shape
    steps = NH // 2 + 1
    return pl.pallas_call(
        project_kernel,
        grid=(steps,),
        in_specs=[
            pl.BlockSpec((rows, width), lambda j: (0, 0)),
            pl.BlockSpec((width, 2 * HD), lambda j: (0, j)),
            pl.BlockSpec((rows, HD), lambda j: (0, 0)),
            pl.BlockSpec((rows, HD), lambda j: (0, 0)),
        ],
        out_specs=pl.BlockSpec((rows, 2 * HD), lambda j: (0, j)),
        out_shape=jax.ShapeDtypeStruct((rows, steps * 2 * HD), jnp.bfloat16),
        compiler_params=pltpu.CompilerParams(vmem_limit_bytes=32 * 2**20),
        cost_estimate=pl.CostEstimate(
            flops=4 * rows * width * steps * HD,
            bytes_accessed=4 * width * steps * HD,
            transcendentals=0,
        ),
        name="project",
    )(normed, weights, *tables)


def score_mask(key_seg_ref, query_seg_ref, block, rows):
    keys = (block + 1) * rows
    same = key_seg_ref[:keys, :] == query_seg_ref[...]
    key_at = lax.broadcasted_iota(jnp.int32, (keys, rows), 0)
    query_at = lax.broadcasted_iota(jnp.int32, (keys, rows), 1) + block * rows
    return same & (key_at <= query_at)


def attend_kernel(at_ref, q_ref, k_ref, v_ref, key_seg_ref, query_seg_ref, context_ref, total_ref):
    scale = HD ** (-0.5)
    rows = q_ref.shape[0]
    for block in range(SEQLEN // rows):

        @pl.when(at_ref[0] == block)
        def _():
            keys = (block + 1) * rows
            scores = dot_last(k_ref[:keys, :], q_ref[...]) * scale
            scores = jnp.where(
                score_mask(key_seg_ref, query_seg_ref, block, rows), scores, MASKED
            )
            highest = jnp.max(scores, axis=0, keepdims=True)
            exponent = jnp.exp(scores - highest)
            totals = jnp.sum(exponent, axis=0, keepdims=True)
            probs_low = (exponent * (1.0 / totals)).astype(jnp.bfloat16)
            context = dot_first(probs_low, v_ref[:keys, :])
            context_ref[...] = context.astype(jnp.bfloat16)
            total_ref[0] = highest + jnp.log(totals)


def attend_back_kernel(
    at_ref,
    q_ref,
    k_ref,
    v_ref,
    grad_ref,
    total_ref,
    key_seg_ref,
    query_seg_ref,
    key_cosine_ref,
    key_sine_ref,
    cosine_ref,
    sine_ref,
    query_grad_ref,
    pair_grad_ref,
    key_sum,
    value_sum,
):
    scale = HD ** (-0.5)
    rows = q_ref.shape[0]
    head = pl.program_id(0)

    @pl.when(head == 0)
    def _():
        key_sum[...] = jnp.zeros_like(key_sum)
        value_sum[...] = jnp.zeros_like(value_sum)

    for block in range(SEQLEN // rows):

        @pl.when(at_ref[0] == block)
        def _():
            keys = (block + 1) * rows
            queries, grads = q_ref[...], grad_ref[...]
            shifted = dot_last(k_ref[:keys, :], queries) * scale - total_ref[0]
            allowed = score_mask(key_seg_ref, query_seg_ref, block, rows)
            probs = jnp.where(allowed, jnp.exp(shifted), 0.0)
            prob_grad = dot_last(v_ref[:keys, :], grads)
            centre = jnp.sum(probs * prob_grad, axis=0, keepdims=True)
            score_grad = (probs * (prob_grad - centre) * scale).astype(jnp.bfloat16)
            value_sum[:keys, :] += jnp.dot(
                probs.astype(jnp.bfloat16), grads, preferred_element_type=jnp.float32
            )
            key_sum[:keys, :] += jnp.dot(score_grad, queries, preferred_element_type=jnp.float32)
            query_grad = dot_first(score_grad, k_ref[:keys, :])
            query_grad_ref[...] = turn_back(query_grad, cosine_ref[...], sine_ref[...]).astype(
                jnp.bfloat16
            )

    @pl.when(head == pl.num_programs(0) - 1)
    def _():
        pair_grad_ref[:, :HD] = turn_back(
            key_sum[...], key_cosine_ref[...], key_sine_ref[...]
        ).astype(jnp.bfloat16)
        pair_grad_ref[:, HD:] = value_sum[...].astype(jnp.bfloat16)


def attention_specs(kinds, rows):
    specs = {
        "at": pl.BlockSpec(memory_space=pltpu.SMEM),
        "head": pl.BlockSpec((rows, HD), lambda h: (0, h)),
        "keys": pl.BlockSpec((SEQLEN, HD), lambda h: (0, 0)),
        "values": pl.BlockSpec((SEQLEN, HD), lambda h: (0, 1)),
        "pair": pl.BlockSpec((SEQLEN, 2 * HD), lambda h: (0, 0)),
        "total": pl.BlockSpec((1, 1, rows), lambda h: (h, 0, 0)),
        "key_seg": pl.BlockSpec((SEQLEN, 1), lambda h: (0, 0)),
        "query_seg": pl.BlockSpec((1, rows), lambda h: (0, 0)),
        "key_table": pl.BlockSpec((SEQLEN, HD), lambda h: (0, 0)),
        "table": pl.BlockSpec((rows, HD), lambda h: (0, 0)),
    }
    return [specs[kind] for kind in kinds]


def attend(at, projected, pairs, key_segs, query_segs):
    rows = projected.shape[0]
    columns = NH * HD
    return pl.pallas_call(
        attend_kernel,
        grid=(NH,),
        in_specs=attention_specs(["at", "head", "keys", "values", "key_seg", "query_seg"], rows),
        out_specs=attention_specs(["head", "total"], rows),
        out_shape=(
            jax.ShapeDtypeStruct((rows, columns), jnp.bfloat16),
            jax.ShapeDtypeStruct((NH, 1, rows), jnp.float32),
        ),
        compiler_params=pltpu.CompilerParams(vmem_limit_bytes=32 * 2**20),
        cost_estimate=pl.CostEstimate(
            flops=4 * rows * SEQLEN * columns,
            bytes_accessed=6 * rows * columns,
            transcendentals=rows * SEQLEN * NH,
        ),
        name="attend",
    )(at, projected, pairs, pairs, key_segs[:, None], query_segs[None, :])


def attend_back(at, projected, pairs, grads, totals, key_segs, query_segs, key_tables, tables):
    rows = projected.shape[0]
    columns = NH * HD
    return pl.pallas_call(
        attend_back_kernel,
        grid=(NH,),
        in_specs=attention_specs(
            ["at", "head", "keys", "values", "head", "total", "key_seg", "query_seg"]
            + ["key_table", "key_table", "table", "table"],
            rows,
        ),
        out_specs=attention_specs(["head", "pair"], rows),
        out_shape=(
            jax.ShapeDtypeStruct((rows, columns), jnp.bfloat16),
            jax.ShapeDtypeStruct((SEQLEN, 2 * HD), jnp.bfloat16),
        ),
        scratch_shapes=[pltpu.VMEM((SEQLEN, HD), jnp.float32)] * 2,
        compiler_params=pltpu.CompilerParams(vmem_limit_bytes=32 * 2**20),
        cost_estimate=pl.CostEstimate(
            flops=10 * rows * SEQLEN * columns,
            bytes_accessed=10 * rows * columns,
            transcendentals=rows * SEQLEN * NH,
        ),
        name="attend_back",
    )(
        at, projected, pairs, pairs, grads, totals, key_segs[:, None], query_segs[None, :],
        *key_tables, *tables,
    )


def pick_kernel(rows, feed_ref, attn_ref, tiles_ref, feed_out, attn_out, sems):
    grp = lax.axis_index("grp")
    width = tiles_ref.shape[2]
    copies = []
    for at in range(feed_ref.shape[0]):
        copies.append(
            (tiles_ref.at[feed_ref[at]], feed_out.at[:, at * width : (at + 1) * width])
        )
    share = pl.ds(pl.multiple_of(grp * rows, rows), rows)
    for at in range(attn_ref.shape[0]):
        copies.append(
            (tiles_ref.at[attn_ref[at], share], attn_out.at[:, at * width : (at + 1) * width])
        )
    copies = [
        pltpu.make_async_copy(source, target, sems.at[at])
        for at, (source, target) in enumerate(copies)
    ]
    for copy in copies:
        copy.start()
    for copy in copies:
        copy.wait()


def pick(tiles, feed_slots, attn_slots):
    _, rows, width = tiles.shape
    share = rows // lax.axis_size("grp")
    feed, attn = feed_slots.shape[0], attn_slots.shape[0]
    return pl.pallas_call(
        functools.partial(pick_kernel, share),
        in_specs=[pl.BlockSpec(memory_space=pltpu.SMEM)] * 2 + [pl.BlockSpec(memory_space=pl.ANY)],
        out_specs=[pl.BlockSpec(memory_space=pl.ANY)] * 2,
        out_shape=[
            jax.ShapeDtypeStruct((rows, feed * width), tiles.dtype),
            jax.ShapeDtypeStruct((share, attn * width), tiles.dtype),
        ],
        scratch_shapes=[pltpu.SemaphoreType.DMA((feed + attn,))],
        cost_estimate=pl.CostEstimate(
            flops=0, bytes_accessed=4 * (rows * feed + share * attn) * width, transcendentals=0
        ),
        name="pick",
    )(feed_slots, attn_slots, tiles)


def adam_kernel(
    at_ref, gate_ref, up_ref, down_ref, share_ref, pair_ref, left_ref, right_ref, master_ref,
    one_ref, two_ref, new_master_ref, new_one_ref, new_two_ref, grad,
):
    kind = at_ref[0, pl.program_id(0)]
    for number, ref in enumerate((gate_ref, up_ref, down_ref, share_ref, pair_ref)):

        @pl.when(kind == number)
        def _():
            grad[...] = ref[...].reshape(grad.shape)

    @pl.when(kind == 5)
    def _():
        grad[...] = jnp.zeros_like(grad)

    low = jnp.bfloat16
    left, right = left_ref[0].astype(low), right_ref[0].astype(low)
    turned = dot_first(grad[...], left)
    turned = dot_first(turned.astype(low), right)
    new_one = BETA_ONE * one_ref[0] + (1.0 - BETA_ONE) * turned
    new_two = BETA_TWO * two_ref[0] + (1.0 - BETA_TWO) * turned * turned
    new_one_ref[0], new_two_ref[0] = new_one, new_two
    scaled = new_one / (jnp.sqrt(new_two) + ADAM_EPS)
    restored = dot_last(scaled.astype(low), right)
    restored = jnp.dot(left, restored.astype(low), preferred_element_type=jnp.float32)
    new_master_ref[0] = master_ref[0] * (1.0 - LEARN_RATE * WEIGHT_DECAY) - LEARN_RATE * restored


def adam(at, gate, up, down, shares, pairs, left, right, master, one, two):
    slots, rows, width = master.shape
    tile = pl.BlockSpec((1, rows, width), lambda i, at: (i, 0, 0))
    shape = jax.ShapeDtypeStruct(master.shape, jnp.float32)
    feed = pl.BlockSpec((1, rows, width), lambda i, at: (at[1, i], 0, at[2, i]))
    return pl.pallas_call(
        adam_kernel,
        grid_spec=pltpu.PrefetchScalarGridSpec(
            num_scalar_prefetch=1,
            grid=(slots,),
            in_specs=[
                feed,
                feed,
                feed,
                pl.BlockSpec((1, rows, width), lambda i, at: (at[3, i], 0, at[4, i])),
                pl.BlockSpec((*pairs.shape[:2], width), lambda i, at: (0, 0, at[5, i])),
                pl.BlockSpec((1, rows, rows), lambda i, at: (i, 0, 0)),
                pl.BlockSpec((1, width, width), lambda i, at: (i, 0, 0)),
                tile,
                tile,
                tile,
            ],
            out_specs=[tile] * 3,
            scratch_shapes=[pltpu.VMEM((rows, width), jnp.bfloat16)],
        ),
        out_shape=[shape] * 3,
        compiler_params=pltpu.CompilerParams(vmem_limit_bytes=32 * 2**20),
        cost_estimate=pl.CostEstimate(
            flops=4 * slots * rows * width * (rows + width),
            bytes_accessed=4 * slots * rows * (rows + 6 * width),
            transcendentals=slots * rows * width,
        ),
        name="adam",
    )(at, gate, up, down, shares, pairs, left, right, master, one, two)


MESH = pl.DeviceIdType.MESH


def remote(source, target, sems, at, device):
    return pltpu.make_async_remote_copy(
        src_ref=source,
        dst_ref=target,
        send_sem=sems[0].at[at],
        recv_sem=sems[1].at[at],
        device_id=device,
        device_id_type=MESH,
    )


def columns_of(ref, index, width):
    return ref.at[:, pl.ds(pl.multiple_of(index * width, width), width)]


def rows_of(ref, index, height):
    return ref.at[pl.ds(pl.multiple_of(index * height, height), height), :]


class Exchange:
    def __init__(self, axis, out_shape, source_view, target_view):
        self.axis, self.out_shape = axis, out_shape
        self.source_view, self.target_view = source_view, target_view
        self.count = lax.axis_size(axis)
        self.sem_count = self.count

    def peers(self, grp, seq):
        me = grp if self.axis == "grp" else seq
        for step in range(1, self.count):
            there = (me + step) % self.count
            yield (there, seq) if self.axis == "grp" else (grp, there)

    def start(self, source, target, sems, grp, seq):
        me = grp if self.axis == "grp" else seq
        self.own = pltpu.make_async_copy(
            self.source_view(source, me), self.target_view(target, me), sems[0].at[0]
        )
        self.own.start()
        self.sent, self.due = [], []
        for step, device in enumerate(self.peers(grp, seq), 1):
            there = (me + step) % self.count
            back = (me + self.count - step) % self.count
            copy = remote(
                self.source_view(source, there), self.target_view(target, me), sems, step, device
            )
            copy.start()
            self.sent.append(copy)
            self.due.append(
                remote(
                    self.source_view(source, back), self.target_view(target, back), sems, step, device
                )
            )

    def forward(self):
        pass

    def finish(self):
        for copy in self.due:
            copy.wait_recv()
        for copy in self.sent:
            copy.wait_send()
        self.own.wait()


class PlaneGather:
    axis = "grp"
    sem_count = 14

    def __init__(self, out_shape, source_view, target_view, half_of):
        self.out_shape = out_shape
        self.source_view, self.target_view, self.half_of = source_view, target_view, half_of

    def around(self, grp):
        core, across_x, across_y = grp % 2, (grp // 2) % 2, grp // 4
        return grp + 1 - 2 * core, grp + 2 - 4 * across_x, grp + 4 - 8 * across_y

    def peers(self, grp, seq):
        for other in self.around(grp):
            yield other, seq

    def start(self, source, target, sems, grp, seq):
        core, side_x, side_y = self.around(grp)

        def part(block, piece):
            view = self.target_view(target, block)
            return view if piece == "all" else self.half_of(view, piece == "b")

        def own(piece):
            view = self.source_view(source, grp)
            return view if piece == "all" else self.half_of(view, piece == "b")

        def across(block):
            return self.around(self.around(block)[1])[2]

        def make(at, block, piece, via, first=False):
            view = own(piece) if first else part(block, piece)
            return remote(view, part(block, piece), sems, at, (via, seq))

        self.out = [
            make(1, grp, "a", side_x, True),
            make(2, grp, "b", side_x, True),
            make(3, side_y, "b", side_x),
            make(4, grp, "b", side_y, True),
            make(5, grp, "a", side_y, True),
            make(6, side_x, "a", side_y),
            make(7, grp, "all", core, True),
            make(8, side_x, "a", core),
            make(9, side_x, "b", core),
            make(10, side_y, "b", core),
            make(11, side_y, "a", core),
            make(12, across(grp), "a", core),
            make(13, across(grp), "b", core),
        ]
        self.due = [
            make(1, side_x, "a", side_x),
            make(2, side_x, "b", side_x),
            make(3, across(grp), "b", side_x),
            make(4, side_y, "b", side_y),
            make(5, side_y, "a", side_y),
            make(6, across(grp), "a", side_y),
            make(7, core, "all", core),
            make(8, self.around(core)[1], "a", core),
            make(9, self.around(core)[1], "b", core),
            make(10, self.around(core)[2], "b", core),
            make(11, self.around(core)[2], "a", core),
            make(12, across(core), "a", core),
            make(13, across(core), "b", core),
        ]
        self.kept = pltpu.make_async_copy(own("all"), part(grp, "all"), sems[0].at[0])
        self.kept.start()
        for at in (1, 4, 2, 5, 7):
            self.out[at - 1].start()

    def forward(self):
        for came, then in ((1, (6, 8)), (4, (3, 10)), (2, (9,)), (5, (11,)), (6, (12,)), (3, (13,))):
            self.due[came - 1].wait_recv()
            for at in then:
                self.out[at - 1].start()

    def finish(self):
        for copy in self.due[6:]:
            copy.wait_recv()
        for copy in self.out:
            copy.wait_send()
        self.kept.wait()


def half_rows(axis, height):
    def half_of(view, second):
        index = (slice(None),) * axis + (pl.ds(height if second else 0, height),)
        return view.at[index]

    return half_of


def whole(ref, index):
    return ref


def block_of(ref, index):
    return ref.at[index]


def gather_plane(shape, split=0, source_view=whole, target_view=block_of, out_shape=None):
    out_shape = out_shape or (lax.axis_size("grp"), *shape)
    if lax.axis_size("grp") == 8:
        return PlaneGather(out_shape, source_view, target_view, half_rows(split, shape[split] // 2))
    return Exchange("grp", out_shape, source_view, target_view)


def exchange_kernel(tasks, wires, arrays, outputs, *refs):
    sources, targets = refs[:arrays], refs[arrays : arrays + outputs]
    sems = refs[arrays + outputs :]
    grp, seq = lax.axis_index("grp"), lax.axis_index("seq")
    barrier = pltpu.get_barrier_semaphore()
    axes = {"grp": [], "seq": []}
    for task in tasks:
        devices = list(task.peers(grp, seq))
        if len(devices) > len(axes[task.axis]):
            axes[task.axis] = devices
    devices = axes["grp"] + axes["seq"]
    for device in devices:
        pl.semaphore_signal(barrier, inc=1, device_id=device, device_id_type=MESH)
    pl.semaphore_wait(barrier, len(devices))

    def start(at):
        after, source, target = wires[at]
        source = targets[source] if after is not None else sources[source]
        tasks[at].start(source, targets[target], sems[2 * at : 2 * at + 2], grp, seq)

    open_tasks = list(range(len(tasks)))
    first = [at for at in open_tasks if wires[at][0] is None]
    for at in first:
        start(at)
    for at in first:
        tasks[at].forward()
    for at in open_tasks[:]:
        after = wires[at][0]
        if after is not None:
            tasks[after].finish()
            open_tasks.remove(after)
            start(at)
            tasks[at].forward()
    for at in open_tasks:
        tasks[at].finish()


def exchange(number, work):
    tasks = [piece[0] for piece in work]
    arrays, shapes, wires = [], [], []
    for piece in work:
        if isinstance(piece[1], int):
            after, source = piece[1], wires[piece[1]][2]
            kind = shapes[source].dtype
        else:
            after, source = None, len(arrays)
            arrays.append(piece[1])
            kind = piece[1].dtype
        if len(piece) == 3:
            target = wires[piece[2]][2]
        else:
            target = len(shapes)
            shapes.append(jax.ShapeDtypeStruct(piece[0].out_shape, kind))
        wires.append((after, source, target))
    scratch = []
    for task in tasks:
        scratch += [pltpu.SemaphoreType.DMA((task.sem_count,))] * 2
    return pl.pallas_call(
        functools.partial(exchange_kernel, tasks, wires, len(arrays), len(shapes)),
        in_specs=[pl.BlockSpec(memory_space=pl.ANY)] * len(arrays),
        out_specs=[pl.BlockSpec(memory_space=pl.ANY)] * len(shapes),
        out_shape=shapes,
        scratch_shapes=scratch,
        compiler_params=pltpu.CompilerParams(collective_id=number, has_side_effects=True),
        name="exchange",
    )(*arrays)


def gather_axis(axis, array):
    task = Exchange(axis, (lax.axis_size(axis), *array.shape), whole, block_of)
    return task, array


def split_rows(axis, array):
    count = lax.axis_size(axis)
    rows, columns = array.shape
    height = rows // count
    task = Exchange(
        axis,
        (count, height, columns),
        lambda ref, index: rows_of(ref, index, height),
        block_of,
    )
    return task, array


def split_columns(axis, array):
    count = lax.axis_size(axis)
    rows, columns = array.shape
    width = columns // count
    task = Exchange(
        axis,
        (count, rows, width),
        lambda ref, index: columns_of(ref, index, width),
        block_of,
    )
    return task, array


def add_rows(total, first, second):
    step = 32

    def some(at, _):
        rows = pl.ds(pl.multiple_of(at * step, step), step)
        total[rows, :] = (
            first[rows, :].astype(jnp.float32) + second[rows, :].astype(jnp.float32)
        ).astype(total.dtype)
        return 0

    lax.fori_loop(0, total.shape[0] // step, some, 0)


def plane_sum_kernel(
    part_ref, total_ref, core_in, chip, half_x, half_y, whole_x, whole_y, send_sems, recv_sems
):
    grp, seq = lax.axis_index("grp"), lax.axis_index("seq")

    def around(device):
        core, across_x, across_y = device % 2, (device // 2) % 2, device // 4
        return device + 1 - 2 * core, device + 2 - 4 * across_x, device + 4 - 8 * across_y

    def order(device):
        _, side_x, side_y = around(device)
        return around(side_x)[2], side_x, side_y, device

    core, side_x, side_y = around(grp)
    half = total_ref.shape[0] // 2
    low, high = pl.ds(0, half), pl.ds(half, half)
    barrier = pltpu.get_barrier_semaphore()
    for device in (core, side_x, side_y):
        pl.semaphore_signal(barrier, inc=1, device_id=(device, seq), device_id_type=MESH)
    pl.semaphore_wait(barrier, 3)

    sems = (send_sems, recv_sems)
    copies = [
        remote(part_ref.at[block], core_in.at[at], sems, at, (core, seq))
        for at, block in enumerate(order(core))
    ]
    copies += [
        remote(chip.at[0, low], half_x, sems, 4, (side_x, seq)),
        remote(chip.at[0, high], half_y, sems, 5, (side_y, seq)),
        remote(chip.at[1, low], whole_x.at[low], sems, 6, (side_x, seq)),
        remote(chip.at[2, high], whole_y.at[high], sems, 7, (side_y, seq)),
        remote(chip.at[1, high], whole_x.at[high], sems, 8, (side_x, seq)),
        remote(chip.at[2, low], whole_y.at[low], sems, 9, (side_y, seq)),
    ]
    for copy in copies[:4]:
        copy.start()
    blocks = order(grp)
    for at, then in ((0, (4, 5)), (1, (6,)), (2, (7,))):
        copies[at].wait_recv()
        add_rows(chip.at[at], part_ref.at[blocks[at]], core_in.at[at])
        for start in then:
            copies[start].start()
    copies[5].wait_recv()
    add_rows(chip.at[1, high], chip.at[1, high], half_y)
    copies[8].start()
    copies[4].wait_recv()
    add_rows(chip.at[2, low], chip.at[2, low], half_x)
    copies[9].start()
    copies[3].wait_recv()
    add_rows(total_ref, part_ref.at[blocks[3]], core_in.at[3])
    for at, came in ((6, whole_x.at[low]), (7, whole_y.at[high]), (8, whole_x.at[high]), (9, whole_y.at[low])):
        copies[at].wait_recv()
        rows = low if at in (6, 9) else high
        add_rows(total_ref.at[rows], total_ref.at[rows], came)
    for copy in copies:
        copy.wait_send()


def plane_sum(number, part):
    count = lax.axis_size("grp")
    rows_all, columns = part.shape
    rows = rows_all // count
    if count != 8:
        return lax.psum_scatter(part, "grp", scatter_dimension=0, tiled=True).astype(jnp.float32)
    low = jnp.bfloat16
    return pl.pallas_call(
        plane_sum_kernel,
        in_specs=[pl.BlockSpec(memory_space=pltpu.VMEM)],
        out_specs=pl.BlockSpec(memory_space=pltpu.VMEM),
        out_shape=jax.ShapeDtypeStruct((rows, columns), jnp.float32),
        scratch_shapes=[
            pltpu.VMEM((4, rows, columns), low),
            pltpu.VMEM((3, rows, columns), low),
            pltpu.VMEM((rows // 2, columns), low),
            pltpu.VMEM((rows // 2, columns), low),
            pltpu.VMEM((rows, columns), low),
            pltpu.VMEM((rows, columns), low),
            pltpu.SemaphoreType.DMA((10,)),
            pltpu.SemaphoreType.DMA((10,)),
        ],
        compiler_params=pltpu.CompilerParams(
            collective_id=number, has_side_effects=True, vmem_limit_bytes=40 * 2**20
        ),
        name="plane_sum",
    )(part.reshape(count, rows, columns))


def behind_gather(array):
    if lax.axis_size("grp") != 8:
        return lax.all_gather(array, "grp", axis=0, tiled=True)
    half = array.shape[0] // 2

    def via(values, bit):
        return lax.ppermute(values, "grp", [(at, at ^ bit) for at in range(8)])

    from_x, from_y = via(array, 2), via(array, 4)
    across = jnp.concatenate([via(from_x[:half], 4), via(from_y[half:], 2)], axis=0)
    chip = jnp.concatenate([array, from_x, from_y, across], axis=0)
    return jnp.concatenate([chip, via(chip, 1)], axis=0)


def behind_order():
    grp = lax.axis_index("grp")
    if lax.axis_size("grp") != 8:
        return jnp.arange(lax.axis_size("grp"), dtype=jnp.int32)
    return jnp.bitwise_xor(grp, jnp.array([0, 2, 4, 6, 1, 3, 5, 7], jnp.int32))


def local(
    tokens,
    cotangent,
    segment_ids,
    tile_owner_slots,
    weights_low,
    master,
    moment_one,
    moment_two,
    left_basis_set,
    right_basis_set,
    gains,
    gain_moment_one,
    gain_moment_two,
):
    grp_count = lax.axis_size("grp")
    seq_count = lax.axis_size("seq")
    grp_here, seq_here = lax.axis_index("grp"), lax.axis_index("seq")
    rows_here = tokens.shape[0]
    slots_here, rows_block, tile_width = weights_low.shape
    tile_count = tile_owner_slots.shape[0]
    query_cols = NH * HD
    value_end = query_cols + 2 * HD
    output_end = value_end + MODEL_WIDTH
    attn_tiles = output_end // tile_width
    query_tiles = query_cols // tile_width
    hidden_tiles = FF // tile_width
    share = -(-hidden_tiles // grp_count)
    share_cols = share * tile_width
    share_width = MODEL_WIDTH // grp_count
    sub_rows = rows_block // grp_count
    halves = 2 if sub_rows >= 32 else 1
    half_block, half_sub = rows_block // halves, sub_rows // halves
    first_place = (seq_here * rows_here) % SEQLEN
    key_tables = turn_tables(jnp.arange(SEQLEN, dtype=jnp.int32))
    tables = [lax.dynamic_slice_in_dim(table, first_place, rows_here) for table in key_tables]

    hidden_ids = grp_here * share + jnp.arange(share, dtype=jnp.int32)
    real = jnp.repeat(hidden_ids < hidden_tiles, tile_width)[None, :]
    hidden_ids = jnp.minimum(hidden_ids, hidden_tiles - 1)
    feed_ids = (
        attn_tiles
        + jnp.arange(3, dtype=jnp.int32)[:, None] * hidden_tiles
        + hidden_ids[None, :]
    ).reshape(-1)
    feed_slots, attn_slots = tile_owner_slots[feed_ids], tile_owner_slots[:attn_tiles]

    def weight_half(at):
        return gather_plane(
            (slots_here, half_block, tile_width),
            split=1,
            source_view=lambda ref, index: ref.at[:, pl.ds(at * half_block, half_block)],
        )

    def attn_half(at):
        return gather_plane(
            (seq_count, half_sub, output_end),
            target_view=lambda ref, index: ref.at[:, at, index],
            out_shape=(seq_count, halves, grp_count, half_sub, output_end),
        )

    flat = (grp_count * slots_here, half_block, tile_width)
    (tiles,) = exchange(0, [(weight_half(0), weights_low)])
    feed_rows, attn_rows = pick(tiles.reshape(flat), feed_slots, attn_slots)
    feed_parts = [lax.all_gather(feed_rows, "seq", axis=0, tiled=False)]
    if halves == 2:
        tiles, attn_first = exchange(
            1, [(weight_half(1), weights_low), gather_axis("seq", attn_rows)]
        )
        feed_rows, attn_rows = pick(tiles.reshape(flat), feed_slots, attn_slots)
        feed_parts.append(lax.all_gather(feed_rows, "seq", axis=0, tiled=False))
        attn_weights, _ = exchange(
            2,
            [(attn_half(0), attn_first), gather_axis("seq", attn_rows), (attn_half(1), 1, 0)],
        )
        feed_weights = jnp.zeros((seq_count, 2, half_block, 3 * share_cols), jnp.bfloat16)
        for at in range(2):
            feed_weights = lax.dynamic_update_slice(
                feed_weights, feed_parts[at][:, None], (0, at, 0, 0)
            )
    else:
        _, attn_weights = exchange(2, [gather_axis("seq", attn_rows), (attn_half(0), 0)])
        feed_weights = feed_parts[0]
    attn_weights = attn_weights.reshape(MODEL_WIDTH, output_end)
    feed_weights = feed_weights.reshape(MODEL_WIDTH, 3 * share_cols)

    tok_float = tokens.astype(jnp.float32)
    inverse_one = lax.rsqrt(jnp.mean(tok_float * tok_float, axis=-1, keepdims=True) + NORM_EPS)
    normed = (tok_float * inverse_one * gains[0]).astype(jnp.bfloat16)
    projected = project(normed, attn_weights, tables)
    pairs, segments = exchange(
        3,
        [
            gather_axis("seq", projected[:, query_cols:]),
            gather_axis("seq", segment_ids.reshape(-1, tile_width)),
        ],
    )
    first_key = seq_here * rows_here - first_place
    pairs = lax.dynamic_slice_in_dim(pairs.reshape(-1, 2 * HD), first_key, SEQLEN)
    key_segs = lax.dynamic_slice_in_dim(segments.reshape(-1), first_key, SEQLEN)
    at = (first_place // rows_here).reshape(1)
    context, log_totals = attend(at, projected, pairs, key_segs, segment_ids)
    branch = jnp.dot(
        context, attn_weights[:, value_end:], preferred_element_type=jnp.float32
    )
    hidden = tok_float + branch
    inverse_two = lax.rsqrt(jnp.mean(hidden * hidden, axis=-1, keepdims=True) + NORM_EPS)
    normed_two = (hidden * inverse_two * gains[1]).astype(jnp.bfloat16)

    second_plane, cot_plane = exchange(
        4,
        [
            (gather_plane(normed_two.shape), normed_two),
            (gather_plane(cotangent.shape), cotangent),
        ],
    )
    second_plane = second_plane.reshape(-1, MODEL_WIDTH)
    cot_plane = cot_plane.reshape(-1, MODEL_WIDTH)
    second_plane, normed, context_late = lax.optimization_barrier((second_plane, normed, context))
    normed_plane = behind_gather(normed)
    context_plane = behind_gather(context_late)
    gating_weights = feed_weights[:, : 2 * share_cols]
    down_weights = feed_weights[:, 2 * share_cols :]
    gate_up = jnp.dot(second_plane, gating_weights, preferred_element_type=jnp.float32)
    gate = gate_up[:, :share_cols]
    upper = gate_up[:, share_cols:]
    sigmoid_gate = jax.nn.sigmoid(gate)
    silu_gate = gate * sigmoid_gate
    activated = jnp.where(real, silu_gate * upper, 0.0).astype(jnp.bfloat16)
    down_grad = contract(cot_plane, activated).astype(jnp.bfloat16)
    down_grad, cot_plane = lax.optimization_barrier((down_grad, cot_plane))
    down_grad = lax.psum_scatter(down_grad, "seq", scatter_dimension=0, tiled=True)
    act_grad = jnp.dot(cot_plane, down_weights, preferred_element_type=jnp.float32)
    act_grad = jnp.where(real, act_grad, 0.0)
    gate_grad = (act_grad * upper * sigmoid_gate * (1.0 + gate * (1.0 - sigmoid_gate))).astype(
        jnp.bfloat16
    )
    up_grad = (act_grad * silu_gate).astype(jnp.bfloat16)
    gate_weight_grad = contract(second_plane, gate_grad).astype(jnp.bfloat16)
    up_weight_grad = contract(second_plane, up_grad).astype(jnp.bfloat16)
    gating_grad = jnp.concatenate([gate_grad, up_grad], axis=1)
    two_part = times_transpose(gating_grad, gating_weights).astype(jnp.bfloat16)
    feed_part = times_transpose(activated, down_weights).astype(jnp.bfloat16)
    two_part, feed_part, gate_weight_grad, up_weight_grad = lax.optimization_barrier(
        (two_part, feed_part, gate_weight_grad, up_weight_grad)
    )
    gate_weight_grad = lax.psum_scatter(gate_weight_grad, "seq", scatter_dimension=0, tiled=True)
    up_weight_grad = lax.psum_scatter(up_weight_grad, "seq", scatter_dimension=0, tiled=True)
    norm_two_grad = plane_sum(5, two_part)

    out_grad = cotangent.astype(jnp.float32)
    gain_two_term = jnp.sum(norm_two_grad * hidden * inverse_two, axis=0)
    hidden_grad = (
        out_grad
        + inverse_two * gains[1] * norm_two_grad
        - hidden
        * inverse_two**3
        * jnp.mean(hidden * gains[1] * norm_two_grad, axis=-1, keepdims=True)
    )
    branch_grad = hidden_grad.astype(jnp.bfloat16)
    context_grad = times_transpose(branch_grad, attn_weights[:, value_end:]).astype(jnp.bfloat16)
    query_grad, pair_part = attend_back(
        at,
        projected,
        pairs,
        context_grad,
        log_totals,
        key_segs,
        segment_ids,
        key_tables,
        tables,
    )
    if seq_count * rows_here > SEQLEN:
        pair_part = lax.dynamic_update_slice_in_dim(
            jnp.zeros((seq_count * rows_here, 2 * HD), pair_part.dtype), pair_part, first_key, 0
        )
    pair_parts, query_share, branch_share = exchange(
        6,
        [
            split_rows("seq", pair_part),
            split_columns("grp", query_grad),
            split_columns("grp", branch_grad),
        ],
    )
    pair_grad = jnp.sum(pair_parts.astype(jnp.float32), axis=0).astype(jnp.bfloat16)
    projected_grad = jnp.concatenate([query_grad, pair_grad], axis=1)
    norm_one_grad = times_transpose(projected_grad, attn_weights[:, :value_end])
    gain_one_term = jnp.sum(norm_one_grad * tok_float * inverse_one, axis=0)
    input_grad = (
        hidden_grad
        + inverse_one * gains[0] * norm_one_grad
        - tok_float
        * inverse_one**3
        * jnp.mean(tok_float * gains[0] * norm_one_grad, axis=-1, keepdims=True)
    )
    pair_plane, gain_parts = exchange(
        7,
        [
            gather_axis("grp", pair_grad),
            gather_axis("grp", jnp.stack([gain_one_term, gain_two_term])),
        ],
    )
    gain_plane = jnp.sum(gain_parts, axis=0)
    order = behind_order()
    normed_rows = lax.dynamic_slice_in_dim(
        normed_plane.reshape(-1, seq_count, grp_count, sub_rows), grp_here, 1, axis=2
    ).reshape(-1, seq_count * sub_rows)
    query_weight_grad = contract(normed_plane, query_share[order].reshape(-1, share_width))
    out_weight_grad = contract(context_plane, branch_share[order].reshape(-1, share_width))
    pair_weight_grad = contract(normed_rows, pair_plane[order].reshape(-1, 2 * HD))
    shares = jnp.concatenate([query_weight_grad, out_weight_grad], axis=1).astype(jnp.bfloat16)
    shares, down_grad, gate_weight_grad = lax.optimization_barrier(
        (shares, down_grad, gate_weight_grad)
    )
    feed_shape = (rows_block, share_cols)
    share_parts, pair_parts, gain_parts, down_plane, gate_plane = exchange(
        8,
        [
            split_rows("seq", shares),
            split_rows("seq", pair_weight_grad.astype(jnp.bfloat16)),
            gather_axis("seq", gain_plane),
            (gather_plane(feed_shape), down_grad),
            (gather_plane(feed_shape), gate_weight_grad),
        ],
    )
    gain_grads = jnp.sum(gain_parts, axis=0)
    shares = jnp.sum(share_parts.astype(jnp.float32), axis=0).astype(jnp.bfloat16)
    pair_rows = jnp.sum(pair_parts.astype(jnp.float32), axis=0).astype(jnp.bfloat16)
    shares, up_weight_grad, feed_part = lax.optimization_barrier((shares, up_weight_grad, feed_part))
    feed_out = lax.psum_scatter(feed_part, "grp", scatter_dimension=0, tiled=True)
    block_out = (hidden + feed_out.astype(jnp.float32)).astype(jnp.bfloat16)
    up_plane, share_plane, pair_plane = exchange(
        9,
        [
            (gather_plane(feed_shape), up_weight_grad),
            (gather_plane(shares.shape), shares),
            (gather_plane(pair_rows.shape), pair_rows),
        ],
    )

    tile_of_slot = (
        jnp.full((grp_count * slots_here,), tile_count, jnp.int32)
        .at[tile_owner_slots]
        .set(jnp.arange(tile_count, dtype=jnp.int32))
    )
    tiles_here = lax.dynamic_slice_in_dim(tile_of_slot, grp_here * slots_here, slots_here)
    feed_at = jnp.clip(tiles_here - attn_tiles, 0, 3 * hidden_tiles - 1)
    which, column = feed_at // hidden_tiles, feed_at % hidden_tiles
    is_query = tiles_here < query_tiles
    is_pair = (tiles_here >= query_tiles) & (tiles_here < query_tiles + 2)
    is_feed = tiles_here >= attn_tiles
    kind = jnp.where(is_feed, jnp.minimum(which, 2), 3)
    kind = jnp.where(is_pair, 4, jnp.where(is_feed, kind, 3))
    kind = jnp.where(tiles_here == tile_count, 5, kind)
    out_at = jnp.clip(tiles_here - query_tiles - 2, 0, query_tiles - 1)
    per_share = share_width // tile_width
    share_at = jnp.where(is_query, jnp.minimum(tiles_here, query_tiles - 1), out_at)
    at = jnp.stack(
        [
            kind,
            column // share,
            column % share,
            share_at // per_share,
            share_at % per_share + jnp.where(is_query, 0, per_share),
            jnp.where(is_pair, tiles_here - query_tiles, 0),
        ]
    )
    new_master, new_one, new_two = adam(
        at,
        gate_plane,
        up_plane,
        down_plane,
        share_plane,
        pair_plane,
        left_basis_set,
        right_basis_set,
        master,
        moment_one,
        moment_two,
    )
    gain_one = BETA_ONE * gain_moment_one + (1.0 - BETA_ONE) * gain_grads
    gain_two = BETA_TWO * gain_moment_two + (1.0 - BETA_TWO) * gain_grads * gain_grads
    new_gains = gains - GAIN_RATE * gain_one / (jnp.sqrt(gain_two) + ADAM_EPS)
    return (
        block_out,
        input_grad,
        new_master,
        new_one,
        new_two,
        gain_grads,
        new_gains,
        gain_one,
        gain_two,
    )


def solution(mesh):
    return jax.shard_map(
        local,
        mesh=mesh,
        in_specs=(
            P(("grp", "seq"), None),
            P(("grp", "seq"), None),
            P(("grp", "seq")),
            P(),
            P("grp", "seq", None),
            P("grp", "seq", None),
            P("grp", "seq", None),
            P("grp", "seq", None),
            P("grp", "seq", None),
            P("grp", "seq", None),
            P(),
            P(),
            P(),
        ),
        out_specs=(
            P(("grp", "seq"), None),
            P(("grp", "seq"), None),
            P("grp", "seq", None),
            P("grp", "seq", None),
            P("grp", "seq", None),
            P(),
            P(),
            P(),
            P(),
        ),
        check_vma=False,
    )
```

```python
import functools

import jax
import jax.numpy as jnp
from jax import lax
from jax.experimental import pallas as pl
from jax.experimental.pallas import tpu as pltpu
from jax.sharding import PartitionSpec as P

MODEL_WIDTH = 2048
NH = 16
HD = 128
FF = 5632
SEQLEN = 1024


NORM_EPS = 1e-05
BETA_ONE = 0.95
BETA_TWO = 0.95
ADAM_EPS = 1e-08
WEIGHT_DECAY = 0.01
LEARN_RATE = 0.03
GAIN_RATE = 1.5
ROPE_BASE = 10000.0
MASKED = -1e30
PRECISE = lax.Precision.HIGHEST


def contract(left_side, right_side):
    return lax.dot_general(
        left_side, right_side, (((0,), (0,)), ((), ())), preferred_element_type=jnp.float32
    )


def times_transpose(left_side, right_side):
    return lax.dot_general(
        left_side, right_side, (((1,), (1,)), ((), ())), preferred_element_type=jnp.float32
    )


def turn_tables(places):
    half_width = HD // 2
    frequency = ROPE_BASE ** (-(jnp.arange(half_width, dtype=jnp.float32) * 2.0) / HD)
    angles = places.astype(jnp.float32)[:, None] * frequency[None, :]
    cosine, sine = jnp.cos(angles), jnp.sin(angles)
    return (
        jnp.concatenate([cosine, cosine], axis=1),
        jnp.concatenate([-sine, sine], axis=1),
    )


def turn(rows, cosine, sine):
    return rows * cosine + pltpu.roll(rows, HD // 2, 1) * sine


def turn_back(rows, cosine, sine):
    return rows * cosine - pltpu.roll(rows, HD // 2, 1) * sine


def dot_last(left_side, right_side):
    return lax.dot_general(
        left_side, right_side, (((1,), (1,)), ((), ())), preferred_element_type=jnp.float32
    )


def dot_first(left_side, right_side):
    return lax.dot_general(
        left_side, right_side, (((0,), (0,)), ((), ())), preferred_element_type=jnp.float32
    )


SMALL_COST = pl.CostEstimate(flops=1, bytes_accessed=1, transcendentals=0)


def project_kernel(x_ref, w_ref, cosine_ref, sine_ref, out_ref):
    made = jnp.dot(x_ref[...], w_ref[...], preferred_element_type=jnp.float32)
    cosine, sine = cosine_ref[...], sine_ref[...]
    first, second = made[:, :HD], made[:, HD:]
    last = pl.program_id(0) == pl.num_programs(0) - 1
    out_ref[:, :HD] = turn(first, cosine, sine).astype(out_ref.dtype)
    out_ref[:, HD:] = jnp.where(last, second, turn(second, cosine, sine)).astype(out_ref.dtype)


def project(normed, weights, tables):
    rows, width = normed.shape
    steps = NH // 2 + 1
    return pl.pallas_call(
        project_kernel,
        grid=(steps,),
        in_specs=[
            pl.BlockSpec((rows, width), lambda j: (0, 0)),
            pl.BlockSpec((width, 2 * HD), lambda j: (0, j)),
            pl.BlockSpec((rows, HD), lambda j: (0, 0)),
            pl.BlockSpec((rows, HD), lambda j: (0, 0)),
        ],
        out_specs=pl.BlockSpec((rows, 2 * HD), lambda j: (0, j)),
        out_shape=jax.ShapeDtypeStruct((rows, steps * 2 * HD), jnp.bfloat16),
        compiler_params=pltpu.CompilerParams(vmem_limit_bytes=56 * 2**20),
        cost_estimate=SMALL_COST,
        name="project",
    )(normed, weights, *tables)


def score_mask(key_seg_ref, query_seg_ref, block, rows):
    keys = (block + 1) * rows
    same = key_seg_ref[:keys, :] == query_seg_ref[...]
    key_at = lax.broadcasted_iota(jnp.int32, (keys, rows), 0)
    query_at = lax.broadcasted_iota(jnp.int32, (keys, rows), 1) + block * rows
    return same & (key_at <= query_at)


def attend_kernel(at_ref, q_ref, k_ref, v_ref, key_seg_ref, query_seg_ref, context_ref, total_ref):
    scale = HD ** (-0.5)
    rows = q_ref.shape[0]
    for block in range(SEQLEN // rows):

        @pl.when(at_ref[0] == block)
        def _():
            keys = (block + 1) * rows
            scores = dot_last(k_ref[:keys, :], q_ref[...]) * scale
            scores = jnp.where(
                score_mask(key_seg_ref, query_seg_ref, block, rows), scores, MASKED
            )
            highest = jnp.max(scores, axis=0, keepdims=True)
            exponent = jnp.exp(scores - highest)
            totals = jnp.sum(exponent, axis=0, keepdims=True)
            probs_low = (exponent * (1.0 / totals)).astype(jnp.bfloat16)
            context = dot_first(probs_low, v_ref[:keys, :])
            context_ref[...] = context.astype(jnp.bfloat16)
            total_ref[0] = highest + jnp.log(totals)


def attend_back_kernel(
    at_ref,
    q_ref,
    k_ref,
    v_ref,
    grad_ref,
    total_ref,
    key_seg_ref,
    query_seg_ref,
    key_cosine_ref,
    key_sine_ref,
    cosine_ref,
    sine_ref,
    query_grad_ref,
    pair_grad_ref,
    key_sum,
    value_sum,
):
    scale = HD ** (-0.5)
    rows = q_ref.shape[0]
    head = pl.program_id(0)

    @pl.when(head == 0)
    def _():
        key_sum[...] = jnp.zeros_like(key_sum)
        value_sum[...] = jnp.zeros_like(value_sum)

    for block in range(SEQLEN // rows):

        @pl.when(at_ref[0] == block)
        def _():
            keys = (block + 1) * rows
            queries, grads = q_ref[...], grad_ref[...]
            shifted = dot_last(k_ref[:keys, :], queries) * scale - total_ref[0]
            allowed = score_mask(key_seg_ref, query_seg_ref, block, rows)
            probs = jnp.where(allowed, jnp.exp(shifted), 0.0)
            prob_grad = dot_last(v_ref[:keys, :], grads)
            centre = jnp.sum(probs * prob_grad, axis=0, keepdims=True)
            score_grad = (probs * (prob_grad - centre) * scale).astype(jnp.bfloat16)
            value_sum[:keys, :] += jnp.dot(
                probs.astype(jnp.bfloat16), grads, preferred_element_type=jnp.float32
            )
            key_sum[:keys, :] += jnp.dot(score_grad, queries, preferred_element_type=jnp.float32)
            query_grad = dot_first(score_grad, k_ref[:keys, :])
            query_grad_ref[...] = turn_back(query_grad, cosine_ref[...], sine_ref[...]).astype(
                jnp.bfloat16
            )

    @pl.when(head == pl.num_programs(0) - 1)
    def _():
        pair_grad_ref[:, :HD] = turn_back(
            key_sum[...], key_cosine_ref[...], key_sine_ref[...]
        ).astype(jnp.bfloat16)
        pair_grad_ref[:, HD:] = value_sum[...].astype(jnp.bfloat16)


def attention_specs(kinds, rows):
    specs = {
        "at": pl.BlockSpec(memory_space=pltpu.SMEM),
        "head": pl.BlockSpec((rows, HD), lambda h: (0, h)),
        "keys": pl.BlockSpec((SEQLEN, HD), lambda h: (0, 0)),
        "values": pl.BlockSpec((SEQLEN, HD), lambda h: (0, 1)),
        "pair": pl.BlockSpec((SEQLEN, 2 * HD), lambda h: (0, 0)),
        "total": pl.BlockSpec((1, 1, rows), lambda h: (h, 0, 0)),
        "key_seg": pl.BlockSpec((SEQLEN, 1), lambda h: (0, 0)),
        "query_seg": pl.BlockSpec((1, rows), lambda h: (0, 0)),
        "key_table": pl.BlockSpec((SEQLEN, HD), lambda h: (0, 0)),
        "table": pl.BlockSpec((rows, HD), lambda h: (0, 0)),
    }
    return [specs[kind] for kind in kinds]


def attend(at, projected, pairs, key_segs, query_segs):
    rows = projected.shape[0]
    columns = NH * HD
    return pl.pallas_call(
        attend_kernel,
        grid=(NH,),
        in_specs=attention_specs(["at", "head", "keys", "values", "key_seg", "query_seg"], rows),
        out_specs=attention_specs(["head", "total"], rows),
        out_shape=(
            jax.ShapeDtypeStruct((rows, columns), jnp.bfloat16),
            jax.ShapeDtypeStruct((NH, 1, rows), jnp.float32),
        ),
        compiler_params=pltpu.CompilerParams(vmem_limit_bytes=32 * 2**20),
        cost_estimate=SMALL_COST,
        name="attend",
    )(at, projected, pairs, pairs, key_segs[:, None], query_segs[None, :])


def attend_back(at, projected, pairs, grads, totals, key_segs, query_segs, key_tables, tables):
    rows = projected.shape[0]
    columns = NH * HD
    return pl.pallas_call(
        attend_back_kernel,
        grid=(NH,),
        in_specs=attention_specs(
            ["at", "head", "keys", "values", "head", "total", "key_seg", "query_seg"]
            + ["key_table", "key_table", "table", "table"],
            rows,
        ),
        out_specs=attention_specs(["head", "pair"], rows),
        out_shape=(
            jax.ShapeDtypeStruct((rows, columns), jnp.bfloat16),
            jax.ShapeDtypeStruct((SEQLEN, 2 * HD), jnp.bfloat16),
        ),
        scratch_shapes=[pltpu.VMEM((SEQLEN, HD), jnp.float32)] * 2,
        compiler_params=pltpu.CompilerParams(vmem_limit_bytes=32 * 2**20),
        cost_estimate=SMALL_COST,
        name="attend_back",
    )(
        at, projected, pairs, pairs, grads, totals, key_segs[:, None], query_segs[None, :],
        *key_tables, *tables,
    )


def feed_kernel(
    real_ref, x_ref, cot_ref, *refs
):
    parts, refs = refs[:-7], refs[-7:]
    act_ref, gate_grad_ref, up_grad_ref, two_ref, out_ref, weights, sems = refs
    cols = act_ref.shape[1]
    count, rows, _ = parts[0].shape
    halves = len(parts)

    @pl.when(pl.program_id(0) == 0)
    def _():
        copies = [
            pltpu.make_async_copy(
                parts[half].at[block],
                weights.at[pl.ds((block * halves + half) * rows, rows)],
                sems.at[block * halves + half],
            )
            for half in range(halves)
            for block in range(count)
        ]
        for copy in copies:
            copy.start()
        for copy in copies:
            copy.wait()

    low = jnp.bfloat16
    wide = jnp.float32
    gate = jnp.dot(x_ref[...], weights[:, :cols], preferred_element_type=wide)
    upper = jnp.dot(x_ref[...], weights[:, cols : 2 * cols], preferred_element_type=wide)
    act_grad = jnp.dot(cot_ref[...], weights[:, 2 * cols :], preferred_element_type=wide)
    real = lax.broadcasted_iota(jnp.int32, gate.shape, 1) < real_ref[0]
    sigmoid = 1.0 / (1.0 + jnp.exp(-gate))
    silu = gate * sigmoid
    activated = jnp.where(real, silu * upper, 0.0).astype(low)
    act_grad = jnp.where(real, act_grad, 0.0)
    gate_grad = (act_grad * upper * sigmoid * (1.0 + gate * (1.0 - sigmoid))).astype(low)
    up_grad = (act_grad * silu).astype(low)
    act_ref[...], gate_grad_ref[...], up_grad_ref[...] = activated, gate_grad, up_grad
    two = dot_last(gate_grad, weights[:, :cols]) + dot_last(up_grad, weights[:, cols : 2 * cols])
    two_ref[...] = two.astype(low)
    out_ref[...] = dot_last(activated, weights[:, 2 * cols :]).astype(low)


def feed_forward(real_cols, x, cot, parts, seq_count):
    tokens_all, width = x.shape
    _, rows, cols = parts[0].shape
    cols = cols // 3
    step = 256
    low = jnp.bfloat16
    block = pl.BlockSpec((step, width), lambda i: (i, 0))
    narrow = pl.BlockSpec((step, cols), lambda i: (i, 0))
    return pl.pallas_call(
        feed_kernel,
        grid=(tokens_all // step,),
        in_specs=[pl.BlockSpec(memory_space=pltpu.SMEM), block, block]
        + [pl.BlockSpec(memory_space=pl.ANY)] * len(parts),
        out_specs=[narrow, narrow, narrow, block, block],
        out_shape=[jax.ShapeDtypeStruct((tokens_all, cols), low)] * 3
        + [jax.ShapeDtypeStruct((tokens_all, width), low)] * 2,
        scratch_shapes=[
            pltpu.VMEM((width, 3 * cols), low),
            pltpu.SemaphoreType.DMA((len(parts) * seq_count,)),
        ],
        compiler_params=pltpu.CompilerParams(vmem_limit_bytes=52 * 2**20),
        cost_estimate=SMALL_COST,
        name="feed_forward",
    )(real_cols, x, cot, *parts)


def pick_kernel(rows, feed_ref, attn_ref, tiles_ref, feed_out, attn_out, sems):
    grp = lax.axis_index("grp")
    width = tiles_ref.shape[2]
    copies = []
    for at in range(feed_ref.shape[0]):
        copies.append(
            (tiles_ref.at[feed_ref[at]], feed_out.at[:, at * width : (at + 1) * width])
        )
    share = pl.ds(pl.multiple_of(grp * rows, rows), rows)
    for at in range(attn_ref.shape[0]):
        copies.append(
            (tiles_ref.at[attn_ref[at], share], attn_out.at[:, at * width : (at + 1) * width])
        )
    copies = [
        pltpu.make_async_copy(source, target, sems.at[at])
        for at, (source, target) in enumerate(copies)
    ]
    for copy in copies:
        copy.start()
    for copy in copies:
        copy.wait()


def pick(tiles, feed_slots, attn_slots):
    _, rows, width = tiles.shape
    share = rows // lax.axis_size("grp")
    feed, attn = feed_slots.shape[0], attn_slots.shape[0]
    return pl.pallas_call(
        functools.partial(pick_kernel, share),
        in_specs=[pl.BlockSpec(memory_space=pltpu.SMEM)] * 2 + [pl.BlockSpec(memory_space=pl.ANY)],
        out_specs=[pl.BlockSpec(memory_space=pltpu.VMEM)] * 2,
        out_shape=[
            jax.ShapeDtypeStruct((rows, feed * width), tiles.dtype),
            jax.ShapeDtypeStruct((share, attn * width), tiles.dtype),
        ],
        scratch_shapes=[pltpu.SemaphoreType.DMA((feed + attn,))],
        cost_estimate=SMALL_COST,
        name="pick",
    )(feed_slots, attn_slots, tiles)


def adam_kernel(
    at_ref, gate_ref, up_ref, down_ref, share_ref, pair_ref, left_ref, right_ref, master_ref,
    one_ref, two_ref, new_master_ref, new_one_ref, new_two_ref, grad,
):
    kind = at_ref[0, pl.program_id(0)]
    for number, ref in enumerate((gate_ref, up_ref, down_ref, share_ref, pair_ref)):

        @pl.when(kind == number)
        def _():
            grad[...] = ref[...].reshape(grad.shape)

    @pl.when(kind == 5)
    def _():
        grad[...] = jnp.zeros_like(grad)

    low = jnp.bfloat16
    left, right = left_ref[0].astype(low), right_ref[0].astype(low)
    turned = dot_first(grad[...], left)
    turned = dot_first(turned.astype(low), right)
    new_one = BETA_ONE * one_ref[0] + (1.0 - BETA_ONE) * turned
    new_two = BETA_TWO * two_ref[0] + (1.0 - BETA_TWO) * turned * turned
    new_one_ref[0], new_two_ref[0] = new_one, new_two
    scaled = new_one / (jnp.sqrt(new_two) + ADAM_EPS)
    restored = dot_last(scaled.astype(low), right)
    restored = jnp.dot(left, restored.astype(low), preferred_element_type=jnp.float32)
    new_master_ref[0] = master_ref[0] * (1.0 - LEARN_RATE * WEIGHT_DECAY) - LEARN_RATE * restored


def adam(at, gate, up, down, shares, pairs, left, right, master, one, two):
    slots, rows, width = master.shape
    tile = pl.BlockSpec((1, rows, width), lambda i, at: (i, 0, 0))
    shape = jax.ShapeDtypeStruct(master.shape, jnp.float32)
    feed = pl.BlockSpec((1, rows, width), lambda i, at: (at[1, i], 0, at[2, i]))
    return pl.pallas_call(
        adam_kernel,
        grid_spec=pltpu.PrefetchScalarGridSpec(
            num_scalar_prefetch=1,
            grid=(slots,),
            in_specs=[
                feed,
                feed,
                feed,
                pl.BlockSpec((1, rows, width), lambda i, at: (at[3, i], 0, at[4, i])),
                pl.BlockSpec((*pairs.shape[:2], width), lambda i, at: (0, 0, at[5, i])),
                pl.BlockSpec((1, rows, rows), lambda i, at: (i, 0, 0)),
                pl.BlockSpec((1, width, width), lambda i, at: (i, 0, 0)),
                tile,
                tile,
                tile,
            ],
            out_specs=[tile] * 3,
            scratch_shapes=[pltpu.VMEM((rows, width), jnp.bfloat16)],
        ),
        out_shape=[shape] * 3,
        compiler_params=pltpu.CompilerParams(vmem_limit_bytes=60 * 2**20),
        cost_estimate=SMALL_COST,
        name="adam",
    )(at, gate, up, down, shares, pairs, left, right, master, one, two)


MESH = pl.DeviceIdType.MESH


def remote(source, target, sems, at, device):
    return pltpu.make_async_remote_copy(
        src_ref=source,
        dst_ref=target,
        send_sem=sems[0].at[at],
        recv_sem=sems[1].at[at],
        device_id=device,
        device_id_type=MESH,
    )


def columns_of(ref, index, width):
    return ref.at[:, pl.ds(pl.multiple_of(index * width, width), width)]


def rows_of(ref, index, height):
    return ref.at[pl.ds(pl.multiple_of(index * height, height), height), :]


class Exchange:
    def __init__(self, axis, out_shape, source_view, target_view):
        self.axis, self.out_shape = axis, out_shape
        self.source_view, self.target_view = source_view, target_view
        self.count = lax.axis_size(axis)
        self.sem_count = self.count

    def peers(self, grp, seq):
        me = grp if self.axis == "grp" else seq
        for step in range(1, self.count):
            there = (me + step) % self.count
            yield (there, seq) if self.axis == "grp" else (grp, there)

    def start(self, source, target, sems, grp, seq):
        me = grp if self.axis == "grp" else seq
        self.own = pltpu.make_async_copy(
            self.source_view(source, me), self.target_view(target, me), sems[0].at[0]
        )
        self.own.start()
        self.sent, self.due = [], []
        for step, device in enumerate(self.peers(grp, seq), 1):
            there = (me + step) % self.count
            back = (me + self.count - step) % self.count
            copy = remote(
                self.source_view(source, there), self.target_view(target, me), sems, step, device
            )
            copy.start()
            self.sent.append(copy)
            self.due.append(
                remote(
                    self.source_view(source, back), self.target_view(target, back), sems, step, device
                )
            )

    def forward(self):
        pass

    def finish(self):
        for copy in self.due:
            copy.wait_recv()
        for copy in self.sent:
            copy.wait_send()
        self.own.wait()


class PlaneGather:
    axis = "grp"
    sem_count = 14

    def __init__(self, out_shape, source_view, target_view, half_of):
        self.out_shape = out_shape
        self.source_view, self.target_view, self.half_of = source_view, target_view, half_of

    def around(self, grp):
        core, across_x, across_y = grp % 2, (grp // 2) % 2, grp // 4
        return grp + 1 - 2 * core, grp + 2 - 4 * across_x, grp + 4 - 8 * across_y

    def peers(self, grp, seq):
        for other in self.around(grp):
            yield other, seq

    def start(self, source, target, sems, grp, seq):
        core, side_x, side_y = self.around(grp)

        def part(block, piece):
            view = self.target_view(target, block)
            return view if piece == "all" else self.half_of(view, piece == "b")

        def own(piece):
            view = self.source_view(source, grp)
            return view if piece == "all" else self.half_of(view, piece == "b")

        def across(block):
            return self.around(self.around(block)[1])[2]

        def make(at, block, piece, via, first=False):
            view = own(piece) if first else part(block, piece)
            return remote(view, part(block, piece), sems, at, (via, seq))

        self.out = [
            make(1, grp, "a", side_x, True),
            make(2, grp, "b", side_x, True),
            make(3, side_y, "b", side_x),
            make(4, grp, "b", side_y, True),
            make(5, grp, "a", side_y, True),
            make(6, side_x, "a", side_y),
            make(7, grp, "all", core, True),
            make(8, side_x, "a", core),
            make(9, side_x, "b", core),
            make(10, side_y, "b", core),
            make(11, side_y, "a", core),
            make(12, across(grp), "a", core),
            make(13, across(grp), "b", core),
        ]
        self.due = [
            make(1, side_x, "a", side_x),
            make(2, side_x, "b", side_x),
            make(3, across(grp), "b", side_x),
            make(4, side_y, "b", side_y),
            make(5, side_y, "a", side_y),
            make(6, across(grp), "a", side_y),
            make(7, core, "all", core),
            make(8, self.around(core)[1], "a", core),
            make(9, self.around(core)[1], "b", core),
            make(10, self.around(core)[2], "b", core),
            make(11, self.around(core)[2], "a", core),
            make(12, across(core), "a", core),
            make(13, across(core), "b", core),
        ]
        self.kept = pltpu.make_async_copy(own("all"), part(grp, "all"), sems[0].at[0])
        self.kept.start()
        for at in (1, 4, 2, 5, 7):
            self.out[at - 1].start()

    def forward(self):
        for came, then in ((1, (6, 8)), (4, (3, 10)), (2, (9,)), (5, (11,)), (6, (12,)), (3, (13,))):
            self.due[came - 1].wait_recv()
            for at in then:
                self.out[at - 1].start()

    def finish(self):
        for copy in self.due[6:]:
            copy.wait_recv()
        for copy in self.out:
            copy.wait_send()
        self.kept.wait()


def half_rows(axis, height):
    def half_of(view, second):
        index = (slice(None),) * axis + (pl.ds(height if second else 0, height),)
        return view.at[index]

    return half_of


def whole(ref, index):
    return ref


def block_of(ref, index):
    return ref.at[index]


def gather_plane(shape, split=0, source_view=whole, target_view=block_of, out_shape=None):
    out_shape = out_shape or (lax.axis_size("grp"), *shape)
    if lax.axis_size("grp") == 8:
        return PlaneGather(out_shape, source_view, target_view, half_rows(split, shape[split] // 2))
    return Exchange("grp", out_shape, source_view, target_view)


def exchange_kernel(tasks, wires, arrays, outputs, *refs):
    sources, targets = refs[:arrays], refs[arrays : arrays + outputs]
    sems = refs[arrays + outputs :]
    grp, seq = lax.axis_index("grp"), lax.axis_index("seq")
    barrier = pltpu.get_barrier_semaphore()
    axes = {"grp": [], "seq": []}
    for task in tasks:
        devices = list(task.peers(grp, seq))
        if len(devices) > len(axes[task.axis]):
            axes[task.axis] = devices
    devices = axes["grp"] + axes["seq"]
    for device in devices:
        pl.semaphore_signal(barrier, inc=1, device_id=device, device_id_type=MESH)
    pl.semaphore_wait(barrier, len(devices))

    def start(at):
        after, source, target = wires[at]
        source = targets[source] if after is not None else sources[source]
        tasks[at].start(source, targets[target], sems[2 * at : 2 * at + 2], grp, seq)

    open_tasks = list(range(len(tasks)))
    first = [at for at in open_tasks if wires[at][0] is None]
    for at in first:
        start(at)
    for at in first:
        tasks[at].forward()
    for at in open_tasks[:]:
        after = wires[at][0]
        if after is not None:
            tasks[after].finish()
            open_tasks.remove(after)
            start(at)
            tasks[at].forward()
    for at in open_tasks:
        tasks[at].finish()


def exchange(number, work):
    tasks = [piece[0] for piece in work]
    arrays, shapes, wires = [], [], []
    for piece in work:
        if isinstance(piece[1], int):
            after, source = piece[1], wires[piece[1]][2]
            kind = shapes[source].dtype
        else:
            after, source = None, len(arrays)
            arrays.append(piece[1])
            kind = piece[1].dtype
        if len(piece) == 3:
            target = wires[piece[2]][2]
        else:
            target = len(shapes)
            shapes.append(jax.ShapeDtypeStruct(piece[0].out_shape, kind))
        wires.append((after, source, target))
    scratch = []
    for task in tasks:
        scratch += [pltpu.SemaphoreType.DMA((task.sem_count,))] * 2
    return pl.pallas_call(
        functools.partial(exchange_kernel, tasks, wires, len(arrays), len(shapes)),
        in_specs=[pl.BlockSpec(memory_space=pl.ANY)] * len(arrays),
        out_specs=[pl.BlockSpec(memory_space=pl.ANY)] * len(shapes),
        out_shape=shapes,
        scratch_shapes=scratch,
        compiler_params=pltpu.CompilerParams(collective_id=number, has_side_effects=True),
        cost_estimate=SMALL_COST,
        name="exchange",
    )(*arrays)


def gather_axis(axis, array):
    task = Exchange(axis, (lax.axis_size(axis), *array.shape), whole, block_of)
    return task, array


def split_rows(axis, array):
    count = lax.axis_size(axis)
    rows, columns = array.shape
    height = rows // count
    task = Exchange(
        axis,
        (count, height, columns),
        lambda ref, index: rows_of(ref, index, height),
        block_of,
    )
    return task, array


def split_columns(axis, array):
    count = lax.axis_size(axis)
    rows, columns = array.shape
    width = columns // count
    task = Exchange(
        axis,
        (count, rows, width),
        lambda ref, index: columns_of(ref, index, width),
        block_of,
    )
    return task, array


def add_rows(total, first, second):
    step = 32

    def some(at, _):
        rows = pl.ds(pl.multiple_of(at * step, step), step)
        total[rows, :] = (
            first[rows, :].astype(jnp.float32) + second[rows, :].astype(jnp.float32)
        ).astype(total.dtype)
        return 0

    lax.fori_loop(0, total.shape[0] // step, some, 0)


def plane_sum_kernel(
    part_ref, total_ref, core_in, chip, half_x, half_y, whole_x, whole_y, send_sems, recv_sems
):
    grp, seq = lax.axis_index("grp"), lax.axis_index("seq")

    def around(device):
        core, across_x, across_y = device % 2, (device // 2) % 2, device // 4
        return device + 1 - 2 * core, device + 2 - 4 * across_x, device + 4 - 8 * across_y

    def order(device):
        _, side_x, side_y = around(device)
        return around(side_x)[2], side_x, side_y, device

    core, side_x, side_y = around(grp)
    half = total_ref.shape[0] // 2
    low, high = pl.ds(0, half), pl.ds(half, half)
    barrier = pltpu.get_barrier_semaphore()
    for device in (core, side_x, side_y):
        pl.semaphore_signal(barrier, inc=1, device_id=(device, seq), device_id_type=MESH)
    pl.semaphore_wait(barrier, 3)

    sems = (send_sems, recv_sems)
    copies = [
        remote(part_ref.at[block], core_in.at[at], sems, at, (core, seq))
        for at, block in enumerate(order(core))
    ]
    copies += [
        remote(chip.at[0, low], half_x, sems, 4, (side_x, seq)),
        remote(chip.at[0, high], half_y, sems, 5, (side_y, seq)),
        remote(chip.at[1, low], whole_x.at[low], sems, 6, (side_x, seq)),
        remote(chip.at[2, high], whole_y.at[high], sems, 7, (side_y, seq)),
        remote(chip.at[1, high], whole_x.at[high], sems, 8, (side_x, seq)),
        remote(chip.at[2, low], whole_y.at[low], sems, 9, (side_y, seq)),
    ]
    for copy in copies[:4]:
        copy.start()
    blocks = order(grp)
    for at, then in ((0, (4, 5)), (1, (6,)), (2, (7,))):
        copies[at].wait_recv()
        add_rows(chip.at[at], part_ref.at[blocks[at]], core_in.at[at])
        for start in then:
            copies[start].start()
    copies[5].wait_recv()
    add_rows(chip.at[1, high], chip.at[1, high], half_y)
    copies[8].start()
    copies[4].wait_recv()
    add_rows(chip.at[2, low], chip.at[2, low], half_x)
    copies[9].start()
    copies[3].wait_recv()
    add_rows(total_ref, part_ref.at[blocks[3]], core_in.at[3])
    for at, came in ((6, whole_x.at[low]), (7, whole_y.at[high]), (8, whole_x.at[high]), (9, whole_y.at[low])):
        copies[at].wait_recv()
        rows = low if at in (6, 9) else high
        add_rows(total_ref.at[rows], total_ref.at[rows], came)
    for copy in copies:
        copy.wait_send()


def plane_sum(number, part):
    count = lax.axis_size("grp")
    rows_all, columns = part.shape
    rows = rows_all // count
    if count != 8:
        return lax.psum_scatter(part, "grp", scatter_dimension=0, tiled=True).astype(jnp.float32)
    low = jnp.bfloat16
    return pl.pallas_call(
        plane_sum_kernel,
        in_specs=[pl.BlockSpec(memory_space=pltpu.VMEM)],
        out_specs=pl.BlockSpec(memory_space=pltpu.VMEM),
        out_shape=jax.ShapeDtypeStruct((rows, columns), jnp.float32),
        scratch_shapes=[
            pltpu.VMEM((4, rows, columns), low),
            pltpu.VMEM((3, rows, columns), low),
            pltpu.VMEM((rows // 2, columns), low),
            pltpu.VMEM((rows // 2, columns), low),
            pltpu.VMEM((rows, columns), low),
            pltpu.VMEM((rows, columns), low),
            pltpu.SemaphoreType.DMA((10,)),
            pltpu.SemaphoreType.DMA((10,)),
        ],
        compiler_params=pltpu.CompilerParams(
            collective_id=number, has_side_effects=True, vmem_limit_bytes=40 * 2**20
        ),
        cost_estimate=SMALL_COST,
        name="plane_sum",
    )(part.reshape(count, rows, columns))


def local(
    tokens,
    cotangent,
    segment_ids,
    tile_owner_slots,
    weights_low,
    master,
    moment_one,
    moment_two,
    left_basis_set,
    right_basis_set,
    gains,
    gain_moment_one,
    gain_moment_two,
):
    grp_count = lax.axis_size("grp")
    seq_count = lax.axis_size("seq")
    grp_here, seq_here = lax.axis_index("grp"), lax.axis_index("seq")
    rows_here = tokens.shape[0]
    slots_here, rows_block, tile_width = weights_low.shape
    tile_count = tile_owner_slots.shape[0]
    query_cols = NH * HD
    value_end = query_cols + 2 * HD
    output_end = value_end + MODEL_WIDTH
    attn_tiles = output_end // tile_width
    query_tiles = query_cols // tile_width
    hidden_tiles = FF // tile_width
    share = -(-hidden_tiles // grp_count)
    share_cols = share * tile_width
    share_width = MODEL_WIDTH // grp_count
    sub_rows = rows_block // grp_count
    halves = 2 if sub_rows >= 32 else 1
    half_block, half_sub = rows_block // halves, sub_rows // halves
    first_place = (seq_here * rows_here) % SEQLEN
    key_tables = turn_tables(jnp.arange(SEQLEN, dtype=jnp.int32))
    tables = [lax.dynamic_slice_in_dim(table, first_place, rows_here) for table in key_tables]

    hidden_ids = grp_here * share + jnp.arange(share, dtype=jnp.int32)
    hidden_ids = jnp.minimum(hidden_ids, hidden_tiles - 1)
    feed_ids = (
        attn_tiles
        + jnp.arange(3, dtype=jnp.int32)[:, None] * hidden_tiles
        + hidden_ids[None, :]
    ).reshape(-1)
    feed_slots, attn_slots = tile_owner_slots[feed_ids], tile_owner_slots[:attn_tiles]

    tok_float = tokens.astype(jnp.float32)
    inverse_one = lax.rsqrt(jnp.mean(tok_float * tok_float, axis=-1, keepdims=True) + NORM_EPS)
    normed = (tok_float * inverse_one * gains[0]).astype(jnp.bfloat16)

    def weight_half(at):
        return gather_plane(
            (slots_here, half_block, tile_width),
            split=1,
            source_view=lambda ref, index: ref.at[:, pl.ds(at * half_block, half_block)],
        )

    def attn_half(at):
        return gather_plane(
            (seq_count, half_sub, output_end),
            target_view=lambda ref, index: ref.at[:, at, index],
            out_shape=(seq_count, halves, grp_count, half_sub, output_end),
        )

    flat = (grp_count * slots_here, half_block, tile_width)
    (tiles,) = exchange(0, [(weight_half(0), weights_low)])
    feed_rows, attn_rows = pick(tiles.reshape(flat), feed_slots, attn_slots)
    feed_parts = [lax.all_gather(feed_rows, "seq", axis=0, tiled=False)]
    if halves == 2:
        tiles, attn_first = exchange(
            1, [(weight_half(1), weights_low), gather_axis("seq", attn_rows)]
        )
        feed_rows, attn_rows = pick(tiles.reshape(flat), feed_slots, attn_slots)
        feed_parts.append(lax.all_gather(feed_rows, "seq", axis=0, tiled=False))
        attn_weights, _, normed_plane = exchange(
            2,
            [
                (attn_half(0), attn_first),
                gather_axis("seq", attn_rows),
                (attn_half(1), 1, 0),
                (gather_plane(normed.shape), normed),
            ],
        )
    else:
        _, attn_weights, normed_plane = exchange(
            2,
            [
                gather_axis("seq", attn_rows),
                (attn_half(0), 0),
                (gather_plane(normed.shape), normed),
            ],
        )
    attn_weights, feed_parts[0] = lax.optimization_barrier((attn_weights, feed_parts[0]))
    attn_weights = attn_weights.reshape(MODEL_WIDTH, output_end)

    projected = project(normed, attn_weights, tables)
    pairs, segments, cot_plane = exchange(
        3,
        [
            gather_axis("seq", projected[:, query_cols:]),
            gather_axis("seq", segment_ids.reshape(-1, tile_width)),
            (gather_plane(cotangent.shape), cotangent),
        ],
    )
    first_key = seq_here * rows_here - first_place
    pairs = lax.dynamic_slice_in_dim(pairs.reshape(-1, 2 * HD), first_key, SEQLEN)
    key_segs = lax.dynamic_slice_in_dim(segments.reshape(-1), first_key, SEQLEN)
    at = (first_place // rows_here).reshape(1)
    context, log_totals = attend(at, projected, pairs, key_segs, segment_ids)
    branch = jnp.dot(
        context, attn_weights[:, value_end:], preferred_element_type=jnp.float32
    )
    hidden = tok_float + branch
    inverse_two = lax.rsqrt(jnp.mean(hidden * hidden, axis=-1, keepdims=True) + NORM_EPS)
    normed_two = (hidden * inverse_two * gains[1]).astype(jnp.bfloat16)

    (second_plane,) = exchange(4, [(gather_plane(normed_two.shape), normed_two)])
    second_plane = second_plane.reshape(-1, MODEL_WIDTH)
    cot_plane = cot_plane.reshape(-1, MODEL_WIDTH)
    real_cols = jnp.clip((hidden_tiles - grp_here * share) * tile_width, 0, share_cols)
    activated, gate_grad, up_grad, two_part, feed_part = feed_forward(
        real_cols.reshape(1), second_plane, cot_plane, feed_parts, seq_count
    )
    down_grad = contract(cot_plane, activated).astype(jnp.bfloat16)
    down_grad, gate_grad, up_grad = lax.optimization_barrier((down_grad, gate_grad, up_grad))
    down_grad = lax.psum_scatter(down_grad, "seq", scatter_dimension=0, tiled=True)
    gate_weight_grad = contract(second_plane, gate_grad).astype(jnp.bfloat16)
    up_weight_grad = contract(second_plane, up_grad).astype(jnp.bfloat16)
    two_part, feed_part, gate_weight_grad, up_weight_grad = lax.optimization_barrier(
        (two_part, feed_part, gate_weight_grad, up_weight_grad)
    )
    gate_weight_grad = lax.psum_scatter(gate_weight_grad, "seq", scatter_dimension=0, tiled=True)
    up_weight_grad = lax.psum_scatter(up_weight_grad, "seq", scatter_dimension=0, tiled=True)
    norm_two_grad = plane_sum(5, two_part)

    out_grad = cotangent.astype(jnp.float32)
    gain_two_term = jnp.sum(norm_two_grad * hidden * inverse_two, axis=0)
    hidden_grad = (
        out_grad
        + inverse_two * gains[1] * norm_two_grad
        - hidden
        * inverse_two**3
        * jnp.mean(hidden * gains[1] * norm_two_grad, axis=-1, keepdims=True)
    )
    branch_grad = hidden_grad.astype(jnp.bfloat16)
    context_grad = times_transpose(branch_grad, attn_weights[:, value_end:]).astype(jnp.bfloat16)
    context_grad, down_grad = lax.optimization_barrier((context_grad, down_grad))
    query_grad, pair_part = attend_back(
        at,
        projected,
        pairs,
        context_grad,
        log_totals,
        key_segs,
        segment_ids,
        key_tables,
        tables,
    )
    if seq_count * rows_here > SEQLEN:
        pair_part = lax.dynamic_update_slice_in_dim(
            jnp.zeros((seq_count * rows_here, 2 * HD), pair_part.dtype), pair_part, first_key, 0
        )
    pair_parts, query_share, branch_share, context_plane = exchange(
        6,
        [
            split_rows("seq", pair_part),
            split_columns("grp", query_grad),
            split_columns("grp", branch_grad),
            (gather_plane(context.shape), context),
        ],
    )
    pair_grad = jnp.sum(pair_parts.astype(jnp.float32), axis=0).astype(jnp.bfloat16)
    pair_grad, gate_weight_grad = lax.optimization_barrier((pair_grad, gate_weight_grad))
    projected_grad = jnp.concatenate([query_grad, pair_grad], axis=1)
    norm_one_grad = times_transpose(projected_grad, attn_weights[:, :value_end])
    gain_one_term = jnp.sum(norm_one_grad * tok_float * inverse_one, axis=0)
    input_grad = (
        hidden_grad
        + inverse_one * gains[0] * norm_one_grad
        - tok_float
        * inverse_one**3
        * jnp.mean(tok_float * gains[0] * norm_one_grad, axis=-1, keepdims=True)
    )
    normed_plane = normed_plane.reshape(-1, MODEL_WIDTH)
    context_plane = context_plane.reshape(-1, MODEL_WIDTH)
    query_weight_grad = contract(normed_plane, query_share.reshape(-1, share_width))
    out_weight_grad = contract(context_plane, branch_share.reshape(-1, share_width))
    pair_weight_grad = contract(normed, pair_grad).astype(jnp.bfloat16)
    shares = jnp.concatenate([query_weight_grad, out_weight_grad], axis=1).astype(jnp.bfloat16)
    shares, down_grad, gate_weight_grad = lax.optimization_barrier(
        (shares, down_grad, gate_weight_grad)
    )
    feed_shape = (rows_block, share_cols)
    pair_task = Exchange(
        "grp",
        (grp_count, seq_count, sub_rows, 2 * HD),
        lambda ref, index: ref.at[:, index],
        block_of,
    )
    share_parts, pair_parts, gain_parts, down_plane, gate_plane = exchange(
        7,
        [
            split_rows("seq", shares),
            (pair_task, pair_weight_grad.reshape(seq_count, grp_count, sub_rows, 2 * HD)),
            gather_axis("seq", jnp.stack([gain_one_term, gain_two_term])),
            (gather_plane(feed_shape), down_grad),
            (gather_plane(feed_shape), gate_weight_grad),
        ],
    )
    gain_seq = jnp.sum(gain_parts, axis=0)
    shares = jnp.sum(share_parts.astype(jnp.float32), axis=0).astype(jnp.bfloat16)
    pair_parts = jnp.sum(pair_parts.astype(jnp.float32), axis=0).astype(jnp.bfloat16)
    pair_task = Exchange("seq", pair_parts.shape, block_of, block_of)
    shares, up_weight_grad, feed_part = lax.optimization_barrier((shares, up_weight_grad, feed_part))
    feed_out = lax.psum_scatter(feed_part, "grp", scatter_dimension=0, tiled=True)
    block_out = (hidden + feed_out.astype(jnp.float32)).astype(jnp.bfloat16)
    _, pair_plane, up_plane, share_plane, gain_parts = exchange(
        8,
        [
            (pair_task, pair_parts),
            (gather_plane(pair_parts.shape), 0),
            (gather_plane(feed_shape), up_weight_grad),
            (gather_plane(shares.shape), shares),
            gather_axis("grp", gain_seq),
        ],
    )
    pair_plane = jnp.sum(pair_plane.astype(jnp.float32), axis=1).astype(jnp.bfloat16)
    gain_grads = jnp.sum(gain_parts, axis=0)

    tile_of_slot = (
        jnp.full((grp_count * slots_here,), tile_count, jnp.int32)
        .at[tile_owner_slots]
        .set(jnp.arange(tile_count, dtype=jnp.int32))
    )
    tiles_here = lax.dynamic_slice_in_dim(tile_of_slot, grp_here * slots_here, slots_here)
    feed_at = jnp.clip(tiles_here - attn_tiles, 0, 3 * hidden_tiles - 1)
    which, column = feed_at // hidden_tiles, feed_at % hidden_tiles
    is_query = tiles_here < query_tiles
    is_pair = (tiles_here >= query_tiles) & (tiles_here < query_tiles + 2)
    is_feed = tiles_here >= attn_tiles
    kind = jnp.where(is_feed, jnp.minimum(which, 2), 3)
    kind = jnp.where(is_pair, 4, jnp.where(is_feed, kind, 3))
    kind = jnp.where(tiles_here == tile_count, 5, kind)
    out_at = jnp.clip(tiles_here - query_tiles - 2, 0, query_tiles - 1)
    per_share = share_width // tile_width
    share_at = jnp.where(is_query, jnp.minimum(tiles_here, query_tiles - 1), out_at)
    at = jnp.stack(
        [
            kind,
            column // share,
            column % share,
            share_at // per_share,
            share_at % per_share + jnp.where(is_query, 0, per_share),
            jnp.where(is_pair, tiles_here - query_tiles, 0),
        ]
    )
    new_master, new_one, new_two = adam(
        at,
        gate_plane,
        up_plane,
        down_plane,
        share_plane,
        pair_plane,
        left_basis_set,
        right_basis_set,
        master,
        moment_one,
        moment_two,
    )
    gain_one = BETA_ONE * gain_moment_one + (1.0 - BETA_ONE) * gain_grads
    gain_two = BETA_TWO * gain_moment_two + (1.0 - BETA_TWO) * gain_grads * gain_grads
    new_gains = gains - GAIN_RATE * gain_one / (jnp.sqrt(gain_two) + ADAM_EPS)
    return (
        block_out,
        input_grad,
        new_master,
        new_one,
        new_two,
        gain_grads,
        new_gains,
        gain_one,
        gain_two,
    )


def solution(mesh):
    return jax.shard_map(
        local,
        mesh=mesh,
        in_specs=(
            P(("grp", "seq"), None),
            P(("grp", "seq"), None),
            P(("grp", "seq")),
            P(),
            P("grp", "seq", None),
            P("grp", "seq", None),
            P("grp", "seq", None),
            P("grp", "seq", None),
            P("grp", "seq", None),
            P("grp", "seq", None),
            P(),
            P(),
            P(),
        ),
        out_specs=(
            P(("grp", "seq"), None),
            P(("grp", "seq"), None),
            P("grp", "seq", None),
            P("grp", "seq", None),
            P("grp", "seq", None),
            P(),
            P(),
            P(),
            P(),
        ),
        check_vma=False,
    )
```

```python
import functools

import jax
import jax.numpy as jnp
from jax import lax
from jax.experimental import pallas as pl
from jax.experimental.pallas import tpu as pltpu
from jax.sharding import PartitionSpec as P

MODEL_WIDTH = 2048
NH = 16
HD = 128
FF = 5632
SEQLEN = 1024


NORM_EPS = 1e-05
BETA_ONE = 0.95
BETA_TWO = 0.95
ADAM_EPS = 1e-08
WEIGHT_DECAY = 0.01
LEARN_RATE = 0.03
GAIN_RATE = 1.5
ROPE_BASE = 10000.0
MASKED = -1e30
PRECISE = lax.Precision.HIGHEST


def contract(left_side, right_side):
    return lax.dot_general(
        left_side, right_side, (((0,), (0,)), ((), ())), preferred_element_type=jnp.float32
    )


def times_transpose(left_side, right_side):
    return lax.dot_general(
        left_side, right_side, (((1,), (1,)), ((), ())), preferred_element_type=jnp.float32
    )


def turn_tables(places):
    half_width = HD // 2
    frequency = ROPE_BASE ** (-(jnp.arange(half_width, dtype=jnp.float32) * 2.0) / HD)
    angles = places.astype(jnp.float32)[:, None] * frequency[None, :]
    cosine, sine = jnp.cos(angles), jnp.sin(angles)
    return (
        jnp.concatenate([cosine, cosine], axis=1),
        jnp.concatenate([-sine, sine], axis=1),
    )


def turn(rows, cosine, sine):
    return rows * cosine + pltpu.roll(rows, HD // 2, 1) * sine


def turn_back(rows, cosine, sine):
    return rows * cosine - pltpu.roll(rows, HD // 2, 1) * sine


def dot_last(left_side, right_side):
    return lax.dot_general(
        left_side, right_side, (((1,), (1,)), ((), ())), preferred_element_type=jnp.float32
    )


def dot_first(left_side, right_side):
    return lax.dot_general(
        left_side, right_side, (((0,), (0,)), ((), ())), preferred_element_type=jnp.float32
    )


SMALL_COST = pl.CostEstimate(flops=1, bytes_accessed=1, transcendentals=0)


def project_kernel(x_ref, w_ref, cosine_ref, sine_ref, out_ref):
    made = jnp.dot(x_ref[...], w_ref[...], preferred_element_type=jnp.float32)
    cosine, sine = cosine_ref[...], sine_ref[...]
    first, second = made[:, :HD], made[:, HD:]
    last = pl.program_id(0) == pl.num_programs(0) - 1
    out_ref[:, :HD] = turn(first, cosine, sine).astype(out_ref.dtype)
    out_ref[:, HD:] = jnp.where(last, second, turn(second, cosine, sine)).astype(out_ref.dtype)


def project(normed, weights, tables):
    rows, width = normed.shape
    steps = NH // 2 + 1
    return pl.pallas_call(
        project_kernel,
        grid=(steps,),
        in_specs=[
            pl.BlockSpec((rows, width), lambda j: (0, 0)),
            pl.BlockSpec((width, 2 * HD), lambda j: (0, j)),
            pl.BlockSpec((rows, HD), lambda j: (0, 0)),
            pl.BlockSpec((rows, HD), lambda j: (0, 0)),
        ],
        out_specs=pl.BlockSpec((rows, 2 * HD), lambda j: (0, j)),
        out_shape=jax.ShapeDtypeStruct((rows, steps * 2 * HD), jnp.bfloat16),
        compiler_params=pltpu.CompilerParams(vmem_limit_bytes=56 * 2**20),
        cost_estimate=SMALL_COST,
        name="project",
    )(normed, weights, *tables)


def score_mask(key_seg_ref, query_seg_ref, block, rows):
    keys = (block + 1) * rows
    same = key_seg_ref[:keys, :] == query_seg_ref[...]
    key_at = lax.broadcasted_iota(jnp.int32, (keys, rows), 0)
    query_at = lax.broadcasted_iota(jnp.int32, (keys, rows), 1) + block * rows
    return same & (key_at <= query_at)


def attend_kernel(at_ref, q_ref, k_ref, v_ref, key_seg_ref, query_seg_ref, context_ref, total_ref):
    scale = HD ** (-0.5)
    rows = q_ref.shape[0]
    for block in range(SEQLEN // rows):

        @pl.when(at_ref[0] == block)
        def _():
            keys = (block + 1) * rows
            scores = dot_last(k_ref[:keys, :], q_ref[...]) * scale
            scores = jnp.where(
                score_mask(key_seg_ref, query_seg_ref, block, rows), scores, MASKED
            )
            highest = jnp.max(scores, axis=0, keepdims=True)
            exponent = jnp.exp(scores - highest)
            totals = jnp.sum(exponent, axis=0, keepdims=True)
            probs_low = (exponent * (1.0 / totals)).astype(jnp.bfloat16)
            context = dot_first(probs_low, v_ref[:keys, :])
            context_ref[...] = context.astype(jnp.bfloat16)
            total_ref[0] = highest + jnp.log(totals)


def attend_back_kernel(
    at_ref,
    q_ref,
    k_ref,
    v_ref,
    grad_ref,
    total_ref,
    key_seg_ref,
    query_seg_ref,
    key_cosine_ref,
    key_sine_ref,
    cosine_ref,
    sine_ref,
    query_grad_ref,
    pair_grad_ref,
    key_sum,
    value_sum,
):
    scale = HD ** (-0.5)
    rows = q_ref.shape[0]
    head = pl.program_id(0)

    @pl.when(head == 0)
    def _():
        key_sum[...] = jnp.zeros_like(key_sum)
        value_sum[...] = jnp.zeros_like(value_sum)

    for block in range(SEQLEN // rows):

        @pl.when(at_ref[0] == block)
        def _():
            keys = (block + 1) * rows
            queries, grads = q_ref[...], grad_ref[...]
            shifted = dot_last(k_ref[:keys, :], queries) * scale - total_ref[0]
            allowed = score_mask(key_seg_ref, query_seg_ref, block, rows)
            probs = jnp.where(allowed, jnp.exp(shifted), 0.0)
            prob_grad = dot_last(v_ref[:keys, :], grads)
            centre = jnp.sum(probs * prob_grad, axis=0, keepdims=True)
            score_grad = (probs * (prob_grad - centre) * scale).astype(jnp.bfloat16)
            value_sum[:keys, :] += jnp.dot(
                probs.astype(jnp.bfloat16), grads, preferred_element_type=jnp.float32
            )
            key_sum[:keys, :] += jnp.dot(score_grad, queries, preferred_element_type=jnp.float32)
            query_grad = dot_first(score_grad, k_ref[:keys, :])
            query_grad_ref[...] = turn_back(query_grad, cosine_ref[...], sine_ref[...]).astype(
                jnp.bfloat16
            )

    @pl.when(head == pl.num_programs(0) - 1)
    def _():
        pair_grad_ref[:, :HD] = turn_back(
            key_sum[...], key_cosine_ref[...], key_sine_ref[...]
        ).astype(jnp.bfloat16)
        pair_grad_ref[:, HD:] = value_sum[...].astype(jnp.bfloat16)


def attention_specs(kinds, rows):
    specs = {
        "at": pl.BlockSpec(memory_space=pltpu.SMEM),
        "head": pl.BlockSpec((rows, HD), lambda h: (0, h)),
        "keys": pl.BlockSpec((SEQLEN, HD), lambda h: (0, 0)),
        "values": pl.BlockSpec((SEQLEN, HD), lambda h: (0, 1)),
        "pair": pl.BlockSpec((SEQLEN, 2 * HD), lambda h: (0, 0)),
        "total": pl.BlockSpec((1, 1, rows), lambda h: (h, 0, 0)),
        "key_seg": pl.BlockSpec((SEQLEN, 1), lambda h: (0, 0)),
        "query_seg": pl.BlockSpec((1, rows), lambda h: (0, 0)),
        "key_table": pl.BlockSpec((SEQLEN, HD), lambda h: (0, 0)),
        "table": pl.BlockSpec((rows, HD), lambda h: (0, 0)),
    }
    return [specs[kind] for kind in kinds]


def attend(at, projected, pairs, key_segs, query_segs):
    rows = projected.shape[0]
    columns = NH * HD
    return pl.pallas_call(
        attend_kernel,
        grid=(NH,),
        in_specs=attention_specs(["at", "head", "keys", "values", "key_seg", "query_seg"], rows),
        out_specs=attention_specs(["head", "total"], rows),
        out_shape=(
            jax.ShapeDtypeStruct((rows, columns), jnp.bfloat16),
            jax.ShapeDtypeStruct((NH, 1, rows), jnp.float32),
        ),
        compiler_params=pltpu.CompilerParams(vmem_limit_bytes=32 * 2**20),
        cost_estimate=SMALL_COST,
        name="attend",
    )(at, projected, pairs, pairs, key_segs[:, None], query_segs[None, :])


def attend_back(at, projected, pairs, grads, totals, key_segs, query_segs, key_tables, tables):
    rows = projected.shape[0]
    columns = NH * HD
    return pl.pallas_call(
        attend_back_kernel,
        grid=(NH,),
        in_specs=attention_specs(
            ["at", "head", "keys", "values", "head", "total", "key_seg", "query_seg"]
            + ["key_table", "key_table", "table", "table"],
            rows,
        ),
        out_specs=attention_specs(["head", "pair"], rows),
        out_shape=(
            jax.ShapeDtypeStruct((rows, columns), jnp.bfloat16),
            jax.ShapeDtypeStruct((SEQLEN, 2 * HD), jnp.bfloat16),
        ),
        scratch_shapes=[pltpu.VMEM((SEQLEN, HD), jnp.float32)] * 2,
        compiler_params=pltpu.CompilerParams(vmem_limit_bytes=32 * 2**20),
        cost_estimate=SMALL_COST,
        name="attend_back",
    )(
        at, projected, pairs, pairs, grads, totals, key_segs[:, None], query_segs[None, :],
        *key_tables, *tables,
    )


def load_weights(parts, weights, sems):
    count, rows, _ = parts[0].shape
    halves = len(parts)
    return [
        pltpu.make_async_copy(
            parts[half].at[block],
            weights.at[pl.ds((block * halves + half) * rows, rows)],
            sems.at[block * halves + half],
        )
        for half in range(halves)
        for block in range(count)
    ]


def feed_block(real, x, cot, weights, act_ref, gate_grad_ref, up_grad_ref, two_ref, out_ref):
    low = jnp.bfloat16
    wide = jnp.float32
    cols = act_ref.shape[0]
    gate = jnp.dot(x, weights[:, :cols], preferred_element_type=wide)
    upper = jnp.dot(x, weights[:, cols : 2 * cols], preferred_element_type=wide)
    act_grad = jnp.dot(cot, weights[:, 2 * cols :], preferred_element_type=wide)
    real = lax.broadcasted_iota(jnp.int32, gate.shape, 1) < real
    sigmoid = 1.0 / (1.0 + jnp.exp(-gate))
    silu = gate * sigmoid
    activated = jnp.where(real, silu * upper, 0.0).astype(low)
    act_grad = jnp.where(real, act_grad, 0.0)
    gate_grad = (act_grad * upper * sigmoid * (1.0 + gate * (1.0 - sigmoid))).astype(low)
    up_grad = (act_grad * silu).astype(low)
    act_ref[...] = jnp.transpose(activated)
    gate_grad_ref[...] = jnp.transpose(gate_grad)
    up_grad_ref[...] = jnp.transpose(up_grad)
    two = dot_last(gate_grad, weights[:, :cols]) + dot_last(up_grad, weights[:, cols : 2 * cols])
    two_ref[...] = two.astype(low)
    out_ref[...] = dot_last(activated, weights[:, 2 * cols :]).astype(low)


def feed_kernel(real_ref, x_ref, cot_ref, *refs):
    parts, refs = refs[:-7], refs[-7:]
    weights, sems = refs[5:]

    @pl.when(pl.program_id(0) == 0)
    def _():
        copies = load_weights(parts, weights, sems)
        for copy in copies:
            copy.start()
        for copy in copies:
            copy.wait()

    feed_block(real_ref[0], x_ref[...], cot_ref[...], weights, *refs[:5])


def feed_forward(real_cols, x, cot, parts, seq_count):
    tokens_all, width = x.shape
    _, rows, cols = parts[0].shape
    cols = cols // 3
    step = 256
    low = jnp.bfloat16
    block = pl.BlockSpec((step, width), lambda i: (i, 0))
    narrow = pl.BlockSpec((cols, step), lambda i: (0, i))
    return pl.pallas_call(
        feed_kernel,
        grid=(tokens_all // step,),
        in_specs=[pl.BlockSpec(memory_space=pltpu.SMEM), block, block]
        + [pl.BlockSpec(memory_space=pl.ANY)] * len(parts),
        out_specs=[narrow, narrow, narrow, block, block],
        out_shape=[jax.ShapeDtypeStruct((cols, tokens_all), low)] * 3
        + [jax.ShapeDtypeStruct((tokens_all, width), low)] * 2,
        scratch_shapes=[
            pltpu.VMEM((width, 3 * cols), low),
            pltpu.SemaphoreType.DMA((len(parts) * seq_count,)),
        ],
        compiler_params=pltpu.CompilerParams(vmem_limit_bytes=52 * 2**20),
        cost_estimate=SMALL_COST,
        name="feed_forward",
    )(real_cols, x, cot, *parts)


def feed_gather_kernel(
    first, second, real_ref, own_ref, context_ref, cot_ref, cot_all_ref, part_ref, gate_grad_ref,
    up_grad_ref, two_ref, out_ref, second_ref, context_plane_ref, down_out, blocks, weights,
    act_block, act, x_block, stage, load_sems, keep_sems, x_sems, out_sems, first_send,
    first_recv, second_send, second_recv,
):
    step = pl.program_id(0)
    grp, seq = lax.axis_index("grp"), lax.axis_index("seq")
    first.start(own_ref, blocks, (first_send, first_recv), grp, seq, begin=False)
    second.start(context_ref, context_plane_ref, (second_send, second_recv), grp, seq, begin=False)
    loads = load_weights([part_ref], weights, load_sems)
    cols = act.shape[0]
    step_rows = act_block.shape[1]
    rows = x_block.shape[2]
    count = cot_all_ref.shape[1] // rows

    @pl.when(step == 0)
    def _():
        for copy in loads:
            copy.start()
        barrier = pltpu.get_barrier_semaphore()
        for device in first.peers(grp, seq):
            pl.semaphore_signal(barrier, inc=1, device_id=device, device_id_type=MESH)
        pl.semaphore_wait(barrier, 3)
        first.begin()
        first.kept.wait()
        for copy in loads:
            copy.wait()

    @pl.when(step == 1)
    def _():
        first.due[7].wait_recv()

    @pl.when(step == 2)
    def _():
        for came in (1, 4, 2):
            first.pass_on(came)

    @pl.when(step == 3)
    def _():
        first.pass_on(5)

    @pl.when(step == 4)
    def _():
        first.due[8].wait_recv()
        first.due[9].wait_recv()
        first.pass_on(6)
        first.pass_on(3)
        second.begin()

    @pl.when(step == 5)
    def _():
        first.due[10].wait_recv()
        first.due[11].wait_recv()

    @pl.when(step == 7)
    def _():
        first.due[12].wait_recv()
        first.due[13].wait_recv()
        second.pass_on(1)
        second.pass_on(4)

    keep = pltpu.make_async_copy(blocks.at[step], second_ref.at[step], keep_sems.at[step])
    keep.start()
    feed_block(
        real_ref[0], blocks[step], cot_ref[...], weights, act_block, gate_grad_ref, up_grad_ref,
        two_ref, out_ref,
    )
    act[:, pl.ds(pl.multiple_of(step * step_rows, step_rows), step_rows)] = act_block[...]

    def x_copy(at):
        view = cot_all_ref.at[:, pl.ds(pl.multiple_of(at * rows, rows), rows)]
        return pltpu.make_async_copy(view, x_block.at[at % 2], x_sems.at[at % 2])

    def out_copy(at):
        place = pl.ds(pl.multiple_of(at * cols, cols), cols)
        return pltpu.make_async_copy(stage.at[at % 2], down_out.at[place], out_sems.at[at % 2])

    @pl.when(step == 7)
    def _():
        x_copy(0).start()
        second.pass_on(2)
        second.pass_on(5)

        def one(at, _):
            @pl.when(at == 2)
            def _():
                second.pass_on(6)
                second.pass_on(3)

            x_copy(at).wait()

            @pl.when(at + 1 < count)
            def _():
                x_copy(at + 1).start()

            @pl.when(at >= 2)
            def _():
                out_copy(at - 2).wait()

            stage[at % 2] = jnp.dot(
                act[...], x_block[at % 2], preferred_element_type=jnp.float32
            ).astype(stage.dtype)
            out_copy(at).start()
            return 0

        lax.fori_loop(0, count, one, 0)
        out_copy(count - 2).wait()
        out_copy(count - 1).wait()
        second.finish()
        for copy in first.out[1:]:
            copy.wait_send()
        for at in range(8):
            pltpu.make_async_copy(blocks.at[at], second_ref.at[at], keep_sems.at[at]).wait()


def feed_gather(number, real_cols, normed, context, cot, part, seq_count):
    rows, width = normed.shape
    cols = part.shape[2] // 3
    low = jnp.bfloat16
    block = pl.BlockSpec((rows, width), lambda i: (i, 0))
    narrow = pl.BlockSpec((cols, rows), lambda i: (0, i))
    first = gather_plane(normed.shape, placed=True)
    second = gather_plane(context.shape, placed=True)
    hbm = pl.BlockSpec(memory_space=pl.ANY)
    plane = jax.ShapeDtypeStruct((8, rows, width), low)
    model_rows = width // seq_count
    return pl.pallas_call(
        functools.partial(feed_gather_kernel, first, second),
        grid=(8,),
        in_specs=[pl.BlockSpec(memory_space=pltpu.SMEM), hbm, hbm, block, hbm, hbm],
        out_specs=[narrow, narrow, block, block, hbm, hbm, hbm],
        out_shape=[jax.ShapeDtypeStruct((cols, 8 * rows), low)] * 2
        + [jax.ShapeDtypeStruct((8 * rows, width), low)] * 2
        + [plane, plane, jax.ShapeDtypeStruct((seq_count * cols, model_rows), low)],
        scratch_shapes=[
            pltpu.VMEM((8, rows, width), low),
            pltpu.VMEM((width, 3 * cols), low),
            pltpu.VMEM((cols, rows), low),
            pltpu.VMEM((cols, 8 * rows), low),
            pltpu.VMEM((2, 8 * rows, model_rows), low),
            pltpu.VMEM((2, cols, model_rows), low),
            pltpu.SemaphoreType.DMA((seq_count,)),
            pltpu.SemaphoreType.DMA((8,)),
            pltpu.SemaphoreType.DMA((2,)),
            pltpu.SemaphoreType.DMA((2,)),
        ]
        + [pltpu.SemaphoreType.DMA((14,))] * 4,
        compiler_params=pltpu.CompilerParams(
            collective_id=number, has_side_effects=True, vmem_limit_bytes=60 * 2**20
        ),
        cost_estimate=SMALL_COST,
        name="feed_gather",
    )(real_cols, normed, context, cot, cot, part)


def weight_grad_kernel(left_ref, x_ref, out_ref):
    out_ref[...] = jnp.dot(
        left_ref[...], x_ref[...], preferred_element_type=jnp.float32
    ).astype(out_ref.dtype)


def weight_grad(left, x, seq_count):
    cols, tokens_all = left.shape
    rows = x.shape[1] // seq_count
    return pl.pallas_call(
        weight_grad_kernel,
        grid=(seq_count,),
        in_specs=[
            pl.BlockSpec((cols, tokens_all), lambda i: (0, 0)),
            pl.BlockSpec((tokens_all, rows), lambda i: (0, i)),
        ],
        out_specs=pl.BlockSpec((cols, rows), lambda i: (i, 0)),
        out_shape=jax.ShapeDtypeStruct((seq_count * cols, rows), jnp.bfloat16),
        compiler_params=pltpu.CompilerParams(vmem_limit_bytes=40 * 2**20),
        cost_estimate=SMALL_COST,
        name="weight_grad",
    )(left, x)


def pick_kernel(share, slots_ref, *refs):
    count = len(refs) - 2
    sources, out_ref, sems = refs[:count], refs[count], refs[count + 1]
    width = sources[0].shape[2]
    start = 0
    copies = []
    for at, source in enumerate(sources):
        rows = source.shape[1]
        if at == 0 and share is not None:
            rows = share
            part = pl.ds(pl.multiple_of(lax.axis_index("grp") * rows, rows), rows)
        else:
            part = pl.ds(0, rows)
        for tile in range(slots_ref.shape[0]):
            copies.append(
                pltpu.make_async_copy(
                    source.at[slots_ref[tile], part],
                    out_ref.at[pl.ds(start, rows), tile * width : (tile + 1) * width],
                    sems.at[len(copies)],
                )
            )
        start += rows
    for copy in copies:
        copy.start()
    for copy in copies:
        copy.wait()


def pick(slots, sources, share=None):
    count, width = slots.shape[0], sources[0].shape[2]
    rows = sum(source.shape[1] for source in sources)
    if share is not None:
        rows += share - sources[0].shape[1]
    return pl.pallas_call(
        functools.partial(pick_kernel, share),
        in_specs=[pl.BlockSpec(memory_space=pltpu.SMEM)]
        + [pl.BlockSpec(memory_space=pl.ANY)] * len(sources),
        out_specs=pl.BlockSpec(memory_space=pltpu.VMEM),
        out_shape=jax.ShapeDtypeStruct((rows, count * width), sources[0].dtype),
        scratch_shapes=[pltpu.SemaphoreType.DMA((count * len(sources),))],
        cost_estimate=SMALL_COST,
        name="pick",
    )(slots, *sources)


def adam_kernel(
    at_ref, gate_ref, up_ref, down_ref, share_ref, pair_ref, left_ref, right_ref, master_ref,
    one_ref, two_ref, new_master_ref, new_one_ref, new_two_ref, grad,
):
    kind = at_ref[0, pl.program_id(0)]
    for number, ref in enumerate((gate_ref, up_ref, down_ref, share_ref)):

        @pl.when(kind == number)
        def _():
            grad[...] = ref[0]

    @pl.when(kind == 4)
    def _():
        pair = pair_ref[...].reshape(grad.shape[1], grad.shape[0])
        grad[...] = jnp.transpose(pair.astype(jnp.float32)).astype(grad.dtype)

    @pl.when(kind == 5)
    def _():
        grad[...] = jnp.zeros_like(grad)

    low = jnp.bfloat16
    left, right = left_ref[0].astype(low), right_ref[0].astype(low)
    turned = jnp.dot(grad[...], left, preferred_element_type=jnp.float32)
    turned = dot_first(turned.astype(low), right)
    new_one = BETA_ONE * one_ref[0] + (1.0 - BETA_ONE) * turned
    new_two = BETA_TWO * two_ref[0] + (1.0 - BETA_TWO) * turned * turned
    new_one_ref[0], new_two_ref[0] = new_one, new_two
    scaled = new_one / (jnp.sqrt(new_two) + ADAM_EPS)
    restored = dot_last(scaled.astype(low), right)
    restored = jnp.dot(left, restored.astype(low), preferred_element_type=jnp.float32)
    new_master_ref[0] = master_ref[0] * (1.0 - LEARN_RATE * WEIGHT_DECAY) - LEARN_RATE * restored


def adam(at, gate, up, down, shares, pairs, left, right, master, one, two):
    slots, rows, width = master.shape
    tile = pl.BlockSpec((1, rows, width), lambda i, at: (i, 0, 0))
    shape = jax.ShapeDtypeStruct(master.shape, jnp.float32)
    feed = pl.BlockSpec((1, width, rows), lambda i, at: (at[1, i], at[2, i], 0))
    return pl.pallas_call(
        adam_kernel,
        grid_spec=pltpu.PrefetchScalarGridSpec(
            num_scalar_prefetch=1,
            grid=(slots,),
            in_specs=[
                feed,
                feed,
                feed,
                pl.BlockSpec((1, width, rows), lambda i, at: (at[3, i], at[4, i], 0)),
                pl.BlockSpec((*pairs.shape[:2], width), lambda i, at: (0, 0, at[5, i])),
                pl.BlockSpec((1, rows, rows), lambda i, at: (i, 0, 0)),
                pl.BlockSpec((1, width, width), lambda i, at: (i, 0, 0)),
                tile,
                tile,
                tile,
            ],
            out_specs=[tile] * 3,
            scratch_shapes=[pltpu.VMEM((width, rows), jnp.bfloat16)],
        ),
        out_shape=[shape] * 3,
        compiler_params=pltpu.CompilerParams(vmem_limit_bytes=60 * 2**20),
        cost_estimate=SMALL_COST,
        name="adam",
    )(at, gate, up, down, shares, pairs, left, right, master, one, two)


MESH = pl.DeviceIdType.MESH


def remote(source, target, sems, at, device):
    return pltpu.make_async_remote_copy(
        src_ref=source,
        dst_ref=target,
        send_sem=sems[0].at[at],
        recv_sem=sems[1].at[at],
        device_id=device,
        device_id_type=MESH,
    )


def columns_of(ref, index, width):
    return ref.at[:, pl.ds(pl.multiple_of(index * width, width), width)]


def rows_of(ref, index, height):
    return ref.at[pl.ds(pl.multiple_of(index * height, height), height), :]


PLACES = {0: 0, 1: 1, 2: 2, 4: 3, 3: 4, 5: 5, 6: 6, 7: 7}


def flip(device, bits):
    core, side_x, side_y = device % 2, (device // 2) % 2, device // 4
    for bit, there in ((1, 1 - 2 * core), (2, 2 - 4 * side_x), (4, 4 - 8 * side_y)):
        if bits & bit:
            device = device + there
    return device


class PlacedExchange:
    axis = "grp"
    sem_count = 8

    def __init__(self, out_shape, source_view):
        self.out_shape, self.source_view = out_shape, source_view

    def peers(self, grp, seq):
        for bits in range(1, 8):
            yield flip(grp, bits), seq

    def start(self, source, target, sems, grp, seq):
        self.own = pltpu.make_async_copy(
            self.source_view(source, grp), target.at[0], sems[0].at[0]
        )
        self.own.start()
        self.copies = []
        for bits in range(1, 8):
            there = flip(grp, bits)
            copy = remote(
                self.source_view(source, there), target.at[PLACES[bits]], sems, bits, (there, seq)
            )
            copy.start()
            self.copies.append(copy)

    def forward(self):
        return iter(())

    def finish(self):
        for copy in self.copies:
            copy.wait()
        self.own.wait()


class Exchange:
    def __init__(self, axis, out_shape, source_view, target_view):
        self.axis, self.out_shape = axis, out_shape
        self.source_view, self.target_view = source_view, target_view
        self.count = lax.axis_size(axis)
        self.sem_count = self.count

    def peers(self, grp, seq):
        me = grp if self.axis == "grp" else seq
        for step in range(1, self.count):
            there = (me + step) % self.count
            yield (there, seq) if self.axis == "grp" else (grp, there)

    def start(self, source, target, sems, grp, seq):
        me = grp if self.axis == "grp" else seq
        self.own = pltpu.make_async_copy(
            self.source_view(source, me), self.target_view(target, me), sems[0].at[0]
        )
        self.own.start()
        self.sent, self.due = [], []
        for step, device in enumerate(self.peers(grp, seq), 1):
            there = (me + step) % self.count
            back = (me + self.count - step) % self.count
            copy = remote(
                self.source_view(source, there), self.target_view(target, me), sems, step, device
            )
            copy.start()
            self.sent.append(copy)
            self.due.append(
                remote(
                    self.source_view(source, back), self.target_view(target, back), sems, step, device
                )
            )

    def forward(self):
        return iter(())

    def finish(self):
        for copy in self.due:
            copy.wait_recv()
        for copy in self.sent:
            copy.wait_send()
        self.own.wait()


class PlaneGather:
    axis = "grp"
    sem_count = 14

    def __init__(self, out_shape, source_view, target_view, half_of, placed):
        self.out_shape, self.placed = out_shape, placed
        self.source_view, self.target_view, self.half_of = source_view, target_view, half_of

    def peers(self, grp, seq):
        for bits in (1, 2, 4):
            yield flip(grp, bits), seq

    def start(self, source, target, sems, grp, seq, begin=True):
        def part(device, bits, piece):
            view = self.target_view(target, PLACES[bits] if self.placed else flip(device, bits))
            return view if piece == "all" else self.half_of(view, piece == "b")

        def own(piece):
            view = self.source_view(source, grp)
            return view if piece == "all" else self.half_of(view, piece == "b")

        self.out, self.due = [None], [None]
        for via, here, there, piece in (
            (2, 0, 2, "a"),
            (2, 0, 2, "b"),
            (2, 4, 6, "b"),
            (4, 0, 4, "b"),
            (4, 0, 4, "a"),
            (4, 2, 6, "a"),
            (1, 0, 1, "all"),
            (1, 2, 3, "a"),
            (1, 2, 3, "b"),
            (1, 4, 5, "b"),
            (1, 4, 5, "a"),
            (1, 6, 7, "a"),
            (1, 6, 7, "b"),
        ):
            device = flip(grp, via)
            view = own(piece) if here == 0 else part(grp, here, piece)
            at = len(self.out)
            self.out.append(remote(view, part(device, there, piece), sems, at, (device, seq)))
            self.due.append(remote(view, part(grp, there, piece), sems, at, (device, seq)))
        self.kept = pltpu.make_async_copy(own("all"), part(grp, 0, "all"), sems[0].at[0])
        if begin:
            self.begin()

    def begin(self):
        self.kept.start()
        for at in (1, 4, 2, 5, 7):
            self.out[at].start()

    def pass_on(self, came):
        self.due[came].wait_recv()
        for at in {1: (6, 8), 4: (3, 10), 2: (9,), 5: (11,), 6: (12,), 3: (13,)}[came]:
            self.out[at].start()

    def forward(self):
        for pair in ((1, 4), (2, 5), (6, 3)):
            for came in pair:
                self.pass_on(came)
            yield

    def finish(self):
        for copy in self.due[7:]:
            copy.wait_recv()
        for copy in self.out[1:]:
            copy.wait_send()
        self.kept.wait()


def add_rows(total, first, second):
    step = 32

    def some(at, _):
        rows = pl.ds(pl.multiple_of(at * step, step), step)
        total[rows, :] = (
            first[rows, :].astype(jnp.float32) + second[rows, :].astype(jnp.float32)
        ).astype(total.dtype)
        return 0

    lax.fori_loop(0, total.shape[0] // step, some, 0)


class PlaneSum:
    axis = "grp"
    sem_count = 15

    def __init__(self, rows, columns):
        self.rows, self.columns = rows, columns
        self.out_shape = (rows, columns)

    def scratch(self):
        low = jnp.bfloat16
        shape = (self.rows, self.columns)
        half = (self.rows // 2, self.columns)
        return [
            pltpu.VMEM((4, *shape), low),
            pltpu.VMEM((4, *shape), low),
            pltpu.VMEM((2, *half), low),
            pltpu.VMEM((2, *shape), low),
        ]

    def peers(self, grp, seq):
        for bits in (1, 2, 4):
            yield flip(grp, bits), seq

    def start(self, source, target, sems, grp, seq, scratch):
        self.target = target
        self.mine, self.core_in, self.halves, self.wholes = scratch
        core, side_x, side_y = [(flip(grp, bits), seq) for bits in (1, 2, 4)]
        half = self.rows // 2
        self.low, self.high = low, high = pl.ds(0, half), pl.ds(half, half)
        mine, halves, wholes = self.mine, self.halves, self.wholes
        self.copies = [
            remote(source.at[PLACES[bits]], self.core_in.at[at], sems, at, core)
            for at, bits in enumerate((7, 3, 5, 1))
        ] + [
            remote(mine.at[0, low], halves.at[0], sems, 4, side_x),
            remote(mine.at[0, high], halves.at[1], sems, 5, side_y),
            remote(mine.at[1, low], wholes.at[0, low], sems, 6, side_x),
            remote(mine.at[2, high], wholes.at[1, high], sems, 7, side_y),
            remote(mine.at[1, high], wholes.at[0, high], sems, 8, side_x),
            remote(mine.at[2, low], wholes.at[1, low], sems, 9, side_y),
        ]
        self.loads = [
            pltpu.make_async_copy(source.at[PLACES[bits]], mine.at[at], sems[0].at[10 + at])
            for at, bits in enumerate((6, 2, 4, 0))
        ]
        self.store = pltpu.make_async_copy(mine.at[3], target, sems[0].at[14])
        for copy in self.copies[:4] + self.loads:
            copy.start()

    def first_sums(self):
        for came, then in ((0, (4, 5)), (1, (6,)), (2, (7,)), (3, ())):
            self.copies[came].wait_recv()
            self.loads[came].wait()
            add_rows(self.mine.at[came], self.mine.at[came], self.core_in.at[came])
            for at in then:
                self.copies[at].start()

    def forward(self):
        mine, low, high = self.mine, self.low, self.high
        yield
        self.copies[5].wait_recv()
        add_rows(mine.at[1, high], mine.at[1, high], self.halves.at[1])
        self.copies[8].start()
        self.copies[4].wait_recv()
        add_rows(mine.at[2, low], mine.at[2, low], self.halves.at[0])
        self.copies[9].start()

    def finish(self):
        mine = self.mine
        for at, side, rows in ((6, 0, self.low), (7, 1, self.high), (8, 0, self.high), (9, 1, self.low)):
            self.copies[at].wait_recv()
            add_rows(mine.at[3, rows], mine.at[3, rows], self.wholes.at[side, rows])
        self.store.start()
        for copy in self.copies:
            copy.wait_send()
        self.store.wait()


class LineGather:
    axis = "seq"

    def __init__(self, shape):
        self.count = lax.axis_size("seq")
        self.out_shape = (self.count, *shape)
        self.sem_count = 2 * self.count

    def peers(self, grp, seq):
        for step in range(1, self.count):
            yield grp, (seq + step) % self.count

    def start(self, source, target, sems, grp, seq):
        self.seq, self.sems = seq, sems
        self.own = pltpu.make_async_copy(source, target.at[seq], sems[0].at[0])
        self.own.start()

        def make(away, up):
            there = (seq + (1 if up else self.count - 1)) % self.count
            block = (seq + (self.count - away if up else away)) % self.count
            view = source if away == 0 else target.at[block]
            at = 1 + away if up else self.count + away
            return remote(view, target.at[block], sems, at, (grp, there))

        def came(away, up):
            block = (seq + (self.count - away if up else away)) % self.count
            at = away if up else self.count + away - 1
            side = (seq + (self.count - 1 if up else 1)) % self.count
            return remote(target.at[block], target.at[block], sems, at, (grp, side))

        self.make, self.came = make, came
        self.has = lambda away, up: (seq - away >= 0) if up else (seq + away < self.count)
        self.last = lambda up: (seq + 1 < self.count) if up else (seq >= 1)
        for up in (True, False):

            @pl.when(self.last(up))
            def _():
                make(0, up).start()

    def forward(self):
        for away in range(1, self.count):
            for up in (True, False):

                @pl.when(self.has(away, up))
                def _():
                    self.came(away, up).wait_recv()
                    if away < self.count - 1:

                        @pl.when(self.last(up))
                        def _():
                            self.make(away, up).start()

            yield

    def finish(self):
        for away in range(self.count - 1):
            for up in (True, False):

                @pl.when(self.has(away, up) & self.last(up))
                def _():
                    self.make(away, up).wait_send()
        self.own.wait()


def half_rows(axis, height):
    def half_of(view, second):
        index = (slice(None),) * axis + (pl.ds(height if second else 0, height),)
        return view.at[index]

    return half_of


def whole(ref, index):
    return ref


def block_of(ref, index):
    return ref.at[index]


def gather_plane(
    shape, split=0, source_view=whole, target_view=block_of, out_shape=None, placed=False
):
    out_shape = out_shape or (lax.axis_size("grp"), *shape)
    if lax.axis_size("grp") == 8:
        halves = half_rows(split, shape[split] // 2)
        return PlaneGather(out_shape, source_view, target_view, halves, placed)
    return Exchange("grp", out_shape, source_view, target_view)


def hand_on(tasks):
    going = [task.forward() for task in tasks]
    while going:
        going = [steps for steps in going if next(steps, going) is not going]


def exchange_kernel(tasks, wires, arrays, outputs, *refs):
    sources, targets = refs[:arrays], refs[arrays : arrays + outputs]
    refs = list(refs[arrays + outputs :])
    sems, scratch = [], []
    for task in tasks:
        sems.append((refs.pop(0), refs.pop(0)))
        held = len(task.scratch()) if isinstance(task, PlaneSum) else 0
        scratch.append([refs.pop(0) for _ in range(held)])
    grp, seq = lax.axis_index("grp"), lax.axis_index("seq")
    barrier = pltpu.get_barrier_semaphore()
    axes = {"grp": [], "seq": []}
    for task in tasks:
        devices = list(task.peers(grp, seq))
        if len(devices) > len(axes[task.axis]):
            axes[task.axis] = devices
    devices = axes["grp"] + axes["seq"]
    for device in devices:
        pl.semaphore_signal(barrier, inc=1, device_id=device, device_id_type=MESH)
    pl.semaphore_wait(barrier, len(devices))

    def start(at):
        after, source, target = wires[at]
        source = targets[source] if after is not None else sources[source]
        more = (scratch[at],) if scratch[at] else ()
        tasks[at].start(source, targets[target], sems[at], grp, seq, *more)

    open_tasks = list(range(len(tasks)))
    first = [at for at in open_tasks if wires[at][0] is None]
    for at in first:
        start(at)
    for at in first:
        if isinstance(tasks[at], PlaneSum):
            tasks[at].first_sums()
    hand_on([tasks[at] for at in first])
    for at in open_tasks[:]:
        after = wires[at][0]
        if after is not None:
            tasks[after].finish()
            open_tasks.remove(after)
            start(at)
            hand_on([tasks[at]])
    for at in open_tasks:
        tasks[at].finish()


def exchange(number, work):
    tasks = [piece[0] for piece in work]
    arrays, shapes, wires = [], [], []
    for piece in work:
        if isinstance(piece[1], int):
            after, source = piece[1], wires[piece[1]][2]
            kind = shapes[source].dtype
        else:
            after, source = None, len(arrays)
            arrays.append(piece[1])
            kind = piece[1].dtype
        if len(piece) == 3:
            target = wires[piece[2]][2]
        else:
            target = len(shapes)
            shapes.append(jax.ShapeDtypeStruct(piece[0].out_shape, kind))
        wires.append((after, source, target))
    scratch = []
    for task in tasks:
        scratch += [pltpu.SemaphoreType.DMA((task.sem_count,))] * 2
        if isinstance(task, PlaneSum):
            scratch += task.scratch()
    return pl.pallas_call(
        functools.partial(exchange_kernel, tasks, wires, len(arrays), len(shapes)),
        in_specs=[pl.BlockSpec(memory_space=pl.ANY)] * len(arrays),
        out_specs=[pl.BlockSpec(memory_space=pl.ANY)] * len(shapes),
        out_shape=shapes,
        scratch_shapes=scratch,
        compiler_params=pltpu.CompilerParams(collective_id=number, has_side_effects=True),
        cost_estimate=SMALL_COST,
        name="exchange",
    )(*arrays)


def gather_axis(axis, array):
    task = Exchange(axis, (lax.axis_size(axis), *array.shape), whole, block_of)
    return task, array


def split_rows(axis, array):
    count = lax.axis_size(axis)
    rows, columns = array.shape
    height = rows // count
    task = Exchange(
        axis,
        (count, height, columns),
        lambda ref, index: rows_of(ref, index, height),
        block_of,
    )
    return task, array


def split_columns(axis, array, placed=False):
    count = lax.axis_size(axis)
    rows, columns = array.shape
    width = columns // count
    if placed and count == 8:
        task = PlacedExchange(
            (count, rows, width), lambda ref, index: columns_of(ref, index, width)
        )
        return task, array
    task = Exchange(
        axis,
        (count, rows, width),
        lambda ref, index: columns_of(ref, index, width),
        block_of,
    )
    return task, array


def plane_sum_kernel(
    part_ref, gate_ref, up_ref, x_ref, total_ref, gate_out, up_out, core_in, chip, half_x, half_y,
    whole_x, whole_y, x_block, stage, send_sems, recv_sems, x_sems, out_sems,
):
    grp, seq = lax.axis_index("grp"), lax.axis_index("seq")
    core, side_x, side_y = [flip(grp, bits) for bits in (1, 2, 4)]
    blocks = [PLACES[bits] for bits in (6, 2, 4, 0)]
    core_blocks = [PLACES[bits] for bits in (7, 3, 5, 1)]
    half = total_ref.shape[0] // 2
    low, high = pl.ds(0, half), pl.ds(half, half)
    cols = gate_ref.shape[0]
    rows = x_block.shape[2]
    count = x_ref.shape[1] // rows

    def x_copy(at):
        view = x_ref.at[:, pl.ds(pl.multiple_of(at * rows, rows), rows)]
        return pltpu.make_async_copy(view, x_block.at[at % 2], x_sems.at[at % 2])

    def out_copies(at):
        place = pl.ds(pl.multiple_of(at * cols, cols), cols)
        return [
            pltpu.make_async_copy(
                stage.at[which, at % 2], out.at[place], out_sems.at[which, at % 2]
            )
            for which, out in enumerate((gate_out, up_out))
        ]

    x_copy(0).start()
    barrier = pltpu.get_barrier_semaphore()
    for device in (core, side_x, side_y):
        pl.semaphore_signal(barrier, inc=1, device_id=(device, seq), device_id_type=MESH)
    pl.semaphore_wait(barrier, 3)

    sems = (send_sems, recv_sems)
    copies = [
        remote(part_ref.at[block], core_in.at[at], sems, at, (core, seq))
        for at, block in enumerate(core_blocks)
    ]
    copies += [
        remote(chip.at[0, low], half_x, sems, 4, (side_x, seq)),
        remote(chip.at[0, high], half_y, sems, 5, (side_y, seq)),
        remote(chip.at[1, low], whole_x.at[low], sems, 6, (side_x, seq)),
        remote(chip.at[2, high], whole_y.at[high], sems, 7, (side_y, seq)),
        remote(chip.at[1, high], whole_x.at[high], sems, 8, (side_x, seq)),
        remote(chip.at[2, low], whole_y.at[low], sems, 9, (side_y, seq)),
    ]
    for copy in copies[:4]:
        copy.start()

    def step(at, _):
        @pl.when(at == 1)
        def _():
            for came, then in ((0, (4, 5)), (1, (6,)), (2, (7,))):
                copies[came].wait_recv()
                add_rows(chip.at[came], part_ref.at[blocks[came]], core_in.at[came])
                for start in then:
                    copies[start].start()

        @pl.when(at == count - 1)
        def _():
            copies[5].wait_recv()
            add_rows(chip.at[1, high], chip.at[1, high], half_y)
            copies[8].start()
            copies[4].wait_recv()
            add_rows(chip.at[2, low], chip.at[2, low], half_x)
            copies[9].start()

        x_copy(at).wait()

        @pl.when(at + 1 < count)
        def _():
            x_copy(at + 1).start()

        @pl.when(at >= 2)
        def _():
            for copy in out_copies(at - 2):
                copy.wait()

        for which, ref in enumerate((gate_ref, up_ref)):
            stage[which, at % 2] = jnp.dot(
                ref[...], x_block[at % 2], preferred_element_type=jnp.float32
            ).astype(stage.dtype)
        for copy in out_copies(at):
            copy.start()
        return 0

    lax.fori_loop(0, count, step, 0)
    copies[3].wait_recv()
    add_rows(total_ref, part_ref.at[blocks[3]], core_in.at[3])
    for at, came, rows_at in (
        (6, whole_x, low),
        (7, whole_y, high),
        (8, whole_x, high),
        (9, whole_y, low),
    ):
        copies[at].wait_recv()
        add_rows(total_ref.at[rows_at], total_ref.at[rows_at], came.at[rows_at])
    for copy in copies:
        copy.wait_send()
    for at in (count - 2, count - 1):
        for copy in out_copies(at):
            copy.wait()


def plane_sum(number, part, gate_grad, up_grad, x, seq_count):
    count = lax.axis_size("grp")
    rows_all, columns = part.shape
    rows = rows_all // count
    if count != 8:
        total = lax.psum_scatter(part, "grp", scatter_dimension=0, tiled=True)
        return (
            total.astype(jnp.float32),
            weight_grad(gate_grad, x, seq_count),
            weight_grad(up_grad, x, seq_count),
        )
    low = jnp.bfloat16
    cols, tokens_all = gate_grad.shape
    width = x.shape[1] // seq_count
    vmem = pl.BlockSpec(memory_space=pltpu.VMEM)
    hbm = pl.BlockSpec(memory_space=pl.ANY)
    grads = jax.ShapeDtypeStruct((seq_count * cols, width), low)
    return pl.pallas_call(
        plane_sum_kernel,
        in_specs=[vmem, vmem, vmem, hbm],
        out_specs=[vmem, hbm, hbm],
        out_shape=[jax.ShapeDtypeStruct((rows, columns), jnp.float32), grads, grads],
        scratch_shapes=[
            pltpu.VMEM((4, rows, columns), low),
            pltpu.VMEM((3, rows, columns), low),
            pltpu.VMEM((rows // 2, columns), low),
            pltpu.VMEM((rows // 2, columns), low),
            pltpu.VMEM((rows, columns), low),
            pltpu.VMEM((rows, columns), low),
            pltpu.VMEM((2, tokens_all, width), low),
            pltpu.VMEM((2, 2, cols, width), low),
            pltpu.SemaphoreType.DMA((10,)),
            pltpu.SemaphoreType.DMA((10,)),
            pltpu.SemaphoreType.DMA((2,)),
            pltpu.SemaphoreType.DMA((2, 2)),
        ],
        compiler_params=pltpu.CompilerParams(
            collective_id=number, has_side_effects=True, vmem_limit_bytes=56 * 2**20
        ),
        cost_estimate=SMALL_COST,
        name="plane_sum",
    )(part.reshape(count, rows, columns), gate_grad, up_grad, x)


def local(
    tokens,
    cotangent,
    segment_ids,
    tile_owner_slots,
    weights_low,
    master,
    moment_one,
    moment_two,
    left_basis_set,
    right_basis_set,
    gains,
    gain_moment_one,
    gain_moment_two,
):
    grp_count = lax.axis_size("grp")
    seq_count = lax.axis_size("seq")
    grp_here, seq_here = lax.axis_index("grp"), lax.axis_index("seq")
    rows_here = tokens.shape[0]
    slots_here, rows_block, tile_width = weights_low.shape
    tile_count = tile_owner_slots.shape[0]
    query_cols = NH * HD
    value_end = query_cols + 2 * HD
    output_end = value_end + MODEL_WIDTH
    attn_tiles = output_end // tile_width
    query_tiles = query_cols // tile_width
    hidden_tiles = FF // tile_width
    share = -(-hidden_tiles // grp_count)
    share_cols = share * tile_width
    share_width = MODEL_WIDTH // grp_count
    sub_rows = rows_block // grp_count
    halves = 2 if sub_rows >= 32 else 1
    half_block, half_sub = rows_block // halves, sub_rows // halves
    first_place = (seq_here * rows_here) % SEQLEN
    key_tables = turn_tables(jnp.arange(SEQLEN, dtype=jnp.int32))
    tables = [lax.dynamic_slice_in_dim(table, first_place, rows_here) for table in key_tables]

    hidden_ids = grp_here * share + jnp.arange(share, dtype=jnp.int32)
    hidden_ids = jnp.minimum(hidden_ids, hidden_tiles - 1)
    feed_ids = (
        attn_tiles
        + jnp.arange(3, dtype=jnp.int32)[:, None] * hidden_tiles
        + hidden_ids[None, :]
    ).reshape(-1)
    feed_slots, attn_slots = tile_owner_slots[feed_ids], tile_owner_slots[:attn_tiles]

    tok_float = tokens.astype(jnp.float32)
    inverse_one = lax.rsqrt(jnp.mean(tok_float * tok_float, axis=-1, keepdims=True) + NORM_EPS)
    normed = (tok_float * inverse_one * gains[0]).astype(jnp.bfloat16)

    def weight_half(at):
        return gather_plane(
            (slots_here, half_block, tile_width),
            split=1,
            source_view=lambda ref, index: ref.at[:, pl.ds(at * half_block, half_block)],
        )

    flat = (grp_count * slots_here, -1, tile_width)
    work = [(weight_half(0), weights_low)]
    if halves == 2:
        late_rows = Exchange(
            "grp",
            (grp_count, slots_here, half_sub, tile_width),
            lambda ref, index: ref.at[:, pl.ds(half_block + index * half_sub, half_sub)],
            block_of,
        )
        work.append((late_rows, weights_low))
    tiles = [part.reshape(flat) for part in exchange(0, work)]
    attn_rows = pick(attn_slots, tiles, half_sub).reshape(halves, half_sub, output_end)
    if grp_count == 8 and seq_count == 4:
        work = [(LineGather(attn_rows.shape), attn_rows)]
    else:
        work = [gather_axis("seq", attn_rows)]
    if halves == 2:
        work.append((weight_half(1), weights_low))
    attn_seq, *more = exchange(1, work)
    tiles = tiles[:1] + [part.reshape(flat) for part in more]
    feed_rows = pick(feed_slots, tiles)
    feed_parts = [lax.all_gather(feed_rows, "seq", axis=0, tiled=False)]
    attn_plane = gather_plane(
        attn_seq.shape,
        target_view=lambda ref, index: ref.at[:, :, index],
        out_shape=(seq_count, halves, grp_count, half_sub, output_end),
    )
    (attn_weights,) = exchange(2, [(attn_plane, attn_seq)])
    attn_weights = attn_weights.reshape(MODEL_WIDTH, output_end)

    projected = project(normed, attn_weights, tables)
    pairs, segments, cot_plane, normed_plane = exchange(
        3,
        [
            gather_axis("seq", projected[:, query_cols:]),
            gather_axis("seq", segment_ids.reshape(-1, tile_width)),
            (gather_plane(cotangent.shape, placed=True), cotangent),
            (gather_plane(normed.shape, placed=True), normed),
        ],
    )
    first_key = seq_here * rows_here - first_place
    pairs = lax.dynamic_slice_in_dim(pairs.reshape(-1, 2 * HD), first_key, SEQLEN)
    key_segs = lax.dynamic_slice_in_dim(segments.reshape(-1), first_key, SEQLEN)
    at = (first_place // rows_here).reshape(1)
    context, log_totals = attend(at, projected, pairs, key_segs, segment_ids)
    branch = jnp.dot(
        context, attn_weights[:, value_end:], preferred_element_type=jnp.float32
    )
    hidden = tok_float + branch
    inverse_two = lax.rsqrt(jnp.mean(hidden * hidden, axis=-1, keepdims=True) + NORM_EPS)
    normed_two = (hidden * inverse_two * gains[1]).astype(jnp.bfloat16)

    cot_plane = cot_plane.reshape(-1, MODEL_WIDTH)
    normed_plane = normed_plane.reshape(-1, MODEL_WIDTH)
    real_cols = jnp.clip((hidden_tiles - grp_here * share) * tile_width, 0, share_cols).reshape(1)
    if grp_count == 8:
        gate_grad, up_grad, two_part, feed_part, second_plane, context_plane, down_grad = (
            feed_gather(
                4, real_cols, normed_two, context, cot_plane, feed_parts[0], seq_count
            )
        )
        second_plane = second_plane.reshape(-1, MODEL_WIDTH)
    else:
        second_plane, context_plane = exchange(
            4,
            [
                (gather_plane(normed_two.shape), normed_two),
                (gather_plane(context.shape), context),
            ],
        )
        second_plane = second_plane.reshape(-1, MODEL_WIDTH)
        activated, gate_grad, up_grad, two_part, feed_part = feed_forward(
            real_cols, second_plane, cot_plane, feed_parts, seq_count
        )
        down_grad = weight_grad(activated, cot_plane, seq_count)
    context_plane = context_plane.reshape(-1, MODEL_WIDTH)
    down_grad, two_part = lax.optimization_barrier((down_grad, two_part))
    down_grad = lax.psum_scatter(down_grad, "seq", scatter_dimension=0, tiled=True)
    norm_two_grad, gate_weight_grad, up_weight_grad = plane_sum(
        5, two_part, gate_grad, up_grad, second_plane, seq_count
    )
    gate_weight_grad = lax.psum_scatter(gate_weight_grad, "seq", scatter_dimension=0, tiled=True)
    up_weight_grad = lax.psum_scatter(up_weight_grad, "seq", scatter_dimension=0, tiled=True)

    out_grad = cotangent.astype(jnp.float32)
    gain_two_term = jnp.sum(norm_two_grad * hidden * inverse_two, axis=0)
    hidden_grad = (
        out_grad
        + inverse_two * gains[1] * norm_two_grad
        - hidden
        * inverse_two**3
        * jnp.mean(hidden * gains[1] * norm_two_grad, axis=-1, keepdims=True)
    )
    branch_grad = hidden_grad.astype(jnp.bfloat16)
    context_grad = times_transpose(branch_grad, attn_weights[:, value_end:]).astype(jnp.bfloat16)
    query_grad, pair_part = attend_back(
        at,
        projected,
        pairs,
        context_grad,
        log_totals,
        key_segs,
        segment_ids,
        key_tables,
        tables,
    )
    if seq_count * rows_here > SEQLEN:
        pair_part = lax.dynamic_update_slice_in_dim(
            jnp.zeros((seq_count * rows_here, 2 * HD), pair_part.dtype), pair_part, first_key, 0
        )
    pair_parts, query_share, branch_share = exchange(
        6,
        [
            split_rows("seq", pair_part),
            split_columns("grp", query_grad, placed=True),
            split_columns("grp", branch_grad, placed=True),
        ],
    )
    pair_grad = jnp.sum(pair_parts.astype(jnp.float32), axis=0).astype(jnp.bfloat16)
    pair_grad, down_grad = lax.optimization_barrier((pair_grad, down_grad))
    projected_grad = jnp.concatenate([query_grad, pair_grad], axis=1)
    norm_one_grad = times_transpose(projected_grad, attn_weights[:, :value_end])
    gain_one_term = jnp.sum(norm_one_grad * tok_float * inverse_one, axis=0)
    input_grad = (
        hidden_grad
        + inverse_one * gains[0] * norm_one_grad
        - tok_float
        * inverse_one**3
        * jnp.mean(tok_float * gains[0] * norm_one_grad, axis=-1, keepdims=True)
    )
    query_weight_grad = contract(query_share.reshape(-1, share_width), normed_plane)
    out_weight_grad = contract(branch_share.reshape(-1, share_width), context_plane)
    pair_weight_grad = contract(normed, pair_grad).astype(jnp.bfloat16)
    shares = jnp.concatenate([query_weight_grad, out_weight_grad], axis=0).astype(jnp.bfloat16)
    shares, down_grad, gate_weight_grad = lax.optimization_barrier(
        (shares, down_grad, gate_weight_grad)
    )
    feed_shape = (share_cols, rows_block)
    pair_task = Exchange(
        "grp",
        (grp_count, seq_count, sub_rows, 2 * HD),
        lambda ref, index: ref.at[:, index],
        block_of,
    )
    work = [
        split_columns("seq", shares),
        (pair_task, pair_weight_grad.reshape(seq_count, grp_count, sub_rows, 2 * HD)),
        gather_axis("seq", jnp.stack([gain_one_term, gain_two_term])),
        (gather_plane(feed_shape), down_grad),
        (gather_plane(feed_shape), gate_weight_grad),
    ]
    if grp_count == 8:
        feed_part = feed_part.reshape(grp_count, rows_here, MODEL_WIDTH)
        work.append((PlaneSum(rows_here, MODEL_WIDTH), feed_part))
    share_parts, pair_parts, gain_parts, down_plane, gate_plane, *feed_out = exchange(7, work)
    if grp_count == 8:
        feed_out = feed_out[0]
    else:
        feed_out = lax.psum_scatter(feed_part, "grp", scatter_dimension=0, tiled=True)
    block_out = (hidden + feed_out.astype(jnp.float32)).astype(jnp.bfloat16)
    gain_seq = jnp.sum(gain_parts, axis=0)
    shares = jnp.sum(share_parts.astype(jnp.float32), axis=0).astype(jnp.bfloat16)
    pair_parts = jnp.sum(pair_parts.astype(jnp.float32), axis=0).astype(jnp.bfloat16)
    pair_task = Exchange("seq", pair_parts.shape, block_of, block_of)
    shares, up_weight_grad = lax.optimization_barrier((shares, up_weight_grad))
    _, pair_plane, up_plane, share_plane, gain_parts = exchange(
        8,
        [
            (pair_task, pair_parts),
            (gather_plane(pair_parts.shape), 0),
            (gather_plane(feed_shape), up_weight_grad),
            (gather_plane(shares.shape), shares),
            gather_axis("grp", gain_seq),
        ],
    )
    pair_plane = jnp.sum(pair_plane.astype(jnp.float32), axis=1).astype(jnp.bfloat16)
    gain_grads = jnp.sum(gain_parts, axis=0)

    tile_of_slot = (
        jnp.full((grp_count * slots_here,), tile_count, jnp.int32)
        .at[tile_owner_slots]
        .set(jnp.arange(tile_count, dtype=jnp.int32))
    )
    tiles_here = lax.dynamic_slice_in_dim(tile_of_slot, grp_here * slots_here, slots_here)
    feed_at = jnp.clip(tiles_here - attn_tiles, 0, 3 * hidden_tiles - 1)
    which, column = feed_at // hidden_tiles, feed_at % hidden_tiles
    is_query = tiles_here < query_tiles
    is_pair = (tiles_here >= query_tiles) & (tiles_here < query_tiles + 2)
    is_feed = tiles_here >= attn_tiles
    kind = jnp.where(is_feed, jnp.minimum(which, 2), 3)
    kind = jnp.where(is_pair, 4, jnp.where(is_feed, kind, 3))
    kind = jnp.where(tiles_here == tile_count, 5, kind)
    out_at = jnp.clip(tiles_here - query_tiles - 2, 0, query_tiles - 1)
    per_share = share_width // tile_width
    share_at = jnp.where(is_query, jnp.minimum(tiles_here, query_tiles - 1), out_at)
    at = jnp.stack(
        [
            kind,
            column // share,
            column % share,
            share_at // per_share,
            share_at % per_share + jnp.where(is_query, 0, per_share),
            jnp.where(is_pair, tiles_here - query_tiles, 0),
        ]
    )
    new_master, new_one, new_two = adam(
        at,
        gate_plane,
        up_plane,
        down_plane,
        share_plane,
        pair_plane,
        left_basis_set,
        right_basis_set,
        master,
        moment_one,
        moment_two,
    )
    gain_one = BETA_ONE * gain_moment_one + (1.0 - BETA_ONE) * gain_grads
    gain_two = BETA_TWO * gain_moment_two + (1.0 - BETA_TWO) * gain_grads * gain_grads
    new_gains = gains - GAIN_RATE * gain_one / (jnp.sqrt(gain_two) + ADAM_EPS)
    return (
        block_out,
        input_grad,
        new_master,
        new_one,
        new_two,
        gain_grads,
        new_gains,
        gain_one,
        gain_two,
    )


def solution(mesh):
    return jax.shard_map(
        local,
        mesh=mesh,
        in_specs=(
            P(("grp", "seq"), None),
            P(("grp", "seq"), None),
            P(("grp", "seq")),
            P(),
            P("grp", "seq", None),
            P("grp", "seq", None),
            P("grp", "seq", None),
            P("grp", "seq", None),
            P("grp", "seq", None),
            P("grp", "seq", None),
            P(),
            P(),
            P(),
        ),
        out_specs=(
            P(("grp", "seq"), None),
            P(("grp", "seq"), None),
            P("grp", "seq", None),
            P("grp", "seq", None),
            P("grp", "seq", None),
            P(),
            P(),
            P(),
            P(),
        ),
        check_vma=False,
    )
```

```python
import functools

import jax
import jax.numpy as jnp
from jax import lax
from jax.experimental import pallas as pl
from jax.experimental.pallas import tpu as pltpu
from jax.sharding import PartitionSpec as P

MODEL_WIDTH = 2048
NH = 16
HD = 128
FF = 5632
SEQLEN = 1024


NORM_EPS = 1e-05
BETA_ONE = 0.95
BETA_TWO = 0.95
ADAM_EPS = 1e-08
WEIGHT_DECAY = 0.01
LEARN_RATE = 0.03
GAIN_RATE = 1.5
ROPE_BASE = 10000.0
MASKED = -1e30
PRECISE = lax.Precision.HIGHEST


def contract(left_side, right_side):
    return lax.dot_general(
        left_side, right_side, (((0,), (0,)), ((), ())), preferred_element_type=jnp.float32
    )


def times_transpose(left_side, right_side):
    return lax.dot_general(
        left_side, right_side, (((1,), (1,)), ((), ())), preferred_element_type=jnp.float32
    )


def turn_tables(places):
    half_width = HD // 2
    frequency = ROPE_BASE ** (-(jnp.arange(half_width, dtype=jnp.float32) * 2.0) / HD)
    angles = places.astype(jnp.float32)[:, None] * frequency[None, :]
    cosine, sine = jnp.cos(angles), jnp.sin(angles)
    return (
        jnp.concatenate([cosine, cosine], axis=1),
        jnp.concatenate([-sine, sine], axis=1),
    )


def turn(rows, cosine, sine):
    return rows * cosine + pltpu.roll(rows, HD // 2, 1) * sine


def turn_back(rows, cosine, sine):
    return rows * cosine - pltpu.roll(rows, HD // 2, 1) * sine


def dot_last(left_side, right_side):
    return lax.dot_general(
        left_side, right_side, (((1,), (1,)), ((), ())), preferred_element_type=jnp.float32
    )


def dot_first(left_side, right_side):
    return lax.dot_general(
        left_side, right_side, (((0,), (0,)), ((), ())), preferred_element_type=jnp.float32
    )


SMALL_COST = pl.CostEstimate(flops=1, bytes_accessed=1, transcendentals=0)


def project_kernel(x_ref, w_ref, cosine_ref, sine_ref, out_ref):
    made = jnp.dot(x_ref[...], w_ref[...], preferred_element_type=jnp.float32)
    cosine, sine = cosine_ref[...], sine_ref[...]
    first, second = made[:, :HD], made[:, HD:]
    last = pl.program_id(0) == pl.num_programs(0) - 1
    out_ref[:, :HD] = turn(first, cosine, sine).astype(out_ref.dtype)
    out_ref[:, HD:] = jnp.where(last, second, turn(second, cosine, sine)).astype(out_ref.dtype)


def project(normed, weights, tables):
    rows, width = normed.shape
    steps = NH // 2 + 1
    return pl.pallas_call(
        project_kernel,
        grid=(steps,),
        in_specs=[
            pl.BlockSpec((rows, width), lambda j: (0, 0)),
            pl.BlockSpec((width, 2 * HD), lambda j: (0, j)),
            pl.BlockSpec((rows, HD), lambda j: (0, 0)),
            pl.BlockSpec((rows, HD), lambda j: (0, 0)),
        ],
        out_specs=pl.BlockSpec((rows, 2 * HD), lambda j: (0, j)),
        out_shape=jax.ShapeDtypeStruct((rows, steps * 2 * HD), jnp.bfloat16),
        compiler_params=pltpu.CompilerParams(vmem_limit_bytes=56 * 2**20),
        cost_estimate=SMALL_COST,
        name="project",
    )(normed, weights, *tables)


def score_mask(key_seg_ref, query_seg_ref, block, rows):
    keys = (block + 1) * rows
    same = key_seg_ref[:keys, :] == query_seg_ref[...]
    key_at = lax.broadcasted_iota(jnp.int32, (keys, rows), 0)
    query_at = lax.broadcasted_iota(jnp.int32, (keys, rows), 1) + block * rows
    return same & (key_at <= query_at)


def attend_kernel(at_ref, q_ref, k_ref, v_ref, key_seg_ref, query_seg_ref, context_ref, total_ref):
    scale = HD ** (-0.5)
    rows = q_ref.shape[0]
    for block in range(SEQLEN // rows):

        @pl.when(at_ref[0] == block)
        def _():
            keys = (block + 1) * rows
            scores = dot_last(k_ref[:keys, :], q_ref[...]) * scale
            scores = jnp.where(
                score_mask(key_seg_ref, query_seg_ref, block, rows), scores, MASKED
            )
            highest = jnp.max(scores, axis=0, keepdims=True)
            exponent = jnp.exp(scores - highest)
            totals = jnp.sum(exponent, axis=0, keepdims=True)
            probs_low = (exponent * (1.0 / totals)).astype(jnp.bfloat16)
            context = dot_first(probs_low, v_ref[:keys, :])
            context_ref[...] = context.astype(jnp.bfloat16)
            total_ref[0] = highest + jnp.log(totals)


def attend_back_head(
    place, q_ref, k_ref, v_ref, grad_ref, total_ref, key_seg_ref, query_seg_ref, key_cosine_ref,
    key_sine_ref, cosine_ref, sine_ref, query_grad_ref, pair_grad_ref, key_sum, value_sum,
):
    scale = HD ** (-0.5)
    rows = q_ref.shape[0]
    head = pl.program_id(0)

    @pl.when(head == 0)
    def _():
        key_sum[...] = jnp.zeros_like(key_sum)
        value_sum[...] = jnp.zeros_like(value_sum)

    for block in range(SEQLEN // rows):

        @pl.when(place == block)
        def _():
            keys = (block + 1) * rows
            queries, grads = q_ref[...], grad_ref[...]
            shifted = dot_last(k_ref[:keys, :], queries) * scale - total_ref[0]
            allowed = score_mask(key_seg_ref, query_seg_ref, block, rows)
            probs = jnp.where(allowed, jnp.exp(shifted), 0.0)
            prob_grad = dot_last(v_ref[:keys, :], grads)
            centre = jnp.sum(probs * prob_grad, axis=0, keepdims=True)
            score_grad = (probs * (prob_grad - centre) * scale).astype(jnp.bfloat16)
            value_sum[:keys, :] += jnp.dot(
                probs.astype(jnp.bfloat16), grads, preferred_element_type=jnp.float32
            )
            key_sum[:keys, :] += jnp.dot(score_grad, queries, preferred_element_type=jnp.float32)
            query_grad = dot_first(score_grad, k_ref[:keys, :])
            query_grad_ref[...] = turn_back(query_grad, cosine_ref[...], sine_ref[...]).astype(
                jnp.bfloat16
            )

    @pl.when(head == pl.num_programs(0) - 1)
    def _():
        pair_grad_ref[:, :HD] = turn_back(
            key_sum[...], key_cosine_ref[...], key_sine_ref[...]
        ).astype(jnp.bfloat16)
        pair_grad_ref[:, HD:] = value_sum[...].astype(jnp.bfloat16)


def attend_back_kernel(at_ref, *refs):
    attend_back_head(at_ref[0], *refs)


def attention_specs(kinds, rows):
    specs = {
        "at": pl.BlockSpec(memory_space=pltpu.SMEM),
        "head": pl.BlockSpec((rows, HD), lambda h: (0, h)),
        "keys": pl.BlockSpec((SEQLEN, HD), lambda h: (0, 0)),
        "values": pl.BlockSpec((SEQLEN, HD), lambda h: (0, 1)),
        "pair": pl.BlockSpec((SEQLEN, 2 * HD), lambda h: (0, 0)),
        "total": pl.BlockSpec((1, 1, rows), lambda h: (h, 0, 0)),
        "key_seg": pl.BlockSpec((SEQLEN, 1), lambda h: (0, 0)),
        "query_seg": pl.BlockSpec((1, rows), lambda h: (0, 0)),
        "key_table": pl.BlockSpec((SEQLEN, HD), lambda h: (0, 0)),
        "table": pl.BlockSpec((rows, HD), lambda h: (0, 0)),
    }
    return [specs[kind] for kind in kinds]


def attend(at, projected, pairs, key_segs, query_segs):
    rows = projected.shape[0]
    columns = NH * HD
    return pl.pallas_call(
        attend_kernel,
        grid=(NH,),
        in_specs=attention_specs(["at", "head", "keys", "values", "key_seg", "query_seg"], rows),
        out_specs=attention_specs(["head", "total"], rows),
        out_shape=(
            jax.ShapeDtypeStruct((rows, columns), jnp.bfloat16),
            jax.ShapeDtypeStruct((NH, 1, rows), jnp.float32),
        ),
        compiler_params=pltpu.CompilerParams(vmem_limit_bytes=32 * 2**20),
        cost_estimate=SMALL_COST,
        name="attend",
    )(at, projected, pairs, pairs, key_segs[:, None], query_segs[None, :])


def attend_back(at, projected, pairs, grads, totals, key_segs, query_segs, key_tables, tables):
    rows = projected.shape[0]
    columns = NH * HD
    return pl.pallas_call(
        attend_back_kernel,
        grid=(NH,),
        in_specs=attention_specs(
            ["at", "head", "keys", "values", "head", "total", "key_seg", "query_seg"]
            + ["key_table", "key_table", "table", "table"],
            rows,
        ),
        out_specs=attention_specs(["head", "pair"], rows),
        out_shape=(
            jax.ShapeDtypeStruct((rows, columns), jnp.bfloat16),
            jax.ShapeDtypeStruct((SEQLEN, 2 * HD), jnp.bfloat16),
        ),
        scratch_shapes=[pltpu.VMEM((SEQLEN, HD), jnp.float32)] * 2,
        compiler_params=pltpu.CompilerParams(vmem_limit_bytes=32 * 2**20),
        cost_estimate=SMALL_COST,
        name="attend_back",
    )(
        at, projected, pairs, pairs, grads, totals, key_segs[:, None], query_segs[None, :],
        *key_tables, *tables,
    )


def load_weights(parts, weights, sems):
    count, rows, _ = parts[0].shape
    halves = len(parts)
    return [
        pltpu.make_async_copy(
            parts[half].at[block],
            weights.at[pl.ds((block * halves + half) * rows, rows)],
            sems.at[block * halves + half],
        )
        for half in range(halves)
        for block in range(count)
    ]


def feed_block(real, x, cot, weights, act_ref, gate_grad_ref, up_grad_ref, two_ref, out_ref):
    low = jnp.bfloat16
    wide = jnp.float32
    cols = act_ref.shape[0]
    gate = jnp.dot(x, weights[:, :cols], preferred_element_type=wide)
    upper = jnp.dot(x, weights[:, cols : 2 * cols], preferred_element_type=wide)
    act_grad = jnp.dot(cot, weights[:, 2 * cols :], preferred_element_type=wide)
    real = lax.broadcasted_iota(jnp.int32, gate.shape, 1) < real
    sigmoid = 1.0 / (1.0 + jnp.exp(-gate))
    silu = gate * sigmoid
    activated = jnp.where(real, silu * upper, 0.0).astype(low)
    act_grad = jnp.where(real, act_grad, 0.0)
    gate_grad = (act_grad * upper * sigmoid * (1.0 + gate * (1.0 - sigmoid))).astype(low)
    up_grad = (act_grad * silu).astype(low)
    act_ref[...] = jnp.transpose(activated)
    gate_grad_ref[...] = jnp.transpose(gate_grad)
    up_grad_ref[...] = jnp.transpose(up_grad)
    two = dot_last(gate_grad, weights[:, :cols]) + dot_last(up_grad, weights[:, cols : 2 * cols])
    two_ref[...] = two.astype(low)
    out_ref[...] = dot_last(activated, weights[:, 2 * cols :]).astype(low)


def feed_kernel(real_ref, x_ref, cot_ref, *refs):
    parts, refs = refs[:-7], refs[-7:]
    weights, sems = refs[5:]

    @pl.when(pl.program_id(0) == 0)
    def _():
        copies = load_weights(parts, weights, sems)
        for copy in copies:
            copy.start()
        for copy in copies:
            copy.wait()

    feed_block(real_ref[0], x_ref[...], cot_ref[...], weights, *refs[:5])


def feed_forward(real_cols, x, cot, parts, seq_count):
    tokens_all, width = x.shape
    _, rows, cols = parts[0].shape
    cols = cols // 3
    step = 256
    low = jnp.bfloat16
    block = pl.BlockSpec((step, width), lambda i: (i, 0))
    narrow = pl.BlockSpec((cols, step), lambda i: (0, i))
    return pl.pallas_call(
        feed_kernel,
        grid=(tokens_all // step,),
        in_specs=[pl.BlockSpec(memory_space=pltpu.SMEM), block, block]
        + [pl.BlockSpec(memory_space=pl.ANY)] * len(parts),
        out_specs=[narrow, narrow, narrow, block, block],
        out_shape=[jax.ShapeDtypeStruct((cols, tokens_all), low)] * 3
        + [jax.ShapeDtypeStruct((tokens_all, width), low)] * 2,
        scratch_shapes=[
            pltpu.VMEM((width, 3 * cols), low),
            pltpu.SemaphoreType.DMA((len(parts) * seq_count,)),
        ],
        compiler_params=pltpu.CompilerParams(vmem_limit_bytes=52 * 2**20),
        cost_estimate=SMALL_COST,
        name="feed_forward",
    )(real_cols, x, cot, *parts)


def feed_gather_kernel(
    first, second, real_ref, own_ref, context_ref, cot_ref, cot_all_ref, part_ref, gate_grad_ref,
    up_grad_ref, two_ref, out_ref, second_ref, context_plane_ref, down_out, blocks, weights,
    act_block, act, x_block, stage, load_sems, keep_sems, x_sems, out_sems, first_send,
    first_recv, second_send, second_recv,
):
    step = pl.program_id(0)
    grp, seq = lax.axis_index("grp"), lax.axis_index("seq")
    first.start(own_ref, blocks, (first_send, first_recv), grp, seq, begin=False)
    second.start(context_ref, context_plane_ref, (second_send, second_recv), grp, seq, begin=False)
    loads = load_weights([part_ref], weights, load_sems)
    cols = act.shape[0]
    step_rows = act_block.shape[1]
    rows = x_block.shape[2]
    count = cot_all_ref.shape[1] // rows

    @pl.when(step == 0)
    def _():
        for copy in loads:
            copy.start()
        barrier = pltpu.get_barrier_semaphore()
        for device in first.peers(grp, seq):
            pl.semaphore_signal(barrier, inc=1, device_id=device, device_id_type=MESH)
        pl.semaphore_wait(barrier, 3)
        first.begin()
        first.kept.wait()
        for copy in loads:
            copy.wait()

    @pl.when(step == 1)
    def _():
        first.due[7].wait_recv()

    @pl.when(step == 2)
    def _():
        for came in (1, 4, 2):
            first.pass_on(came)

    @pl.when(step == 3)
    def _():
        first.pass_on(5)

    @pl.when(step == 4)
    def _():
        first.due[8].wait_recv()
        first.due[9].wait_recv()
        first.pass_on(6)
        first.pass_on(3)
        second.begin()

    @pl.when(step == 5)
    def _():
        first.due[10].wait_recv()
        first.due[11].wait_recv()

    @pl.when(step == 7)
    def _():
        first.due[12].wait_recv()
        first.due[13].wait_recv()
        second.pass_on(1)
        second.pass_on(4)

    keep = pltpu.make_async_copy(blocks.at[step], second_ref.at[step], keep_sems.at[step])
    keep.start()
    feed_block(
        real_ref[0], blocks[step], cot_ref[...], weights, act_block, gate_grad_ref, up_grad_ref,
        two_ref, out_ref,
    )
    act[:, pl.ds(pl.multiple_of(step * step_rows, step_rows), step_rows)] = act_block[...]

    def x_copy(at):
        view = cot_all_ref.at[:, pl.ds(pl.multiple_of(at * rows, rows), rows)]
        return pltpu.make_async_copy(view, x_block.at[at % 2], x_sems.at[at % 2])

    def out_copy(at):
        place = pl.ds(pl.multiple_of(at * cols, cols), cols)
        return pltpu.make_async_copy(stage.at[at % 2], down_out.at[place], out_sems.at[at % 2])

    @pl.when(step == 7)
    def _():
        x_copy(0).start()
        second.pass_on(2)
        second.pass_on(5)

        def one(at, _):
            @pl.when(at == 2)
            def _():
                second.pass_on(6)
                second.pass_on(3)

            x_copy(at).wait()

            @pl.when(at + 1 < count)
            def _():
                x_copy(at + 1).start()

            @pl.when(at >= 2)
            def _():
                out_copy(at - 2).wait()

            stage[at % 2] = jnp.dot(
                act[...], x_block[at % 2], preferred_element_type=jnp.float32
            ).astype(stage.dtype)
            out_copy(at).start()
            return 0

        lax.fori_loop(0, count, one, 0)
        out_copy(count - 2).wait()
        out_copy(count - 1).wait()
        second.finish()
        for copy in first.out[1:]:
            copy.wait_send()
        for at in range(8):
            pltpu.make_async_copy(blocks.at[at], second_ref.at[at], keep_sems.at[at]).wait()


def feed_gather(number, real_cols, normed, context, cot, part, seq_count):
    rows, width = normed.shape
    cols = part.shape[2] // 3
    low = jnp.bfloat16
    block = pl.BlockSpec((rows, width), lambda i: (i, 0))
    narrow = pl.BlockSpec((cols, rows), lambda i: (0, i))
    first = gather_plane(normed.shape, placed=True)
    second = gather_plane(context.shape, placed=True)
    hbm = pl.BlockSpec(memory_space=pl.ANY)
    plane = jax.ShapeDtypeStruct((8, rows, width), low)
    model_rows = width // seq_count
    return pl.pallas_call(
        functools.partial(feed_gather_kernel, first, second),
        grid=(8,),
        in_specs=[pl.BlockSpec(memory_space=pltpu.SMEM), hbm, hbm, block, hbm, hbm],
        out_specs=[narrow, narrow, block, block, hbm, hbm, hbm],
        out_shape=[jax.ShapeDtypeStruct((cols, 8 * rows), low)] * 2
        + [jax.ShapeDtypeStruct((8 * rows, width), low)] * 2
        + [plane, plane, jax.ShapeDtypeStruct((seq_count * cols, model_rows), low)],
        scratch_shapes=[
            pltpu.VMEM((8, rows, width), low),
            pltpu.VMEM((width, 3 * cols), low),
            pltpu.VMEM((cols, rows), low),
            pltpu.VMEM((cols, 8 * rows), low),
            pltpu.VMEM((2, 8 * rows, model_rows), low),
            pltpu.VMEM((2, cols, model_rows), low),
            pltpu.SemaphoreType.DMA((seq_count,)),
            pltpu.SemaphoreType.DMA((8,)),
            pltpu.SemaphoreType.DMA((2,)),
            pltpu.SemaphoreType.DMA((2,)),
        ]
        + [pltpu.SemaphoreType.DMA((14,))] * 4,
        compiler_params=pltpu.CompilerParams(
            collective_id=number, has_side_effects=True, vmem_limit_bytes=60 * 2**20
        ),
        cost_estimate=SMALL_COST,
        name="feed_gather",
    )(real_cols, normed, context, cot, cot, part)


def weight_grad_kernel(left_ref, x_ref, out_ref):
    out_ref[...] = jnp.dot(
        left_ref[...], x_ref[...], preferred_element_type=jnp.float32
    ).astype(out_ref.dtype)


def weight_grad(left, x, seq_count):
    cols, tokens_all = left.shape
    rows = x.shape[1] // seq_count
    return pl.pallas_call(
        weight_grad_kernel,
        grid=(seq_count,),
        in_specs=[
            pl.BlockSpec((cols, tokens_all), lambda i: (0, 0)),
            pl.BlockSpec((tokens_all, rows), lambda i: (0, i)),
        ],
        out_specs=pl.BlockSpec((cols, rows), lambda i: (i, 0)),
        out_shape=jax.ShapeDtypeStruct((seq_count * cols, rows), jnp.bfloat16),
        compiler_params=pltpu.CompilerParams(vmem_limit_bytes=40 * 2**20),
        cost_estimate=SMALL_COST,
        name="weight_grad",
    )(left, x)


def pick_kernel(share, slots_ref, *refs):
    count = len(refs) - 2
    sources, out_ref, sems = refs[:count], refs[count], refs[count + 1]
    width = sources[0].shape[2]
    start = 0
    copies = []
    for at, source in enumerate(sources):
        rows = source.shape[1]
        if at == 0 and share is not None:
            rows = share
            part = pl.ds(pl.multiple_of(lax.axis_index("grp") * rows, rows), rows)
        else:
            part = pl.ds(0, rows)
        for tile in range(slots_ref.shape[0]):
            copies.append(
                pltpu.make_async_copy(
                    source.at[slots_ref[tile], part],
                    out_ref.at[pl.ds(start, rows), tile * width : (tile + 1) * width],
                    sems.at[len(copies)],
                )
            )
        start += rows
    for copy in copies:
        copy.start()
    for copy in copies:
        copy.wait()


def pick(slots, sources, share=None):
    count, width = slots.shape[0], sources[0].shape[2]
    rows = sum(source.shape[1] for source in sources)
    if share is not None:
        rows += share - sources[0].shape[1]
    return pl.pallas_call(
        functools.partial(pick_kernel, share),
        in_specs=[pl.BlockSpec(memory_space=pltpu.SMEM)]
        + [pl.BlockSpec(memory_space=pl.ANY)] * len(sources),
        out_specs=pl.BlockSpec(memory_space=pltpu.VMEM),
        out_shape=jax.ShapeDtypeStruct((rows, count * width), sources[0].dtype),
        scratch_shapes=[pltpu.SemaphoreType.DMA((count * len(sources),))],
        cost_estimate=SMALL_COST,
        name="pick",
    )(slots, *sources)


def adam_kernel(group, at_ref, *refs):
    feeds = [refs[at * group : (at + 1) * group] for at in range(5)]
    left_ref, right_ref, master_ref, one_ref, two_ref = refs[5 * group : 5 * group + 5]
    new_master_ref, new_one_ref, new_two_ref, grad = refs[5 * group + 5 :]
    low = jnp.bfloat16
    for slot in range(group):
        kind = at_ref[0, pl.program_id(0) * group + slot]
        for number in range(4):

            @pl.when(kind == number)
            def _():
                grad[slot] = feeds[number][slot][0]

        @pl.when(kind == 4)
        def _():
            pair = feeds[4][slot][...].reshape(grad.shape[2], grad.shape[1])
            grad[slot] = jnp.transpose(pair.astype(jnp.float32)).astype(grad.dtype)

        @pl.when(kind == 5)
        def _():
            grad[slot] = jnp.zeros(grad.shape[1:], grad.dtype)

    slots = range(group)
    left = [left_ref[slot].astype(low) for slot in slots]
    right = [right_ref[slot].astype(low) for slot in slots]
    turned = [
        jnp.dot(grad[slot], left[slot], preferred_element_type=jnp.float32) for slot in slots
    ]
    turned = [dot_first(turned[slot].astype(low), right[slot]) for slot in slots]
    scaled = []
    for slot in slots:
        new_one = BETA_ONE * one_ref[slot] + (1.0 - BETA_ONE) * turned[slot]
        new_two = BETA_TWO * two_ref[slot] + (1.0 - BETA_TWO) * turned[slot] * turned[slot]
        new_one_ref[slot], new_two_ref[slot] = new_one, new_two
        scaled.append((new_one / (jnp.sqrt(new_two) + ADAM_EPS)).astype(low))
    restored = [dot_last(scaled[slot], right[slot]).astype(low) for slot in slots]
    restored = [
        jnp.dot(left[slot], restored[slot], preferred_element_type=jnp.float32) for slot in slots
    ]
    for slot in slots:
        new_master_ref[slot] = (
            master_ref[slot] * (1.0 - LEARN_RATE * WEIGHT_DECAY) - LEARN_RATE * restored[slot]
        )


def adam(at, gate, up, down, shares, pairs, left, right, master, one, two):
    slots, rows, width = master.shape
    group = 3 if slots % 3 == 0 else 1
    tile = pl.BlockSpec((group, rows, width), lambda i, at: (i, 0, 0))
    shape = jax.ShapeDtypeStruct(master.shape, jnp.float32)

    def feed(block, column):
        return [
            pl.BlockSpec(
                (1, width, rows),
                lambda i, at, slot=slot: (at[block, i * group + slot], at[column, i * group + slot], 0),
            )
            for slot in range(group)
        ]

    pair = [
        pl.BlockSpec(
            (*pairs.shape[:2], width), lambda i, at, slot=slot: (0, 0, at[5, i * group + slot])
        )
        for slot in range(group)
    ]
    return pl.pallas_call(
        functools.partial(adam_kernel, group),
        grid_spec=pltpu.PrefetchScalarGridSpec(
            num_scalar_prefetch=1,
            grid=(slots // group,),
            in_specs=feed(1, 2) * 3
            + feed(3, 4)
            + pair
            + [
                pl.BlockSpec((group, rows, rows), lambda i, at: (i, 0, 0)),
                pl.BlockSpec((group, width, width), lambda i, at: (i, 0, 0)),
                tile,
                tile,
                tile,
            ],
            out_specs=[tile] * 3,
            scratch_shapes=[pltpu.VMEM((group, width, rows), jnp.bfloat16)],
        ),
        out_shape=[shape] * 3,
        compiler_params=pltpu.CompilerParams(vmem_limit_bytes=60 * 2**20),
        cost_estimate=SMALL_COST,
        name="adam",
    )(
        at, *[gate] * group, *[up] * group, *[down] * group, *[shares] * group, *[pairs] * group,
        left, right, master, one, two,
    )


MESH = pl.DeviceIdType.MESH


def remote(source, target, sems, at, device):
    return pltpu.make_async_remote_copy(
        src_ref=source,
        dst_ref=target,
        send_sem=sems[0].at[at],
        recv_sem=sems[1].at[at],
        device_id=device,
        device_id_type=MESH,
    )


def columns_of(ref, index, width):
    return ref.at[:, pl.ds(pl.multiple_of(index * width, width), width)]


def rows_of(ref, index, height):
    return ref.at[pl.ds(pl.multiple_of(index * height, height), height), :]


PLACES = {0: 0, 1: 1, 2: 2, 4: 3, 3: 4, 5: 5, 6: 6, 7: 7}


def flip(device, bits):
    core, side_x, side_y = device % 2, (device // 2) % 2, device // 4
    for bit, there in ((1, 1 - 2 * core), (2, 2 - 4 * side_x), (4, 4 - 8 * side_y)):
        if bits & bit:
            device = device + there
    return device


class PlacedExchange:
    axis = "grp"
    sem_count = 8

    def __init__(self, out_shape, source_view):
        self.out_shape, self.source_view = out_shape, source_view

    def peers(self, grp, seq):
        for bits in range(1, 8):
            yield flip(grp, bits), seq

    def start(self, source, target, sems, grp, seq):
        self.own = pltpu.make_async_copy(
            self.source_view(source, grp), target.at[0], sems[0].at[0]
        )
        self.own.start()
        self.copies = []
        for bits in range(1, 8):
            there = flip(grp, bits)
            copy = remote(
                self.source_view(source, there), target.at[PLACES[bits]], sems, bits, (there, seq)
            )
            copy.start()
            self.copies.append(copy)

    def forward(self):
        return iter(())

    def finish(self):
        for copy in self.copies:
            copy.wait()
        self.own.wait()


class Exchange:
    def __init__(self, axis, out_shape, source_view, target_view):
        self.axis, self.out_shape = axis, out_shape
        self.source_view, self.target_view = source_view, target_view
        self.count = lax.axis_size(axis)
        self.sem_count = self.count

    def peers(self, grp, seq):
        me = grp if self.axis == "grp" else seq
        for step in range(1, self.count):
            there = (me + step) % self.count
            yield (there, seq) if self.axis == "grp" else (grp, there)

    def start(self, source, target, sems, grp, seq, begin=True):
        me = grp if self.axis == "grp" else seq
        self.own = pltpu.make_async_copy(
            self.source_view(source, me), self.target_view(target, me), sems[0].at[0]
        )
        self.sent, self.due = [], []
        for step, device in enumerate(self.peers(grp, seq), 1):
            there = (me + step) % self.count
            back = (me + self.count - step) % self.count
            self.sent.append(
                remote(
                    self.source_view(source, there), self.target_view(target, me), sems, step, device
                )
            )
            self.due.append(
                remote(
                    self.source_view(source, back), self.target_view(target, back), sems, step, device
                )
            )
        if begin:
            self.begin()

    def begin(self):
        for copy in [self.own] + self.sent:
            copy.start()

    def forward(self):
        return iter(())

    def finish(self):
        for copy in self.due:
            copy.wait_recv()
        for copy in self.sent:
            copy.wait_send()
        self.own.wait()


class PlaneGather:
    axis = "grp"
    sem_count = 14

    def __init__(self, out_shape, source_view, target_view, half_of, placed):
        self.out_shape, self.placed = out_shape, placed
        self.source_view, self.target_view, self.half_of = source_view, target_view, half_of

    def peers(self, grp, seq):
        for bits in (1, 2, 4):
            yield flip(grp, bits), seq

    def start(self, source, target, sems, grp, seq, begin=True):
        def part(device, bits, piece):
            view = self.target_view(target, PLACES[bits] if self.placed else flip(device, bits))
            return view if piece == "all" else self.half_of(view, piece == "b")

        def own(piece):
            view = self.source_view(source, grp)
            return view if piece == "all" else self.half_of(view, piece == "b")

        self.out, self.due = [None], [None]
        for via, here, there, piece in (
            (2, 0, 2, "a"),
            (2, 0, 2, "b"),
            (2, 4, 6, "b"),
            (4, 0, 4, "b"),
            (4, 0, 4, "a"),
            (4, 2, 6, "a"),
            (1, 0, 1, "all"),
            (1, 2, 3, "a"),
            (1, 2, 3, "b"),
            (1, 4, 5, "b"),
            (1, 4, 5, "a"),
            (1, 6, 7, "a"),
            (1, 6, 7, "b"),
        ):
            device = flip(grp, via)
            view = own(piece) if here == 0 else part(grp, here, piece)
            at = len(self.out)
            self.out.append(remote(view, part(device, there, piece), sems, at, (device, seq)))
            self.due.append(remote(view, part(grp, there, piece), sems, at, (device, seq)))
        self.kept = pltpu.make_async_copy(own("all"), part(grp, 0, "all"), sems[0].at[0])
        if begin:
            self.begin()

    def begin(self):
        self.kept.start()
        for at in (1, 4, 2, 5, 7):
            self.out[at].start()

    def pass_on(self, came):
        self.due[came].wait_recv()
        for at in {1: (6, 8), 4: (3, 10), 2: (9,), 5: (11,), 6: (12,), 3: (13,)}[came]:
            self.out[at].start()

    def forward(self):
        for pair in ((1, 4), (2, 5), (6, 3)):
            for came in pair:
                self.pass_on(came)
            yield

    def finish(self):
        for copy in self.due[7:]:
            copy.wait_recv()
        for copy in self.out[1:]:
            copy.wait_send()
        self.kept.wait()


def add_rows(total, first, second):
    step = 32

    def some(at, _):
        rows = pl.ds(pl.multiple_of(at * step, step), step)
        total[rows, :] = (
            first[rows, :].astype(jnp.float32) + second[rows, :].astype(jnp.float32)
        ).astype(total.dtype)
        return 0

    lax.fori_loop(0, total.shape[0] // step, some, 0)


class PlaneSum:
    axis = "grp"
    sem_count = 15

    def __init__(self, rows, columns):
        self.rows, self.columns = rows, columns
        self.out_shape = (rows, columns)

    def scratch(self):
        low = jnp.bfloat16
        shape = (self.rows, self.columns)
        half = (self.rows // 2, self.columns)
        return [
            pltpu.VMEM((4, *shape), low),
            pltpu.VMEM((4, *shape), low),
            pltpu.VMEM((2, *half), low),
            pltpu.VMEM((2, *shape), low),
        ]

    def peers(self, grp, seq):
        for bits in (1, 2, 4):
            yield flip(grp, bits), seq

    def start(self, source, target, sems, grp, seq, scratch, begin=True):
        self.mine, self.core_in, self.halves, self.wholes = scratch
        core, side_x, side_y = [(flip(grp, bits), seq) for bits in (1, 2, 4)]
        half = self.rows // 2
        self.low, self.high = low, high = pl.ds(0, half), pl.ds(half, half)
        mine, halves, wholes = self.mine, self.halves, self.wholes
        self.copies = [
            remote(source.at[PLACES[bits]], self.core_in.at[at], sems, at, core)
            for at, bits in enumerate((7, 3, 5, 1))
        ] + [
            remote(mine.at[0, low], halves.at[0], sems, 4, side_x),
            remote(mine.at[0, high], halves.at[1], sems, 5, side_y),
            remote(mine.at[1, low], wholes.at[0, low], sems, 6, side_x),
            remote(mine.at[2, high], wholes.at[1, high], sems, 7, side_y),
            remote(mine.at[1, high], wholes.at[0, high], sems, 8, side_x),
            remote(mine.at[2, low], wholes.at[1, low], sems, 9, side_y),
        ]
        self.loads = [
            pltpu.make_async_copy(source.at[PLACES[bits]], mine.at[at], sems[0].at[10 + at])
            for at, bits in enumerate((6, 2, 4, 0))
        ]
        self.store = pltpu.make_async_copy(mine.at[3], target, sems[0].at[14])
        if begin:
            self.begin()

    def begin(self):
        for copy in self.copies[:4] + self.loads:
            copy.start()

    def first_sums(self):
        for came, then in ((0, (4, 5)), (1, (6,)), (2, (7,)), (3, ())):
            self.copies[came].wait_recv()
            self.loads[came].wait()
            add_rows(self.mine.at[came], self.mine.at[came], self.core_in.at[came])
            for at in then:
                self.copies[at].start()

    def forward(self):
        mine, low, high = self.mine, self.low, self.high
        yield
        self.copies[5].wait_recv()
        add_rows(mine.at[1, high], mine.at[1, high], self.halves.at[1])
        self.copies[8].start()
        self.copies[4].wait_recv()
        add_rows(mine.at[2, low], mine.at[2, low], self.halves.at[0])
        self.copies[9].start()

    def finish(self):
        mine = self.mine
        for at, side, rows in ((6, 0, self.low), (7, 1, self.high), (8, 0, self.high), (9, 1, self.low)):
            self.copies[at].wait_recv()
            add_rows(mine.at[3, rows], mine.at[3, rows], self.wholes.at[side, rows])
        self.store.start()
        for copy in self.copies:
            copy.wait_send()
        self.store.wait()


class LineGather:
    axis = "seq"

    def __init__(self, shape):
        self.count = lax.axis_size("seq")
        self.out_shape = (self.count, *shape)
        self.sem_count = 2 * self.count

    def peers(self, grp, seq):
        for step in range(1, self.count):
            yield grp, (seq + step) % self.count

    def start(self, source, target, sems, grp, seq):
        self.seq, self.sems = seq, sems
        self.own = pltpu.make_async_copy(source, target.at[seq], sems[0].at[0])
        self.own.start()

        def make(away, up):
            there = (seq + (1 if up else self.count - 1)) % self.count
            block = (seq + (self.count - away if up else away)) % self.count
            view = source if away == 0 else target.at[block]
            at = 1 + away if up else self.count + away
            return remote(view, target.at[block], sems, at, (grp, there))

        def came(away, up):
            block = (seq + (self.count - away if up else away)) % self.count
            at = away if up else self.count + away - 1
            side = (seq + (self.count - 1 if up else 1)) % self.count
            return remote(target.at[block], target.at[block], sems, at, (grp, side))

        self.make, self.came = make, came
        self.has = lambda away, up: (seq - away >= 0) if up else (seq + away < self.count)
        self.last = lambda up: (seq + 1 < self.count) if up else (seq >= 1)
        for up in (True, False):

            @pl.when(self.last(up))
            def _():
                make(0, up).start()

    def forward(self):
        for away in range(1, self.count):
            for up in (True, False):

                @pl.when(self.has(away, up))
                def _():
                    self.came(away, up).wait_recv()
                    if away < self.count - 1:

                        @pl.when(self.last(up))
                        def _():
                            self.make(away, up).start()

            yield

    def finish(self):
        for away in range(self.count - 1):
            for up in (True, False):

                @pl.when(self.has(away, up) & self.last(up))
                def _():
                    self.make(away, up).wait_send()
        self.own.wait()


def attend_back_sum_kernel(
    sum_task, gather_task, q_ref, k_ref, v_ref, grad_ref, total_ref, key_seg_ref, query_seg_ref,
    key_cosine_ref, key_sine_ref, cosine_ref, sine_ref, part_hbm, down_hbm, query_grad_ref,
    pair_grad_ref, sum_hbm, down_plane, key_sum, value_sum, mine, core_in, halves, wholes,
    sum_send, sum_recv, gather_send, gather_recv,
):
    step = pl.program_id(0)
    grp, seq = lax.axis_index("grp"), lax.axis_index("seq")
    scratch = (mine, core_in, halves, wholes)
    sum_task.start(part_hbm, sum_hbm, (sum_send, sum_recv), grp, seq, scratch, begin=False)
    gather_task.start(down_hbm, down_plane, (gather_send, gather_recv), grp, seq, begin=False)

    @pl.when(step == 0)
    def _():
        barrier = pltpu.get_barrier_semaphore()
        for device in sum_task.peers(grp, seq):
            pl.semaphore_signal(barrier, inc=1, device_id=device, device_id_type=MESH)
        pl.semaphore_wait(barrier, 3)
        sum_task.begin()
        gather_task.begin()

    @pl.when(step == 6)
    def _():
        sum_task.first_sums()

    attend_back_head(
        seq, q_ref, k_ref, v_ref, grad_ref, total_ref, key_seg_ref, query_seg_ref, key_cosine_ref,
        key_sine_ref, cosine_ref, sine_ref, query_grad_ref, pair_grad_ref, key_sum, value_sum,
    )

    @pl.when(step == pl.num_programs(0) - 1)
    def _():
        hand_on([gather_task, sum_task])
        gather_task.finish()
        sum_task.finish()


def attend_back_sum(
    number, projected, pairs, grads, totals, key_segs, query_segs, key_tables, tables, part, down
):
    rows = projected.shape[0]
    columns = NH * HD
    low = jnp.bfloat16
    sum_task = PlaneSum(*part.shape[1:])
    gather_task = gather_plane(down.shape)
    hbm = pl.BlockSpec(memory_space=pl.ANY)
    return pl.pallas_call(
        functools.partial(attend_back_sum_kernel, sum_task, gather_task),
        grid=(NH,),
        in_specs=attention_specs(
            ["head", "keys", "values", "head", "total", "key_seg", "query_seg"]
            + ["key_table", "key_table", "table", "table"],
            rows,
        )
        + [hbm, hbm],
        out_specs=attention_specs(["head", "pair"], rows) + [hbm, hbm],
        out_shape=[
            jax.ShapeDtypeStruct((rows, columns), low),
            jax.ShapeDtypeStruct((SEQLEN, 2 * HD), low),
            jax.ShapeDtypeStruct(sum_task.out_shape, low),
            jax.ShapeDtypeStruct(gather_task.out_shape, low),
        ],
        scratch_shapes=[pltpu.VMEM((SEQLEN, HD), jnp.float32)] * 2
        + sum_task.scratch()
        + [pltpu.SemaphoreType.DMA((sum_task.sem_count,))] * 2
        + [pltpu.SemaphoreType.DMA((gather_task.sem_count,))] * 2,
        compiler_params=pltpu.CompilerParams(
            collective_id=number, has_side_effects=True, vmem_limit_bytes=48 * 2**20
        ),
        cost_estimate=SMALL_COST,
        name="attend_back_sum",
    )(
        projected, pairs, pairs, grads, totals, key_segs[:, None], query_segs[None, :],
        *key_tables, *tables, part, down,
    )


def block_kernel(
    first, second, pair_task, key_seg_ref, query_seg_ref, normed_ref, tokens_ref, gain_ref,
    cosine_ref, sine_ref, cot_hbm, normed_hbm, w_ref, projected_ref, pairs_ref, context_ref,
    total_ref, hidden_ref, second_ref, inverse_ref, cot_plane, normed_plane, own_pair, pairs,
    first_send, first_recv, second_send, second_recv, pair_send, pair_recv,
):
    step = pl.program_id(0)
    grp, seq = lax.axis_index("grp"), lax.axis_index("seq")
    first.start(cot_hbm, cot_plane, (first_send, first_recv), grp, seq, begin=False)
    second.start(normed_hbm, normed_plane, (second_send, second_recv), grp, seq, begin=False)
    pair_task.start(own_pair, pairs, (pair_send, pair_recv), grp, seq, begin=False)
    low = jnp.bfloat16
    rows = normed_ref.shape[0]
    wide = 2 * HD
    couples = NH // 2
    attend_at = 1 + couples
    out_at = attend_at + NH
    end = out_at + MODEL_WIDTH // wide

    @pl.when(step == 0)
    def _():
        barrier = pltpu.get_barrier_semaphore()
        devices = list(first.peers(grp, seq)) + list(pair_task.peers(grp, seq))
        for device in devices:
            pl.semaphore_signal(barrier, inc=1, device_id=device, device_id_type=MESH)
        pl.semaphore_wait(barrier, len(devices))
        first.begin()
        second.begin()

    @pl.when(step < attend_at)
    def _():
        made = jnp.dot(normed_ref[...], w_ref[...], preferred_element_type=jnp.float32)
        cosine, sine = cosine_ref[...], sine_ref[...]
        left = turn(made[:, :HD], cosine, sine).astype(low)
        right = made[:, HD:]

        @pl.when(step == 0)
        def _():
            own_pair[:, :HD] = left
            own_pair[:, HD:] = right.astype(low)
            pair_task.begin()
            projected_ref[:, NH * HD :] = own_pair[...]

        @pl.when(step > 0)
        def _():
            place = pl.multiple_of((step - 1) * wide, wide)
            projected_ref[:, pl.ds(place, HD)] = left
            projected_ref[:, pl.ds(pl.multiple_of(place + HD, HD), HD)] = turn(
                right, cosine, sine
            ).astype(low)

    @pl.when(step == attend_at)
    def _():
        pair_task.finish()
        for at in range(pairs.shape[0]):
            pairs_ref[at * rows : (at + 1) * rows, :] = pairs[at]

    @pl.when(step == attend_at + 2)
    def _():
        first.pass_on(1)
        first.pass_on(4)

    @pl.when(step == out_at)
    def _():
        first.pass_on(2)
        first.pass_on(5)

    @pl.when((step >= attend_at) & (step < out_at))
    def _():
        head = step - attend_at
        place = pl.ds(pl.multiple_of(head * HD, HD), HD)
        scale = HD ** (-0.5)
        for block in range(SEQLEN // rows):

            @pl.when(seq == block)
            def _():
                keys = (block + 1) * rows
                scores = dot_last(pairs_ref[:keys, :HD], projected_ref[:, place]) * scale
                scores = jnp.where(
                    score_mask(key_seg_ref, query_seg_ref, block, rows), scores, MASKED
                )
                highest = jnp.max(scores, axis=0, keepdims=True)
                exponent = jnp.exp(scores - highest)
                totals = jnp.sum(exponent, axis=0, keepdims=True)
                probs_low = (exponent * (1.0 / totals)).astype(low)
                context = dot_first(probs_low, pairs_ref[:keys, HD:])
                context_ref[:, place] = context.astype(low)
                total_ref[head] = highest + jnp.log(totals)

    @pl.when(step >= out_at)
    def _():
        place = pl.ds(pl.multiple_of((step - out_at) * wide, wide), wide)
        branch = jnp.dot(context_ref[...], w_ref[...], preferred_element_type=jnp.float32)
        hidden_ref[:, place] = tokens_ref[:, place].astype(jnp.float32) + branch

    @pl.when(step == end - 1)
    def _():
        chunk = 32
        gain = gain_ref[1:2, :]

        def some(at, _):
            part = pl.ds(pl.multiple_of(at * chunk, chunk), chunk)
            hidden = hidden_ref[part, :]
            inverse = lax.rsqrt(jnp.mean(hidden * hidden, axis=-1, keepdims=True) + NORM_EPS)
            inverse_ref[part, :] = inverse
            second_ref[part, :] = (hidden * inverse * gain).astype(low)
            return 0

        lax.fori_loop(0, rows // chunk, some, 0)
        first.pass_on(6)
        first.pass_on(3)
        for came in (1, 4, 2, 5, 6, 3):
            second.pass_on(came)
        first.finish()
        second.finish()


def attention_block(number, normed, tokens, gains, tables, key_segs, query_segs, cotangent, weights):
    rows, width = normed.shape
    low, wide = jnp.bfloat16, 2 * HD
    couples = NH // 2
    count = SEQLEN // rows
    first = gather_plane(cotangent.shape, placed=True)
    second = gather_plane(normed.shape, placed=True)
    pair_task = Exchange("seq", (count, rows, wide), whole, block_of)

    def weight_block(step):
        turned = step - NH
        return (0, jnp.where(step == 0, couples, jnp.where(step <= couples, step - 1, jnp.maximum(turned, couples + 1))))

    def full(shape):
        return pl.BlockSpec(shape, lambda step: (0,) * len(shape))

    hbm = pl.BlockSpec(memory_space=pl.ANY)
    steps = 1 + couples + NH + width // wide
    plane = jax.ShapeDtypeStruct((8, rows, width), low)
    shapes = [
        jax.ShapeDtypeStruct((rows, NH * HD + wide), low),
        jax.ShapeDtypeStruct((SEQLEN, wide), low),
        jax.ShapeDtypeStruct((rows, NH * HD), low),
        jax.ShapeDtypeStruct((NH, 1, rows), jnp.float32),
        jax.ShapeDtypeStruct((rows, width), jnp.float32),
        jax.ShapeDtypeStruct((rows, width), low),
        jax.ShapeDtypeStruct((rows, 1), jnp.float32),
    ]
    return pl.pallas_call(
        functools.partial(block_kernel, first, second, pair_task),
        grid=(steps,),
        in_specs=[
            full((SEQLEN, 1)),
            full((1, rows)),
            full((rows, width)),
            full((rows, width)),
            full((2, width)),
            full((rows, HD)),
            full((rows, HD)),
            hbm,
            hbm,
            pl.BlockSpec((width, wide), weight_block),
        ],
        out_specs=[full(shape.shape) for shape in shapes] + [hbm, hbm],
        out_shape=shapes + [plane, plane],
        scratch_shapes=[pltpu.VMEM((rows, wide), low), pltpu.VMEM((count, rows, wide), low)]
        + [pltpu.SemaphoreType.DMA((14,))] * 4
        + [pltpu.SemaphoreType.DMA((pair_task.sem_count,))] * 2,
        compiler_params=pltpu.CompilerParams(
            collective_id=number, has_side_effects=True, vmem_limit_bytes=56 * 2**20
        ),
        cost_estimate=SMALL_COST,
        name="attention_block",
    )(
        key_segs[:, None], query_segs[None, :], normed, tokens, gains, *tables, cotangent, normed,
        weights,
    )


def half_rows(axis, height):
    def half_of(view, second):
        index = (slice(None),) * axis + (pl.ds(height if second else 0, height),)
        return view.at[index]

    return half_of


def whole(ref, index):
    return ref


def block_of(ref, index):
    return ref.at[index]


def gather_plane(
    shape, split=0, source_view=whole, target_view=block_of, out_shape=None, placed=False
):
    out_shape = out_shape or (lax.axis_size("grp"), *shape)
    if lax.axis_size("grp") == 8:
        halves = half_rows(split, shape[split] // 2)
        return PlaneGather(out_shape, source_view, target_view, halves, placed)
    return Exchange("grp", out_shape, source_view, target_view)


def hand_on(tasks):
    going = [task.forward() for task in tasks]
    while going:
        going = [steps for steps in going if next(steps, going) is not going]


def exchange_kernel(tasks, wires, arrays, outputs, *refs):
    sources, targets = refs[:arrays], refs[arrays : arrays + outputs]
    refs = list(refs[arrays + outputs :])
    sems, scratch = [], []
    for task in tasks:
        sems.append((refs.pop(0), refs.pop(0)))
        held = len(task.scratch()) if isinstance(task, PlaneSum) else 0
        scratch.append([refs.pop(0) for _ in range(held)])
    grp, seq = lax.axis_index("grp"), lax.axis_index("seq")
    barrier = pltpu.get_barrier_semaphore()
    axes = {"grp": [], "seq": []}
    for task in tasks:
        devices = list(task.peers(grp, seq))
        if len(devices) > len(axes[task.axis]):
            axes[task.axis] = devices
    devices = axes["grp"] + axes["seq"]
    for device in devices:
        pl.semaphore_signal(barrier, inc=1, device_id=device, device_id_type=MESH)
    pl.semaphore_wait(barrier, len(devices))

    def start(at):
        after, source, target = wires[at]
        source = targets[source] if after is not None else sources[source]
        more = (scratch[at],) if scratch[at] else ()
        tasks[at].start(source, targets[target], sems[at], grp, seq, *more)

    open_tasks = list(range(len(tasks)))
    first = [at for at in open_tasks if wires[at][0] is None]
    for at in first:
        start(at)
    for at in first:
        if isinstance(tasks[at], PlaneSum):
            tasks[at].first_sums()
    hand_on([tasks[at] for at in first])
    for at in open_tasks[:]:
        after = wires[at][0]
        if after is not None:
            tasks[after].finish()
            open_tasks.remove(after)
            start(at)
            hand_on([tasks[at]])
    for at in open_tasks:
        tasks[at].finish()


def exchange(number, work):
    tasks = [piece[0] for piece in work]
    arrays, shapes, wires = [], [], []
    for piece in work:
        if isinstance(piece[1], int):
            after, source = piece[1], wires[piece[1]][2]
            kind = shapes[source].dtype
        else:
            after, source = None, len(arrays)
            arrays.append(piece[1])
            kind = piece[1].dtype
        if len(piece) == 3:
            target = wires[piece[2]][2]
        else:
            target = len(shapes)
            shapes.append(jax.ShapeDtypeStruct(piece[0].out_shape, kind))
        wires.append((after, source, target))
    scratch = []
    for task in tasks:
        scratch += [pltpu.SemaphoreType.DMA((task.sem_count,))] * 2
        if isinstance(task, PlaneSum):
            scratch += task.scratch()
    return pl.pallas_call(
        functools.partial(exchange_kernel, tasks, wires, len(arrays), len(shapes)),
        in_specs=[pl.BlockSpec(memory_space=pl.ANY)] * len(arrays),
        out_specs=[pl.BlockSpec(memory_space=pl.ANY)] * len(shapes),
        out_shape=shapes,
        scratch_shapes=scratch,
        compiler_params=pltpu.CompilerParams(collective_id=number, has_side_effects=True),
        cost_estimate=SMALL_COST,
        name="exchange",
    )(*arrays)


def gather_axis(axis, array):
    task = Exchange(axis, (lax.axis_size(axis), *array.shape), whole, block_of)
    return task, array


def split_rows(axis, array):
    count = lax.axis_size(axis)
    rows, columns = array.shape
    height = rows // count
    task = Exchange(
        axis,
        (count, height, columns),
        lambda ref, index: rows_of(ref, index, height),
        block_of,
    )
    return task, array


def split_columns(axis, array, placed=False):
    count = lax.axis_size(axis)
    rows, columns = array.shape
    width = columns // count
    if placed and count == 8:
        task = PlacedExchange(
            (count, rows, width), lambda ref, index: columns_of(ref, index, width)
        )
        return task, array
    task = Exchange(
        axis,
        (count, rows, width),
        lambda ref, index: columns_of(ref, index, width),
        block_of,
    )
    return task, array


def plane_sum_kernel(
    part_ref, gate_ref, up_ref, x_ref, total_ref, gate_out, up_out, core_in, chip, half_x, half_y,
    whole_x, whole_y, x_block, stage, send_sems, recv_sems, x_sems, out_sems,
):
    grp, seq = lax.axis_index("grp"), lax.axis_index("seq")
    core, side_x, side_y = [flip(grp, bits) for bits in (1, 2, 4)]
    blocks = [PLACES[bits] for bits in (6, 2, 4, 0)]
    core_blocks = [PLACES[bits] for bits in (7, 3, 5, 1)]
    half = total_ref.shape[0] // 2
    low, high = pl.ds(0, half), pl.ds(half, half)
    cols = gate_ref.shape[0]
    rows = x_block.shape[2]
    count = x_ref.shape[1] // rows

    def x_copy(at):
        view = x_ref.at[:, pl.ds(pl.multiple_of(at * rows, rows), rows)]
        return pltpu.make_async_copy(view, x_block.at[at % 2], x_sems.at[at % 2])

    def out_copies(at):
        place = pl.ds(pl.multiple_of(at * cols, cols), cols)
        return [
            pltpu.make_async_copy(
                stage.at[which, at % 2], out.at[place], out_sems.at[which, at % 2]
            )
            for which, out in enumerate((gate_out, up_out))
        ]

    x_copy(0).start()
    barrier = pltpu.get_barrier_semaphore()
    for device in (core, side_x, side_y):
        pl.semaphore_signal(barrier, inc=1, device_id=(device, seq), device_id_type=MESH)
    pl.semaphore_wait(barrier, 3)

    sems = (send_sems, recv_sems)
    copies = [
        remote(part_ref.at[block], core_in.at[at], sems, at, (core, seq))
        for at, block in enumerate(core_blocks)
    ]
    copies += [
        remote(chip.at[0, low], half_x, sems, 4, (side_x, seq)),
        remote(chip.at[0, high], half_y, sems, 5, (side_y, seq)),
        remote(chip.at[1, low], whole_x.at[low], sems, 6, (side_x, seq)),
        remote(chip.at[2, high], whole_y.at[high], sems, 7, (side_y, seq)),
        remote(chip.at[1, high], whole_x.at[high], sems, 8, (side_x, seq)),
        remote(chip.at[2, low], whole_y.at[low], sems, 9, (side_y, seq)),
    ]
    for copy in copies[:4]:
        copy.start()

    def step(at, _):
        @pl.when(at == 1)
        def _():
            for came, then in ((0, (4, 5)), (1, (6,)), (2, (7,))):
                copies[came].wait_recv()
                add_rows(chip.at[came], part_ref.at[blocks[came]], core_in.at[came])
                for start in then:
                    copies[start].start()

        @pl.when(at == count - 1)
        def _():
            copies[5].wait_recv()
            add_rows(chip.at[1, high], chip.at[1, high], half_y)
            copies[8].start()
            copies[4].wait_recv()
            add_rows(chip.at[2, low], chip.at[2, low], half_x)
            copies[9].start()

        x_copy(at).wait()

        @pl.when(at + 1 < count)
        def _():
            x_copy(at + 1).start()

        @pl.when(at >= 2)
        def _():
            for copy in out_copies(at - 2):
                copy.wait()

        for which, ref in enumerate((gate_ref, up_ref)):
            stage[which, at % 2] = jnp.dot(
                ref[...], x_block[at % 2], preferred_element_type=jnp.float32
            ).astype(stage.dtype)
        for copy in out_copies(at):
            copy.start()
        return 0

    lax.fori_loop(0, count, step, 0)
    copies[3].wait_recv()
    add_rows(total_ref, part_ref.at[blocks[3]], core_in.at[3])
    for at, came, rows_at in (
        (6, whole_x, low),
        (7, whole_y, high),
        (8, whole_x, high),
        (9, whole_y, low),
    ):
        copies[at].wait_recv()
        add_rows(total_ref.at[rows_at], total_ref.at[rows_at], came.at[rows_at])
    for copy in copies:
        copy.wait_send()
    for at in (count - 2, count - 1):
        for copy in out_copies(at):
            copy.wait()


def plane_sum(number, part, gate_grad, up_grad, x, seq_count):
    count = lax.axis_size("grp")
    rows_all, columns = part.shape
    rows = rows_all // count
    if count != 8:
        total = lax.psum_scatter(part, "grp", scatter_dimension=0, tiled=True)
        return (
            total.astype(jnp.float32),
            weight_grad(gate_grad, x, seq_count),
            weight_grad(up_grad, x, seq_count),
        )
    low = jnp.bfloat16
    cols, tokens_all = gate_grad.shape
    width = x.shape[1] // seq_count
    vmem = pl.BlockSpec(memory_space=pltpu.VMEM)
    hbm = pl.BlockSpec(memory_space=pl.ANY)
    grads = jax.ShapeDtypeStruct((seq_count * cols, width), low)
    return pl.pallas_call(
        plane_sum_kernel,
        in_specs=[vmem, vmem, vmem, hbm],
        out_specs=[vmem, hbm, hbm],
        out_shape=[jax.ShapeDtypeStruct((rows, columns), jnp.float32), grads, grads],
        scratch_shapes=[
            pltpu.VMEM((4, rows, columns), low),
            pltpu.VMEM((3, rows, columns), low),
            pltpu.VMEM((rows // 2, columns), low),
            pltpu.VMEM((rows // 2, columns), low),
            pltpu.VMEM((rows, columns), low),
            pltpu.VMEM((rows, columns), low),
            pltpu.VMEM((2, tokens_all, width), low),
            pltpu.VMEM((2, 2, cols, width), low),
            pltpu.SemaphoreType.DMA((10,)),
            pltpu.SemaphoreType.DMA((10,)),
            pltpu.SemaphoreType.DMA((2,)),
            pltpu.SemaphoreType.DMA((2, 2)),
        ],
        compiler_params=pltpu.CompilerParams(
            collective_id=number, has_side_effects=True, vmem_limit_bytes=56 * 2**20
        ),
        cost_estimate=SMALL_COST,
        name="plane_sum",
    )(part.reshape(count, rows, columns), gate_grad, up_grad, x)


def local(
    tokens,
    cotangent,
    segment_ids,
    tile_owner_slots,
    weights_low,
    master,
    moment_one,
    moment_two,
    left_basis_set,
    right_basis_set,
    gains,
    gain_moment_one,
    gain_moment_two,
):
    grp_count = lax.axis_size("grp")
    seq_count = lax.axis_size("seq")
    grp_here, seq_here = lax.axis_index("grp"), lax.axis_index("seq")
    rows_here = tokens.shape[0]
    slots_here, rows_block, tile_width = weights_low.shape
    tile_count = tile_owner_slots.shape[0]
    query_cols = NH * HD
    value_end = query_cols + 2 * HD
    output_end = value_end + MODEL_WIDTH
    attn_tiles = output_end // tile_width
    query_tiles = query_cols // tile_width
    hidden_tiles = FF // tile_width
    share = -(-hidden_tiles // grp_count)
    share_cols = share * tile_width
    share_width = MODEL_WIDTH // grp_count
    sub_rows = rows_block // grp_count
    halves = 2 if sub_rows >= 32 else 1
    half_block, half_sub = rows_block // halves, sub_rows // halves
    first_place = (seq_here * rows_here) % SEQLEN
    key_tables = turn_tables(jnp.arange(SEQLEN, dtype=jnp.int32))
    tables = [lax.dynamic_slice_in_dim(table, first_place, rows_here) for table in key_tables]

    hidden_ids = grp_here * share + jnp.arange(share, dtype=jnp.int32)
    hidden_ids = jnp.minimum(hidden_ids, hidden_tiles - 1)
    feed_ids = (
        attn_tiles
        + jnp.arange(3, dtype=jnp.int32)[:, None] * hidden_tiles
        + hidden_ids[None, :]
    ).reshape(-1)
    feed_slots, attn_slots = tile_owner_slots[feed_ids], tile_owner_slots[:attn_tiles]

    tok_float = tokens.astype(jnp.float32)
    inverse_one = lax.rsqrt(jnp.mean(tok_float * tok_float, axis=-1, keepdims=True) + NORM_EPS)
    normed = (tok_float * inverse_one * gains[0]).astype(jnp.bfloat16)

    def weight_half(at):
        return gather_plane(
            (slots_here, half_block, tile_width),
            split=1,
            source_view=lambda ref, index: ref.at[:, pl.ds(at * half_block, half_block)],
        )

    flat = (grp_count * slots_here, -1, tile_width)
    work = [(weight_half(0), weights_low)]
    if halves == 2:
        late_rows = Exchange(
            "grp",
            (grp_count, slots_here, half_sub, tile_width),
            lambda ref, index: ref.at[:, pl.ds(half_block + index * half_sub, half_sub)],
            block_of,
        )
        work.append((late_rows, weights_low))
    work.append(gather_axis("seq", segment_ids.reshape(-1, tile_width)))
    *tiles, segments = exchange(0, work)
    tiles = [part.reshape(flat) for part in tiles]
    attn_rows = pick(attn_slots, tiles, half_sub).reshape(halves, half_sub, output_end)
    if grp_count == 8 and seq_count == 4:
        work = [(LineGather(attn_rows.shape), attn_rows)]
    else:
        work = [gather_axis("seq", attn_rows)]
    if halves == 2:
        work.append((weight_half(1), weights_low))
    attn_seq, *more = exchange(1, work)
    tiles = tiles[:1] + [part.reshape(flat) for part in more]
    feed_rows = pick(feed_slots, tiles)
    feed_parts = [lax.all_gather(feed_rows, "seq", axis=0, tiled=False)]
    attn_plane = gather_plane(
        attn_seq.shape,
        target_view=lambda ref, index: ref.at[:, :, index],
        out_shape=(seq_count, halves, grp_count, half_sub, output_end),
    )
    (attn_weights,) = exchange(2, [(attn_plane, attn_seq)])
    attn_weights = attn_weights.reshape(MODEL_WIDTH, output_end)

    first_key = seq_here * rows_here - first_place
    key_segs = lax.dynamic_slice_in_dim(segments.reshape(-1), first_key, SEQLEN)
    at = (first_place // rows_here).reshape(1)
    if grp_count == 8 and seq_count * rows_here == SEQLEN:
        (
            projected, pairs, context, log_totals, hidden, normed_two, inverse_two, cot_plane,
            normed_plane,
        ) = attention_block(
            3, normed, tokens, gains, tables, key_segs, segment_ids, cotangent, attn_weights
        )
    else:
        projected = project(normed, attn_weights, tables)
        pairs, cot_plane, normed_plane = exchange(
            3,
            [
                gather_axis("seq", projected[:, query_cols:]),
                (gather_plane(cotangent.shape, placed=True), cotangent),
                (gather_plane(normed.shape, placed=True), normed),
            ],
        )
        pairs = lax.dynamic_slice_in_dim(pairs.reshape(-1, 2 * HD), first_key, SEQLEN)
        context, log_totals = attend(at, projected, pairs, key_segs, segment_ids)
        branch = jnp.dot(
            context, attn_weights[:, value_end:], preferred_element_type=jnp.float32
        )
        hidden = tok_float + branch
        inverse_two = lax.rsqrt(jnp.mean(hidden * hidden, axis=-1, keepdims=True) + NORM_EPS)
        normed_two = (hidden * inverse_two * gains[1]).astype(jnp.bfloat16)

    cot_plane = cot_plane.reshape(-1, MODEL_WIDTH)
    normed_plane = normed_plane.reshape(-1, MODEL_WIDTH)
    real_cols = jnp.clip((hidden_tiles - grp_here * share) * tile_width, 0, share_cols).reshape(1)
    if grp_count == 8:
        gate_grad, up_grad, two_part, feed_part, second_plane, context_plane, down_grad = (
            feed_gather(
                4, real_cols, normed_two, context, cot_plane, feed_parts[0], seq_count
            )
        )
        second_plane = second_plane.reshape(-1, MODEL_WIDTH)
    else:
        second_plane, context_plane = exchange(
            4,
            [
                (gather_plane(normed_two.shape), normed_two),
                (gather_plane(context.shape), context),
            ],
        )
        second_plane = second_plane.reshape(-1, MODEL_WIDTH)
        activated, gate_grad, up_grad, two_part, feed_part = feed_forward(
            real_cols, second_plane, cot_plane, feed_parts, seq_count
        )
        down_grad = weight_grad(activated, cot_plane, seq_count)
    context_plane = context_plane.reshape(-1, MODEL_WIDTH)
    down_grad, two_part = lax.optimization_barrier((down_grad, two_part))
    down_grad = lax.psum_scatter(down_grad, "seq", scatter_dimension=0, tiled=True)
    norm_two_grad, gate_weight_grad, up_weight_grad = plane_sum(
        5, two_part, gate_grad, up_grad, second_plane, seq_count
    )
    gate_weight_grad = lax.psum_scatter(gate_weight_grad, "seq", scatter_dimension=0, tiled=True)
    up_weight_grad = lax.psum_scatter(up_weight_grad, "seq", scatter_dimension=0, tiled=True)

    out_grad = cotangent.astype(jnp.float32)
    gain_two_term = jnp.sum(norm_two_grad * hidden * inverse_two, axis=0)
    hidden_grad = (
        out_grad
        + inverse_two * gains[1] * norm_two_grad
        - hidden
        * inverse_two**3
        * jnp.mean(hidden * gains[1] * norm_two_grad, axis=-1, keepdims=True)
    )
    branch_grad = hidden_grad.astype(jnp.bfloat16)
    context_grad = times_transpose(branch_grad, attn_weights[:, value_end:]).astype(jnp.bfloat16)
    fused = grp_count == 8 and seq_count * rows_here == SEQLEN
    if fused:
        feed_part = feed_part.reshape(grp_count, rows_here, MODEL_WIDTH)
        query_grad, pair_part, feed_out, down_plane = attend_back_sum(
            6, projected, pairs, context_grad, log_totals, key_segs, segment_ids, key_tables,
            tables, feed_part, down_grad,
        )
    else:
        query_grad, pair_part = attend_back(
            at, projected, pairs, context_grad, log_totals, key_segs, segment_ids, key_tables, tables
        )
        feed_out = lax.psum_scatter(
            feed_part.reshape(-1, MODEL_WIDTH), "grp", scatter_dimension=0, tiled=True
        )
        (down_plane,) = exchange(10, [(gather_plane(down_grad.shape), down_grad)])
    block_out = (hidden + feed_out.astype(jnp.float32)).astype(jnp.bfloat16)
    if seq_count * rows_here > SEQLEN:
        pair_part = lax.dynamic_update_slice_in_dim(
            jnp.zeros((seq_count * rows_here, 2 * HD), pair_part.dtype), pair_part, first_key, 0
        )
    pair_parts, query_share, branch_share = exchange(
        7,
        [
            split_rows("seq", pair_part),
            split_columns("grp", query_grad, placed=True),
            split_columns("grp", branch_grad, placed=True),
        ],
    )
    pair_grad = jnp.sum(pair_parts.astype(jnp.float32), axis=0).astype(jnp.bfloat16)
    pair_grad, gate_weight_grad = lax.optimization_barrier((pair_grad, gate_weight_grad))
    projected_grad = jnp.concatenate([query_grad, pair_grad], axis=1)
    norm_one_grad = times_transpose(projected_grad, attn_weights[:, :value_end])
    gain_one_term = jnp.sum(norm_one_grad * tok_float * inverse_one, axis=0)
    input_grad = (
        hidden_grad
        + inverse_one * gains[0] * norm_one_grad
        - tok_float
        * inverse_one**3
        * jnp.mean(tok_float * gains[0] * norm_one_grad, axis=-1, keepdims=True)
    )
    query_weight_grad = contract(query_share.reshape(-1, share_width), normed_plane)
    out_weight_grad = contract(branch_share.reshape(-1, share_width), context_plane)
    pair_weight_grad = contract(normed, pair_grad).astype(jnp.bfloat16)
    shares = jnp.concatenate([query_weight_grad, out_weight_grad], axis=0).astype(jnp.bfloat16)
    feed_shape = (share_cols, rows_block)
    pair_task = Exchange(
        "grp",
        (grp_count, seq_count, sub_rows, 2 * HD),
        lambda ref, index: ref.at[:, index],
        block_of,
    )
    work = [
        split_columns("seq", shares),
        (pair_task, pair_weight_grad.reshape(seq_count, grp_count, sub_rows, 2 * HD)),
        gather_axis("seq", jnp.stack([gain_one_term, gain_two_term])),
        (gather_plane(feed_shape), gate_weight_grad),
        (gather_plane(feed_shape), up_weight_grad),
    ]
    share_parts, pair_parts, gain_parts, gate_plane, up_plane = exchange(8, work)
    gain_seq = jnp.sum(gain_parts, axis=0)
    shares = jnp.sum(share_parts.astype(jnp.float32), axis=0).astype(jnp.bfloat16)
    pair_parts = jnp.sum(pair_parts.astype(jnp.float32), axis=0).astype(jnp.bfloat16)
    pair_task = Exchange("seq", pair_parts.shape, block_of, block_of)
    _, pair_plane, share_plane, gain_parts = exchange(
        9,
        [
            (pair_task, pair_parts),
            (gather_plane(pair_parts.shape), 0),
            (gather_plane(shares.shape), shares),
            gather_axis("grp", gain_seq),
        ],
    )
    pair_plane = jnp.sum(pair_plane.astype(jnp.float32), axis=1).astype(jnp.bfloat16)
    gain_grads = jnp.sum(gain_parts, axis=0)

    tile_of_slot = (
        jnp.full((grp_count * slots_here,), tile_count, jnp.int32)
        .at[tile_owner_slots]
        .set(jnp.arange(tile_count, dtype=jnp.int32))
    )
    tiles_here = lax.dynamic_slice_in_dim(tile_of_slot, grp_here * slots_here, slots_here)
    feed_at = jnp.clip(tiles_here - attn_tiles, 0, 3 * hidden_tiles - 1)
    which, column = feed_at // hidden_tiles, feed_at % hidden_tiles
    is_query = tiles_here < query_tiles
    is_pair = (tiles_here >= query_tiles) & (tiles_here < query_tiles + 2)
    is_feed = tiles_here >= attn_tiles
    kind = jnp.where(is_feed, jnp.minimum(which, 2), 3)
    kind = jnp.where(is_pair, 4, jnp.where(is_feed, kind, 3))
    kind = jnp.where(tiles_here == tile_count, 5, kind)
    out_at = jnp.clip(tiles_here - query_tiles - 2, 0, query_tiles - 1)
    per_share = share_width // tile_width
    share_at = jnp.where(is_query, jnp.minimum(tiles_here, query_tiles - 1), out_at)
    at = jnp.stack(
        [
            kind,
            column // share,
            column % share,
            share_at // per_share,
            share_at % per_share + jnp.where(is_query, 0, per_share),
            jnp.where(is_pair, tiles_here - query_tiles, 0),
        ]
    )
    new_master, new_one, new_two = adam(
        at,
        gate_plane,
        up_plane,
        down_plane,
        share_plane,
        pair_plane,
        left_basis_set,
        right_basis_set,
        master,
        moment_one,
        moment_two,
    )
    gain_one = BETA_ONE * gain_moment_one + (1.0 - BETA_ONE) * gain_grads
    gain_two = BETA_TWO * gain_moment_two + (1.0 - BETA_TWO) * gain_grads * gain_grads
    new_gains = gains - GAIN_RATE * gain_one / (jnp.sqrt(gain_two) + ADAM_EPS)
    return (
        block_out,
        input_grad,
        new_master,
        new_one,
        new_two,
        gain_grads,
        new_gains,
        gain_one,
        gain_two,
    )


def solution(mesh):
    return jax.shard_map(
        local,
        mesh=mesh,
        in_specs=(
            P(("grp", "seq"), None),
            P(("grp", "seq"), None),
            P(("grp", "seq")),
            P(),
            P("grp", "seq", None),
            P("grp", "seq", None),
            P("grp", "seq", None),
            P("grp", "seq", None),
            P("grp", "seq", None),
            P("grp", "seq", None),
            P(),
            P(),
            P(),
        ),
        out_specs=(
            P(("grp", "seq"), None),
            P(("grp", "seq"), None),
            P("grp", "seq", None),
            P("grp", "seq", None),
            P("grp", "seq", None),
            P(),
            P(),
            P(),
            P(),
        ),
        check_vma=False,
    )
```

```python
import functools

import jax
import jax.numpy as jnp
from jax import lax
from jax.experimental import pallas as pl
from jax.experimental.pallas import tpu as pltpu
from jax.sharding import PartitionSpec as P

MODEL_WIDTH = 2048
NH = 16
HD = 128
FF = 5632
SEQLEN = 1024


NORM_EPS = 1e-05
BETA_ONE = 0.95
BETA_TWO = 0.95
ADAM_EPS = 1e-08
WEIGHT_DECAY = 0.01
LEARN_RATE = 0.03
GAIN_RATE = 1.5
ROPE_BASE = 10000.0
MASKED = -1e30
PRECISE = lax.Precision.HIGHEST


def contract(left_side, right_side):
    return lax.dot_general(
        left_side, right_side, (((0,), (0,)), ((), ())), preferred_element_type=jnp.float32
    )


def times_transpose(left_side, right_side):
    return lax.dot_general(
        left_side, right_side, (((1,), (1,)), ((), ())), preferred_element_type=jnp.float32
    )


def turn_tables(places):
    half_width = HD // 2
    frequency = ROPE_BASE ** (-(jnp.arange(half_width, dtype=jnp.float32) * 2.0) / HD)
    angles = places.astype(jnp.float32)[:, None] * frequency[None, :]
    cosine, sine = jnp.cos(angles), jnp.sin(angles)
    return (
        jnp.concatenate([cosine, cosine], axis=1),
        jnp.concatenate([-sine, sine], axis=1),
    )


def turn(rows, cosine, sine):
    return rows * cosine + pltpu.roll(rows, HD // 2, 1) * sine


def turn_back(rows, cosine, sine):
    return rows * cosine - pltpu.roll(rows, HD // 2, 1) * sine


def dot_last(left_side, right_side):
    return lax.dot_general(
        left_side, right_side, (((1,), (1,)), ((), ())), preferred_element_type=jnp.float32
    )


def dot_first(left_side, right_side):
    return lax.dot_general(
        left_side, right_side, (((0,), (0,)), ((), ())), preferred_element_type=jnp.float32
    )


SMALL_COST = pl.CostEstimate(flops=1, bytes_accessed=1, transcendentals=0)


def project_kernel(x_ref, w_ref, cosine_ref, sine_ref, out_ref):
    made = jnp.dot(x_ref[...], w_ref[...], preferred_element_type=jnp.float32)
    cosine, sine = cosine_ref[...], sine_ref[...]
    first, second = made[:, :HD], made[:, HD:]
    last = pl.program_id(0) == pl.num_programs(0) - 1
    out_ref[:, :HD] = turn(first, cosine, sine).astype(out_ref.dtype)
    out_ref[:, HD:] = jnp.where(last, second, turn(second, cosine, sine)).astype(out_ref.dtype)


def project(normed, weights, tables):
    rows, width = normed.shape
    steps = NH // 2 + 1
    return pl.pallas_call(
        project_kernel,
        grid=(steps,),
        in_specs=[
            pl.BlockSpec((rows, width), lambda j: (0, 0)),
            pl.BlockSpec((width, 2 * HD), lambda j: (0, j)),
            pl.BlockSpec((rows, HD), lambda j: (0, 0)),
            pl.BlockSpec((rows, HD), lambda j: (0, 0)),
        ],
        out_specs=pl.BlockSpec((rows, 2 * HD), lambda j: (0, j)),
        out_shape=jax.ShapeDtypeStruct((rows, steps * 2 * HD), jnp.bfloat16),
        compiler_params=pltpu.CompilerParams(vmem_limit_bytes=56 * 2**20),
        cost_estimate=SMALL_COST,
        name="project",
    )(normed, weights, *tables)


def score_mask(key_seg_ref, query_seg_ref, block, rows):
    keys = (block + 1) * rows
    same = key_seg_ref[:keys, :] == query_seg_ref[...]
    key_at = lax.broadcasted_iota(jnp.int32, (keys, rows), 0)
    query_at = lax.broadcasted_iota(jnp.int32, (keys, rows), 1) + block * rows
    return same & (key_at <= query_at)


def attend_kernel(at_ref, q_ref, k_ref, v_ref, key_seg_ref, query_seg_ref, context_ref, total_ref):
    scale = HD ** (-0.5)
    rows = q_ref.shape[0]
    for block in range(SEQLEN // rows):

        @pl.when(at_ref[0] == block)
        def _():
            keys = (block + 1) * rows
            scores = dot_last(k_ref[:keys, :], q_ref[...]) * scale
            scores = jnp.where(
                score_mask(key_seg_ref, query_seg_ref, block, rows), scores, MASKED
            )
            highest = jnp.max(scores, axis=0, keepdims=True)
            exponent = jnp.exp(scores - highest)
            totals = jnp.sum(exponent, axis=0, keepdims=True)
            probs_low = (exponent * (1.0 / totals)).astype(jnp.bfloat16)
            context = dot_first(probs_low, v_ref[:keys, :])
            context_ref[...] = context.astype(jnp.bfloat16)
            total_ref[0] = highest + jnp.log(totals)


def attend_back_head(
    place, q_ref, k_ref, v_ref, grad_ref, total_ref, key_seg_ref, query_seg_ref, key_cosine_ref,
    key_sine_ref, cosine_ref, sine_ref, query_grad_ref, pair_grad_ref, key_sum, value_sum,
):
    scale = HD ** (-0.5)
    rows = q_ref.shape[0]
    head = pl.program_id(0)

    @pl.when(head == 0)
    def _():
        key_sum[...] = jnp.zeros_like(key_sum)
        value_sum[...] = jnp.zeros_like(value_sum)

    for block in range(SEQLEN // rows):

        @pl.when(place == block)
        def _():
            keys = (block + 1) * rows
            queries, grads = q_ref[...], grad_ref[...]
            shifted = dot_last(k_ref[:keys, :], queries) * scale - total_ref[0]
            allowed = score_mask(key_seg_ref, query_seg_ref, block, rows)
            probs = jnp.where(allowed, jnp.exp(shifted), 0.0)
            prob_grad = dot_last(v_ref[:keys, :], grads)
            centre = jnp.sum(probs * prob_grad, axis=0, keepdims=True)
            score_grad = (probs * (prob_grad - centre) * scale).astype(jnp.bfloat16)
            value_sum[:keys, :] += jnp.dot(
                probs.astype(jnp.bfloat16), grads, preferred_element_type=jnp.float32
            )
            key_sum[:keys, :] += jnp.dot(score_grad, queries, preferred_element_type=jnp.float32)
            query_grad = dot_first(score_grad, k_ref[:keys, :])
            query_grad_ref[...] = turn_back(query_grad, cosine_ref[...], sine_ref[...]).astype(
                jnp.bfloat16
            )

    @pl.when(head == pl.num_programs(0) - 1)
    def _():
        pair_grad_ref[:, :HD] = turn_back(
            key_sum[...], key_cosine_ref[...], key_sine_ref[...]
        ).astype(jnp.bfloat16)
        pair_grad_ref[:, HD:] = value_sum[...].astype(jnp.bfloat16)


def attend_back_kernel(at_ref, *refs):
    attend_back_head(at_ref[0], *refs)


def attention_specs(kinds, rows):
    specs = {
        "at": pl.BlockSpec(memory_space=pltpu.SMEM),
        "head": pl.BlockSpec((rows, HD), lambda h: (0, h)),
        "keys": pl.BlockSpec((SEQLEN, HD), lambda h: (0, 0)),
        "values": pl.BlockSpec((SEQLEN, HD), lambda h: (0, 1)),
        "pair": pl.BlockSpec((SEQLEN, 2 * HD), lambda h: (0, 0)),
        "total": pl.BlockSpec((1, 1, rows), lambda h: (h, 0, 0)),
        "key_seg": pl.BlockSpec((SEQLEN, 1), lambda h: (0, 0)),
        "query_seg": pl.BlockSpec((1, rows), lambda h: (0, 0)),
        "key_table": pl.BlockSpec((SEQLEN, HD), lambda h: (0, 0)),
        "table": pl.BlockSpec((rows, HD), lambda h: (0, 0)),
    }
    return [specs[kind] for kind in kinds]


def attend(at, projected, pairs, key_segs, query_segs):
    rows = projected.shape[0]
    columns = NH * HD
    return pl.pallas_call(
        attend_kernel,
        grid=(NH,),
        in_specs=attention_specs(["at", "head", "keys", "values", "key_seg", "query_seg"], rows),
        out_specs=attention_specs(["head", "total"], rows),
        out_shape=(
            jax.ShapeDtypeStruct((rows, columns), jnp.bfloat16),
            jax.ShapeDtypeStruct((NH, 1, rows), jnp.float32),
        ),
        compiler_params=pltpu.CompilerParams(vmem_limit_bytes=32 * 2**20),
        cost_estimate=SMALL_COST,
        name="attend",
    )(at, projected, pairs, pairs, key_segs[:, None], query_segs[None, :])


def attend_back(at, projected, pairs, grads, totals, key_segs, query_segs, key_tables, tables):
    rows = projected.shape[0]
    columns = NH * HD
    return pl.pallas_call(
        attend_back_kernel,
        grid=(NH,),
        in_specs=attention_specs(
            ["at", "head", "keys", "values", "head", "total", "key_seg", "query_seg"]
            + ["key_table", "key_table", "table", "table"],
            rows,
        ),
        out_specs=attention_specs(["head", "pair"], rows),
        out_shape=(
            jax.ShapeDtypeStruct((rows, columns), jnp.bfloat16),
            jax.ShapeDtypeStruct((SEQLEN, 2 * HD), jnp.bfloat16),
        ),
        scratch_shapes=[pltpu.VMEM((SEQLEN, HD), jnp.float32)] * 2,
        compiler_params=pltpu.CompilerParams(vmem_limit_bytes=32 * 2**20),
        cost_estimate=SMALL_COST,
        name="attend_back",
    )(
        at, projected, pairs, pairs, grads, totals, key_segs[:, None], query_segs[None, :],
        *key_tables, *tables,
    )


def load_weights(parts, weights, sems):
    count, rows, _ = parts[0].shape
    halves = len(parts)
    return [
        pltpu.make_async_copy(
            parts[half].at[block],
            weights.at[pl.ds((block * halves + half) * rows, rows)],
            sems.at[block * halves + half],
        )
        for half in range(halves)
        for block in range(count)
    ]


def feed_block(real, x, cot, weights, act_ref, gate_grad_ref, up_grad_ref, two_ref, out_ref):
    low = jnp.bfloat16
    wide = jnp.float32
    cols = act_ref.shape[0]
    gate = jnp.dot(x, weights[:, :cols], preferred_element_type=wide)
    upper = jnp.dot(x, weights[:, cols : 2 * cols], preferred_element_type=wide)
    act_grad = jnp.dot(cot, weights[:, 2 * cols :], preferred_element_type=wide)
    real = lax.broadcasted_iota(jnp.int32, gate.shape, 1) < real
    sigmoid = 1.0 / (1.0 + jnp.exp(-gate))
    silu = gate * sigmoid
    activated = jnp.where(real, silu * upper, 0.0).astype(low)
    act_grad = jnp.where(real, act_grad, 0.0)
    gate_grad = (act_grad * upper * sigmoid * (1.0 + gate * (1.0 - sigmoid))).astype(low)
    up_grad = (act_grad * silu).astype(low)
    act_ref[...] = jnp.transpose(activated)
    gate_grad_ref[...] = jnp.transpose(gate_grad)
    up_grad_ref[...] = jnp.transpose(up_grad)
    two = dot_last(gate_grad, weights[:, :cols]) + dot_last(up_grad, weights[:, cols : 2 * cols])
    two_ref[...] = two.astype(low)
    out_ref[...] = dot_last(activated, weights[:, 2 * cols :]).astype(low)


def feed_kernel(real_ref, x_ref, cot_ref, *refs):
    parts, refs = refs[:-7], refs[-7:]
    weights, sems = refs[5:]

    @pl.when(pl.program_id(0) == 0)
    def _():
        copies = load_weights(parts, weights, sems)
        for copy in copies:
            copy.start()
        for copy in copies:
            copy.wait()

    feed_block(real_ref[0], x_ref[...], cot_ref[...], weights, *refs[:5])


def feed_forward(real_cols, x, cot, parts, seq_count):
    tokens_all, width = x.shape
    _, rows, cols = parts[0].shape
    cols = cols // 3
    step = 256
    low = jnp.bfloat16
    block = pl.BlockSpec((step, width), lambda i: (i, 0))
    narrow = pl.BlockSpec((cols, step), lambda i: (0, i))
    return pl.pallas_call(
        feed_kernel,
        grid=(tokens_all // step,),
        in_specs=[pl.BlockSpec(memory_space=pltpu.SMEM), block, block]
        + [pl.BlockSpec(memory_space=pl.ANY)] * len(parts),
        out_specs=[narrow, narrow, narrow, block, block],
        out_shape=[jax.ShapeDtypeStruct((cols, tokens_all), low)] * 3
        + [jax.ShapeDtypeStruct((tokens_all, width), low)] * 2,
        scratch_shapes=[
            pltpu.VMEM((width, 3 * cols), low),
            pltpu.SemaphoreType.DMA((len(parts) * seq_count,)),
        ],
        compiler_params=pltpu.CompilerParams(vmem_limit_bytes=52 * 2**20),
        cost_estimate=SMALL_COST,
        name="feed_forward",
    )(real_cols, x, cot, *parts)


def feed_gather_kernel(
    first, second, halves, real_ref, own_ref, context_ref, cot_ref, cot_all_ref, *refs
):
    parts, refs = refs[:halves], refs[halves:]
    (
        gate_grad_ref, up_grad_ref, two_ref, out_ref, second_ref, context_plane_ref, down_out,
        blocks, weights, act_block, act, x_block, stage, load_sems, keep_sems, x_sems, out_sems,
        first_send, first_recv, second_send, second_recv,
    ) = refs
    step = pl.program_id(0)
    grp, seq = lax.axis_index("grp"), lax.axis_index("seq")
    first.start(own_ref, blocks, (first_send, first_recv), grp, seq, begin=False)
    second.start(context_ref, context_plane_ref, (second_send, second_recv), grp, seq, begin=False)
    loads = load_weights(parts, weights, load_sems)
    cols = act.shape[0]
    step_rows = act_block.shape[1]
    rows = x_block.shape[2]
    count = cot_all_ref.shape[1] // rows

    @pl.when(step == 0)
    def _():
        for copy in loads:
            copy.start()
        barrier = pltpu.get_barrier_semaphore()
        for device in first.peers(grp, seq):
            pl.semaphore_signal(barrier, inc=1, device_id=device, device_id_type=MESH)
        pl.semaphore_wait(barrier, 3)
        first.begin()
        first.kept.wait()
        for copy in loads:
            copy.wait()

    @pl.when(step == 1)
    def _():
        first.due[7].wait_recv()

    @pl.when(step == 2)
    def _():
        for came in (1, 4, 2):
            first.pass_on(came)

    @pl.when(step == 3)
    def _():
        first.pass_on(5)

    @pl.when(step == 4)
    def _():
        first.due[8].wait_recv()
        first.due[9].wait_recv()
        first.pass_on(6)
        first.pass_on(3)
        second.begin()

    @pl.when(step == 5)
    def _():
        first.due[10].wait_recv()
        first.due[11].wait_recv()

    @pl.when(step == 7)
    def _():
        first.due[12].wait_recv()
        first.due[13].wait_recv()
        second.pass_on(1)
        second.pass_on(4)

    keep = pltpu.make_async_copy(blocks.at[step], second_ref.at[step], keep_sems.at[step])
    keep.start()
    feed_block(
        real_ref[0], blocks[step], cot_ref[...], weights, act_block, gate_grad_ref, up_grad_ref,
        two_ref, out_ref,
    )
    act[:, pl.ds(pl.multiple_of(step * step_rows, step_rows), step_rows)] = act_block[...]

    def x_copy(at):
        view = cot_all_ref.at[:, pl.ds(pl.multiple_of(at * rows, rows), rows)]
        return pltpu.make_async_copy(view, x_block.at[at % 2], x_sems.at[at % 2])

    def out_copy(at):
        place = pl.ds(pl.multiple_of(at * cols, cols), cols)
        return pltpu.make_async_copy(stage.at[at % 2], down_out.at[place], out_sems.at[at % 2])

    @pl.when(step == 7)
    def _():
        x_copy(0).start()
        second.pass_on(2)
        second.pass_on(5)

        def one(at, _):
            @pl.when(at == 2)
            def _():
                second.pass_on(6)
                second.pass_on(3)

            x_copy(at).wait()

            @pl.when(at + 1 < count)
            def _():
                x_copy(at + 1).start()

            @pl.when(at >= 2)
            def _():
                out_copy(at - 2).wait()

            stage[at % 2] = jnp.dot(
                act[...], x_block[at % 2], preferred_element_type=jnp.float32
            ).astype(stage.dtype)
            out_copy(at).start()
            return 0

        lax.fori_loop(0, count, one, 0)
        out_copy(count - 2).wait()
        out_copy(count - 1).wait()
        second.finish()
        for copy in first.out[1:]:
            copy.wait_send()
        for at in range(8):
            pltpu.make_async_copy(blocks.at[at], second_ref.at[at], keep_sems.at[at]).wait()


def feed_gather(number, real_cols, normed, context, cot, parts, seq_count):
    rows, width = normed.shape
    cols = parts[0].shape[2] // 3
    low = jnp.bfloat16
    block = pl.BlockSpec((rows, width), lambda i: (i, 0))
    narrow = pl.BlockSpec((cols, rows), lambda i: (0, i))
    first = gather_plane(normed.shape, placed=True)
    second = gather_plane(context.shape, placed=True)
    hbm = pl.BlockSpec(memory_space=pl.ANY)
    plane = jax.ShapeDtypeStruct((8, rows, width), low)
    model_rows = width // seq_count
    return pl.pallas_call(
        functools.partial(feed_gather_kernel, first, second, len(parts)),
        grid=(8,),
        in_specs=[pl.BlockSpec(memory_space=pltpu.SMEM), hbm, hbm, block, hbm]
        + [hbm] * len(parts),
        out_specs=[narrow, narrow, block, block, hbm, hbm, hbm],
        out_shape=[jax.ShapeDtypeStruct((cols, 8 * rows), low)] * 2
        + [jax.ShapeDtypeStruct((8 * rows, width), low)] * 2
        + [plane, plane, jax.ShapeDtypeStruct((seq_count * cols, model_rows), low)],
        scratch_shapes=[
            pltpu.VMEM((8, rows, width), low),
            pltpu.VMEM((width, 3 * cols), low),
            pltpu.VMEM((cols, rows), low),
            pltpu.VMEM((cols, 8 * rows), low),
            pltpu.VMEM((2, 8 * rows, model_rows), low),
            pltpu.VMEM((2, cols, model_rows), low),
            pltpu.SemaphoreType.DMA((seq_count * len(parts),)),
            pltpu.SemaphoreType.DMA((8,)),
            pltpu.SemaphoreType.DMA((2,)),
            pltpu.SemaphoreType.DMA((2,)),
        ]
        + [pltpu.SemaphoreType.DMA((14,))] * 4,
        compiler_params=pltpu.CompilerParams(
            collective_id=number, has_side_effects=True, vmem_limit_bytes=60 * 2**20
        ),
        cost_estimate=SMALL_COST,
        name="feed_gather",
    )(real_cols, normed, context, cot, cot, *parts)


def weight_grad_kernel(left_ref, x_ref, out_ref):
    out_ref[...] = jnp.dot(
        left_ref[...], x_ref[...], preferred_element_type=jnp.float32
    ).astype(out_ref.dtype)


def weight_grad(left, x, seq_count):
    cols, tokens_all = left.shape
    rows = x.shape[1] // seq_count
    return pl.pallas_call(
        weight_grad_kernel,
        grid=(seq_count,),
        in_specs=[
            pl.BlockSpec((cols, tokens_all), lambda i: (0, 0)),
            pl.BlockSpec((tokens_all, rows), lambda i: (0, i)),
        ],
        out_specs=pl.BlockSpec((cols, rows), lambda i: (i, 0)),
        out_shape=jax.ShapeDtypeStruct((seq_count * cols, rows), jnp.bfloat16),
        compiler_params=pltpu.CompilerParams(vmem_limit_bytes=40 * 2**20),
        cost_estimate=SMALL_COST,
        name="weight_grad",
    )(left, x)


def share_grad_kernel(query_ref, out_ref, normed_ref, context_ref, grads_ref):
    half = query_ref.shape[1]
    for at, (left, right) in enumerate(((query_ref, normed_ref), (out_ref, context_ref))):
        made = dot_first(left[...], right[...])
        grads_ref[at * half : (at + 1) * half, :] = made.astype(grads_ref.dtype)


def share_grad(query_share, out_share, normed, context):
    tokens_all, width = normed.shape
    columns = query_share.shape[1]
    step = 512
    narrow = pl.BlockSpec((tokens_all, columns), lambda i: (0, 0))
    block = pl.BlockSpec((tokens_all, step), lambda i: (0, i))
    return pl.pallas_call(
        share_grad_kernel,
        grid=(width // step,),
        in_specs=[narrow, narrow, block, block],
        out_specs=pl.BlockSpec((2 * columns, step), lambda i: (0, i)),
        out_shape=jax.ShapeDtypeStruct((2 * columns, width), jnp.bfloat16),
        compiler_params=pltpu.CompilerParams(vmem_limit_bytes=60 * 2**20),
        cost_estimate=SMALL_COST,
        name="share_grad",
    )(query_share, out_share, normed, context)


def pick_kernel(rows, feed_ref, attn_ref, tiles_ref, feed_out, attn_out, sems):
    grp = lax.axis_index("grp")
    width = tiles_ref.shape[2]
    copies = []
    for at in range(feed_ref.shape[0]):
        copies.append(
            (tiles_ref.at[feed_ref[at]], feed_out.at[:, at * width : (at + 1) * width])
        )
    share = pl.ds(pl.multiple_of(grp * rows, rows), rows)
    for at in range(attn_ref.shape[0]):
        copies.append(
            (tiles_ref.at[attn_ref[at], share], attn_out.at[:, at * width : (at + 1) * width])
        )
    copies = [
        pltpu.make_async_copy(source, target, sems.at[at])
        for at, (source, target) in enumerate(copies)
    ]
    for copy in copies:
        copy.start()
    for copy in copies:
        copy.wait()


def pick(tiles, feed_slots, attn_slots):
    _, rows, width = tiles.shape
    share = rows // lax.axis_size("grp")
    feed, attn = feed_slots.shape[0], attn_slots.shape[0]
    return pl.pallas_call(
        functools.partial(pick_kernel, share),
        in_specs=[pl.BlockSpec(memory_space=pltpu.SMEM)] * 2 + [pl.BlockSpec(memory_space=pl.ANY)],
        out_specs=[pl.BlockSpec(memory_space=pltpu.VMEM)] * 2,
        out_shape=[
            jax.ShapeDtypeStruct((rows, feed * width), tiles.dtype),
            jax.ShapeDtypeStruct((share, attn * width), tiles.dtype),
        ],
        scratch_shapes=[pltpu.SemaphoreType.DMA((feed + attn,))],
        cost_estimate=SMALL_COST,
        name="pick",
    )(feed_slots, attn_slots, tiles)


def adam_kernel(group, at_ref, *refs):
    feeds = [refs[at * group : (at + 1) * group] for at in range(4)]
    left_ref, right_ref, master_ref, one_ref, two_ref = refs[4 * group : 4 * group + 5]
    new_master_ref, new_one_ref, new_two_ref, grad = refs[4 * group + 5 :]
    low = jnp.bfloat16
    for slot in range(group):
        kind = at_ref[0, pl.program_id(0) * group + slot]
        for number in range(3):

            @pl.when(kind == number)
            def _():
                grad[slot] = feeds[number][slot][0]

        @pl.when(kind == 3)
        def _():
            pair = feeds[3][slot][...].reshape(grad.shape[2], grad.shape[1])
            grad[slot] = jnp.transpose(pair.astype(jnp.float32)).astype(grad.dtype)

        @pl.when(kind == 4)
        def _():
            grad[slot] = jnp.zeros(grad.shape[1:], grad.dtype)

    slots = range(group)
    left = [left_ref[slot].astype(low) for slot in slots]
    right = [right_ref[slot].astype(low) for slot in slots]
    turned = [
        jnp.dot(grad[slot], left[slot], preferred_element_type=jnp.float32) for slot in slots
    ]
    turned = [dot_first(turned[slot].astype(low), right[slot]) for slot in slots]
    scaled = []
    for slot in slots:
        new_one = BETA_ONE * one_ref[slot] + (1.0 - BETA_ONE) * turned[slot]
        new_two = BETA_TWO * two_ref[slot] + (1.0 - BETA_TWO) * turned[slot] * turned[slot]
        new_one_ref[slot], new_two_ref[slot] = new_one, new_two
        scaled.append((new_one / (jnp.sqrt(new_two) + ADAM_EPS)).astype(low))
    restored = [dot_last(scaled[slot], right[slot]).astype(low) for slot in slots]
    restored = [
        jnp.dot(left[slot], restored[slot], preferred_element_type=jnp.float32) for slot in slots
    ]
    for slot in slots:
        new_master_ref[slot] = (
            master_ref[slot] * (1.0 - LEARN_RATE * WEIGHT_DECAY) - LEARN_RATE * restored[slot]
        )


def adam(at, gating, down, shares, pairs, left, right, master, one, two):
    slots, rows, width = master.shape
    group = 3 if slots % 3 == 0 else 1
    tile = pl.BlockSpec((group, rows, width), lambda i, at: (i, 0, 0))
    shape = jax.ShapeDtypeStruct(master.shape, jnp.float32)

    def feed(block, column):
        return [
            pl.BlockSpec(
                (1, width, rows),
                lambda i, at, slot=slot: (at[block, i * group + slot], at[column, i * group + slot], 0),
            )
            for slot in range(group)
        ]

    pair = [
        pl.BlockSpec(
            (*pairs.shape[:2], width), lambda i, at, slot=slot: (0, 0, at[6, i * group + slot])
        )
        for slot in range(group)
    ]
    return pl.pallas_call(
        functools.partial(adam_kernel, group),
        grid_spec=pltpu.PrefetchScalarGridSpec(
            num_scalar_prefetch=1,
            grid=(slots // group,),
            in_specs=feed(1, 2)
            + feed(1, 3)
            + feed(4, 5)
            + pair
            + [
                pl.BlockSpec((group, rows, rows), lambda i, at: (i, 0, 0)),
                pl.BlockSpec((group, width, width), lambda i, at: (i, 0, 0)),
                tile,
                tile,
                tile,
            ],
            out_specs=[tile] * 3,
            scratch_shapes=[pltpu.VMEM((group, width, rows), jnp.bfloat16)],
        ),
        out_shape=[shape] * 3,
        compiler_params=pltpu.CompilerParams(vmem_limit_bytes=60 * 2**20),
        cost_estimate=SMALL_COST,
        name="adam",
    )(
        at, *[gating] * group, *[down] * group, *[shares] * group, *[pairs] * group,
        left, right, master, one, two,
    )


MESH = pl.DeviceIdType.MESH


def remote(source, target, sems, at, device):
    return pltpu.make_async_remote_copy(
        src_ref=source,
        dst_ref=target,
        send_sem=sems[0].at[at],
        recv_sem=sems[1].at[at],
        device_id=device,
        device_id_type=MESH,
    )


def columns_of(ref, index, width):
    return ref.at[:, pl.ds(pl.multiple_of(index * width, width), width)]


def rows_of(ref, index, height):
    return ref.at[pl.ds(pl.multiple_of(index * height, height), height), :]


PLACES = {0: 0, 1: 1, 2: 2, 4: 3, 3: 4, 5: 5, 6: 6, 7: 7}


def flip(device, bits):
    core, side_x, side_y = device % 2, (device // 2) % 2, device // 4
    for bit, there in ((1, 1 - 2 * core), (2, 2 - 4 * side_x), (4, 4 - 8 * side_y)):
        if bits & bit:
            device = device + there
    return device


class PlacedExchange:
    axis = "grp"
    sem_count = 8

    def __init__(self, out_shape, source_view):
        self.out_shape, self.source_view = out_shape, source_view

    def peers(self, grp, seq):
        for bits in range(1, 8):
            yield flip(grp, bits), seq

    def start(self, source, target, sems, grp, seq):
        self.own = pltpu.make_async_copy(
            self.source_view(source, grp), target.at[0], sems[0].at[0]
        )
        self.own.start()
        self.copies = []
        for bits in range(1, 8):
            there = flip(grp, bits)
            copy = remote(
                self.source_view(source, there), target.at[PLACES[bits]], sems, bits, (there, seq)
            )
            copy.start()
            self.copies.append(copy)

    def forward(self):
        return iter(())

    def finish(self):
        for copy in self.copies:
            copy.wait()
        self.own.wait()


class Exchange:
    def __init__(self, axis, out_shape, source_view, target_view):
        self.axis, self.out_shape = axis, out_shape
        self.source_view, self.target_view = source_view, target_view
        self.count = lax.axis_size(axis)
        self.sem_count = self.count

    def peers(self, grp, seq):
        me = grp if self.axis == "grp" else seq
        for step in range(1, self.count):
            there = (me + step) % self.count
            yield (there, seq) if self.axis == "grp" else (grp, there)

    def start(self, source, target, sems, grp, seq, begin=True):
        me = grp if self.axis == "grp" else seq
        self.own = pltpu.make_async_copy(
            self.source_view(source, me), self.target_view(target, me), sems[0].at[0]
        )
        self.sent, self.due = [], []
        for step, device in enumerate(self.peers(grp, seq), 1):
            there = (me + step) % self.count
            back = (me + self.count - step) % self.count
            self.sent.append(
                remote(
                    self.source_view(source, there), self.target_view(target, me), sems, step, device
                )
            )
            self.due.append(
                remote(
                    self.source_view(source, back), self.target_view(target, back), sems, step, device
                )
            )
        if begin:
            self.begin()

    def begin(self):
        for copy in [self.own] + self.sent:
            copy.start()

    def forward(self):
        return iter(())

    def finish(self):
        for copy in self.due:
            copy.wait_recv()
        for copy in self.sent:
            copy.wait_send()
        self.own.wait()


class PlaneGather:
    axis = "grp"
    sem_count = 14

    def __init__(self, out_shape, source_view, target_view, half_of, placed):
        self.out_shape, self.placed = out_shape, placed
        self.source_view, self.target_view, self.half_of = source_view, target_view, half_of

    def peers(self, grp, seq):
        for bits in (1, 2, 4):
            yield flip(grp, bits), seq

    def start(self, source, target, sems, grp, seq, begin=True):
        def part(device, bits, piece):
            view = self.target_view(target, PLACES[bits] if self.placed else flip(device, bits))
            return view if piece == "all" else self.half_of(view, piece == "b")

        def own(piece):
            view = self.source_view(source, grp)
            return view if piece == "all" else self.half_of(view, piece == "b")

        self.out, self.due = [None], [None]
        for via, here, there, piece in (
            (2, 0, 2, "a"),
            (2, 0, 2, "b"),
            (2, 4, 6, "b"),
            (4, 0, 4, "b"),
            (4, 0, 4, "a"),
            (4, 2, 6, "a"),
            (1, 0, 1, "all"),
            (1, 2, 3, "a"),
            (1, 2, 3, "b"),
            (1, 4, 5, "b"),
            (1, 4, 5, "a"),
            (1, 6, 7, "a"),
            (1, 6, 7, "b"),
        ):
            device = flip(grp, via)
            view = own(piece) if here == 0 else part(grp, here, piece)
            at = len(self.out)
            self.out.append(remote(view, part(device, there, piece), sems, at, (device, seq)))
            self.due.append(remote(view, part(grp, there, piece), sems, at, (device, seq)))
        self.kept = pltpu.make_async_copy(own("all"), part(grp, 0, "all"), sems[0].at[0])
        if begin:
            self.begin()

    def begin(self):
        self.kept.start()
        for at in (1, 4, 2, 5, 7):
            self.out[at].start()

    def pass_on(self, came):
        self.due[came].wait_recv()
        for at in {1: (6, 8), 4: (3, 10), 2: (9,), 5: (11,), 6: (12,), 3: (13,)}[came]:
            self.out[at].start()

    def forward(self):
        for pair in ((1, 4), (2, 5), (6, 3)):
            for came in pair:
                self.pass_on(came)
            yield

    def finish(self):
        for copy in self.due[7:]:
            copy.wait_recv()
        for copy in self.out[1:]:
            copy.wait_send()
        self.kept.wait()


def add_rows(total, first, second):
    step = 32

    def some(at, _):
        rows = pl.ds(pl.multiple_of(at * step, step), step)
        total[rows, :] = (
            first[rows, :].astype(jnp.float32) + second[rows, :].astype(jnp.float32)
        ).astype(total.dtype)
        return 0

    lax.fori_loop(0, total.shape[0] // step, some, 0)


class PlaneSum:
    axis = "grp"
    sem_count = 15

    def __init__(self, rows, columns, placed=True):
        self.rows, self.columns, self.placed = rows, columns, placed
        self.out_shape = (rows, columns)

    def scratch(self):
        low = jnp.bfloat16
        shape = (self.rows, self.columns)
        half = (self.rows // 2, self.columns)
        return [
            pltpu.VMEM((4, *shape), low),
            pltpu.VMEM((4, *shape), low),
            pltpu.VMEM((2, *half), low),
            pltpu.VMEM((2, *shape), low),
        ]

    def peers(self, grp, seq):
        for bits in (1, 2, 4):
            yield flip(grp, bits), seq

    def start(self, source, target, sems, grp, seq, scratch, begin=True):
        self.mine, self.core_in, self.halves, self.wholes = scratch
        core, side_x, side_y = [(flip(grp, bits), seq) for bits in (1, 2, 4)]
        half = self.rows // 2
        self.low, self.high = low, high = pl.ds(0, half), pl.ds(half, half)
        mine, halves, wholes = self.mine, self.halves, self.wholes

        def block(bits):
            return source.at[PLACES[bits] if self.placed else flip(grp, bits)]

        self.copies = [
            remote(block(bits), self.core_in.at[at], sems, at, core)
            for at, bits in enumerate((7, 3, 5, 1))
        ] + [
            remote(mine.at[0, low], halves.at[0], sems, 4, side_x),
            remote(mine.at[0, high], halves.at[1], sems, 5, side_y),
            remote(mine.at[1, low], wholes.at[0, low], sems, 6, side_x),
            remote(mine.at[2, high], wholes.at[1, high], sems, 7, side_y),
            remote(mine.at[1, high], wholes.at[0, high], sems, 8, side_x),
            remote(mine.at[2, low], wholes.at[1, low], sems, 9, side_y),
        ]
        self.loads = [
            pltpu.make_async_copy(block(bits), mine.at[at], sems[0].at[10 + at])
            for at, bits in enumerate((6, 2, 4, 0))
        ]
        if target is not None:
            self.store = pltpu.make_async_copy(mine.at[3], target, sems[0].at[14])
        if begin:
            self.begin()

    def begin(self):
        for copy in self.copies[:4] + self.loads:
            copy.start()

    def first_sums(self):
        for came, then in ((0, (4, 5)), (1, (6,)), (2, (7,)), (3, ())):
            self.copies[came].wait_recv()
            self.loads[came].wait()
            add_rows(self.mine.at[came], self.mine.at[came], self.core_in.at[came])
            for at in then:
                self.copies[at].start()

    def forward(self):
        mine, low, high = self.mine, self.low, self.high
        yield
        self.copies[5].wait_recv()
        add_rows(mine.at[1, high], mine.at[1, high], self.halves.at[1])
        self.copies[8].start()
        self.copies[4].wait_recv()
        add_rows(mine.at[2, low], mine.at[2, low], self.halves.at[0])
        self.copies[9].start()

    def total(self):
        mine = self.mine
        for at, side, rows in ((6, 0, self.low), (7, 1, self.high), (8, 0, self.high), (9, 1, self.low)):
            self.copies[at].wait_recv()
            add_rows(mine.at[3, rows], mine.at[3, rows], self.wholes.at[side, rows])
        return mine.at[3]

    def finish(self):
        self.total()
        self.store.start()
        for copy in self.copies:
            copy.wait_send()
        self.store.wait()


class LineGather:
    axis = "seq"

    def __init__(self, shape):
        self.count = lax.axis_size("seq")
        self.out_shape = (self.count, *shape)
        self.sem_count = 2 * self.count

    def peers(self, grp, seq):
        for step in range(1, self.count):
            yield grp, (seq + step) % self.count

    def start(self, source, target, sems, grp, seq):
        self.seq, self.sems = seq, sems
        self.own = pltpu.make_async_copy(source, target.at[seq], sems[0].at[0])
        self.own.start()

        def make(away, up):
            there = (seq + (1 if up else self.count - 1)) % self.count
            block = (seq + (self.count - away if up else away)) % self.count
            view = source if away == 0 else target.at[block]
            at = 1 + away if up else self.count + away
            return remote(view, target.at[block], sems, at, (grp, there))

        def came(away, up):
            block = (seq + (self.count - away if up else away)) % self.count
            at = away if up else self.count + away - 1
            side = (seq + (self.count - 1 if up else 1)) % self.count
            return remote(target.at[block], target.at[block], sems, at, (grp, side))

        self.make, self.came = make, came
        self.has = lambda away, up: (seq - away >= 0) if up else (seq + away < self.count)
        self.last = lambda up: (seq + 1 < self.count) if up else (seq >= 1)
        for up in (True, False):

            @pl.when(self.last(up))
            def _():
                make(0, up).start()

    def forward(self):
        for away in range(1, self.count):
            for up in (True, False):

                @pl.when(self.has(away, up))
                def _():
                    self.came(away, up).wait_recv()
                    if away < self.count - 1:

                        @pl.when(self.last(up))
                        def _():
                            self.make(away, up).start()

            yield

    def finish(self):
        for away in range(self.count - 1):
            for up in (True, False):

                @pl.when(self.has(away, up) & self.last(up))
                def _():
                    self.make(away, up).wait_send()
        self.own.wait()


def attend_back_sum_kernel(
    sum_task, gather_task, q_ref, k_ref, v_ref, grad_ref, total_ref, key_seg_ref, query_seg_ref,
    key_cosine_ref, key_sine_ref, cosine_ref, sine_ref, part_hbm, down_hbm, query_grad_ref,
    pair_grad_ref, sum_hbm, down_plane, key_sum, value_sum, mine, core_in, halves, wholes,
    sum_send, sum_recv, gather_send, gather_recv,
):
    step = pl.program_id(0)
    grp, seq = lax.axis_index("grp"), lax.axis_index("seq")
    scratch = (mine, core_in, halves, wholes)
    sum_task.start(part_hbm, sum_hbm, (sum_send, sum_recv), grp, seq, scratch, begin=False)
    gather_task.start(down_hbm, down_plane, (gather_send, gather_recv), grp, seq, begin=False)

    @pl.when(step == 0)
    def _():
        barrier = pltpu.get_barrier_semaphore()
        for device in sum_task.peers(grp, seq):
            pl.semaphore_signal(barrier, inc=1, device_id=device, device_id_type=MESH)
        pl.semaphore_wait(barrier, 3)
        sum_task.begin()
        gather_task.begin()

    @pl.when(step == 6)
    def _():
        sum_task.first_sums()

    attend_back_head(
        seq, q_ref, k_ref, v_ref, grad_ref, total_ref, key_seg_ref, query_seg_ref, key_cosine_ref,
        key_sine_ref, cosine_ref, sine_ref, query_grad_ref, pair_grad_ref, key_sum, value_sum,
    )

    @pl.when(step == pl.num_programs(0) - 1)
    def _():
        hand_on([gather_task, sum_task])
        gather_task.finish()
        sum_task.finish()


def attend_back_sum(
    number, projected, pairs, grads, totals, key_segs, query_segs, key_tables, tables, part, down
):
    rows = projected.shape[0]
    columns = NH * HD
    low = jnp.bfloat16
    sum_task = PlaneSum(*part.shape[1:])
    gather_task = gather_plane(down.shape)
    hbm = pl.BlockSpec(memory_space=pl.ANY)
    return pl.pallas_call(
        functools.partial(attend_back_sum_kernel, sum_task, gather_task),
        grid=(NH,),
        in_specs=attention_specs(
            ["head", "keys", "values", "head", "total", "key_seg", "query_seg"]
            + ["key_table", "key_table", "table", "table"],
            rows,
        )
        + [hbm, hbm],
        out_specs=attention_specs(["head", "pair"], rows) + [hbm, hbm],
        out_shape=[
            jax.ShapeDtypeStruct((rows, columns), low),
            jax.ShapeDtypeStruct((SEQLEN, 2 * HD), low),
            jax.ShapeDtypeStruct(sum_task.out_shape, low),
            jax.ShapeDtypeStruct(gather_task.out_shape, low),
        ],
        scratch_shapes=[pltpu.VMEM((SEQLEN, HD), jnp.float32)] * 2
        + sum_task.scratch()
        + [pltpu.SemaphoreType.DMA((sum_task.sem_count,))] * 2
        + [pltpu.SemaphoreType.DMA((gather_task.sem_count,))] * 2,
        compiler_params=pltpu.CompilerParams(
            collective_id=number, has_side_effects=True, vmem_limit_bytes=48 * 2**20
        ),
        cost_estimate=SMALL_COST,
        name="attend_back_sum",
    )(
        projected, pairs, pairs, grads, totals, key_segs[:, None], query_segs[None, :],
        *key_tables, *tables, part, down,
    )


def block_kernel(
    first, second, pair_task, key_seg_ref, query_seg_ref, normed_ref, tokens_ref, gain_ref,
    cosine_ref, sine_ref, cot_hbm, normed_hbm, w_ref, projected_ref, pairs_ref, context_ref,
    total_ref, hidden_ref, second_ref, inverse_ref, cot_plane, normed_plane, own_pair, pairs,
    first_send, first_recv, second_send, second_recv, pair_send, pair_recv,
):
    step = pl.program_id(0)
    grp, seq = lax.axis_index("grp"), lax.axis_index("seq")
    first.start(cot_hbm, cot_plane, (first_send, first_recv), grp, seq, begin=False)
    second.start(normed_hbm, normed_plane, (second_send, second_recv), grp, seq, begin=False)
    pair_task.start(own_pair, pairs, (pair_send, pair_recv), grp, seq, begin=False)
    low = jnp.bfloat16
    rows = normed_ref.shape[0]
    wide = 2 * HD
    couples = NH // 2
    attend_at = 1 + couples
    out_at = attend_at + NH
    end = out_at + MODEL_WIDTH // wide

    @pl.when(step == 0)
    def _():
        barrier = pltpu.get_barrier_semaphore()
        devices = list(first.peers(grp, seq)) + list(pair_task.peers(grp, seq))
        for device in devices:
            pl.semaphore_signal(barrier, inc=1, device_id=device, device_id_type=MESH)
        pl.semaphore_wait(barrier, len(devices))
        first.begin()
        second.begin()

    @pl.when(step < attend_at)
    def _():
        made = jnp.dot(normed_ref[...], w_ref[...], preferred_element_type=jnp.float32)
        cosine, sine = cosine_ref[...], sine_ref[...]
        left = turn(made[:, :HD], cosine, sine).astype(low)
        right = made[:, HD:]

        @pl.when(step == 0)
        def _():
            own_pair[:, :HD] = left
            own_pair[:, HD:] = right.astype(low)
            pair_task.begin()
            projected_ref[:, NH * HD :] = own_pair[...]

        @pl.when(step > 0)
        def _():
            place = pl.multiple_of((step - 1) * wide, wide)
            projected_ref[:, pl.ds(place, HD)] = left
            projected_ref[:, pl.ds(pl.multiple_of(place + HD, HD), HD)] = turn(
                right, cosine, sine
            ).astype(low)

    @pl.when(step == attend_at)
    def _():
        pair_task.finish()
        for at in range(pairs.shape[0]):
            pairs_ref[at * rows : (at + 1) * rows, :] = pairs[at]

    @pl.when(step == attend_at + 2)
    def _():
        first.pass_on(1)
        first.pass_on(4)

    @pl.when(step == out_at)
    def _():
        first.pass_on(2)
        first.pass_on(5)

    @pl.when((step >= attend_at) & (step < out_at))
    def _():
        head = step - attend_at
        place = pl.ds(pl.multiple_of(head * HD, HD), HD)
        scale = HD ** (-0.5)
        for block in range(SEQLEN // rows):

            @pl.when(seq == block)
            def _():
                keys = (block + 1) * rows
                scores = dot_last(pairs_ref[:keys, :HD], projected_ref[:, place]) * scale
                scores = jnp.where(
                    score_mask(key_seg_ref, query_seg_ref, block, rows), scores, MASKED
                )
                highest = jnp.max(scores, axis=0, keepdims=True)
                exponent = jnp.exp(scores - highest)
                totals = jnp.sum(exponent, axis=0, keepdims=True)
                probs_low = (exponent * (1.0 / totals)).astype(low)
                context = dot_first(probs_low, pairs_ref[:keys, HD:])
                context_ref[:, place] = context.astype(low)
                total_ref[head] = highest + jnp.log(totals)

    @pl.when(step >= out_at)
    def _():
        place = pl.ds(pl.multiple_of((step - out_at) * wide, wide), wide)
        branch = jnp.dot(context_ref[...], w_ref[...], preferred_element_type=jnp.float32)
        hidden_ref[:, place] = tokens_ref[:, place].astype(jnp.float32) + branch

    @pl.when(step == end - 1)
    def _():
        chunk = 32
        gain = gain_ref[1:2, :]

        def some(at, _):
            part = pl.ds(pl.multiple_of(at * chunk, chunk), chunk)
            hidden = hidden_ref[part, :]
            inverse = lax.rsqrt(jnp.mean(hidden * hidden, axis=-1, keepdims=True) + NORM_EPS)
            inverse_ref[part, :] = inverse
            second_ref[part, :] = (hidden * inverse * gain).astype(low)
            return 0

        lax.fori_loop(0, rows // chunk, some, 0)
        first.pass_on(6)
        first.pass_on(3)
        for came in (1, 4, 2, 5, 6, 3):
            second.pass_on(came)
        first.finish()
        second.finish()


def attention_block(number, normed, tokens, gains, tables, key_segs, query_segs, cotangent, weights):
    rows, width = normed.shape
    low, wide = jnp.bfloat16, 2 * HD
    couples = NH // 2
    count = SEQLEN // rows
    first = gather_plane(cotangent.shape, placed=True)
    second = gather_plane(normed.shape, placed=True)
    pair_task = Exchange("seq", (count, rows, wide), whole, block_of)

    def weight_block(step):
        turned = step - NH
        return (0, jnp.where(step == 0, couples, jnp.where(step <= couples, step - 1, jnp.maximum(turned, couples + 1))))

    def full(shape):
        return pl.BlockSpec(shape, lambda step: (0,) * len(shape))

    hbm = pl.BlockSpec(memory_space=pl.ANY)
    steps = 1 + couples + NH + width // wide
    plane = jax.ShapeDtypeStruct((8, rows, width), low)
    shapes = [
        jax.ShapeDtypeStruct((rows, NH * HD + wide), low),
        jax.ShapeDtypeStruct((SEQLEN, wide), low),
        jax.ShapeDtypeStruct((rows, NH * HD), low),
        jax.ShapeDtypeStruct((NH, 1, rows), jnp.float32),
        jax.ShapeDtypeStruct((rows, width), jnp.float32),
        jax.ShapeDtypeStruct((rows, width), low),
        jax.ShapeDtypeStruct((rows, 1), jnp.float32),
    ]
    return pl.pallas_call(
        functools.partial(block_kernel, first, second, pair_task),
        grid=(steps,),
        in_specs=[
            full((SEQLEN, 1)),
            full((1, rows)),
            full((rows, width)),
            full((rows, width)),
            full((2, width)),
            full((rows, HD)),
            full((rows, HD)),
            hbm,
            hbm,
            pl.BlockSpec((width, wide), weight_block),
        ],
        out_specs=[full(shape.shape) for shape in shapes] + [hbm, hbm],
        out_shape=shapes + [plane, plane],
        scratch_shapes=[pltpu.VMEM((rows, wide), low), pltpu.VMEM((count, rows, wide), low)]
        + [pltpu.SemaphoreType.DMA((14,))] * 4
        + [pltpu.SemaphoreType.DMA((pair_task.sem_count,))] * 2,
        compiler_params=pltpu.CompilerParams(
            collective_id=number, has_side_effects=True, vmem_limit_bytes=56 * 2**20
        ),
        cost_estimate=SMALL_COST,
        name="attention_block",
    )(
        key_segs[:, None], query_segs[None, :], normed, tokens, gains, *tables, cotangent, normed,
        weights,
    )


def add_blocks(total, blocks):
    step = min(32, total.shape[0])

    def some(at, _):
        rows = pl.ds(pl.multiple_of(at * step, step), step)
        made = blocks[0, rows, :].astype(jnp.float32)
        for block in range(1, blocks.shape[0]):
            made = made + blocks[block, rows, :].astype(jnp.float32)
        total[rows, :] = made.astype(total.dtype)
        return 0

    lax.fori_loop(0, total.shape[0] // step, some, 0)


def tail_kernel(
    tasks, shares_hbm, pair_hbm, gain_ref, gating_hbm, gating_plane, share_plane, pair_plane,
    gain_plane, share_parts, share_sum, mine, core_in, halves, wholes, pair_parts, pair_sum,
    gain_parts, gain_sum, *sems,
):
    gating, pair, gain_seq, gain_grp, pair_seq, pair_gather, *halves_of = tasks
    shares, share_gathers = halves_of[:2], halves_of[2:]
    grp, seq = lax.axis_index("grp"), lax.axis_index("seq")
    barrier = pltpu.get_barrier_semaphore()
    devices = list(gain_grp.peers(grp, seq)) + list(gain_seq.peers(grp, seq))
    for device in devices:
        pl.semaphore_signal(barrier, inc=1, device_id=device, device_id_type=MESH)
    pl.semaphore_wait(barrier, len(devices))
    sems = [(sems[2 * at], sems[2 * at + 1]) for at in range(len(tasks))]

    def share_part(at):
        shares[at].finish()
        add_blocks(share_sum.at[at], share_parts.at[at])
        share_gathers[at].start(share_sum.at[at], share_plane, sems[8 + at], grp, seq)

    for at in range(2):
        shares[at].start(shares_hbm, share_parts.at[at], sems[6 + at], grp, seq)
    pair.start(pair_hbm, None, sems[1], grp, seq, (mine, core_in, halves, wholes))
    gain_seq.start(gain_ref, gain_parts, sems[2], grp, seq)
    gating.start(gating_hbm, gating_plane, sems[0], grp, seq, begin=False)
    gating.kept.start()
    for at in (1, 4, 7):
        gating.out[at].start()
    pair.first_sums()
    for at in (2, 5):
        gating.out[at].start()
    gain_seq.finish()
    gain_sum[...] = jnp.sum(gain_parts[...], axis=0)
    gain_grp.start(gain_sum, gain_plane, sems[3], grp, seq)
    handing = gating.forward()
    next(handing)
    for _ in pair.forward():
        pass
    share_part(0)
    next(handing)
    pair_seq.start(pair.total(), pair_parts, sems[4], grp, seq)
    share_part(1)
    next(handing)
    pair_seq.finish()
    add_blocks(pair_sum, pair_parts)
    pair_gather.start(pair_sum, pair_plane, sems[5], grp, seq)
    hand_on([share_gathers[0], share_gathers[1], pair_gather])
    for copy in pair.copies:
        copy.wait_send()
    for task in (gain_grp, gating, pair_gather, *share_gathers):
        task.finish()


def tail_exchange(number, shares, pair, gain_terms, gating):
    seq_count = lax.axis_size("seq")
    low = jnp.bfloat16
    columns, rows_all = shares.shape
    rows = rows_all // seq_count
    _, pair_rows, pair_columns = pair.shape
    sub = pair_rows // seq_count
    half = columns // 2

    def share_task(at):
        return Exchange(
            "seq",
            (seq_count, half, rows),
            lambda ref, index: ref.at[
                pl.ds(at * half, half), pl.ds(pl.multiple_of(index * rows, rows), rows)
            ],
            block_of,
        )

    def share_gather(at):
        return gather_plane(
            (half, rows),
            target_view=lambda ref, index: ref.at[index, pl.ds(at * half, half)],
            out_shape=(8, columns, rows),
        )

    tasks = [
        gather_plane(gating.shape),
        PlaneSum(pair_rows, pair_columns, placed=False),
        gather_axis("seq", gain_terms)[0],
        gather_axis("grp", gain_terms)[0],
        Exchange(
            "seq",
            (seq_count, sub, pair_columns),
            lambda ref, index: rows_of(ref, index, sub),
            block_of,
        ),
        gather_plane((sub, pair_columns)),
        share_task(0),
        share_task(1),
        share_gather(0),
        share_gather(1),
    ]
    hbm = pl.BlockSpec(memory_space=pl.ANY)
    vmem = pl.BlockSpec(memory_space=pltpu.VMEM)
    scratch = [
        pltpu.VMEM((2, seq_count, half, rows), low),
        pltpu.VMEM((2, half, rows), low),
        *tasks[1].scratch(),
        pltpu.VMEM((seq_count, sub, pair_columns), low),
        pltpu.VMEM((sub, pair_columns), low),
        pltpu.VMEM((seq_count, *gain_terms.shape), jnp.float32),
        pltpu.VMEM(gain_terms.shape, jnp.float32),
    ]
    for task in tasks:
        scratch += [pltpu.SemaphoreType.DMA((task.sem_count,))] * 2
    return pl.pallas_call(
        functools.partial(tail_kernel, tasks),
        in_specs=[hbm, hbm, vmem, hbm],
        out_specs=[hbm] * 4,
        out_shape=[
            jax.ShapeDtypeStruct(tasks[0].out_shape, low),
            jax.ShapeDtypeStruct((8, columns, rows), low),
            jax.ShapeDtypeStruct((8, sub, pair_columns), low),
            jax.ShapeDtypeStruct((8, *gain_terms.shape), jnp.float32),
        ],
        scratch_shapes=scratch,
        compiler_params=pltpu.CompilerParams(
            collective_id=number, has_side_effects=True, vmem_limit_bytes=60 * 2**20
        ),
        cost_estimate=SMALL_COST,
        name="tail_exchange",
    )(shares, pair, gain_terms, gating)


def half_rows(axis, height):
    def half_of(view, second):
        index = (slice(None),) * axis + (pl.ds(height if second else 0, height),)
        return view.at[index]

    return half_of


def whole(ref, index):
    return ref


def block_of(ref, index):
    return ref.at[index]


def gather_plane(
    shape, split=0, source_view=whole, target_view=block_of, out_shape=None, placed=False
):
    out_shape = out_shape or (lax.axis_size("grp"), *shape)
    if lax.axis_size("grp") == 8:
        halves = half_rows(split, shape[split] // 2)
        return PlaneGather(out_shape, source_view, target_view, halves, placed)
    return Exchange("grp", out_shape, source_view, target_view)


def hand_on(tasks):
    going = [task.forward() for task in tasks]
    while going:
        going = [steps for steps in going if next(steps, going) is not going]


def exchange_kernel(tasks, wires, arrays, outputs, *refs):
    sources, targets = refs[:arrays], refs[arrays : arrays + outputs]
    refs = list(refs[arrays + outputs :])
    sems, scratch = [], []
    for task in tasks:
        sems.append((refs.pop(0), refs.pop(0)))
        held = len(task.scratch()) if isinstance(task, PlaneSum) else 0
        scratch.append([refs.pop(0) for _ in range(held)])
    grp, seq = lax.axis_index("grp"), lax.axis_index("seq")
    barrier = pltpu.get_barrier_semaphore()
    axes = {"grp": [], "seq": []}
    for task in tasks:
        devices = list(task.peers(grp, seq))
        if len(devices) > len(axes[task.axis]):
            axes[task.axis] = devices
    devices = axes["grp"] + axes["seq"]
    for device in devices:
        pl.semaphore_signal(barrier, inc=1, device_id=device, device_id_type=MESH)
    pl.semaphore_wait(barrier, len(devices))

    def start(at):
        after, source, target = wires[at]
        source = targets[source] if after is not None else sources[source]
        more = (scratch[at],) if scratch[at] else ()
        tasks[at].start(source, targets[target], sems[at], grp, seq, *more)

    open_tasks = list(range(len(tasks)))
    first = [at for at in open_tasks if wires[at][0] is None]
    for at in first:
        start(at)
    for at in first:
        if isinstance(tasks[at], PlaneSum):
            tasks[at].first_sums()
    hand_on([tasks[at] for at in first])
    for at in open_tasks[:]:
        after = wires[at][0]
        if after is not None:
            tasks[after].finish()
            open_tasks.remove(after)
            start(at)
            hand_on([tasks[at]])
    for at in open_tasks:
        tasks[at].finish()


def exchange(number, work):
    tasks = [piece[0] for piece in work]
    arrays, shapes, wires = [], [], []
    for piece in work:
        if isinstance(piece[1], int):
            after, source = piece[1], wires[piece[1]][2]
            kind = shapes[source].dtype
        else:
            after, source = None, len(arrays)
            arrays.append(piece[1])
            kind = piece[1].dtype
        if len(piece) == 3:
            target = wires[piece[2]][2]
        else:
            target = len(shapes)
            shapes.append(jax.ShapeDtypeStruct(piece[0].out_shape, kind))
        wires.append((after, source, target))
    scratch = []
    for task in tasks:
        scratch += [pltpu.SemaphoreType.DMA((task.sem_count,))] * 2
        if isinstance(task, PlaneSum):
            scratch += task.scratch()
    return pl.pallas_call(
        functools.partial(exchange_kernel, tasks, wires, len(arrays), len(shapes)),
        in_specs=[pl.BlockSpec(memory_space=pl.ANY)] * len(arrays),
        out_specs=[pl.BlockSpec(memory_space=pl.ANY)] * len(shapes),
        out_shape=shapes,
        scratch_shapes=scratch,
        compiler_params=pltpu.CompilerParams(collective_id=number, has_side_effects=True),
        cost_estimate=SMALL_COST,
        name="exchange",
    )(*arrays)


def gather_axis(axis, array):
    task = Exchange(axis, (lax.axis_size(axis), *array.shape), whole, block_of)
    return task, array


def split_rows(axis, array):
    count = lax.axis_size(axis)
    rows, columns = array.shape
    height = rows // count
    task = Exchange(
        axis,
        (count, height, columns),
        lambda ref, index: rows_of(ref, index, height),
        block_of,
    )
    return task, array


def split_columns(axis, array, placed=False):
    count = lax.axis_size(axis)
    rows, columns = array.shape
    width = columns // count
    if placed and count == 8:
        task = PlacedExchange(
            (count, rows, width), lambda ref, index: columns_of(ref, index, width)
        )
        return task, array
    task = Exchange(
        axis,
        (count, rows, width),
        lambda ref, index: columns_of(ref, index, width),
        block_of,
    )
    return task, array


def plane_sum_kernel(
    part_ref, gate_ref, up_ref, x_ref, total_ref, grads_out, core_in, chip, half_x, half_y,
    whole_x, whole_y, x_block, stage, send_sems, recv_sems, x_sems, out_sems,
):
    grp, seq = lax.axis_index("grp"), lax.axis_index("seq")
    core, side_x, side_y = [flip(grp, bits) for bits in (1, 2, 4)]
    blocks = [PLACES[bits] for bits in (6, 2, 4, 0)]
    core_blocks = [PLACES[bits] for bits in (7, 3, 5, 1)]
    half = total_ref.shape[0] // 2
    low, high = pl.ds(0, half), pl.ds(half, half)
    cols = gate_ref.shape[0]
    rows = x_block.shape[2]
    count = x_ref.shape[1] // rows

    def x_copy(at):
        view = x_ref.at[:, pl.ds(pl.multiple_of(at * rows, rows), rows)]
        return pltpu.make_async_copy(view, x_block.at[at % 2], x_sems.at[at % 2])

    def out_copies(at):
        return [
            pltpu.make_async_copy(
                stage.at[which, at % 2],
                grads_out.at[pl.ds(pl.multiple_of((2 * at + which) * cols, cols), cols)],
                out_sems.at[which, at % 2],
            )
            for which in range(2)
        ]

    x_copy(0).start()
    barrier = pltpu.get_barrier_semaphore()
    for device in (core, side_x, side_y):
        pl.semaphore_signal(barrier, inc=1, device_id=(device, seq), device_id_type=MESH)
    pl.semaphore_wait(barrier, 3)

    sems = (send_sems, recv_sems)
    copies = [
        remote(part_ref.at[block], core_in.at[at], sems, at, (core, seq))
        for at, block in enumerate(core_blocks)
    ]
    copies += [
        remote(chip.at[0, low], half_x, sems, 4, (side_x, seq)),
        remote(chip.at[0, high], half_y, sems, 5, (side_y, seq)),
        remote(chip.at[1, low], whole_x.at[low], sems, 6, (side_x, seq)),
        remote(chip.at[2, high], whole_y.at[high], sems, 7, (side_y, seq)),
        remote(chip.at[1, high], whole_x.at[high], sems, 8, (side_x, seq)),
        remote(chip.at[2, low], whole_y.at[low], sems, 9, (side_y, seq)),
    ]
    for copy in copies[:4]:
        copy.start()

    def step(at, _):
        @pl.when(at == 1)
        def _():
            for came, then in ((0, (4, 5)), (1, (6,)), (2, (7,))):
                copies[came].wait_recv()
                add_rows(chip.at[came], part_ref.at[blocks[came]], core_in.at[came])
                for start in then:
                    copies[start].start()

        @pl.when(at == count - 1)
        def _():
            copies[5].wait_recv()
            add_rows(chip.at[1, high], chip.at[1, high], half_y)
            copies[8].start()
            copies[4].wait_recv()
            add_rows(chip.at[2, low], chip.at[2, low], half_x)
            copies[9].start()

        x_copy(at).wait()

        @pl.when(at + 1 < count)
        def _():
            x_copy(at + 1).start()

        @pl.when(at >= 2)
        def _():
            for copy in out_copies(at - 2):
                copy.wait()

        for which, ref in enumerate((gate_ref, up_ref)):
            stage[which, at % 2] = jnp.dot(
                ref[...], x_block[at % 2], preferred_element_type=jnp.float32
            ).astype(stage.dtype)
        for copy in out_copies(at):
            copy.start()
        return 0

    lax.fori_loop(0, count, step, 0)
    copies[3].wait_recv()
    add_rows(total_ref, part_ref.at[blocks[3]], core_in.at[3])
    for at, came, rows_at in (
        (6, whole_x, low),
        (7, whole_y, high),
        (8, whole_x, high),
        (9, whole_y, low),
    ):
        copies[at].wait_recv()
        add_rows(total_ref.at[rows_at], total_ref.at[rows_at], came.at[rows_at])
    for copy in copies:
        copy.wait_send()
    for at in (count - 2, count - 1):
        for copy in out_copies(at):
            copy.wait()


def plane_sum(number, part, gate_grad, up_grad, x, seq_count):
    count = lax.axis_size("grp")
    rows_all, columns = part.shape
    rows = rows_all // count
    if count != 8:
        total = lax.psum_scatter(part, "grp", scatter_dimension=0, tiled=True)
        both = jnp.concatenate([gate_grad, up_grad], axis=0)
        return total.astype(jnp.float32), weight_grad(both, x, seq_count)
    low = jnp.bfloat16
    cols, tokens_all = gate_grad.shape
    width = x.shape[1] // seq_count
    vmem = pl.BlockSpec(memory_space=pltpu.VMEM)
    hbm = pl.BlockSpec(memory_space=pl.ANY)
    grads = jax.ShapeDtypeStruct((2 * seq_count * cols, width), low)
    return pl.pallas_call(
        plane_sum_kernel,
        in_specs=[vmem, vmem, vmem, hbm],
        out_specs=[vmem, hbm],
        out_shape=[jax.ShapeDtypeStruct((rows, columns), jnp.float32), grads],
        scratch_shapes=[
            pltpu.VMEM((4, rows, columns), low),
            pltpu.VMEM((3, rows, columns), low),
            pltpu.VMEM((rows // 2, columns), low),
            pltpu.VMEM((rows // 2, columns), low),
            pltpu.VMEM((rows, columns), low),
            pltpu.VMEM((rows, columns), low),
            pltpu.VMEM((2, tokens_all, width), low),
            pltpu.VMEM((2, 2, cols, width), low),
            pltpu.SemaphoreType.DMA((10,)),
            pltpu.SemaphoreType.DMA((10,)),
            pltpu.SemaphoreType.DMA((2,)),
            pltpu.SemaphoreType.DMA((2, 2)),
        ],
        compiler_params=pltpu.CompilerParams(
            collective_id=number, has_side_effects=True, vmem_limit_bytes=56 * 2**20
        ),
        cost_estimate=SMALL_COST,
        name="plane_sum",
    )(part.reshape(count, rows, columns), gate_grad, up_grad, x)


def local(
    tokens,
    cotangent,
    segment_ids,
    tile_owner_slots,
    weights_low,
    master,
    moment_one,
    moment_two,
    left_basis_set,
    right_basis_set,
    gains,
    gain_moment_one,
    gain_moment_two,
):
    grp_count = lax.axis_size("grp")
    seq_count = lax.axis_size("seq")
    grp_here, seq_here = lax.axis_index("grp"), lax.axis_index("seq")
    rows_here = tokens.shape[0]
    slots_here, rows_block, tile_width = weights_low.shape
    tile_count = tile_owner_slots.shape[0]
    query_cols = NH * HD
    value_end = query_cols + 2 * HD
    output_end = value_end + MODEL_WIDTH
    attn_tiles = output_end // tile_width
    query_tiles = query_cols // tile_width
    hidden_tiles = FF // tile_width
    share = -(-hidden_tiles // grp_count)
    share_cols = share * tile_width
    share_width = MODEL_WIDTH // grp_count
    sub_rows = rows_block // grp_count
    halves = 2 if sub_rows >= 32 else 1
    half_block, half_sub = rows_block // halves, sub_rows // halves
    first_place = (seq_here * rows_here) % SEQLEN
    key_tables = turn_tables(jnp.arange(SEQLEN, dtype=jnp.int32))
    tables = [lax.dynamic_slice_in_dim(table, first_place, rows_here) for table in key_tables]

    hidden_ids = grp_here * share + jnp.arange(share, dtype=jnp.int32)
    hidden_ids = jnp.minimum(hidden_ids, hidden_tiles - 1)
    feed_ids = (
        attn_tiles
        + jnp.arange(3, dtype=jnp.int32)[:, None] * hidden_tiles
        + hidden_ids[None, :]
    ).reshape(-1)
    feed_slots, attn_slots = tile_owner_slots[feed_ids], tile_owner_slots[:attn_tiles]

    tok_float = tokens.astype(jnp.float32)
    inverse_one = lax.rsqrt(jnp.mean(tok_float * tok_float, axis=-1, keepdims=True) + NORM_EPS)
    normed = (tok_float * inverse_one * gains[0]).astype(jnp.bfloat16)

    def weight_half(at):
        return gather_plane(
            (slots_here, half_block, tile_width),
            split=1,
            source_view=lambda ref, index: ref.at[:, pl.ds(at * half_block, half_block)],
        )

    def attn_half(at):
        return gather_plane(
            (seq_count, half_sub, output_end),
            target_view=lambda ref, index: ref.at[:, at, index],
            out_shape=(seq_count, halves, grp_count, half_sub, output_end),
        )

    flat = (grp_count * slots_here, half_block, tile_width)
    tiles, segments = exchange(
        0,
        [(weight_half(0), weights_low), gather_axis("seq", segment_ids.reshape(-1, tile_width))],
    )
    feed_rows, attn_rows = pick(tiles.reshape(flat), feed_slots, attn_slots)
    feed_parts = [lax.all_gather(feed_rows, "seq", axis=0, tiled=False)]
    if halves == 2:
        tiles, attn_first = exchange(
            1, [(weight_half(1), weights_low), gather_axis("seq", attn_rows)]
        )
        feed_rows, attn_rows = pick(tiles.reshape(flat), feed_slots, attn_slots)
        feed_parts.append(lax.all_gather(feed_rows, "seq", axis=0, tiled=False))
        attn_weights, _ = exchange(
            2,
            [(attn_half(0), attn_first), gather_axis("seq", attn_rows), (attn_half(1), 1, 0)],
        )
    else:
        _, attn_weights = exchange(2, [gather_axis("seq", attn_rows), (attn_half(0), 0)])
    attn_weights = attn_weights.reshape(MODEL_WIDTH, output_end)

    first_key = seq_here * rows_here - first_place
    key_segs = lax.dynamic_slice_in_dim(segments.reshape(-1), first_key, SEQLEN)
    at = (first_place // rows_here).reshape(1)
    if grp_count == 8 and seq_count * rows_here == SEQLEN:
        (
            projected, pairs, context, log_totals, hidden, normed_two, inverse_two, cot_plane,
            normed_plane,
        ) = attention_block(
            3, normed, tokens, gains, tables, key_segs, segment_ids, cotangent, attn_weights
        )
    else:
        projected = project(normed, attn_weights, tables)
        pairs, cot_plane, normed_plane = exchange(
            3,
            [
                gather_axis("seq", projected[:, query_cols:]),
                (gather_plane(cotangent.shape, placed=True), cotangent),
                (gather_plane(normed.shape, placed=True), normed),
            ],
        )
        pairs = lax.dynamic_slice_in_dim(pairs.reshape(-1, 2 * HD), first_key, SEQLEN)
        context, log_totals = attend(at, projected, pairs, key_segs, segment_ids)
        branch = jnp.dot(
            context, attn_weights[:, value_end:], preferred_element_type=jnp.float32
        )
        hidden = tok_float + branch
        inverse_two = lax.rsqrt(jnp.mean(hidden * hidden, axis=-1, keepdims=True) + NORM_EPS)
        normed_two = (hidden * inverse_two * gains[1]).astype(jnp.bfloat16)

    cot_plane = cot_plane.reshape(-1, MODEL_WIDTH)
    normed_plane = normed_plane.reshape(-1, MODEL_WIDTH)
    real_cols = jnp.clip((hidden_tiles - grp_here * share) * tile_width, 0, share_cols).reshape(1)
    if halves == 2:
        some = jnp.sum(feed_parts[0][0, :8, :tile_width].astype(jnp.float32)) * 0.0
        real_cols = real_cols + some.astype(jnp.int32)
    if grp_count == 8:
        gate_grad, up_grad, two_part, feed_part, second_plane, context_plane, down_grad = (
            feed_gather(
                4, real_cols, normed_two, context, cot_plane, feed_parts, seq_count
            )
        )
        second_plane = second_plane.reshape(-1, MODEL_WIDTH)
    else:
        second_plane, context_plane = exchange(
            4,
            [
                (gather_plane(normed_two.shape), normed_two),
                (gather_plane(context.shape), context),
            ],
        )
        second_plane = second_plane.reshape(-1, MODEL_WIDTH)
        activated, gate_grad, up_grad, two_part, feed_part = feed_forward(
            real_cols, second_plane, cot_plane, feed_parts, seq_count
        )
        down_grad = weight_grad(activated, cot_plane, seq_count)
    context_plane = context_plane.reshape(-1, MODEL_WIDTH)
    down_grad, two_part = lax.optimization_barrier((down_grad, two_part))
    down_grad = lax.psum_scatter(down_grad, "seq", scatter_dimension=0, tiled=True)
    norm_two_grad, gating_grads = plane_sum(
        5, two_part, gate_grad, up_grad, second_plane, seq_count
    )
    gating_grads = lax.psum_scatter(gating_grads, "seq", scatter_dimension=0, tiled=True)

    out_grad = cotangent.astype(jnp.float32)
    gain_two_term = jnp.sum(norm_two_grad * hidden * inverse_two, axis=0)
    hidden_grad = (
        out_grad
        + inverse_two * gains[1] * norm_two_grad
        - hidden
        * inverse_two**3
        * jnp.mean(hidden * gains[1] * norm_two_grad, axis=-1, keepdims=True)
    )
    branch_grad = hidden_grad.astype(jnp.bfloat16)
    context_grad = times_transpose(branch_grad, attn_weights[:, value_end:]).astype(jnp.bfloat16)
    fused = grp_count == 8 and seq_count * rows_here == SEQLEN
    if fused:
        feed_part = feed_part.reshape(grp_count, rows_here, MODEL_WIDTH)
        query_grad, pair_part, feed_out, down_plane = attend_back_sum(
            6, projected, pairs, context_grad, log_totals, key_segs, segment_ids, key_tables,
            tables, feed_part, down_grad,
        )
    else:
        query_grad, pair_part = attend_back(
            at, projected, pairs, context_grad, log_totals, key_segs, segment_ids, key_tables, tables
        )
        feed_out = lax.psum_scatter(
            feed_part.reshape(-1, MODEL_WIDTH), "grp", scatter_dimension=0, tiled=True
        )
        (down_plane,) = exchange(10, [(gather_plane(down_grad.shape), down_grad)])
    block_out = (hidden + feed_out.astype(jnp.float32)).astype(jnp.bfloat16)
    if seq_count * rows_here > SEQLEN:
        pair_part = lax.dynamic_update_slice_in_dim(
            jnp.zeros((seq_count * rows_here, 2 * HD), pair_part.dtype), pair_part, first_key, 0
        )
    pair_parts, query_share, branch_share = exchange(
        7,
        [
            split_rows("seq", pair_part),
            split_columns("grp", query_grad, placed=True),
            split_columns("grp", branch_grad, placed=True),
        ],
    )
    pair_grad = jnp.sum(pair_parts.astype(jnp.float32), axis=0).astype(jnp.bfloat16)
    projected_grad = jnp.concatenate([query_grad, pair_grad], axis=1)
    norm_one_grad = times_transpose(projected_grad, attn_weights[:, :value_end])
    gain_one_term = jnp.sum(norm_one_grad * tok_float * inverse_one, axis=0)
    input_grad = (
        hidden_grad
        + inverse_one * gains[0] * norm_one_grad
        - tok_float
        * inverse_one**3
        * jnp.mean(tok_float * gains[0] * norm_one_grad, axis=-1, keepdims=True)
    )
    shares = share_grad(
        query_share.reshape(-1, share_width),
        branch_share.reshape(-1, share_width),
        normed_plane,
        context_plane,
    )
    pair_weight_grad = contract(normed, pair_grad).astype(jnp.bfloat16)
    gain_terms = jnp.stack([gain_one_term, gain_two_term])
    pair_blocks = pair_weight_grad.reshape(seq_count, grp_count, sub_rows, 2 * HD)
    if grp_count == 8:
        pair_blocks = jnp.transpose(pair_blocks, (1, 0, 2, 3))
        gating_plane, share_plane, pair_plane, gain_parts = tail_exchange(
            8,
            shares,
            pair_blocks.reshape(grp_count, seq_count * sub_rows, 2 * HD),
            gain_terms,
            gating_grads,
        )
    else:
        pair_task = Exchange(
            "grp",
            (grp_count, seq_count, sub_rows, 2 * HD),
            lambda ref, index: ref.at[:, index],
            block_of,
        )
        work = [
            split_columns("seq", shares),
            (pair_task, pair_blocks),
            gather_axis("seq", gain_terms),
            (gather_plane(gating_grads.shape), gating_grads),
        ]
        share_parts, pair_parts, gain_parts, gating_plane = exchange(8, work)
        gain_seq = jnp.sum(gain_parts, axis=0)
        shares = jnp.sum(share_parts.astype(jnp.float32), axis=0).astype(jnp.bfloat16)
        pair_parts = jnp.sum(pair_parts.astype(jnp.float32), axis=0).astype(jnp.bfloat16)
        pair_task = Exchange("seq", pair_parts.shape, block_of, block_of)
        _, pair_plane, share_plane, gain_parts = exchange(
            9,
            [
                (pair_task, pair_parts),
                (gather_plane(pair_parts.shape), 0),
                (gather_plane(shares.shape), shares),
                gather_axis("grp", gain_seq),
            ],
        )
        pair_plane = jnp.sum(pair_plane.astype(jnp.float32), axis=1).astype(jnp.bfloat16)

    gain_grads = jnp.sum(gain_parts, axis=0)

    tile_of_slot = (
        jnp.full((grp_count * slots_here,), tile_count, jnp.int32)
        .at[tile_owner_slots]
        .set(jnp.arange(tile_count, dtype=jnp.int32))
    )
    tiles_here = lax.dynamic_slice_in_dim(tile_of_slot, grp_here * slots_here, slots_here)
    feed_at = jnp.clip(tiles_here - attn_tiles, 0, 3 * hidden_tiles - 1)
    which, column = feed_at // hidden_tiles, feed_at % hidden_tiles
    is_query = tiles_here < query_tiles
    is_pair = (tiles_here >= query_tiles) & (tiles_here < query_tiles + 2)
    is_feed = tiles_here >= attn_tiles
    kind = jnp.where(is_feed, jnp.where(which < 2, 0, 1), jnp.where(is_pair, 3, 2))
    kind = jnp.where(tiles_here == tile_count, 4, kind)
    out_at = jnp.clip(tiles_here - query_tiles - 2, 0, query_tiles - 1)
    per_share = share_width // tile_width
    share_at = jnp.where(is_query, jnp.minimum(tiles_here, query_tiles - 1), out_at)
    at = jnp.stack(
        [
            kind,
            column // share,
            jnp.minimum(which, 1) * share + column % share,
            column % share,
            share_at // per_share,
            share_at % per_share + jnp.where(is_query, 0, per_share),
            jnp.where(is_pair, tiles_here - query_tiles, 0),
        ]
    )
    new_master, new_one, new_two = adam(
        at,
        gating_plane,
        down_plane,
        share_plane,
        pair_plane,
        left_basis_set,
        right_basis_set,
        master,
        moment_one,
        moment_two,
    )
    gain_one = BETA_ONE * gain_moment_one + (1.0 - BETA_ONE) * gain_grads
    gain_two = BETA_TWO * gain_moment_two + (1.0 - BETA_TWO) * gain_grads * gain_grads
    new_gains = gains - GAIN_RATE * gain_one / (jnp.sqrt(gain_two) + ADAM_EPS)
    return (
        block_out,
        input_grad,
        new_master,
        new_one,
        new_two,
        gain_grads,
        new_gains,
        gain_one,
        gain_two,
    )


def solution(mesh):
    return jax.shard_map(
        local,
        mesh=mesh,
        in_specs=(
            P(("grp", "seq"), None),
            P(("grp", "seq"), None),
            P(("grp", "seq")),
            P(),
            P("grp", "seq", None),
            P("grp", "seq", None),
            P("grp", "seq", None),
            P("grp", "seq", None),
            P("grp", "seq", None),
            P("grp", "seq", None),
            P(),
            P(),
            P(),
        ),
        out_specs=(
            P(("grp", "seq"), None),
            P(("grp", "seq"), None),
            P("grp", "seq", None),
            P("grp", "seq", None),
            P("grp", "seq", None),
            P(),
            P(),
            P(),
            P(),
        ),
        check_vma=False,
    )
```

```python
import functools
import math

import jax
import jax.numpy as jnp
from jax import lax
from jax.experimental import pallas as pl
from jax.experimental.pallas import tpu as pltpu
from jax.sharding import PartitionSpec as P

MODEL_WIDTH = 2048
NH = 16
HD = 128
FF = 5632
SEQLEN = 1024


NORM_EPS = 1e-05
BETA_ONE = 0.95
BETA_TWO = 0.95
ADAM_EPS = 1e-08
WEIGHT_DECAY = 0.01
LEARN_RATE = 0.03
GAIN_RATE = 1.5
ROPE_BASE = 10000.0
MASKED = -1e30
PRECISE = lax.Precision.HIGHEST


def contract(left_side, right_side):
    return lax.dot_general(
        left_side, right_side, (((0,), (0,)), ((), ())), preferred_element_type=jnp.float32
    )


def times_transpose(left_side, right_side):
    return lax.dot_general(
        left_side, right_side, (((1,), (1,)), ((), ())), preferred_element_type=jnp.float32
    )


def turn_tables(places):
    half_width = HD // 2
    frequency = ROPE_BASE ** (-(jnp.arange(half_width, dtype=jnp.float32) * 2.0) / HD)
    angles = places.astype(jnp.float32)[:, None] * frequency[None, :]
    cosine, sine = jnp.cos(angles), jnp.sin(angles)
    return (
        jnp.concatenate([cosine, cosine], axis=1),
        jnp.concatenate([-sine, sine], axis=1),
    )


def turn(rows, cosine, sine):
    return rows * cosine + pltpu.roll(rows, HD // 2, 1) * sine


def turn_back(rows, cosine, sine):
    return rows * cosine - pltpu.roll(rows, HD // 2, 1) * sine


def dot_last(left_side, right_side):
    return lax.dot_general(
        left_side, right_side, (((1,), (1,)), ((), ())), preferred_element_type=jnp.float32
    )


def dot_first(left_side, right_side):
    return lax.dot_general(
        left_side, right_side, (((0,), (0,)), ((), ())), preferred_element_type=jnp.float32
    )


SMALL_COST = pl.CostEstimate(flops=1, bytes_accessed=1, transcendentals=0)


def project_kernel(x_ref, w_ref, cosine_ref, sine_ref, out_ref):
    made = jnp.dot(x_ref[...], w_ref[...], preferred_element_type=jnp.float32)
    cosine, sine = cosine_ref[...], sine_ref[...]
    first, second = made[:, :HD], made[:, HD:]
    last = pl.program_id(0) == pl.num_programs(0) - 1
    out_ref[:, :HD] = turn(first, cosine, sine).astype(out_ref.dtype)
    out_ref[:, HD:] = jnp.where(last, second, turn(second, cosine, sine)).astype(out_ref.dtype)


def project(normed, weights, tables):
    rows, width = normed.shape
    steps = NH // 2 + 1
    return pl.pallas_call(
        project_kernel,
        grid=(steps,),
        in_specs=[
            pl.BlockSpec((rows, width), lambda j: (0, 0)),
            pl.BlockSpec((width, 2 * HD), lambda j: (0, j)),
            pl.BlockSpec((rows, HD), lambda j: (0, 0)),
            pl.BlockSpec((rows, HD), lambda j: (0, 0)),
        ],
        out_specs=pl.BlockSpec((rows, 2 * HD), lambda j: (0, j)),
        out_shape=jax.ShapeDtypeStruct((rows, steps * 2 * HD), jnp.bfloat16),
        compiler_params=pltpu.CompilerParams(vmem_limit_bytes=56 * 2**20),
        cost_estimate=SMALL_COST,
        name="project",
    )(normed, weights, *tables)


def score_mask(key_seg_ref, query_seg_ref, block, rows):
    keys = (block + 1) * rows
    same = key_seg_ref[:keys, :] == query_seg_ref[...]
    key_at = lax.broadcasted_iota(jnp.int32, (keys, rows), 0)
    query_at = lax.broadcasted_iota(jnp.int32, (keys, rows), 1) + block * rows
    return same & (key_at <= query_at)


def attend_kernel(at_ref, q_ref, k_ref, v_ref, key_seg_ref, query_seg_ref, context_ref, total_ref):
    scale = HD ** (-0.5)
    rows = q_ref.shape[0]
    for block in range(SEQLEN // rows):

        @pl.when(at_ref[0] == block)
        def _():
            keys = (block + 1) * rows
            scores = dot_last(k_ref[:keys, :], q_ref[...]) * scale
            scores = jnp.where(
                score_mask(key_seg_ref, query_seg_ref, block, rows), scores, MASKED
            )
            highest = jnp.max(scores, axis=0, keepdims=True)
            exponent = jnp.exp(scores - highest)
            totals = jnp.sum(exponent, axis=0, keepdims=True)
            probs_low = (exponent * (1.0 / totals)).astype(jnp.bfloat16)
            context = dot_first(probs_low, v_ref[:keys, :])
            context_ref[...] = context.astype(jnp.bfloat16)
            total_ref[0] = highest + jnp.log(totals)


def attend_back_head(
    place, q_ref, k_ref, v_ref, grad_ref, total_ref, key_seg_ref, query_seg_ref, key_cosine_ref,
    key_sine_ref, cosine_ref, sine_ref, query_grad_ref, pair_grad_ref, key_sum, value_sum,
):
    scale = HD ** (-0.5)
    rows = q_ref.shape[0]
    head = pl.program_id(0)

    @pl.when(head == 0)
    def _():
        key_sum[...] = jnp.zeros_like(key_sum)
        value_sum[...] = jnp.zeros_like(value_sum)

    for block in range(SEQLEN // rows):

        @pl.when(place == block)
        def _():
            keys = (block + 1) * rows
            queries, grads = q_ref[...], grad_ref[...]
            shifted = dot_last(k_ref[:keys, :], queries) * scale - total_ref[0]
            allowed = score_mask(key_seg_ref, query_seg_ref, block, rows)
            probs = jnp.where(allowed, jnp.exp(shifted), 0.0)
            prob_grad = dot_last(v_ref[:keys, :], grads)
            centre = jnp.sum(probs * prob_grad, axis=0, keepdims=True)
            score_grad = (probs * (prob_grad - centre) * scale).astype(jnp.bfloat16)
            value_sum[:keys, :] += jnp.dot(
                probs.astype(jnp.bfloat16), grads, preferred_element_type=jnp.float32
            )
            key_sum[:keys, :] += jnp.dot(score_grad, queries, preferred_element_type=jnp.float32)
            query_grad = dot_first(score_grad, k_ref[:keys, :])
            query_grad_ref[...] = turn_back(query_grad, cosine_ref[...], sine_ref[...]).astype(
                jnp.bfloat16
            )

    @pl.when(head == pl.num_programs(0) - 1)
    def _():
        pair_grad_ref[:, :HD] = turn_back(
            key_sum[...], key_cosine_ref[...], key_sine_ref[...]
        ).astype(jnp.bfloat16)
        pair_grad_ref[:, HD:] = value_sum[...].astype(jnp.bfloat16)


def attend_back_kernel(at_ref, *refs):
    attend_back_head(at_ref[0], *refs)


def attention_specs(kinds, rows):
    specs = {
        "at": pl.BlockSpec(memory_space=pltpu.SMEM),
        "head": pl.BlockSpec((rows, HD), lambda h: (0, h)),
        "keys": pl.BlockSpec((SEQLEN, HD), lambda h: (0, 0)),
        "values": pl.BlockSpec((SEQLEN, HD), lambda h: (0, 1)),
        "pair": pl.BlockSpec((SEQLEN, 2 * HD), lambda h: (0, 0)),
        "total": pl.BlockSpec((1, 1, rows), lambda h: (h, 0, 0)),
        "key_seg": pl.BlockSpec((SEQLEN, 1), lambda h: (0, 0)),
        "query_seg": pl.BlockSpec((1, rows), lambda h: (0, 0)),
        "key_table": pl.BlockSpec((SEQLEN, HD), lambda h: (0, 0)),
        "table": pl.BlockSpec((rows, HD), lambda h: (0, 0)),
    }
    return [specs[kind] for kind in kinds]


def attend(at, projected, pairs, key_segs, query_segs):
    rows = projected.shape[0]
    columns = NH * HD
    return pl.pallas_call(
        attend_kernel,
        grid=(NH,),
        in_specs=attention_specs(["at", "head", "keys", "values", "key_seg", "query_seg"], rows),
        out_specs=attention_specs(["head", "total"], rows),
        out_shape=(
            jax.ShapeDtypeStruct((rows, columns), jnp.bfloat16),
            jax.ShapeDtypeStruct((NH, 1, rows), jnp.float32),
        ),
        compiler_params=pltpu.CompilerParams(vmem_limit_bytes=32 * 2**20),
        cost_estimate=SMALL_COST,
        name="attend",
    )(at, projected, pairs, pairs, key_segs[:, None], query_segs[None, :])


def attend_back(at, projected, pairs, grads, totals, key_segs, query_segs, key_tables, tables):
    rows = projected.shape[0]
    columns = NH * HD
    return pl.pallas_call(
        attend_back_kernel,
        grid=(NH,),
        in_specs=attention_specs(
            ["at", "head", "keys", "values", "head", "total", "key_seg", "query_seg"]
            + ["key_table", "key_table", "table", "table"],
            rows,
        ),
        out_specs=attention_specs(["head", "pair"], rows),
        out_shape=(
            jax.ShapeDtypeStruct((rows, columns), jnp.bfloat16),
            jax.ShapeDtypeStruct((SEQLEN, 2 * HD), jnp.bfloat16),
        ),
        scratch_shapes=[pltpu.VMEM((SEQLEN, HD), jnp.float32)] * 2,
        compiler_params=pltpu.CompilerParams(vmem_limit_bytes=32 * 2**20),
        cost_estimate=SMALL_COST,
        name="attend_back",
    )(
        at, projected, pairs, pairs, grads, totals, key_segs[:, None], query_segs[None, :],
        *key_tables, *tables,
    )


def own_columns(grp, own):
    return pl.ds(pl.multiple_of((grp * own) % 128, math.gcd(own, 128)), own)


def load_weights(parts, weights, sems):
    count, rows, _ = parts[0].shape
    halves = len(parts)
    return [
        pltpu.make_async_copy(
            parts[half].at[block],
            weights.at[pl.ds((block * halves + half) * rows, rows)],
            sems.at[block * halves + half],
        )
        for half in range(halves)
        for block in range(count)
    ]


def feed_block(own, first, x, cot, weights, act_ref, gate_grad_ref, up_grad_ref, two_ref, out_ref):
    low = jnp.bfloat16
    wide = jnp.float32
    cols = act_ref.shape[0]
    gate = jnp.dot(x, weights[:, :cols], preferred_element_type=wide)
    upper = jnp.dot(x, weights[:, cols : 2 * cols], preferred_element_type=wide)
    act_grad = jnp.dot(cot, weights[:, 2 * cols :], preferred_element_type=wide)
    column = lax.broadcasted_iota(jnp.int32, gate.shape, 1)
    real = (column >= first) & (column < first + own)
    sigmoid = 1.0 / (1.0 + jnp.exp(-gate))
    silu = gate * sigmoid
    activated = jnp.where(real, silu * upper, 0.0).astype(low)
    act_grad = jnp.where(real, act_grad, 0.0)
    gate_grad = (act_grad * upper * sigmoid * (1.0 + gate * (1.0 - sigmoid))).astype(low)
    up_grad = (act_grad * silu).astype(low)
    act_ref[...] = jnp.transpose(activated)
    gate_grad_ref[...] = jnp.transpose(gate_grad)
    up_grad_ref[...] = jnp.transpose(up_grad)
    two = dot_last(gate_grad, weights[:, :cols]) + dot_last(up_grad, weights[:, cols : 2 * cols])
    two_ref[...] = two.astype(low)
    out_ref[...] = dot_last(activated, weights[:, 2 * cols :]).astype(low)


def feed_kernel(own, real_ref, x_ref, cot_ref, *refs):
    parts, refs = refs[:-7], refs[-7:]
    weights, sems = refs[5:]

    @pl.when(pl.program_id(0) == 0)
    def _():
        copies = load_weights(parts, weights, sems)
        for copy in copies:
            copy.start()
        for copy in copies:
            copy.wait()

    feed_block(own, real_ref[0], x_ref[...], cot_ref[...], weights, *refs[:5])


def feed_forward(own, real_cols, x, cot, parts, seq_count):
    tokens_all, width = x.shape
    _, rows, cols = parts[0].shape
    cols = cols // 3
    step = 256
    low = jnp.bfloat16
    block = pl.BlockSpec((step, width), lambda i: (i, 0))
    narrow = pl.BlockSpec((cols, step), lambda i: (0, i))
    return pl.pallas_call(
        functools.partial(feed_kernel, own),
        grid=(tokens_all // step,),
        in_specs=[pl.BlockSpec(memory_space=pltpu.SMEM), block, block]
        + [pl.BlockSpec(memory_space=pl.ANY)] * len(parts),
        out_specs=[narrow, narrow, narrow, block, block],
        out_shape=[jax.ShapeDtypeStruct((cols, tokens_all), low)] * 3
        + [jax.ShapeDtypeStruct((tokens_all, width), low)] * 2,
        scratch_shapes=[
            pltpu.VMEM((width, 3 * cols), low),
            pltpu.SemaphoreType.DMA((len(parts) * seq_count,)),
        ],
        compiler_params=pltpu.CompilerParams(vmem_limit_bytes=52 * 2**20),
        cost_estimate=SMALL_COST,
        name="feed_forward",
    )(real_cols, x, cot, *parts)


def feed_gather_kernel(
    own, first, second, halves, real_ref, own_ref, context_ref, cot_ref, cot_all_ref, *refs
):
    parts, refs = refs[:halves], refs[halves:]
    (
        gate_grad_ref, up_grad_ref, two_ref, out_ref, second_ref, context_plane_ref, down_out,
        blocks, weights, act_block, act, x_block, stage, load_sems, keep_sems, x_sems, out_sems,
        first_send, first_recv, second_send, second_recv,
    ) = refs
    step = pl.program_id(0)
    grp, seq = lax.axis_index("grp"), lax.axis_index("seq")
    first.start(own_ref, blocks, (first_send, first_recv), grp, seq, begin=False)
    second.start(context_ref, context_plane_ref, (second_send, second_recv), grp, seq, begin=False)
    loads = load_weights(parts, weights, load_sems)
    cols = act.shape[0]
    step_rows = act_block.shape[1]
    rows = x_block.shape[2]
    count = cot_all_ref.shape[1] // rows

    @pl.when(step == 0)
    def _():
        for copy in loads:
            copy.start()
        barrier = pltpu.get_barrier_semaphore()
        for device in first.peers(grp, seq):
            pl.semaphore_signal(barrier, inc=1, device_id=device, device_id_type=MESH)
        pl.semaphore_wait(barrier, 3)
        first.begin()
        first.kept.wait()
        for copy in loads:
            copy.wait()

    @pl.when(step == 1)
    def _():
        first.due[7].wait_recv()

    @pl.when(step == 2)
    def _():
        for came in (1, 4, 2):
            first.pass_on(came)

    @pl.when(step == 3)
    def _():
        first.pass_on(5)

    @pl.when(step == 4)
    def _():
        first.due[8].wait_recv()
        first.due[9].wait_recv()
        first.pass_on(6)
        first.pass_on(3)
        second.begin()

    @pl.when(step == 5)
    def _():
        first.due[10].wait_recv()
        first.due[11].wait_recv()

    @pl.when(step == 7)
    def _():
        first.due[12].wait_recv()
        first.due[13].wait_recv()
        second.pass_on(1)
        second.pass_on(4)

    keep = pltpu.make_async_copy(blocks.at[step], second_ref.at[step], keep_sems.at[step])
    keep.start()
    feed_block(
        own, real_ref[0], blocks[step], cot_ref[...], weights, act_block, gate_grad_ref, up_grad_ref,
        two_ref, out_ref,
    )
    act[:, pl.ds(pl.multiple_of(step * step_rows, step_rows), step_rows)] = act_block[...]

    def x_copy(at):
        view = cot_all_ref.at[:, pl.ds(pl.multiple_of(at * rows, rows), rows)]
        return pltpu.make_async_copy(view, x_block.at[at % 2], x_sems.at[at % 2])

    def out_copy(at):
        place = pl.ds(pl.multiple_of(at * own, own), own)
        mine = stage.at[at % 2, own_columns(grp, own)]
        return pltpu.make_async_copy(mine, down_out.at[place], out_sems.at[at % 2])

    @pl.when(step == 7)
    def _():
        x_copy(0).start()
        second.pass_on(2)
        second.pass_on(5)

        def one(at, _):
            @pl.when(at == 2)
            def _():
                second.pass_on(6)
                second.pass_on(3)

            x_copy(at).wait()

            @pl.when(at + 1 < count)
            def _():
                x_copy(at + 1).start()

            @pl.when(at >= 2)
            def _():
                out_copy(at - 2).wait()

            stage[at % 2] = jnp.dot(
                act[...], x_block[at % 2], preferred_element_type=jnp.float32
            ).astype(stage.dtype)
            out_copy(at).start()
            return 0

        lax.fori_loop(0, count, one, 0)
        out_copy(count - 2).wait()
        out_copy(count - 1).wait()
        second.finish()
        for copy in first.out[1:]:
            copy.wait_send()
        for at in range(8):
            pltpu.make_async_copy(blocks.at[at], second_ref.at[at], keep_sems.at[at]).wait()


def feed_gather(number, own, real_cols, normed, context, cot, parts, seq_count):
    rows, width = normed.shape
    cols = parts[0].shape[2] // 3
    low = jnp.bfloat16
    block = pl.BlockSpec((rows, width), lambda i: (i, 0))
    narrow = pl.BlockSpec((cols, rows), lambda i: (0, i))
    first = gather_plane(normed.shape, placed=True)
    second = gather_plane(context.shape, placed=True)
    hbm = pl.BlockSpec(memory_space=pl.ANY)
    plane = jax.ShapeDtypeStruct((8, rows, width), low)
    model_rows = width // seq_count
    return pl.pallas_call(
        functools.partial(feed_gather_kernel, own, first, second, len(parts)),
        grid=(8,),
        in_specs=[pl.BlockSpec(memory_space=pltpu.SMEM), hbm, hbm, block, hbm]
        + [hbm] * len(parts),
        out_specs=[narrow, narrow, block, block, hbm, hbm, hbm],
        out_shape=[jax.ShapeDtypeStruct((cols, 8 * rows), low)] * 2
        + [jax.ShapeDtypeStruct((8 * rows, width), low)] * 2
        + [plane, plane, jax.ShapeDtypeStruct((seq_count * own, model_rows), low)],
        scratch_shapes=[
            pltpu.VMEM((8, rows, width), low),
            pltpu.VMEM((width, 3 * cols), low),
            pltpu.VMEM((cols, rows), low),
            pltpu.VMEM((cols, 8 * rows), low),
            pltpu.VMEM((2, 8 * rows, model_rows), low),
            pltpu.VMEM((2, cols, model_rows), low),
            pltpu.SemaphoreType.DMA((seq_count * len(parts),)),
            pltpu.SemaphoreType.DMA((8,)),
            pltpu.SemaphoreType.DMA((2,)),
            pltpu.SemaphoreType.DMA((2,)),
        ]
        + [pltpu.SemaphoreType.DMA((14,))] * 4,
        compiler_params=pltpu.CompilerParams(
            collective_id=number, has_side_effects=True, vmem_limit_bytes=60 * 2**20
        ),
        cost_estimate=SMALL_COST,
        name="feed_gather",
    )(real_cols, normed, context, cot, cot, *parts)


def weight_grad_kernel(left_ref, x_ref, out_ref):
    out_ref[...] = jnp.dot(
        left_ref[...], x_ref[...], preferred_element_type=jnp.float32
    ).astype(out_ref.dtype)


def weight_grad(left, x, seq_count):
    cols, tokens_all = left.shape
    rows = x.shape[1] // seq_count
    return pl.pallas_call(
        weight_grad_kernel,
        grid=(seq_count,),
        in_specs=[
            pl.BlockSpec((cols, tokens_all), lambda i: (0, 0)),
            pl.BlockSpec((tokens_all, rows), lambda i: (0, i)),
        ],
        out_specs=pl.BlockSpec((cols, rows), lambda i: (i, 0)),
        out_shape=jax.ShapeDtypeStruct((seq_count * cols, rows), jnp.bfloat16),
        compiler_params=pltpu.CompilerParams(vmem_limit_bytes=40 * 2**20),
        cost_estimate=SMALL_COST,
        name="weight_grad",
    )(left, x)


def share_grad_kernel(query_ref, out_ref, normed_ref, context_ref, grads_ref, turned):
    half = query_ref.shape[1]

    @pl.when(pl.program_id(0) == 0)
    def _():
        turned[0], turned[1] = jnp.transpose(query_ref[...]), jnp.transpose(out_ref[...])

    for at, right in enumerate((normed_ref, context_ref)):
        made = jnp.dot(turned[at], right[...], preferred_element_type=jnp.float32)
        grads_ref[at * half : (at + 1) * half, :] = made.astype(grads_ref.dtype)


def share_grad(query_share, out_share, normed, context):
    tokens_all, width = normed.shape
    columns = query_share.shape[1]
    step = 512
    narrow = pl.BlockSpec((tokens_all, columns), lambda i: (0, 0))
    block = pl.BlockSpec((tokens_all, step), lambda i: (0, i))
    return pl.pallas_call(
        share_grad_kernel,
        grid=(width // step,),
        in_specs=[narrow, narrow, block, block],
        out_specs=pl.BlockSpec((2 * columns, step), lambda i: (0, i)),
        out_shape=jax.ShapeDtypeStruct((2 * columns, width), jnp.bfloat16),
        scratch_shapes=[pltpu.VMEM((2, columns, tokens_all), jnp.bfloat16)],
        compiler_params=pltpu.CompilerParams(vmem_limit_bytes=60 * 2**20),
        cost_estimate=SMALL_COST,
        name="share_grad",
    )(query_share, out_share, normed, context)


def pick_kernel(rows, feed_ref, attn_ref, tiles_ref, feed_out, attn_out, sems):
    grp = lax.axis_index("grp")
    width = tiles_ref.shape[2]
    copies = []
    for at in range(feed_ref.shape[0]):
        copies.append(
            (tiles_ref.at[feed_ref[at]], feed_out.at[:, at * width : (at + 1) * width])
        )
    share = pl.ds(pl.multiple_of(grp * rows, rows), rows)
    for at in range(attn_ref.shape[0]):
        copies.append(
            (tiles_ref.at[attn_ref[at], share], attn_out.at[:, at * width : (at + 1) * width])
        )
    copies = [
        pltpu.make_async_copy(source, target, sems.at[at])
        for at, (source, target) in enumerate(copies)
    ]
    for copy in copies:
        copy.start()
    for copy in copies:
        copy.wait()


def pick(tiles, feed_slots, attn_slots):
    _, rows, width = tiles.shape
    share = rows // lax.axis_size("grp")
    feed, attn = feed_slots.shape[0], attn_slots.shape[0]
    return pl.pallas_call(
        functools.partial(pick_kernel, share),
        in_specs=[pl.BlockSpec(memory_space=pltpu.SMEM)] * 2 + [pl.BlockSpec(memory_space=pl.ANY)],
        out_specs=[pl.BlockSpec(memory_space=pltpu.VMEM)] * 2,
        out_shape=[
            jax.ShapeDtypeStruct((rows, feed * width), tiles.dtype),
            jax.ShapeDtypeStruct((share, attn * width), tiles.dtype),
        ],
        scratch_shapes=[pltpu.SemaphoreType.DMA((feed + attn,))],
        cost_estimate=SMALL_COST,
        name="pick",
    )(feed_slots, attn_slots, tiles)


def adam_kernel(group, at_ref, *refs):
    feeds = [refs[at * group : (at + 1) * group] for at in range(4)]
    left_ref, right_ref, master_ref, one_ref, two_ref = refs[4 * group : 4 * group + 5]
    new_master_ref, new_one_ref, new_two_ref, grad = refs[4 * group + 5 :]
    low = jnp.bfloat16
    for slot in range(group):
        kind = at_ref[0, pl.program_id(0) * group + slot]
        for number in range(3):

            @pl.when(kind == number)
            def _():
                grad[slot] = feeds[number][slot][...]

        @pl.when(kind == 3)
        def _():
            pair = feeds[3][slot][...].reshape(grad.shape[2], grad.shape[1])
            grad[slot] = jnp.transpose(pair.astype(jnp.float32)).astype(grad.dtype)

        @pl.when(kind == 4)
        def _():
            grad[slot] = jnp.zeros(grad.shape[1:], grad.dtype)

    slots = range(group)
    left = [left_ref[slot].astype(low) for slot in slots]
    right = [right_ref[slot].astype(low) for slot in slots]
    turned = [
        jnp.dot(grad[slot], left[slot], preferred_element_type=jnp.float32) for slot in slots
    ]
    turned = [dot_first(turned[slot].astype(low), right[slot]) for slot in slots]
    scaled = []
    for slot in slots:
        new_one = BETA_ONE * one_ref[slot] + (1.0 - BETA_ONE) * turned[slot]
        new_two = BETA_TWO * two_ref[slot] + (1.0 - BETA_TWO) * turned[slot] * turned[slot]
        new_one_ref[slot], new_two_ref[slot] = new_one, new_two
        scaled.append((new_one / (jnp.sqrt(new_two) + ADAM_EPS)).astype(low))
    restored = [dot_last(scaled[slot], right[slot]).astype(low) for slot in slots]
    restored = [
        jnp.dot(left[slot], restored[slot], preferred_element_type=jnp.float32) for slot in slots
    ]
    for slot in slots:
        new_master_ref[slot] = (
            master_ref[slot] * (1.0 - LEARN_RATE * WEIGHT_DECAY) - LEARN_RATE * restored[slot]
        )


def adam(at, gating, down, shares, pairs, left, right, master, one, two):
    slots, rows, width = master.shape
    group = 3 if slots % 3 == 0 else 1
    tile = pl.BlockSpec((group, rows, width), lambda i, at: (i, 0, 0))
    shape = jax.ShapeDtypeStruct(master.shape, jnp.float32)

    def feed(row):
        return [
            pl.BlockSpec((width, rows), lambda i, at, slot=slot: (at[row, i * group + slot], 0))
            for slot in range(group)
        ]

    pair = [
        pl.BlockSpec(
            (*pairs.shape[:2], width), lambda i, at, slot=slot: (0, 0, at[4, i * group + slot])
        )
        for slot in range(group)
    ]
    return pl.pallas_call(
        functools.partial(adam_kernel, group),
        grid_spec=pltpu.PrefetchScalarGridSpec(
            num_scalar_prefetch=1,
            grid=(slots // group,),
            in_specs=feed(1)
            + feed(2)
            + feed(3)
            + pair
            + [
                pl.BlockSpec((group, rows, rows), lambda i, at: (i, 0, 0)),
                pl.BlockSpec((group, width, width), lambda i, at: (i, 0, 0)),
                tile,
                tile,
                tile,
            ],
            out_specs=[tile] * 3,
            scratch_shapes=[pltpu.VMEM((group, width, rows), jnp.bfloat16)],
        ),
        out_shape=[shape] * 3,
        compiler_params=pltpu.CompilerParams(vmem_limit_bytes=60 * 2**20),
        cost_estimate=SMALL_COST,
        name="adam",
    )(
        at, *[gating] * group, *[down] * group, *[shares] * group, *[pairs] * group,
        left, right, master, one, two,
    )


MESH = pl.DeviceIdType.MESH


def remote(source, target, sems, at, device):
    return pltpu.make_async_remote_copy(
        src_ref=source,
        dst_ref=target,
        send_sem=sems[0].at[at],
        recv_sem=sems[1].at[at],
        device_id=device,
        device_id_type=MESH,
    )


def columns_of(ref, index, width):
    return ref.at[:, pl.ds(pl.multiple_of(index * width, width), width)]


def rows_of(ref, index, height):
    return ref.at[pl.ds(pl.multiple_of(index * height, height), height), :]


PLACES = {0: 0, 1: 1, 2: 2, 4: 3, 3: 4, 5: 5, 6: 6, 7: 7}


def flip(device, bits):
    core, side_x, side_y = device % 2, (device // 2) % 2, device // 4
    for bit, there in ((1, 1 - 2 * core), (2, 2 - 4 * side_x), (4, 4 - 8 * side_y)):
        if bits & bit:
            device = device + there
    return device


class PlacedExchange:
    axis = "grp"
    sem_count = 8

    def __init__(self, out_shape, source_view):
        self.out_shape, self.source_view = out_shape, source_view

    def peers(self, grp, seq):
        for bits in range(1, 8):
            yield flip(grp, bits), seq

    def start(self, source, target, sems, grp, seq):
        self.own = pltpu.make_async_copy(
            self.source_view(source, grp), target.at[0], sems[0].at[0]
        )
        self.own.start()
        self.copies = []
        for bits in range(1, 8):
            there = flip(grp, bits)
            copy = remote(
                self.source_view(source, there), target.at[PLACES[bits]], sems, bits, (there, seq)
            )
            copy.start()
            self.copies.append(copy)

    def forward(self):
        return iter(())

    def finish(self):
        for copy in self.copies:
            copy.wait()
        self.own.wait()


class Exchange:
    def __init__(self, axis, out_shape, source_view, target_view):
        self.axis, self.out_shape = axis, out_shape
        self.source_view, self.target_view = source_view, target_view
        self.count = lax.axis_size(axis)
        self.sem_count = self.count

    def peers(self, grp, seq):
        me = grp if self.axis == "grp" else seq
        for step in range(1, self.count):
            there = (me + step) % self.count
            yield (there, seq) if self.axis == "grp" else (grp, there)

    def start(self, source, target, sems, grp, seq, begin=True):
        me = grp if self.axis == "grp" else seq
        self.own = pltpu.make_async_copy(
            self.source_view(source, me), self.target_view(target, me), sems[0].at[0]
        )
        self.sent, self.due = [], []
        for step, device in enumerate(self.peers(grp, seq), 1):
            there = (me + step) % self.count
            back = (me + self.count - step) % self.count
            self.sent.append(
                remote(
                    self.source_view(source, there), self.target_view(target, me), sems, step, device
                )
            )
            self.due.append(
                remote(
                    self.source_view(source, back), self.target_view(target, back), sems, step, device
                )
            )
        if begin:
            self.begin()

    def begin(self):
        for copy in [self.own] + self.sent:
            copy.start()

    def forward(self):
        return iter(())

    def finish(self):
        for copy in self.due:
            copy.wait_recv()
        for copy in self.sent:
            copy.wait_send()
        self.own.wait()


class PlaneGather:
    axis = "grp"
    sem_count = 14

    def __init__(self, out_shape, source_view, target_view, half_of, placed):
        self.out_shape, self.placed = out_shape, placed
        self.source_view, self.target_view, self.half_of = source_view, target_view, half_of

    def peers(self, grp, seq):
        for bits in (1, 2, 4):
            yield flip(grp, bits), seq

    def start(self, source, target, sems, grp, seq, begin=True):
        def part(device, bits, piece):
            view = self.target_view(target, PLACES[bits] if self.placed else flip(device, bits))
            return view if piece == "all" else self.half_of(view, piece == "b")

        def own(piece):
            view = self.source_view(source, grp)
            return view if piece == "all" else self.half_of(view, piece == "b")

        self.out, self.due = [None], [None]
        for via, here, there, piece in (
            (2, 0, 2, "a"),
            (2, 0, 2, "b"),
            (2, 4, 6, "b"),
            (4, 0, 4, "b"),
            (4, 0, 4, "a"),
            (4, 2, 6, "a"),
            (1, 0, 1, "all"),
            (1, 2, 3, "a"),
            (1, 2, 3, "b"),
            (1, 4, 5, "b"),
            (1, 4, 5, "a"),
            (1, 6, 7, "a"),
            (1, 6, 7, "b"),
        ):
            device = flip(grp, via)
            view = own(piece) if here == 0 else part(grp, here, piece)
            at = len(self.out)
            self.out.append(remote(view, part(device, there, piece), sems, at, (device, seq)))
            self.due.append(remote(view, part(grp, there, piece), sems, at, (device, seq)))
        self.kept = pltpu.make_async_copy(own("all"), part(grp, 0, "all"), sems[0].at[0])
        if begin:
            self.begin()

    def begin(self):
        self.kept.start()
        for at in (1, 4, 2, 5, 7):
            self.out[at].start()

    def pass_on(self, came):
        self.due[came].wait_recv()
        for at in {1: (6, 8), 4: (3, 10), 2: (9,), 5: (11,), 6: (12,), 3: (13,)}[came]:
            self.out[at].start()

    def forward(self):
        for pair in ((1, 4), (2, 5), (6, 3)):
            for came in pair:
                self.pass_on(came)
            yield

    def finish(self):
        for copy in self.due[7:]:
            copy.wait_recv()
        for copy in self.out[1:]:
            copy.wait_send()
        self.kept.wait()


def add_rows(total, first, second):
    step = 32

    def some(at, _):
        rows = pl.ds(pl.multiple_of(at * step, step), step)
        total[rows, :] = (
            first[rows, :].astype(jnp.float32) + second[rows, :].astype(jnp.float32)
        ).astype(total.dtype)
        return 0

    lax.fori_loop(0, total.shape[0] // step, some, 0)


class PlaneSum:
    axis = "grp"
    sem_count = 15

    def __init__(self, rows, columns, placed=True):
        self.rows, self.columns, self.placed = rows, columns, placed
        self.out_shape = (rows, columns)

    def scratch(self):
        low = jnp.bfloat16
        shape = (self.rows, self.columns)
        half = (self.rows // 2, self.columns)
        return [
            pltpu.VMEM((4, *shape), low),
            pltpu.VMEM((4, *shape), low),
            pltpu.VMEM((2, *half), low),
            pltpu.VMEM((2, *shape), low),
        ]

    def peers(self, grp, seq):
        for bits in (1, 2, 4):
            yield flip(grp, bits), seq

    def start(self, source, target, sems, grp, seq, scratch, begin=True):
        self.mine, self.core_in, self.halves, self.wholes = scratch
        core, side_x, side_y = [(flip(grp, bits), seq) for bits in (1, 2, 4)]
        half = self.rows // 2
        self.low, self.high = low, high = pl.ds(0, half), pl.ds(half, half)
        mine, halves, wholes = self.mine, self.halves, self.wholes

        def block(bits):
            return source.at[PLACES[bits] if self.placed else flip(grp, bits)]

        self.copies = [
            remote(block(bits), self.core_in.at[at], sems, at, core)
            for at, bits in enumerate((7, 3, 5, 1))
        ] + [
            remote(mine.at[0, low], halves.at[0], sems, 4, side_x),
            remote(mine.at[0, high], halves.at[1], sems, 5, side_y),
            remote(mine.at[1, low], wholes.at[0, low], sems, 6, side_x),
            remote(mine.at[2, high], wholes.at[1, high], sems, 7, side_y),
            remote(mine.at[1, high], wholes.at[0, high], sems, 8, side_x),
            remote(mine.at[2, low], wholes.at[1, low], sems, 9, side_y),
        ]
        self.loads = [
            pltpu.make_async_copy(block(bits), mine.at[at], sems[0].at[10 + at])
            for at, bits in enumerate((6, 2, 4, 0))
        ]
        if target is not None:
            self.store = pltpu.make_async_copy(mine.at[3], target, sems[0].at[14])
        if begin:
            self.begin()

    def begin(self):
        for copy in self.copies[:4] + self.loads:
            copy.start()

    def first_sums(self):
        for came, then in ((0, (4, 5)), (1, (6,)), (2, (7,)), (3, ())):
            self.copies[came].wait_recv()
            self.loads[came].wait()
            add_rows(self.mine.at[came], self.mine.at[came], self.core_in.at[came])
            for at in then:
                self.copies[at].start()

    def forward(self):
        mine, low, high = self.mine, self.low, self.high
        yield
        self.copies[5].wait_recv()
        add_rows(mine.at[1, high], mine.at[1, high], self.halves.at[1])
        self.copies[8].start()
        self.copies[4].wait_recv()
        add_rows(mine.at[2, low], mine.at[2, low], self.halves.at[0])
        self.copies[9].start()

    def total(self):
        mine = self.mine
        for at, side, rows in ((6, 0, self.low), (7, 1, self.high), (8, 0, self.high), (9, 1, self.low)):
            self.copies[at].wait_recv()
            add_rows(mine.at[3, rows], mine.at[3, rows], self.wholes.at[side, rows])
        return mine.at[3]

    def finish(self):
        self.total()
        self.store.start()
        for copy in self.copies:
            copy.wait_send()
        self.store.wait()


class LineGather:
    axis = "seq"

    def __init__(self, shape):
        self.count = lax.axis_size("seq")
        self.out_shape = (self.count, *shape)
        self.sem_count = 2 * self.count

    def peers(self, grp, seq):
        for step in range(1, self.count):
            yield grp, (seq + step) % self.count

    def start(self, source, target, sems, grp, seq):
        self.seq, self.sems = seq, sems
        self.own = pltpu.make_async_copy(source, target.at[seq], sems[0].at[0])
        self.own.start()

        def make(away, up):
            there = (seq + (1 if up else self.count - 1)) % self.count
            block = (seq + (self.count - away if up else away)) % self.count
            view = source if away == 0 else target.at[block]
            at = 1 + away if up else self.count + away
            return remote(view, target.at[block], sems, at, (grp, there))

        def came(away, up):
            block = (seq + (self.count - away if up else away)) % self.count
            at = away if up else self.count + away - 1
            side = (seq + (self.count - 1 if up else 1)) % self.count
            return remote(target.at[block], target.at[block], sems, at, (grp, side))

        self.make, self.came = make, came
        self.has = lambda away, up: (seq - away >= 0) if up else (seq + away < self.count)
        self.last = lambda up: (seq + 1 < self.count) if up else (seq >= 1)
        for up in (True, False):

            @pl.when(self.last(up))
            def _():
                make(0, up).start()

    def forward(self):
        for away in range(1, self.count):
            for up in (True, False):

                @pl.when(self.has(away, up))
                def _():
                    self.came(away, up).wait_recv()
                    if away < self.count - 1:

                        @pl.when(self.last(up))
                        def _():
                            self.make(away, up).start()

            yield

    def finish(self):
        for away in range(self.count - 1):
            for up in (True, False):

                @pl.when(self.has(away, up) & self.last(up))
                def _():
                    self.make(away, up).wait_send()
        self.own.wait()


def attend_back_sum_kernel(
    sum_task, gather_task, q_ref, k_ref, v_ref, grad_ref, total_ref, key_seg_ref, query_seg_ref,
    key_cosine_ref, key_sine_ref, cosine_ref, sine_ref, part_hbm, down_hbm, query_grad_ref,
    pair_grad_ref, sum_hbm, down_plane, key_sum, value_sum, mine, core_in, halves, wholes,
    sum_send, sum_recv, gather_send, gather_recv,
):
    step = pl.program_id(0)
    grp, seq = lax.axis_index("grp"), lax.axis_index("seq")
    scratch = (mine, core_in, halves, wholes)
    sum_task.start(part_hbm, sum_hbm, (sum_send, sum_recv), grp, seq, scratch, begin=False)
    gather_task.start(down_hbm, down_plane, (gather_send, gather_recv), grp, seq, begin=False)

    @pl.when(step == 0)
    def _():
        barrier = pltpu.get_barrier_semaphore()
        for device in sum_task.peers(grp, seq):
            pl.semaphore_signal(barrier, inc=1, device_id=device, device_id_type=MESH)
        pl.semaphore_wait(barrier, 3)
        sum_task.begin()
        gather_task.begin()

    @pl.when(step == 6)
    def _():
        sum_task.first_sums()

    attend_back_head(
        seq, q_ref, k_ref, v_ref, grad_ref, total_ref, key_seg_ref, query_seg_ref, key_cosine_ref,
        key_sine_ref, cosine_ref, sine_ref, query_grad_ref, pair_grad_ref, key_sum, value_sum,
    )

    @pl.when(step == pl.num_programs(0) - 1)
    def _():
        hand_on([gather_task, sum_task])
        gather_task.finish()
        sum_task.finish()


def attend_back_sum(
    number, projected, pairs, grads, totals, key_segs, query_segs, key_tables, tables, part, down
):
    rows = projected.shape[0]
    columns = NH * HD
    low = jnp.bfloat16
    sum_task = PlaneSum(*part.shape[1:])
    gather_task = gather_plane(down.shape)
    hbm = pl.BlockSpec(memory_space=pl.ANY)
    return pl.pallas_call(
        functools.partial(attend_back_sum_kernel, sum_task, gather_task),
        grid=(NH,),
        in_specs=attention_specs(
            ["head", "keys", "values", "head", "total", "key_seg", "query_seg"]
            + ["key_table", "key_table", "table", "table"],
            rows,
        )
        + [hbm, hbm],
        out_specs=attention_specs(["head", "pair"], rows) + [hbm, hbm],
        out_shape=[
            jax.ShapeDtypeStruct((rows, columns), low),
            jax.ShapeDtypeStruct((SEQLEN, 2 * HD), low),
            jax.ShapeDtypeStruct(sum_task.out_shape, low),
            jax.ShapeDtypeStruct(gather_task.out_shape, low),
        ],
        scratch_shapes=[pltpu.VMEM((SEQLEN, HD), jnp.float32)] * 2
        + sum_task.scratch()
        + [pltpu.SemaphoreType.DMA((sum_task.sem_count,))] * 2
        + [pltpu.SemaphoreType.DMA((gather_task.sem_count,))] * 2,
        compiler_params=pltpu.CompilerParams(
            collective_id=number, has_side_effects=True, vmem_limit_bytes=48 * 2**20
        ),
        cost_estimate=SMALL_COST,
        name="attend_back_sum",
    )(
        projected, pairs, pairs, grads, totals, key_segs[:, None], query_segs[None, :],
        *key_tables, *tables, part, down,
    )


def block_kernel(
    first, second, pair_task, key_seg_ref, query_seg_ref, normed_ref, tokens_ref, gain_ref,
    cosine_ref, sine_ref, cot_hbm, normed_hbm, w_ref, projected_ref, pairs_ref, context_ref,
    total_ref, hidden_ref, second_ref, inverse_ref, cot_plane, normed_plane, own_pair, pairs,
    first_send, first_recv, second_send, second_recv, pair_send, pair_recv,
):
    step = pl.program_id(0)
    grp, seq = lax.axis_index("grp"), lax.axis_index("seq")
    first.start(cot_hbm, cot_plane, (first_send, first_recv), grp, seq, begin=False)
    second.start(normed_hbm, normed_plane, (second_send, second_recv), grp, seq, begin=False)
    pair_task.start(own_pair, pairs, (pair_send, pair_recv), grp, seq, begin=False)
    low = jnp.bfloat16
    rows = normed_ref.shape[0]
    wide = 2 * HD
    couples = NH // 2
    attend_at = 1 + couples
    out_at = attend_at + NH
    end = out_at + MODEL_WIDTH // wide

    @pl.when(step == 0)
    def _():
        barrier = pltpu.get_barrier_semaphore()
        devices = list(first.peers(grp, seq)) + list(pair_task.peers(grp, seq))
        for device in devices:
            pl.semaphore_signal(barrier, inc=1, device_id=device, device_id_type=MESH)
        pl.semaphore_wait(barrier, len(devices))
        first.begin()
        second.begin()

    @pl.when(step < attend_at)
    def _():
        made = jnp.dot(normed_ref[...], w_ref[...], preferred_element_type=jnp.float32)
        cosine, sine = cosine_ref[...], sine_ref[...]
        left = turn(made[:, :HD], cosine, sine).astype(low)
        right = made[:, HD:]

        @pl.when(step == 0)
        def _():
            own_pair[:, :HD] = left
            own_pair[:, HD:] = right.astype(low)
            pair_task.begin()
            projected_ref[:, NH * HD :] = own_pair[...]

        @pl.when(step > 0)
        def _():
            place = pl.multiple_of((step - 1) * wide, wide)
            projected_ref[:, pl.ds(place, HD)] = left
            projected_ref[:, pl.ds(pl.multiple_of(place + HD, HD), HD)] = turn(
                right, cosine, sine
            ).astype(low)

    @pl.when(step == attend_at)
    def _():
        pair_task.finish()
        for at in range(pairs.shape[0]):
            pairs_ref[at * rows : (at + 1) * rows, :] = pairs[at]

    @pl.when(step == attend_at + 2)
    def _():
        first.pass_on(1)
        first.pass_on(4)

    @pl.when(step == out_at)
    def _():
        first.pass_on(2)
        first.pass_on(5)

    @pl.when((step >= attend_at) & (step < out_at))
    def _():
        head = step - attend_at
        place = pl.ds(pl.multiple_of(head * HD, HD), HD)
        scale = HD ** (-0.5)
        for block in range(SEQLEN // rows):

            @pl.when(seq == block)
            def _():
                keys = (block + 1) * rows
                scores = dot_last(pairs_ref[:keys, :HD], projected_ref[:, place]) * scale
                scores = jnp.where(
                    score_mask(key_seg_ref, query_seg_ref, block, rows), scores, MASKED
                )
                highest = jnp.max(scores, axis=0, keepdims=True)
                exponent = jnp.exp(scores - highest)
                totals = jnp.sum(exponent, axis=0, keepdims=True)
                probs_low = (exponent * (1.0 / totals)).astype(low)
                context = dot_first(probs_low, pairs_ref[:keys, HD:])
                context_ref[:, place] = context.astype(low)
                total_ref[head] = highest + jnp.log(totals)

    @pl.when(step >= out_at)
    def _():
        place = pl.ds(pl.multiple_of((step - out_at) * wide, wide), wide)
        branch = jnp.dot(context_ref[...], w_ref[...], preferred_element_type=jnp.float32)
        hidden_ref[:, place] = tokens_ref[:, place].astype(jnp.float32) + branch

    @pl.when(step == end - 1)
    def _():
        chunk = 32
        gain = gain_ref[1:2, :]

        def some(at, _):
            part = pl.ds(pl.multiple_of(at * chunk, chunk), chunk)
            hidden = hidden_ref[part, :]
            inverse = lax.rsqrt(jnp.mean(hidden * hidden, axis=-1, keepdims=True) + NORM_EPS)
            inverse_ref[part, :] = inverse
            second_ref[part, :] = (hidden * inverse * gain).astype(low)
            return 0

        lax.fori_loop(0, rows // chunk, some, 0)
        first.pass_on(6)
        first.pass_on(3)
        for came in (1, 4, 2, 5, 6, 3):
            second.pass_on(came)
        first.finish()
        second.finish()


def attention_block(number, normed, tokens, gains, tables, key_segs, query_segs, cotangent, weights):
    rows, width = normed.shape
    low, wide = jnp.bfloat16, 2 * HD
    couples = NH // 2
    count = SEQLEN // rows
    first = gather_plane(cotangent.shape, placed=True)
    second = gather_plane(normed.shape, placed=True)
    pair_task = Exchange("seq", (count, rows, wide), whole, block_of)

    def weight_block(step):
        turned = step - NH
        return (0, jnp.where(step == 0, couples, jnp.where(step <= couples, step - 1, jnp.maximum(turned, couples + 1))))

    def full(shape):
        return pl.BlockSpec(shape, lambda step: (0,) * len(shape))

    hbm = pl.BlockSpec(memory_space=pl.ANY)
    steps = 1 + couples + NH + width // wide
    plane = jax.ShapeDtypeStruct((8, rows, width), low)
    shapes = [
        jax.ShapeDtypeStruct((rows, NH * HD + wide), low),
        jax.ShapeDtypeStruct((SEQLEN, wide), low),
        jax.ShapeDtypeStruct((rows, NH * HD), low),
        jax.ShapeDtypeStruct((NH, 1, rows), jnp.float32),
        jax.ShapeDtypeStruct((rows, width), jnp.float32),
        jax.ShapeDtypeStruct((rows, width), low),
        jax.ShapeDtypeStruct((rows, 1), jnp.float32),
    ]
    return pl.pallas_call(
        functools.partial(block_kernel, first, second, pair_task),
        grid=(steps,),
        in_specs=[
            full((SEQLEN, 1)),
            full((1, rows)),
            full((rows, width)),
            full((rows, width)),
            full((2, width)),
            full((rows, HD)),
            full((rows, HD)),
            hbm,
            hbm,
            pl.BlockSpec((width, wide), weight_block),
        ],
        out_specs=[full(shape.shape) for shape in shapes] + [hbm, hbm],
        out_shape=shapes + [plane, plane],
        scratch_shapes=[pltpu.VMEM((rows, wide), low), pltpu.VMEM((count, rows, wide), low)]
        + [pltpu.SemaphoreType.DMA((14,))] * 4
        + [pltpu.SemaphoreType.DMA((pair_task.sem_count,))] * 2,
        compiler_params=pltpu.CompilerParams(
            collective_id=number, has_side_effects=True, vmem_limit_bytes=56 * 2**20
        ),
        cost_estimate=SMALL_COST,
        name="attention_block",
    )(
        key_segs[:, None], query_segs[None, :], normed, tokens, gains, *tables, cotangent, normed,
        weights,
    )


def add_blocks(total, blocks):
    step = min(32, total.shape[0])

    def some(at, _):
        rows = pl.ds(pl.multiple_of(at * step, step), step)
        made = blocks[0, rows, :].astype(jnp.float32)
        for block in range(1, blocks.shape[0]):
            made = made + blocks[block, rows, :].astype(jnp.float32)
        total[rows, :] = made.astype(total.dtype)
        return 0

    lax.fori_loop(0, total.shape[0] // step, some, 0)


def norm_one_back(
    weights_hbm, query_grad_ref, pair_grad_ref, hidden_grad_ref, tokens_ref, inverse_ref, gain_ref,
    gain_two_ref, input_grad_ref, gain_terms, w_block, norm_grad, w_sems,
):
    width, query_columns = tokens_ref.shape[1], query_grad_ref.shape[1]
    rows, columns = w_block.shape[1:]
    count = width // rows

    def w_copy(at):
        view = weights_hbm.at[pl.ds(pl.multiple_of(at * rows, rows), rows), pl.ds(0, columns)]
        return pltpu.make_async_copy(view, w_block.at[at % 2], w_sems.at[at % 2])

    w_copy(0).start()

    def one(at, _):
        w_copy(at).wait()

        @pl.when(at + 1 < count)
        def _():
            w_copy(at + 1).start()

        made = dot_last(query_grad_ref[...], w_block[at % 2, :, :query_columns])
        made = made + dot_last(pair_grad_ref[...], w_block[at % 2, :, query_columns:])
        norm_grad[:, pl.ds(pl.multiple_of(at * rows, rows), rows)] = made
        return 0

    lax.fori_loop(0, count, one, 0)
    chunk = 32
    gain = gain_ref[0:1, :]

    def some(at, sums):
        part = pl.ds(pl.multiple_of(at * chunk, chunk), chunk)
        inverse, token = inverse_ref[part, :], tokens_ref[part, :].astype(jnp.float32)
        made = norm_grad[part, :]
        scaled = gain * made
        mean = jnp.mean(token * scaled, axis=-1, keepdims=True)
        input_grad_ref[part, :] = (
            hidden_grad_ref[part, :] + inverse * scaled - token * (inverse * inverse * inverse * mean)
        )
        return sums + jnp.sum(made * token * inverse, axis=0, keepdims=True)

    zeros = jnp.zeros((1, width), jnp.float32)
    gain_terms[0:1, :] = lax.fori_loop(0, tokens_ref.shape[0] // chunk, some, zeros)
    gain_terms[1:2, :] = gain_two_ref[...]


def tail_kernel(
    tasks, shares_hbm, pair_hbm, gating_hbm, weights_hbm, query_grad_ref, pair_grad_ref,
    hidden_grad_ref, tokens_ref, inverse_ref, gain_ref, gain_two_ref, gating_plane, share_plane,
    pair_plane, gain_plane, input_grad_ref, share_parts, share_sum, mine, core_in, halves, wholes,
    pair_parts, pair_sum, gain_terms, gain_parts, gain_sum, w_block, norm_grad, w_sems, *sems,
):
    gating, pair, gain_seq, gain_grp, pair_seq, pair_gather, *halves_of = tasks
    shares, share_gathers = halves_of[:2], halves_of[2:]
    grp, seq = lax.axis_index("grp"), lax.axis_index("seq")
    barrier = pltpu.get_barrier_semaphore()
    devices = list(gain_grp.peers(grp, seq)) + list(gain_seq.peers(grp, seq))
    for device in devices:
        pl.semaphore_signal(barrier, inc=1, device_id=device, device_id_type=MESH)
    pl.semaphore_wait(barrier, len(devices))
    sems = [(sems[2 * at], sems[2 * at + 1]) for at in range(len(tasks))]

    def share_part(at):
        shares[at].finish()
        add_blocks(share_sum.at[at], share_parts.at[at])
        share_gathers[at].start(share_sum.at[at], share_plane, sems[8 + at], grp, seq)

    shares[0].start(shares_hbm, share_parts.at[0], sems[6], grp, seq)
    pair.start(pair_hbm, None, sems[1], grp, seq, (mine, core_in, halves, wholes))
    gating.start(gating_hbm, gating_plane, sems[0], grp, seq, begin=False)
    gating.kept.start()
    for at in (1, 4, 7):
        gating.out[at].start()
    pair.first_sums()
    norm_one_back(
        weights_hbm, query_grad_ref, pair_grad_ref, hidden_grad_ref, tokens_ref, inverse_ref,
        gain_ref, gain_two_ref, input_grad_ref, gain_terms, w_block, norm_grad, w_sems,
    )
    gain_seq.start(gain_terms, gain_parts, sems[2], grp, seq)
    for _ in pair.forward():
        pass
    for at in (2, 5):
        gating.out[at].start()
    handing = gating.forward()
    next(handing)
    pair_seq.start(pair.total(), pair_parts, sems[4], grp, seq)
    shares[1].start(shares_hbm, share_parts.at[1], sems[7], grp, seq)
    gain_seq.finish()
    gain_sum[...] = jnp.sum(gain_parts[...], axis=0)
    gain_grp.start(gain_sum, gain_plane, sems[3], grp, seq)
    share_part(0)
    pair_seq.finish()
    add_blocks(pair_sum, pair_parts)
    pair_gather.start(pair_sum, pair_plane, sems[5], grp, seq)
    next(handing)
    share_part(1)
    next(handing)
    hand_on([share_gathers[0], pair_gather, share_gathers[1]])
    for copy in pair.copies:
        copy.wait_send()
    for task in (gain_grp, gating, pair_gather, *share_gathers):
        task.finish()


def gather_gating(shape):
    return gather_plane(
        shape,
        split=1,
        target_view=lambda ref, index: ref.at[:, index],
        out_shape=(shape[0], lax.axis_size("grp"), *shape[1:]),
    )


def tail_exchange(number, shares, pair, gating, weights, back):
    gain_terms = jax.ShapeDtypeStruct((2, back[3].shape[1]), jnp.float32)
    tokens_here = back[3].shape[0]
    seq_count = lax.axis_size("seq")
    low = jnp.bfloat16
    columns, rows_all = shares.shape
    rows = rows_all // seq_count
    _, pair_rows, pair_columns = pair.shape
    sub = pair_rows // seq_count
    half = columns // 2

    def share_task(at):
        return Exchange(
            "seq",
            (seq_count, half, rows),
            lambda ref, index: ref.at[
                pl.ds(at * half, half), pl.ds(pl.multiple_of(index * rows, rows), rows)
            ],
            block_of,
        )

    def share_gather(at):
        return gather_plane(
            (half, rows),
            target_view=lambda ref, index: ref.at[index, pl.ds(at * half, half)],
            out_shape=(8, columns, rows),
        )

    tasks = [
        gather_gating(gating.shape),
        PlaneSum(pair_rows, pair_columns, placed=False),
        gather_axis("seq", gain_terms)[0],
        gather_axis("grp", gain_terms)[0],
        Exchange(
            "seq",
            (seq_count, sub, pair_columns),
            lambda ref, index: rows_of(ref, index, sub),
            block_of,
        ),
        gather_plane((sub, pair_columns)),
        share_task(0),
        share_task(1),
        share_gather(0),
        share_gather(1),
    ]
    hbm = pl.BlockSpec(memory_space=pl.ANY)
    vmem = pl.BlockSpec(memory_space=pltpu.VMEM)
    scratch = [
        pltpu.VMEM((2, seq_count, half, rows), low),
        pltpu.VMEM((2, half, rows), low),
        *tasks[1].scratch(),
        pltpu.VMEM((seq_count, sub, pair_columns), low),
        pltpu.VMEM((sub, pair_columns), low),
        pltpu.VMEM(gain_terms.shape, jnp.float32),
        pltpu.VMEM((seq_count, *gain_terms.shape), jnp.float32),
        pltpu.VMEM(gain_terms.shape, jnp.float32),
        pltpu.VMEM((2, 2 * HD, (NH + 2) * HD), low),
        pltpu.VMEM((tokens_here, back[3].shape[1]), jnp.float32),
        pltpu.SemaphoreType.DMA((2,)),
    ]
    for task in tasks:
        scratch += [pltpu.SemaphoreType.DMA((task.sem_count,))] * 2
    return pl.pallas_call(
        functools.partial(tail_kernel, tasks),
        in_specs=[hbm] * 4 + [vmem] * len(back),
        out_specs=[hbm] * 4 + [vmem],
        out_shape=[
            jax.ShapeDtypeStruct(tasks[0].out_shape, low),
            jax.ShapeDtypeStruct((8, columns, rows), low),
            jax.ShapeDtypeStruct((8, sub, pair_columns), low),
            jax.ShapeDtypeStruct((8, *gain_terms.shape), jnp.float32),
            jax.ShapeDtypeStruct((tokens_here, back[3].shape[1]), jnp.float32),
        ],
        scratch_shapes=scratch,
        compiler_params=pltpu.CompilerParams(
            collective_id=number, has_side_effects=True, vmem_limit_bytes=60 * 2**20
        ),
        cost_estimate=SMALL_COST,
        name="tail_exchange",
    )(shares, pair, gating, weights, *back)


def half_rows(axis, height):
    def half_of(view, second):
        index = (slice(None),) * axis + (pl.ds(height if second else 0, height),)
        return view.at[index]

    return half_of


def whole(ref, index):
    return ref


def block_of(ref, index):
    return ref.at[index]


def gather_plane(
    shape, split=0, source_view=whole, target_view=block_of, out_shape=None, placed=False
):
    out_shape = out_shape or (lax.axis_size("grp"), *shape)
    if lax.axis_size("grp") == 8:
        halves = half_rows(split, shape[split] // 2)
        return PlaneGather(out_shape, source_view, target_view, halves, placed)
    return Exchange("grp", out_shape, source_view, target_view)


def hand_on(tasks):
    going = [task.forward() for task in tasks]
    while going:
        going = [steps for steps in going if next(steps, going) is not going]


def exchange_kernel(tasks, wires, arrays, outputs, *refs):
    sources, targets = refs[:arrays], refs[arrays : arrays + outputs]
    refs = list(refs[arrays + outputs :])
    sems, scratch = [], []
    for task in tasks:
        sems.append((refs.pop(0), refs.pop(0)))
        held = len(task.scratch()) if isinstance(task, PlaneSum) else 0
        scratch.append([refs.pop(0) for _ in range(held)])
    grp, seq = lax.axis_index("grp"), lax.axis_index("seq")
    barrier = pltpu.get_barrier_semaphore()
    axes = {"grp": [], "seq": []}
    for task in tasks:
        devices = list(task.peers(grp, seq))
        if len(devices) > len(axes[task.axis]):
            axes[task.axis] = devices
    devices = axes["grp"] + axes["seq"]
    for device in devices:
        pl.semaphore_signal(barrier, inc=1, device_id=device, device_id_type=MESH)
    pl.semaphore_wait(barrier, len(devices))

    def start(at):
        after, source, target = wires[at]
        source = targets[source] if after is not None else sources[source]
        more = (scratch[at],) if scratch[at] else ()
        tasks[at].start(source, targets[target], sems[at], grp, seq, *more)

    open_tasks = list(range(len(tasks)))
    first = [at for at in open_tasks if wires[at][0] is None]
    for at in first:
        start(at)
    for at in first:
        if isinstance(tasks[at], PlaneSum):
            tasks[at].first_sums()
    hand_on([tasks[at] for at in first])
    for at in open_tasks[:]:
        after = wires[at][0]
        if after is not None:
            tasks[after].finish()
            open_tasks.remove(after)
            start(at)
            hand_on([tasks[at]])
    for at in open_tasks:
        tasks[at].finish()


def exchange(number, work):
    tasks = [piece[0] for piece in work]
    arrays, shapes, wires = [], [], []
    for piece in work:
        if isinstance(piece[1], int):
            after, source = piece[1], wires[piece[1]][2]
            kind = shapes[source].dtype
        else:
            after, source = None, len(arrays)
            arrays.append(piece[1])
            kind = piece[1].dtype
        if len(piece) == 3:
            target = wires[piece[2]][2]
        else:
            target = len(shapes)
            shapes.append(jax.ShapeDtypeStruct(piece[0].out_shape, kind))
        wires.append((after, source, target))
    scratch = []
    for task in tasks:
        scratch += [pltpu.SemaphoreType.DMA((task.sem_count,))] * 2
        if isinstance(task, PlaneSum):
            scratch += task.scratch()
    return pl.pallas_call(
        functools.partial(exchange_kernel, tasks, wires, len(arrays), len(shapes)),
        in_specs=[pl.BlockSpec(memory_space=pl.ANY)] * len(arrays),
        out_specs=[pl.BlockSpec(memory_space=pl.ANY)] * len(shapes),
        out_shape=shapes,
        scratch_shapes=scratch,
        compiler_params=pltpu.CompilerParams(collective_id=number, has_side_effects=True),
        cost_estimate=SMALL_COST,
        name="exchange",
    )(*arrays)


def gather_axis(axis, array):
    task = Exchange(axis, (lax.axis_size(axis), *array.shape), whole, block_of)
    return task, array


def split_rows(axis, array):
    count = lax.axis_size(axis)
    rows, columns = array.shape
    height = rows // count
    task = Exchange(
        axis,
        (count, height, columns),
        lambda ref, index: rows_of(ref, index, height),
        block_of,
    )
    return task, array


def split_columns(axis, array, placed=False):
    count = lax.axis_size(axis)
    rows, columns = array.shape
    width = columns // count
    if placed and count == 8:
        task = PlacedExchange(
            (count, rows, width), lambda ref, index: columns_of(ref, index, width)
        )
        return task, array
    task = Exchange(
        axis,
        (count, rows, width),
        lambda ref, index: columns_of(ref, index, width),
        block_of,
    )
    return task, array


def plane_sum_kernel(
    own, part_ref, gate_ref, up_ref, x_ref, total_ref, grads_out, core_in, chip, half_x, half_y,
    whole_x, whole_y, x_block, stage, send_sems, recv_sems, x_sems, out_sems,
):
    grp, seq = lax.axis_index("grp"), lax.axis_index("seq")
    core, side_x, side_y = [flip(grp, bits) for bits in (1, 2, 4)]
    blocks = [PLACES[bits] for bits in (6, 2, 4, 0)]
    core_blocks = [PLACES[bits] for bits in (7, 3, 5, 1)]
    half = total_ref.shape[0] // 2
    low, high = pl.ds(0, half), pl.ds(half, half)
    rows = x_block.shape[2]
    count = x_ref.shape[1] // rows

    def x_copy(at):
        view = x_ref.at[:, pl.ds(pl.multiple_of(at * rows, rows), rows)]
        return pltpu.make_async_copy(view, x_block.at[at % 2], x_sems.at[at % 2])

    def out_copies(at):
        return [
            pltpu.make_async_copy(
                stage.at[which, at % 2, own_columns(grp, own)],
                grads_out.at[pl.ds(pl.multiple_of((2 * at + which) * own, own), own)],
                out_sems.at[which, at % 2],
            )
            for which in range(2)
        ]

    x_copy(0).start()
    barrier = pltpu.get_barrier_semaphore()
    for device in (core, side_x, side_y):
        pl.semaphore_signal(barrier, inc=1, device_id=(device, seq), device_id_type=MESH)
    pl.semaphore_wait(barrier, 3)

    sems = (send_sems, recv_sems)
    copies = [
        remote(part_ref.at[block], core_in.at[at], sems, at, (core, seq))
        for at, block in enumerate(core_blocks)
    ]
    copies += [
        remote(chip.at[0, low], half_x, sems, 4, (side_x, seq)),
        remote(chip.at[0, high], half_y, sems, 5, (side_y, seq)),
        remote(chip.at[1, low], whole_x.at[low], sems, 6, (side_x, seq)),
        remote(chip.at[2, high], whole_y.at[high], sems, 7, (side_y, seq)),
        remote(chip.at[1, high], whole_x.at[high], sems, 8, (side_x, seq)),
        remote(chip.at[2, low], whole_y.at[low], sems, 9, (side_y, seq)),
    ]
    for copy in copies[:4]:
        copy.start()

    def step(at, _):
        @pl.when(at == 1)
        def _():
            for came, then in ((0, (4, 5)), (1, (6,)), (2, (7,))):
                copies[came].wait_recv()
                add_rows(chip.at[came], part_ref.at[blocks[came]], core_in.at[came])
                for start in then:
                    copies[start].start()

        @pl.when(at == count - 1)
        def _():
            copies[5].wait_recv()
            add_rows(chip.at[1, high], chip.at[1, high], half_y)
            copies[8].start()
            copies[4].wait_recv()
            add_rows(chip.at[2, low], chip.at[2, low], half_x)
            copies[9].start()

        x_copy(at).wait()

        @pl.when(at + 1 < count)
        def _():
            x_copy(at + 1).start()

        @pl.when(at >= 2)
        def _():
            for copy in out_copies(at - 2):
                copy.wait()

        for which, ref in enumerate((gate_ref, up_ref)):
            stage[which, at % 2] = jnp.dot(
                ref[...], x_block[at % 2], preferred_element_type=jnp.float32
            ).astype(stage.dtype)
        for copy in out_copies(at):
            copy.start()
        return 0

    lax.fori_loop(0, count, step, 0)
    copies[3].wait_recv()
    add_rows(total_ref, part_ref.at[blocks[3]], core_in.at[3])
    for at, came, rows_at in (
        (6, whole_x, low),
        (7, whole_y, high),
        (8, whole_x, high),
        (9, whole_y, low),
    ):
        copies[at].wait_recv()
        add_rows(total_ref.at[rows_at], total_ref.at[rows_at], came.at[rows_at])
    for copy in copies:
        copy.wait_send()
    for at in (count - 2, count - 1):
        for copy in out_copies(at):
            copy.wait()


def plane_sum(number, own, part, gate_grad, up_grad, x, seq_count):
    count = lax.axis_size("grp")
    rows_all, columns = part.shape
    rows = rows_all // count
    if count != 8:
        total = lax.psum_scatter(part, "grp", scatter_dimension=0, tiled=True)
        begin = (lax.axis_index("grp") * own) % 128
        both = jnp.concatenate(
            [lax.dynamic_slice_in_dim(grad, begin, own) for grad in (gate_grad, up_grad)], axis=0
        )
        return total.astype(jnp.float32), weight_grad(both, x, seq_count)
    low = jnp.bfloat16
    cols, tokens_all = gate_grad.shape
    width = x.shape[1] // seq_count
    vmem = pl.BlockSpec(memory_space=pltpu.VMEM)
    hbm = pl.BlockSpec(memory_space=pl.ANY)
    grads = jax.ShapeDtypeStruct((2 * seq_count * own, width), low)
    return pl.pallas_call(
        functools.partial(plane_sum_kernel, own),
        in_specs=[vmem, vmem, vmem, hbm],
        out_specs=[vmem, hbm],
        out_shape=[jax.ShapeDtypeStruct((rows, columns), jnp.float32), grads],
        scratch_shapes=[
            pltpu.VMEM((4, rows, columns), low),
            pltpu.VMEM((3, rows, columns), low),
            pltpu.VMEM((rows // 2, columns), low),
            pltpu.VMEM((rows // 2, columns), low),
            pltpu.VMEM((rows, columns), low),
            pltpu.VMEM((rows, columns), low),
            pltpu.VMEM((2, tokens_all, width), low),
            pltpu.VMEM((2, 2, cols, width), low),
            pltpu.SemaphoreType.DMA((10,)),
            pltpu.SemaphoreType.DMA((10,)),
            pltpu.SemaphoreType.DMA((2,)),
            pltpu.SemaphoreType.DMA((2, 2)),
        ],
        compiler_params=pltpu.CompilerParams(
            collective_id=number, has_side_effects=True, vmem_limit_bytes=56 * 2**20
        ),
        cost_estimate=SMALL_COST,
        name="plane_sum",
    )(part.reshape(count, rows, columns), gate_grad, up_grad, x)


def local(
    tokens,
    cotangent,
    segment_ids,
    tile_owner_slots,
    weights_low,
    master,
    moment_one,
    moment_two,
    left_basis_set,
    right_basis_set,
    gains,
    gain_moment_one,
    gain_moment_two,
):
    grp_count = lax.axis_size("grp")
    seq_count = lax.axis_size("seq")
    grp_here, seq_here = lax.axis_index("grp"), lax.axis_index("seq")
    rows_here = tokens.shape[0]
    slots_here, rows_block, tile_width = weights_low.shape
    tile_count = tile_owner_slots.shape[0]
    query_cols = NH * HD
    value_end = query_cols + 2 * HD
    output_end = value_end + MODEL_WIDTH
    attn_tiles = output_end // tile_width
    query_tiles = query_cols // tile_width
    hidden_tiles = FF // tile_width
    own = FF // grp_count
    share = max(-(-((at * own) % tile_width + own) // tile_width) for at in range(grp_count))
    share_width = MODEL_WIDTH // grp_count
    sub_rows = rows_block // grp_count
    halves = 2 if sub_rows >= 32 else 1
    half_block, half_sub = rows_block // halves, sub_rows // halves
    first_place = (seq_here * rows_here) % SEQLEN
    key_tables = turn_tables(jnp.arange(SEQLEN, dtype=jnp.int32))
    tables = [lax.dynamic_slice_in_dim(table, first_place, rows_here) for table in key_tables]

    hidden_ids = grp_here * own // tile_width + jnp.arange(share, dtype=jnp.int32)
    hidden_ids = jnp.minimum(hidden_ids, hidden_tiles - 1)
    feed_ids = (
        attn_tiles
        + jnp.arange(3, dtype=jnp.int32)[:, None] * hidden_tiles
        + hidden_ids[None, :]
    ).reshape(-1)
    feed_slots, attn_slots = tile_owner_slots[feed_ids], tile_owner_slots[:attn_tiles]

    tok_float = tokens.astype(jnp.float32)
    inverse_one = lax.rsqrt(jnp.mean(tok_float * tok_float, axis=-1, keepdims=True) + NORM_EPS)
    normed = (tok_float * inverse_one * gains[0]).astype(jnp.bfloat16)

    def weight_half(at):
        return gather_plane(
            (slots_here, half_block, tile_width),
            split=1,
            source_view=lambda ref, index: ref.at[:, pl.ds(at * half_block, half_block)],
        )

    def attn_half(at):
        return gather_plane(
            (seq_count, half_sub, output_end),
            target_view=lambda ref, index: ref.at[:, at, index],
            out_shape=(seq_count, halves, grp_count, half_sub, output_end),
        )

    flat = (grp_count * slots_here, half_block, tile_width)
    tiles, segments = exchange(
        0,
        [(weight_half(0), weights_low), gather_axis("seq", segment_ids.reshape(-1, tile_width))],
    )
    feed_rows, attn_rows = pick(tiles.reshape(flat), feed_slots, attn_slots)
    feed_parts = [lax.all_gather(feed_rows, "seq", axis=0, tiled=False)]
    if halves == 2:
        tiles, attn_first = exchange(
            1, [(weight_half(1), weights_low), gather_axis("seq", attn_rows)]
        )
        feed_rows, attn_rows = pick(tiles.reshape(flat), feed_slots, attn_slots)
        feed_parts.append(lax.all_gather(feed_rows, "seq", axis=0, tiled=False))
        attn_weights, _ = exchange(
            2,
            [(attn_half(0), attn_first), gather_axis("seq", attn_rows), (attn_half(1), 1, 0)],
        )
    else:
        _, attn_weights = exchange(2, [gather_axis("seq", attn_rows), (attn_half(0), 0)])
    attn_weights = attn_weights.reshape(MODEL_WIDTH, output_end)

    first_key = seq_here * rows_here - first_place
    key_segs = lax.dynamic_slice_in_dim(segments.reshape(-1), first_key, SEQLEN)
    at = (first_place // rows_here).reshape(1)
    if grp_count == 8 and seq_count * rows_here == SEQLEN:
        (
            projected, pairs, context, log_totals, hidden, normed_two, inverse_two, cot_plane,
            normed_plane,
        ) = attention_block(
            3, normed, tokens, gains, tables, key_segs, segment_ids, cotangent, attn_weights
        )
    else:
        projected = project(normed, attn_weights, tables)
        pairs, cot_plane, normed_plane = exchange(
            3,
            [
                gather_axis("seq", projected[:, query_cols:]),
                (gather_plane(cotangent.shape, placed=True), cotangent),
                (gather_plane(normed.shape, placed=True), normed),
            ],
        )
        pairs = lax.dynamic_slice_in_dim(pairs.reshape(-1, 2 * HD), first_key, SEQLEN)
        context, log_totals = attend(at, projected, pairs, key_segs, segment_ids)
        branch = jnp.dot(
            context, attn_weights[:, value_end:], preferred_element_type=jnp.float32
        )
        hidden = tok_float + branch
        inverse_two = lax.rsqrt(jnp.mean(hidden * hidden, axis=-1, keepdims=True) + NORM_EPS)
        normed_two = (hidden * inverse_two * gains[1]).astype(jnp.bfloat16)

    cot_plane = cot_plane.reshape(-1, MODEL_WIDTH)
    normed_plane = normed_plane.reshape(-1, MODEL_WIDTH)
    real_cols = ((grp_here * own) % tile_width).reshape(1)
    if halves == 2:
        some = jnp.max(feed_parts[0][0, :8, :tile_width].astype(jnp.float32)) * 0.0
        real_cols = real_cols + some.astype(jnp.int32)
    if grp_count == 8:
        gate_grad, up_grad, two_part, feed_part, second_plane, context_plane, down_grad = (
            feed_gather(
                4, own, real_cols, normed_two, context, cot_plane, feed_parts, seq_count
            )
        )
        second_plane = second_plane.reshape(-1, MODEL_WIDTH)
    else:
        second_plane, context_plane = exchange(
            4,
            [
                (gather_plane(normed_two.shape), normed_two),
                (gather_plane(context.shape), context),
            ],
        )
        second_plane = second_plane.reshape(-1, MODEL_WIDTH)
        activated, gate_grad, up_grad, two_part, feed_part = feed_forward(
            own, real_cols, second_plane, cot_plane, feed_parts, seq_count
        )
        activated = lax.dynamic_slice_in_dim(activated, (grp_here * own) % tile_width, own)
        down_grad = weight_grad(activated, cot_plane, seq_count)
    context_plane = context_plane.reshape(-1, MODEL_WIDTH)
    down_grad, two_part = lax.optimization_barrier((down_grad, two_part))
    down_grad = lax.psum_scatter(down_grad, "seq", scatter_dimension=0, tiled=True)
    norm_two_grad, gating_grads = plane_sum(
        5, own, two_part, gate_grad, up_grad, second_plane, seq_count
    )
    gating_grads = lax.psum_scatter(gating_grads, "seq", scatter_dimension=0, tiled=True)
    gating_grads = gating_grads.reshape(2, own, rows_block)

    out_grad = cotangent.astype(jnp.float32)
    gain_two_term = jnp.sum(norm_two_grad * hidden * inverse_two, axis=0)
    hidden_grad = (
        out_grad
        + inverse_two * gains[1] * norm_two_grad
        - hidden
        * inverse_two**3
        * jnp.mean(hidden * gains[1] * norm_two_grad, axis=-1, keepdims=True)
    )
    branch_grad = hidden_grad.astype(jnp.bfloat16)
    context_grad = times_transpose(branch_grad, attn_weights[:, value_end:]).astype(jnp.bfloat16)
    fused = grp_count == 8 and seq_count * rows_here == SEQLEN
    if fused:
        feed_part = feed_part.reshape(grp_count, rows_here, MODEL_WIDTH)
        query_grad, pair_part, feed_out, down_plane = attend_back_sum(
            6, projected, pairs, context_grad, log_totals, key_segs, segment_ids, key_tables,
            tables, feed_part, down_grad,
        )
    else:
        query_grad, pair_part = attend_back(
            at, projected, pairs, context_grad, log_totals, key_segs, segment_ids, key_tables, tables
        )
        feed_out = lax.psum_scatter(
            feed_part.reshape(-1, MODEL_WIDTH), "grp", scatter_dimension=0, tiled=True
        )
        (down_plane,) = exchange(10, [(gather_plane(down_grad.shape), down_grad)])
    block_out = (hidden + feed_out.astype(jnp.float32)).astype(jnp.bfloat16)
    if seq_count * rows_here > SEQLEN:
        pair_part = lax.dynamic_update_slice_in_dim(
            jnp.zeros((seq_count * rows_here, 2 * HD), pair_part.dtype), pair_part, first_key, 0
        )
    pair_parts, query_share, branch_share = exchange(
        7,
        [
            split_rows("seq", pair_part),
            split_columns("grp", query_grad, placed=True),
            split_columns("grp", branch_grad, placed=True),
        ],
    )
    pair_grad = jnp.sum(pair_parts.astype(jnp.float32), axis=0).astype(jnp.bfloat16)
    shares = share_grad(
        query_share.reshape(-1, share_width),
        branch_share.reshape(-1, share_width),
        normed_plane,
        context_plane,
    )
    pair_weight_grad = contract(normed, pair_grad).astype(jnp.bfloat16)
    pair_blocks = pair_weight_grad.reshape(seq_count, grp_count, sub_rows, 2 * HD)
    if grp_count == 8:
        pair_blocks = jnp.transpose(pair_blocks, (1, 0, 2, 3))
        gating_plane, share_plane, pair_plane, gain_parts, input_grad = tail_exchange(
            8,
            shares,
            pair_blocks.reshape(grp_count, seq_count * sub_rows, 2 * HD),
            gating_grads,
            attn_weights,
            (query_grad, pair_grad, hidden_grad, tokens, inverse_one, gains, gain_two_term[None, :]),
        )
    else:
        projected_grad = jnp.concatenate([query_grad, pair_grad], axis=1)
        norm_one_grad = times_transpose(projected_grad, attn_weights[:, :value_end])
        gain_one_term = jnp.sum(norm_one_grad * tok_float * inverse_one, axis=0)
        input_grad = (
            hidden_grad
            + inverse_one * gains[0] * norm_one_grad
            - tok_float
            * inverse_one**3
            * jnp.mean(tok_float * gains[0] * norm_one_grad, axis=-1, keepdims=True)
        )
        gain_terms = jnp.stack([gain_one_term, gain_two_term])
        pair_task = Exchange(
            "grp",
            (grp_count, seq_count, sub_rows, 2 * HD),
            lambda ref, index: ref.at[:, index],
            block_of,
        )
        work = [
            split_columns("seq", shares),
            (pair_task, pair_blocks),
            gather_axis("seq", gain_terms),
            (gather_gating(gating_grads.shape), gating_grads),
        ]
        share_parts, pair_parts, gain_parts, gating_plane = exchange(8, work)
        gain_seq = jnp.sum(gain_parts, axis=0)
        shares = jnp.sum(share_parts.astype(jnp.float32), axis=0).astype(jnp.bfloat16)
        pair_parts = jnp.sum(pair_parts.astype(jnp.float32), axis=0).astype(jnp.bfloat16)
        pair_task = Exchange("seq", pair_parts.shape, block_of, block_of)
        _, pair_plane, share_plane, gain_parts = exchange(
            9,
            [
                (pair_task, pair_parts),
                (gather_plane(pair_parts.shape), 0),
                (gather_plane(shares.shape), shares),
                gather_axis("grp", gain_seq),
            ],
        )
        pair_plane = jnp.sum(pair_plane.astype(jnp.float32), axis=1).astype(jnp.bfloat16)

    gain_grads = jnp.sum(gain_parts, axis=0)

    tile_of_slot = (
        jnp.full((grp_count * slots_here,), tile_count, jnp.int32)
        .at[tile_owner_slots]
        .set(jnp.arange(tile_count, dtype=jnp.int32))
    )
    tiles_here = lax.dynamic_slice_in_dim(tile_of_slot, grp_here * slots_here, slots_here)
    feed_at = jnp.clip(tiles_here - attn_tiles, 0, 3 * hidden_tiles - 1)
    which, column = feed_at // hidden_tiles, feed_at % hidden_tiles
    is_query = tiles_here < query_tiles
    is_pair = (tiles_here >= query_tiles) & (tiles_here < query_tiles + 2)
    is_feed = tiles_here >= attn_tiles
    kind = jnp.where(is_feed, jnp.where(which < 2, 0, 1), jnp.where(is_pair, 3, 2))
    kind = jnp.where(tiles_here == tile_count, 4, kind)
    out_at = jnp.clip(tiles_here - query_tiles - 2, 0, query_tiles - 1)
    per_share = share_width // tile_width
    share_at = jnp.where(is_query, jnp.minimum(tiles_here, query_tiles - 1), out_at)
    at = jnp.stack(
        [
            kind,
            jnp.minimum(which, 1) * hidden_tiles + column,
            column,
            share_at // per_share * 2 * per_share
            + share_at % per_share
            + jnp.where(is_query, 0, per_share),
            jnp.where(is_pair, tiles_here - query_tiles, 0),
        ]
    )
    new_master, new_one, new_two = adam(
        at,
        gating_plane.reshape(-1, rows_block),
        down_plane.reshape(-1, rows_block),
        share_plane.reshape(-1, rows_block),
        pair_plane,
        left_basis_set,
        right_basis_set,
        master,
        moment_one,
        moment_two,
    )
    gain_one = BETA_ONE * gain_moment_one + (1.0 - BETA_ONE) * gain_grads
    gain_two = BETA_TWO * gain_moment_two + (1.0 - BETA_TWO) * gain_grads * gain_grads
    new_gains = gains - GAIN_RATE * gain_one / (jnp.sqrt(gain_two) + ADAM_EPS)
    return (
        block_out,
        input_grad,
        new_master,
        new_one,
        new_two,
        gain_grads,
        new_gains,
        gain_one,
        gain_two,
    )


def solution(mesh):
    return jax.shard_map(
        local,
        mesh=mesh,
        in_specs=(
            P(("grp", "seq"), None),
            P(("grp", "seq"), None),
            P(("grp", "seq")),
            P(),
            P("grp", "seq", None),
            P("grp", "seq", None),
            P("grp", "seq", None),
            P("grp", "seq", None),
            P("grp", "seq", None),
            P("grp", "seq", None),
            P(),
            P(),
            P(),
        ),
        out_specs=(
            P(("grp", "seq"), None),
            P(("grp", "seq"), None),
            P("grp", "seq", None),
            P("grp", "seq", None),
            P("grp", "seq", None),
            P(),
            P(),
            P(),
            P(),
        ),
        check_vma=False,
    )
```

```python
import functools
import math

import jax
import jax.numpy as jnp
from jax import lax
from jax.experimental import pallas as pl
from jax.experimental.pallas import tpu as pltpu
from jax.sharding import PartitionSpec as P

MODEL_WIDTH = 2048
NH = 16
HD = 128
FF = 5632
SEQLEN = 1024


NORM_EPS = 1e-05
BETA_ONE = 0.95
BETA_TWO = 0.95
ADAM_EPS = 1e-08
WEIGHT_DECAY = 0.01
LEARN_RATE = 0.03
GAIN_RATE = 1.5
ROPE_BASE = 10000.0
MASKED = -1e30
PRECISE = lax.Precision.HIGHEST


def contract(left_side, right_side):
    return lax.dot_general(
        left_side, right_side, (((0,), (0,)), ((), ())), preferred_element_type=jnp.float32
    )


def times_transpose(left_side, right_side):
    return lax.dot_general(
        left_side, right_side, (((1,), (1,)), ((), ())), preferred_element_type=jnp.float32
    )


def turn_tables(places):
    half_width = HD // 2
    frequency = ROPE_BASE ** (-(jnp.arange(half_width, dtype=jnp.float32) * 2.0) / HD)
    angles = places.astype(jnp.float32)[:, None] * frequency[None, :]
    cosine, sine = jnp.cos(angles), jnp.sin(angles)
    return (
        jnp.concatenate([cosine, cosine], axis=1),
        jnp.concatenate([-sine, sine], axis=1),
    )


def turn(rows, cosine, sine):
    return rows * cosine + pltpu.roll(rows, HD // 2, 1) * sine


def turn_back(rows, cosine, sine):
    return rows * cosine - pltpu.roll(rows, HD // 2, 1) * sine


def dot_last(left_side, right_side):
    return lax.dot_general(
        left_side, right_side, (((1,), (1,)), ((), ())), preferred_element_type=jnp.float32
    )


def dot_first(left_side, right_side):
    return lax.dot_general(
        left_side, right_side, (((0,), (0,)), ((), ())), preferred_element_type=jnp.float32
    )


SMALL_COST = pl.CostEstimate(flops=1, bytes_accessed=1, transcendentals=0)


def project_kernel(x_ref, w_ref, cosine_ref, sine_ref, out_ref):
    made = jnp.dot(x_ref[...], w_ref[...], preferred_element_type=jnp.float32)
    cosine, sine = cosine_ref[...], sine_ref[...]
    first, second = made[:, :HD], made[:, HD:]
    last = pl.program_id(0) == pl.num_programs(0) - 1
    out_ref[:, :HD] = turn(first, cosine, sine).astype(out_ref.dtype)
    out_ref[:, HD:] = jnp.where(last, second, turn(second, cosine, sine)).astype(out_ref.dtype)


def project(normed, weights, tables):
    rows, width = normed.shape
    steps = NH // 2 + 1
    return pl.pallas_call(
        project_kernel,
        grid=(steps,),
        in_specs=[
            pl.BlockSpec((rows, width), lambda j: (0, 0)),
            pl.BlockSpec((width, 2 * HD), lambda j: (0, j)),
            pl.BlockSpec((rows, HD), lambda j: (0, 0)),
            pl.BlockSpec((rows, HD), lambda j: (0, 0)),
        ],
        out_specs=pl.BlockSpec((rows, 2 * HD), lambda j: (0, j)),
        out_shape=jax.ShapeDtypeStruct((rows, steps * 2 * HD), jnp.bfloat16),
        compiler_params=pltpu.CompilerParams(vmem_limit_bytes=56 * 2**20),
        cost_estimate=SMALL_COST,
        name="project",
    )(normed, weights, *tables)


def score_mask(key_seg_ref, query_seg_ref, block, rows):
    keys = (block + 1) * rows
    same = key_seg_ref[:keys, :] == query_seg_ref[...]
    key_at = lax.broadcasted_iota(jnp.int32, (keys, rows), 0)
    query_at = lax.broadcasted_iota(jnp.int32, (keys, rows), 1) + block * rows
    return same & (key_at <= query_at)


def attend_kernel(at_ref, q_ref, k_ref, v_ref, key_seg_ref, query_seg_ref, context_ref, total_ref):
    scale = HD ** (-0.5)
    rows = q_ref.shape[0]
    for block in range(SEQLEN // rows):

        @pl.when(at_ref[0] == block)
        def _():
            keys = (block + 1) * rows
            scores = dot_last(k_ref[:keys, :], q_ref[...]) * scale
            scores = jnp.where(
                score_mask(key_seg_ref, query_seg_ref, block, rows), scores, MASKED
            )
            highest = jnp.max(scores, axis=0, keepdims=True)
            exponent = jnp.exp(scores - highest)
            totals = jnp.sum(exponent, axis=0, keepdims=True)
            probs_low = (exponent * (1.0 / totals)).astype(jnp.bfloat16)
            context = dot_first(probs_low, v_ref[:keys, :])
            context_ref[...] = context.astype(jnp.bfloat16)
            total_ref[0] = highest + jnp.log(totals)


def attend_back_head(
    place, q_ref, k_ref, v_ref, grad_ref, total_ref, key_seg_ref, query_seg_ref, key_cosine_ref,
    key_sine_ref, cosine_ref, sine_ref, query_grad_ref, pair_grad_ref, key_sum, value_sum,
):
    scale = HD ** (-0.5)
    rows = q_ref.shape[0]
    head = pl.program_id(0)

    @pl.when(head == 0)
    def _():
        key_sum[...] = jnp.zeros_like(key_sum)
        value_sum[...] = jnp.zeros_like(value_sum)

    for block in range(SEQLEN // rows):

        @pl.when(place == block)
        def _():
            keys = (block + 1) * rows
            queries, grads = q_ref[...], grad_ref[...]
            shifted = dot_last(k_ref[:keys, :], queries) * scale - total_ref[0]
            allowed = score_mask(key_seg_ref, query_seg_ref, block, rows)
            probs = jnp.where(allowed, jnp.exp(shifted), 0.0)
            prob_grad = dot_last(v_ref[:keys, :], grads)
            centre = jnp.sum(probs * prob_grad, axis=0, keepdims=True)
            score_grad = (probs * (prob_grad - centre) * scale).astype(jnp.bfloat16)
            value_sum[:keys, :] += jnp.dot(
                probs.astype(jnp.bfloat16), grads, preferred_element_type=jnp.float32
            )
            key_sum[:keys, :] += jnp.dot(score_grad, queries, preferred_element_type=jnp.float32)
            query_grad = dot_first(score_grad, k_ref[:keys, :])
            query_grad_ref[...] = turn_back(query_grad, cosine_ref[...], sine_ref[...]).astype(
                jnp.bfloat16
            )

    @pl.when(head == pl.num_programs(0) - 1)
    def _():
        pair_grad_ref[:, :HD] = turn_back(
            key_sum[...], key_cosine_ref[...], key_sine_ref[...]
        ).astype(jnp.bfloat16)
        pair_grad_ref[:, HD:] = value_sum[...].astype(jnp.bfloat16)


def attend_back_kernel(at_ref, *refs):
    attend_back_head(at_ref[0], *refs)


def attention_specs(kinds, rows):
    specs = {
        "at": pl.BlockSpec(memory_space=pltpu.SMEM),
        "head": pl.BlockSpec((rows, HD), lambda h: (0, h)),
        "branch": pl.BlockSpec((rows, MODEL_WIDTH), lambda h: (0, 0)),
        "keys": pl.BlockSpec((SEQLEN, HD), lambda h: (0, 0)),
        "values": pl.BlockSpec((SEQLEN, HD), lambda h: (0, 1)),
        "pair": pl.BlockSpec((SEQLEN, 2 * HD), lambda h: (0, 0)),
        "total": pl.BlockSpec((1, 1, rows), lambda h: (h, 0, 0)),
        "key_seg": pl.BlockSpec((SEQLEN, 1), lambda h: (0, 0)),
        "query_seg": pl.BlockSpec((1, rows), lambda h: (0, 0)),
        "key_table": pl.BlockSpec((SEQLEN, HD), lambda h: (0, 0)),
        "table": pl.BlockSpec((rows, HD), lambda h: (0, 0)),
    }
    return [specs[kind] for kind in kinds]


def attend(at, projected, pairs, key_segs, query_segs):
    rows = projected.shape[0]
    columns = NH * HD
    return pl.pallas_call(
        attend_kernel,
        grid=(NH,),
        in_specs=attention_specs(["at", "head", "keys", "values", "key_seg", "query_seg"], rows),
        out_specs=attention_specs(["head", "total"], rows),
        out_shape=(
            jax.ShapeDtypeStruct((rows, columns), jnp.bfloat16),
            jax.ShapeDtypeStruct((NH, 1, rows), jnp.float32),
        ),
        compiler_params=pltpu.CompilerParams(vmem_limit_bytes=32 * 2**20),
        cost_estimate=SMALL_COST,
        name="attend",
    )(at, projected, pairs, pairs, key_segs[:, None], query_segs[None, :])


def attend_back(at, projected, pairs, grads, totals, key_segs, query_segs, key_tables, tables):
    rows = projected.shape[0]
    columns = NH * HD
    return pl.pallas_call(
        attend_back_kernel,
        grid=(NH,),
        in_specs=attention_specs(
            ["at", "head", "keys", "values", "head", "total", "key_seg", "query_seg"]
            + ["key_table", "key_table", "table", "table"],
            rows,
        ),
        out_specs=attention_specs(["head", "pair"], rows),
        out_shape=(
            jax.ShapeDtypeStruct((rows, columns), jnp.bfloat16),
            jax.ShapeDtypeStruct((SEQLEN, 2 * HD), jnp.bfloat16),
        ),
        scratch_shapes=[pltpu.VMEM((SEQLEN, HD), jnp.float32)] * 2,
        compiler_params=pltpu.CompilerParams(vmem_limit_bytes=32 * 2**20),
        cost_estimate=SMALL_COST,
        name="attend_back",
    )(
        at, projected, pairs, pairs, grads, totals, key_segs[:, None], query_segs[None, :],
        *key_tables, *tables,
    )


def own_columns(grp, own):
    return pl.ds(pl.multiple_of((grp * own) % 128, math.gcd(own, 128)), own)


def load_weights(parts, weights, sems):
    count, rows, _ = parts[0].shape
    halves = len(parts)
    return [
        pltpu.make_async_copy(
            parts[half].at[block],
            weights.at[pl.ds((block * halves + half) * rows, rows)],
            sems.at[block * halves + half],
        )
        for half in range(halves)
        for block in range(count)
    ]


def feed_block(own, first, x, cot, weights, act_ref, gate_grad_ref, up_grad_ref, two_ref, out_ref):
    low = jnp.bfloat16
    wide = jnp.float32
    cols = act_ref.shape[0]
    gate = jnp.dot(x, weights[:, :cols], preferred_element_type=wide)
    upper = jnp.dot(x, weights[:, cols : 2 * cols], preferred_element_type=wide)
    act_grad = jnp.dot(cot, weights[:, 2 * cols :], preferred_element_type=wide)
    column = lax.broadcasted_iota(jnp.int32, gate.shape, 1)
    real = (column >= first) & (column < first + own)
    sigmoid = 1.0 / (1.0 + jnp.exp(-gate))
    silu = gate * sigmoid
    activated = jnp.where(real, silu * upper, 0.0).astype(low)
    act_grad = jnp.where(real, act_grad, 0.0)
    gate_grad = (act_grad * upper * sigmoid * (1.0 + gate * (1.0 - sigmoid))).astype(low)
    up_grad = (act_grad * silu).astype(low)
    act_ref[...] = jnp.transpose(activated)
    gate_grad_ref[...] = jnp.transpose(gate_grad)
    up_grad_ref[...] = jnp.transpose(up_grad)
    two = dot_last(gate_grad, weights[:, :cols]) + dot_last(up_grad, weights[:, cols : 2 * cols])
    two_ref[...] = two.astype(low)
    out_ref[...] = dot_last(activated, weights[:, 2 * cols :]).astype(low)


def feed_kernel(own, real_ref, x_ref, cot_ref, *refs):
    parts, refs = refs[:-7], refs[-7:]
    weights, sems = refs[5:]

    @pl.when(pl.program_id(0) == 0)
    def _():
        copies = load_weights(parts, weights, sems)
        for copy in copies:
            copy.start()
        for copy in copies:
            copy.wait()

    feed_block(own, real_ref[0], x_ref[...], cot_ref[...], weights, *refs[:5])


def feed_forward(own, real_cols, x, cot, parts, seq_count):
    tokens_all, width = x.shape
    _, rows, cols = parts[0].shape
    cols = cols // 3
    step = 256
    low = jnp.bfloat16
    block = pl.BlockSpec((step, width), lambda i: (i, 0))
    narrow = pl.BlockSpec((cols, step), lambda i: (0, i))
    return pl.pallas_call(
        functools.partial(feed_kernel, own),
        grid=(tokens_all // step,),
        in_specs=[pl.BlockSpec(memory_space=pltpu.SMEM), block, block]
        + [pl.BlockSpec(memory_space=pl.ANY)] * len(parts),
        out_specs=[narrow, narrow, narrow, block, block],
        out_shape=[jax.ShapeDtypeStruct((cols, tokens_all), low)] * 3
        + [jax.ShapeDtypeStruct((tokens_all, width), low)] * 2,
        scratch_shapes=[
            pltpu.VMEM((width, 3 * cols), low),
            pltpu.SemaphoreType.DMA((len(parts) * seq_count,)),
        ],
        compiler_params=pltpu.CompilerParams(vmem_limit_bytes=52 * 2**20),
        cost_estimate=SMALL_COST,
        name="feed_forward",
    )(real_cols, x, cot, *parts)


def feed_gather_kernel(
    own, first, second, halves, real_ref, own_ref, context_ref, cot_ref, cot_all_ref, *refs
):
    parts, refs = refs[:halves], refs[halves:]
    (
        gate_grad_ref, up_grad_ref, two_ref, out_ref, second_ref, context_plane_ref, down_out,
        blocks, weights, act_block, act, x_block, stage, load_sems, keep_sems, x_sems, out_sems,
        first_send, first_recv, second_send, second_recv,
    ) = refs
    step = pl.program_id(0)
    grp, seq = lax.axis_index("grp"), lax.axis_index("seq")
    first.start(own_ref, blocks, (first_send, first_recv), grp, seq, begin=False)
    second.start(context_ref, context_plane_ref, (second_send, second_recv), grp, seq, begin=False)
    loads = load_weights(parts, weights, load_sems)
    cols = act.shape[0]
    step_rows = act_block.shape[1]
    rows = x_block.shape[2]
    count = cot_all_ref.shape[1] // rows

    @pl.when(step == 0)
    def _():
        for copy in loads:
            copy.start()
        barrier = pltpu.get_barrier_semaphore()
        for device in first.peers(grp, seq):
            pl.semaphore_signal(barrier, inc=1, device_id=device, device_id_type=MESH)
        pl.semaphore_wait(barrier, 3)
        first.begin()
        first.kept.wait()
        for copy in loads:
            copy.wait()

    @pl.when(step == 1)
    def _():
        first.due[7].wait_recv()

    @pl.when(step == 2)
    def _():
        for came in (1, 4, 2):
            first.pass_on(came)

    @pl.when(step == 3)
    def _():
        first.pass_on(5)

    @pl.when(step == 4)
    def _():
        first.due[8].wait_recv()
        first.due[9].wait_recv()
        first.pass_on(6)
        first.pass_on(3)
        second.begin()

    @pl.when(step == 5)
    def _():
        first.due[10].wait_recv()
        first.due[11].wait_recv()

    @pl.when(step == 7)
    def _():
        first.due[12].wait_recv()
        first.due[13].wait_recv()
        second.pass_on(1)
        second.pass_on(4)

    keep = pltpu.make_async_copy(blocks.at[step], second_ref.at[step], keep_sems.at[step])
    keep.start()
    feed_block(
        own, real_ref[0], blocks[step], cot_ref[...], weights, act_block, gate_grad_ref, up_grad_ref,
        two_ref, out_ref,
    )
    act[:, pl.ds(pl.multiple_of(step * step_rows, step_rows), step_rows)] = act_block[...]

    def x_copy(at):
        view = cot_all_ref.at[:, pl.ds(pl.multiple_of(at * rows, rows), rows)]
        return pltpu.make_async_copy(view, x_block.at[at % 2], x_sems.at[at % 2])

    def out_copy(at):
        place = pl.ds(pl.multiple_of(at * own, own), own)
        mine = stage.at[at % 2, own_columns(grp, own)]
        return pltpu.make_async_copy(mine, down_out.at[place], out_sems.at[at % 2])

    @pl.when(step == 7)
    def _():
        x_copy(0).start()
        second.pass_on(2)
        second.pass_on(5)

        def one(at, _):
            @pl.when(at == 2)
            def _():
                second.pass_on(6)
                second.pass_on(3)

            x_copy(at).wait()

            @pl.when(at + 1 < count)
            def _():
                x_copy(at + 1).start()

            @pl.when(at >= 2)
            def _():
                out_copy(at - 2).wait()

            stage[at % 2] = jnp.dot(
                act[...], x_block[at % 2], preferred_element_type=jnp.float32
            ).astype(stage.dtype)
            out_copy(at).start()
            return 0

        lax.fori_loop(0, count, one, 0)
        out_copy(count - 2).wait()
        out_copy(count - 1).wait()
        second.finish()
        for copy in first.out[1:]:
            copy.wait_send()
        for at in range(8):
            pltpu.make_async_copy(blocks.at[at], second_ref.at[at], keep_sems.at[at]).wait()


def feed_gather(number, own, real_cols, normed, context, cot, parts, seq_count):
    rows, width = normed.shape
    cols = parts[0].shape[2] // 3
    low = jnp.bfloat16
    block = pl.BlockSpec((rows, width), lambda i: (i, 0))
    narrow = pl.BlockSpec((cols, rows), lambda i: (0, i))
    first = gather_plane(normed.shape, placed=True)
    second = gather_plane(context.shape, placed=True)
    hbm = pl.BlockSpec(memory_space=pl.ANY)
    plane = jax.ShapeDtypeStruct((8, rows, width), low)
    model_rows = width // seq_count
    return pl.pallas_call(
        functools.partial(feed_gather_kernel, own, first, second, len(parts)),
        grid=(8,),
        in_specs=[pl.BlockSpec(memory_space=pltpu.SMEM), hbm, hbm, block, hbm]
        + [hbm] * len(parts),
        out_specs=[narrow, narrow, block, block, hbm, hbm, hbm],
        out_shape=[jax.ShapeDtypeStruct((cols, 8 * rows), low)] * 2
        + [jax.ShapeDtypeStruct((8 * rows, width), low)] * 2
        + [plane, plane, jax.ShapeDtypeStruct((seq_count * own, model_rows), low)],
        scratch_shapes=[
            pltpu.VMEM((8, rows, width), low),
            pltpu.VMEM((width, 3 * cols), low),
            pltpu.VMEM((cols, rows), low),
            pltpu.VMEM((cols, 8 * rows), low),
            pltpu.VMEM((2, 8 * rows, model_rows), low),
            pltpu.VMEM((2, cols, model_rows), low),
            pltpu.SemaphoreType.DMA((seq_count * len(parts),)),
            pltpu.SemaphoreType.DMA((8,)),
            pltpu.SemaphoreType.DMA((2,)),
            pltpu.SemaphoreType.DMA((2,)),
        ]
        + [pltpu.SemaphoreType.DMA((14,))] * 4,
        compiler_params=pltpu.CompilerParams(
            collective_id=number, has_side_effects=True, vmem_limit_bytes=60 * 2**20
        ),
        cost_estimate=SMALL_COST,
        name="feed_gather",
    )(real_cols, normed, context, cot, cot, *parts)


def weight_grad_kernel(left_ref, x_ref, out_ref):
    out_ref[...] = jnp.dot(
        left_ref[...], x_ref[...], preferred_element_type=jnp.float32
    ).astype(out_ref.dtype)


def weight_grad(left, x, seq_count):
    cols, tokens_all = left.shape
    rows = x.shape[1] // seq_count
    return pl.pallas_call(
        weight_grad_kernel,
        grid=(seq_count,),
        in_specs=[
            pl.BlockSpec((cols, tokens_all), lambda i: (0, 0)),
            pl.BlockSpec((tokens_all, rows), lambda i: (0, i)),
        ],
        out_specs=pl.BlockSpec((cols, rows), lambda i: (i, 0)),
        out_shape=jax.ShapeDtypeStruct((seq_count * cols, rows), jnp.bfloat16),
        compiler_params=pltpu.CompilerParams(vmem_limit_bytes=40 * 2**20),
        cost_estimate=SMALL_COST,
        name="weight_grad",
    )(left, x)


def share_grad_kernel(query_ref, out_ref, normed_ref, context_ref, grads_ref, turned):
    half = query_ref.shape[1]

    @pl.when(pl.program_id(0) == 0)
    def _():
        turned[0], turned[1] = jnp.transpose(query_ref[...]), jnp.transpose(out_ref[...])

    for at, right in enumerate((normed_ref, context_ref)):
        made = jnp.dot(turned[at], right[...], preferred_element_type=jnp.float32)
        grads_ref[at * half : (at + 1) * half, :] = made.astype(grads_ref.dtype)


def share_grad(query_share, out_share, normed, context):
    tokens_all, width = normed.shape
    columns = query_share.shape[1]
    step = 512
    narrow = pl.BlockSpec((tokens_all, columns), lambda i: (0, 0))
    block = pl.BlockSpec((tokens_all, step), lambda i: (0, i))
    return pl.pallas_call(
        share_grad_kernel,
        grid=(width // step,),
        in_specs=[narrow, narrow, block, block],
        out_specs=pl.BlockSpec((2 * columns, step), lambda i: (0, i)),
        out_shape=jax.ShapeDtypeStruct((2 * columns, width), jnp.bfloat16),
        scratch_shapes=[pltpu.VMEM((2, columns, tokens_all), jnp.bfloat16)],
        compiler_params=pltpu.CompilerParams(vmem_limit_bytes=60 * 2**20),
        cost_estimate=SMALL_COST,
        name="share_grad",
    )(query_share, out_share, normed, context)


def pick_kernel(rows, feed_ref, attn_ref, tiles_ref, feed_out, attn_out, sems):
    grp = lax.axis_index("grp")
    width = tiles_ref.shape[2]
    copies = []
    for at in range(feed_ref.shape[0]):
        copies.append(
            (tiles_ref.at[feed_ref[at]], feed_out.at[:, at * width : (at + 1) * width])
        )
    share = pl.ds(pl.multiple_of(grp * rows, rows), rows)
    for at in range(attn_ref.shape[0]):
        copies.append(
            (tiles_ref.at[attn_ref[at], share], attn_out.at[:, at * width : (at + 1) * width])
        )
    copies = [
        pltpu.make_async_copy(source, target, sems.at[at])
        for at, (source, target) in enumerate(copies)
    ]
    for copy in copies:
        copy.start()
    for copy in copies:
        copy.wait()


def pick(tiles, feed_slots, attn_slots):
    _, rows, width = tiles.shape
    share = rows // lax.axis_size("grp")
    feed, attn = feed_slots.shape[0], attn_slots.shape[0]
    return pl.pallas_call(
        functools.partial(pick_kernel, share),
        in_specs=[pl.BlockSpec(memory_space=pltpu.SMEM)] * 2 + [pl.BlockSpec(memory_space=pl.ANY)],
        out_specs=[pl.BlockSpec(memory_space=pltpu.VMEM)] * 2,
        out_shape=[
            jax.ShapeDtypeStruct((rows, feed * width), tiles.dtype),
            jax.ShapeDtypeStruct((share, attn * width), tiles.dtype),
        ],
        scratch_shapes=[pltpu.SemaphoreType.DMA((feed + attn,))],
        cost_estimate=SMALL_COST,
        name="pick",
    )(feed_slots, attn_slots, tiles)


def adam_kernel(group, at_ref, *refs):
    feeds = [refs[at * group : (at + 1) * group] for at in range(4)]
    left_ref, right_ref, master_ref, one_ref, two_ref = refs[4 * group : 4 * group + 5]
    new_master_ref, new_one_ref, new_two_ref, grad = refs[4 * group + 5 :]
    low = jnp.bfloat16
    for slot in range(group):
        kind = at_ref[0, pl.program_id(0) * group + slot]
        for number in range(3):

            @pl.when(kind == number)
            def _():
                grad[slot] = feeds[number][slot][...]

        @pl.when(kind == 3)
        def _():
            pair = feeds[3][slot][...].reshape(grad.shape[2], grad.shape[1])
            grad[slot] = jnp.transpose(pair.astype(jnp.float32)).astype(grad.dtype)

        @pl.when(kind == 4)
        def _():
            grad[slot] = jnp.zeros(grad.shape[1:], grad.dtype)

    slots = range(group)
    left = [left_ref[slot].astype(low) for slot in slots]
    right = [right_ref[slot].astype(low) for slot in slots]
    turned = [
        jnp.dot(grad[slot], left[slot], preferred_element_type=jnp.float32) for slot in slots
    ]
    turned = [dot_first(turned[slot].astype(low), right[slot]) for slot in slots]
    scaled = []
    for slot in slots:
        new_one = BETA_ONE * one_ref[slot] + (1.0 - BETA_ONE) * turned[slot]
        new_two = BETA_TWO * two_ref[slot] + (1.0 - BETA_TWO) * turned[slot] * turned[slot]
        new_one_ref[slot], new_two_ref[slot] = new_one, new_two
        scaled.append((new_one / (jnp.sqrt(new_two) + ADAM_EPS)).astype(low))
    restored = [dot_last(scaled[slot], right[slot]).astype(low) for slot in slots]
    restored = [
        jnp.dot(left[slot], restored[slot], preferred_element_type=jnp.float32) for slot in slots
    ]
    for slot in slots:
        new_master_ref[slot] = (
            master_ref[slot] * (1.0 - LEARN_RATE * WEIGHT_DECAY) - LEARN_RATE * restored[slot]
        )


def adam(at, gating, down, shares, pairs, left, right, master, one, two):
    slots, rows, width = master.shape
    group = 3 if slots % 3 == 0 else 1
    tile = pl.BlockSpec((group, rows, width), lambda i, at: (i, 0, 0))
    shape = jax.ShapeDtypeStruct(master.shape, jnp.float32)

    def feed(row):
        return [
            pl.BlockSpec((width, rows), lambda i, at, slot=slot: (at[row, i * group + slot], 0))
            for slot in range(group)
        ]

    pair = [
        pl.BlockSpec(
            (*pairs.shape[:2], width), lambda i, at, slot=slot: (0, 0, at[4, i * group + slot])
        )
        for slot in range(group)
    ]
    return pl.pallas_call(
        functools.partial(adam_kernel, group),
        grid_spec=pltpu.PrefetchScalarGridSpec(
            num_scalar_prefetch=1,
            grid=(slots // group,),
            in_specs=feed(1)
            + feed(2)
            + feed(3)
            + pair
            + [
                pl.BlockSpec((group, rows, rows), lambda i, at: (i, 0, 0)),
                pl.BlockSpec((group, width, width), lambda i, at: (i, 0, 0)),
                tile,
                tile,
                tile,
            ],
            out_specs=[tile] * 3,
            scratch_shapes=[pltpu.VMEM((group, width, rows), jnp.bfloat16)],
        ),
        out_shape=[shape] * 3,
        compiler_params=pltpu.CompilerParams(vmem_limit_bytes=60 * 2**20),
        cost_estimate=SMALL_COST,
        name="adam",
    )(
        at, *[gating] * group, *[down] * group, *[shares] * group, *[pairs] * group,
        left, right, master, one, two,
    )


MESH = pl.DeviceIdType.MESH


def remote(source, target, sems, at, device):
    return pltpu.make_async_remote_copy(
        src_ref=source,
        dst_ref=target,
        send_sem=sems[0].at[at],
        recv_sem=sems[1].at[at],
        device_id=device,
        device_id_type=MESH,
    )


def columns_of(ref, index, width):
    return ref.at[:, pl.ds(pl.multiple_of(index * width, width), width)]


def rows_of(ref, index, height):
    return ref.at[pl.ds(pl.multiple_of(index * height, height), height), :]


PLACES = {0: 0, 1: 1, 2: 2, 4: 3, 3: 4, 5: 5, 6: 6, 7: 7}


def flip(device, bits):
    core, side_x, side_y = device % 2, (device // 2) % 2, device // 4
    for bit, there in ((1, 1 - 2 * core), (2, 2 - 4 * side_x), (4, 4 - 8 * side_y)):
        if bits & bit:
            device = device + there
    return device


class PlacedExchange:
    axis = "grp"
    sem_count = 8

    def __init__(self, out_shape, source_view):
        self.out_shape, self.source_view = out_shape, source_view

    def peers(self, grp, seq):
        for bits in range(1, 8):
            yield flip(grp, bits), seq

    def start(self, source, target, sems, grp, seq):
        self.own = pltpu.make_async_copy(
            self.source_view(source, grp), target.at[0], sems[0].at[0]
        )
        self.own.start()
        self.copies = []
        for bits in range(1, 8):
            there = flip(grp, bits)
            copy = remote(
                self.source_view(source, there), target.at[PLACES[bits]], sems, bits, (there, seq)
            )
            copy.start()
            self.copies.append(copy)

    def forward(self):
        return iter(())

    def finish(self):
        for copy in self.copies:
            copy.wait()
        self.own.wait()


class Exchange:
    def __init__(self, axis, out_shape, source_view, target_view):
        self.axis, self.out_shape = axis, out_shape
        self.source_view, self.target_view = source_view, target_view
        self.count = lax.axis_size(axis)
        self.sem_count = self.count

    def peers(self, grp, seq):
        me = grp if self.axis == "grp" else seq
        for step in range(1, self.count):
            there = (me + step) % self.count
            yield (there, seq) if self.axis == "grp" else (grp, there)

    def start(self, source, target, sems, grp, seq, begin=True):
        me = grp if self.axis == "grp" else seq
        self.own = pltpu.make_async_copy(
            self.source_view(source, me), self.target_view(target, me), sems[0].at[0]
        )
        self.sent, self.due = [], []
        for step, device in enumerate(self.peers(grp, seq), 1):
            there = (me + step) % self.count
            back = (me + self.count - step) % self.count
            self.sent.append(
                remote(
                    self.source_view(source, there), self.target_view(target, me), sems, step, device
                )
            )
            self.due.append(
                remote(
                    self.source_view(source, back), self.target_view(target, back), sems, step, device
                )
            )
        if begin:
            self.begin()

    def begin(self):
        for copy in [self.own] + self.sent:
            copy.start()

    def forward(self):
        return iter(())

    def finish(self):
        for copy in self.due:
            copy.wait_recv()
        for copy in self.sent:
            copy.wait_send()
        self.own.wait()


class PlaneGather:
    axis = "grp"
    sem_count = 14

    def __init__(self, out_shape, source_view, target_view, half_of, placed):
        self.out_shape, self.placed = out_shape, placed
        self.source_view, self.target_view, self.half_of = source_view, target_view, half_of

    def peers(self, grp, seq):
        for bits in (1, 2, 4):
            yield flip(grp, bits), seq

    def start(self, source, target, sems, grp, seq, begin=True):
        def part(device, bits, piece):
            view = self.target_view(target, PLACES[bits] if self.placed else flip(device, bits))
            return view if piece == "all" else self.half_of(view, piece == "b")

        def own(piece):
            view = self.source_view(source, grp)
            return view if piece == "all" else self.half_of(view, piece == "b")

        self.out, self.due = [None], [None]
        for via, here, there, piece in (
            (2, 0, 2, "a"),
            (2, 0, 2, "b"),
            (2, 4, 6, "b"),
            (4, 0, 4, "b"),
            (4, 0, 4, "a"),
            (4, 2, 6, "a"),
            (1, 0, 1, "all"),
            (1, 2, 3, "a"),
            (1, 2, 3, "b"),
            (1, 4, 5, "b"),
            (1, 4, 5, "a"),
            (1, 6, 7, "a"),
            (1, 6, 7, "b"),
        ):
            device = flip(grp, via)
            view = own(piece) if here == 0 else part(grp, here, piece)
            at = len(self.out)
            self.out.append(remote(view, part(device, there, piece), sems, at, (device, seq)))
            self.due.append(remote(view, part(grp, there, piece), sems, at, (device, seq)))
        self.kept = pltpu.make_async_copy(own("all"), part(grp, 0, "all"), sems[0].at[0])
        if begin:
            self.begin()

    def begin(self):
        self.kept.start()
        for at in (1, 4, 2, 5, 7):
            self.out[at].start()

    def pass_on(self, came):
        self.due[came].wait_recv()
        for at in {1: (6, 8), 4: (3, 10), 2: (9,), 5: (11,), 6: (12,), 3: (13,)}[came]:
            self.out[at].start()

    def forward(self):
        for pair in ((1, 4), (2, 5), (6, 3)):
            for came in pair:
                self.pass_on(came)
            yield

    def finish(self):
        for copy in self.due[7:]:
            copy.wait_recv()
        for copy in self.out[1:]:
            copy.wait_send()
        self.kept.wait()


def add_rows(total, first, second):
    step = 32

    def some(at, _):
        rows = pl.ds(pl.multiple_of(at * step, step), step)
        total[rows, :] = (
            first[rows, :].astype(jnp.float32) + second[rows, :].astype(jnp.float32)
        ).astype(total.dtype)
        return 0

    lax.fori_loop(0, total.shape[0] // step, some, 0)


class PlaneSum:
    axis = "grp"
    sem_count = 15

    def __init__(self, rows, columns, placed=True):
        self.rows, self.columns, self.placed = rows, columns, placed
        self.out_shape = (rows, columns)

    def scratch(self):
        low = jnp.bfloat16
        shape = (self.rows, self.columns)
        half = (self.rows // 2, self.columns)
        return [
            pltpu.VMEM((4, *shape), low),
            pltpu.VMEM((4, *shape), low),
            pltpu.VMEM((2, *half), low),
            pltpu.VMEM((2, *shape), low),
        ]

    def peers(self, grp, seq):
        for bits in (1, 2, 4):
            yield flip(grp, bits), seq

    def start(self, source, target, sems, grp, seq, scratch, begin=True):
        self.mine, self.core_in, self.halves, self.wholes = scratch
        core, side_x, side_y = [(flip(grp, bits), seq) for bits in (1, 2, 4)]
        half = self.rows // 2
        self.low, self.high = low, high = pl.ds(0, half), pl.ds(half, half)
        mine, halves, wholes = self.mine, self.halves, self.wholes

        def block(bits):
            return source.at[PLACES[bits] if self.placed else flip(grp, bits)]

        self.copies = [
            remote(block(bits), self.core_in.at[at], sems, at, core)
            for at, bits in enumerate((7, 3, 5, 1))
        ] + [
            remote(mine.at[0, low], halves.at[0], sems, 4, side_x),
            remote(mine.at[0, high], halves.at[1], sems, 5, side_y),
            remote(mine.at[1, low], wholes.at[0, low], sems, 6, side_x),
            remote(mine.at[2, high], wholes.at[1, high], sems, 7, side_y),
            remote(mine.at[1, high], wholes.at[0, high], sems, 8, side_x),
            remote(mine.at[2, low], wholes.at[1, low], sems, 9, side_y),
        ]
        self.loads = [
            pltpu.make_async_copy(block(bits), mine.at[at], sems[0].at[10 + at])
            for at, bits in enumerate((6, 2, 4, 0))
        ]
        if target is not None:
            self.store = pltpu.make_async_copy(mine.at[3], target, sems[0].at[14])
        if begin:
            self.begin()

    def begin(self):
        for copy in self.copies[:4] + self.loads:
            copy.start()

    def first_sums(self):
        for came, then in ((0, (4, 5)), (1, (6,)), (2, (7,)), (3, ())):
            self.copies[came].wait_recv()
            self.loads[came].wait()
            add_rows(self.mine.at[came], self.mine.at[came], self.core_in.at[came])
            for at in then:
                self.copies[at].start()

    def forward(self):
        mine, low, high = self.mine, self.low, self.high
        yield
        self.copies[5].wait_recv()
        add_rows(mine.at[1, high], mine.at[1, high], self.halves.at[1])
        self.copies[8].start()
        self.copies[4].wait_recv()
        add_rows(mine.at[2, low], mine.at[2, low], self.halves.at[0])
        self.copies[9].start()

    def total(self):
        mine = self.mine
        for at, side, rows in ((6, 0, self.low), (7, 1, self.high), (8, 0, self.high), (9, 1, self.low)):
            self.copies[at].wait_recv()
            add_rows(mine.at[3, rows], mine.at[3, rows], self.wholes.at[side, rows])
        return mine.at[3]

    def finish(self):
        self.total()
        self.store.start()
        for copy in self.copies:
            copy.wait_send()
        self.store.wait()


class LineGather:
    axis = "seq"

    def __init__(self, shape):
        self.count = lax.axis_size("seq")
        self.out_shape = (self.count, *shape)
        self.sem_count = 2 * self.count

    def peers(self, grp, seq):
        for step in range(1, self.count):
            yield grp, (seq + step) % self.count

    def start(self, source, target, sems, grp, seq):
        self.seq, self.sems = seq, sems
        self.own = pltpu.make_async_copy(source, target.at[seq], sems[0].at[0])
        self.own.start()

        def make(away, up):
            there = (seq + (1 if up else self.count - 1)) % self.count
            block = (seq + (self.count - away if up else away)) % self.count
            view = source if away == 0 else target.at[block]
            at = 1 + away if up else self.count + away
            return remote(view, target.at[block], sems, at, (grp, there))

        def came(away, up):
            block = (seq + (self.count - away if up else away)) % self.count
            at = away if up else self.count + away - 1
            side = (seq + (self.count - 1 if up else 1)) % self.count
            return remote(target.at[block], target.at[block], sems, at, (grp, side))

        self.make, self.came = make, came
        self.has = lambda away, up: (seq - away >= 0) if up else (seq + away < self.count)
        self.last = lambda up: (seq + 1 < self.count) if up else (seq >= 1)
        for up in (True, False):

            @pl.when(self.last(up))
            def _():
                make(0, up).start()

    def forward(self):
        for away in range(1, self.count):
            for up in (True, False):

                @pl.when(self.has(away, up))
                def _():
                    self.came(away, up).wait_recv()
                    if away < self.count - 1:

                        @pl.when(self.last(up))
                        def _():
                            self.make(away, up).start()

            yield

    def finish(self):
        for away in range(self.count - 1):
            for up in (True, False):

                @pl.when(self.has(away, up) & self.last(up))
                def _():
                    self.make(away, up).wait_send()
        self.own.wait()


def attend_back_sum_kernel(
    sum_task, gather_task, q_ref, k_ref, v_ref, branch_ref, total_ref, key_seg_ref, query_seg_ref,
    key_cosine_ref, key_sine_ref, cosine_ref, sine_ref, part_hbm, down_hbm, weights_hbm,
    query_grad_ref, pair_grad_ref, sum_hbm, down_plane, key_sum, value_sum, grad_ref, w_block,
    w_sems, mine, core_in, halves, wholes, sum_send, sum_recv, gather_send, gather_recv,
):
    step = pl.program_id(0)
    grp, seq = lax.axis_index("grp"), lax.axis_index("seq")
    scratch = (mine, core_in, halves, wholes)
    sum_task.start(part_hbm, sum_hbm, (sum_send, sum_recv), grp, seq, scratch, begin=False)
    gather_task.start(down_hbm, down_plane, (gather_send, gather_recv), grp, seq, begin=False)

    def w_copy(at):
        rows = pl.ds(pl.multiple_of(at * HD, HD), HD)
        view = weights_hbm.at[rows, pl.ds((NH + 2) * HD, MODEL_WIDTH)]
        return pltpu.make_async_copy(view, w_block.at[at % 2], w_sems.at[at % 2])

    @pl.when(step == 0)
    def _():
        w_copy(step).start()
        barrier = pltpu.get_barrier_semaphore()
        for device in sum_task.peers(grp, seq):
            pl.semaphore_signal(barrier, inc=1, device_id=device, device_id_type=MESH)
        pl.semaphore_wait(barrier, 3)
        sum_task.begin()
        gather_task.begin()

    @pl.when(step == 6)
    def _():
        sum_task.first_sums()

    w_copy(step).wait()

    @pl.when(step + 1 < pl.num_programs(0))
    def _():
        w_copy(step + 1).start()

    grad_ref[...] = dot_last(branch_ref[...], w_block[step % 2]).astype(grad_ref.dtype)
    attend_back_head(
        seq, q_ref, k_ref, v_ref, grad_ref, total_ref, key_seg_ref, query_seg_ref, key_cosine_ref,
        key_sine_ref, cosine_ref, sine_ref, query_grad_ref, pair_grad_ref, key_sum, value_sum,
    )

    @pl.when(step == pl.num_programs(0) - 1)
    def _():
        hand_on([gather_task, sum_task])
        gather_task.finish()
        sum_task.finish()


def attend_back_sum(
    number, projected, pairs, branch_grad, totals, key_segs, query_segs, key_tables, tables, part,
    down, weights,
):
    rows = projected.shape[0]
    columns = NH * HD
    low = jnp.bfloat16
    sum_task = PlaneSum(*part.shape[1:])
    gather_task = gather_plane(down.shape)
    hbm = pl.BlockSpec(memory_space=pl.ANY)
    return pl.pallas_call(
        functools.partial(attend_back_sum_kernel, sum_task, gather_task),
        grid=(NH,),
        in_specs=attention_specs(
            ["head", "keys", "values", "branch", "total", "key_seg", "query_seg"]
            + ["key_table", "key_table", "table", "table"],
            rows,
        )
        + [hbm, hbm, hbm],
        out_specs=attention_specs(["head", "pair"], rows) + [hbm, hbm],
        out_shape=[
            jax.ShapeDtypeStruct((rows, columns), low),
            jax.ShapeDtypeStruct((SEQLEN, 2 * HD), low),
            jax.ShapeDtypeStruct(sum_task.out_shape, low),
            jax.ShapeDtypeStruct(gather_task.out_shape, low),
        ],
        scratch_shapes=[pltpu.VMEM((SEQLEN, HD), jnp.float32)] * 2
        + [
            pltpu.VMEM((rows, HD), low),
            pltpu.VMEM((2, HD, MODEL_WIDTH), low),
            pltpu.SemaphoreType.DMA((2,)),
        ]
        + sum_task.scratch()
        + [pltpu.SemaphoreType.DMA((sum_task.sem_count,))] * 2
        + [pltpu.SemaphoreType.DMA((gather_task.sem_count,))] * 2,
        compiler_params=pltpu.CompilerParams(
            collective_id=number, has_side_effects=True, vmem_limit_bytes=48 * 2**20
        ),
        cost_estimate=SMALL_COST,
        name="attend_back_sum",
    )(
        projected, pairs, pairs, branch_grad, totals, key_segs[:, None], query_segs[None, :],
        *key_tables, *tables, part, down, weights,
    )


def block_kernel(
    first, second, pair_task, key_seg_ref, query_seg_ref, normed_ref, tokens_ref, gain_ref,
    cosine_ref, sine_ref, cot_hbm, normed_hbm, w_ref, projected_ref, pairs_ref, context_ref,
    total_ref, hidden_ref, second_ref, inverse_ref, cot_plane, normed_plane, own_pair, pairs,
    first_send, first_recv, second_send, second_recv, pair_send, pair_recv,
):
    step = pl.program_id(0)
    grp, seq = lax.axis_index("grp"), lax.axis_index("seq")
    first.start(cot_hbm, cot_plane, (first_send, first_recv), grp, seq, begin=False)
    second.start(normed_hbm, normed_plane, (second_send, second_recv), grp, seq, begin=False)
    pair_task.start(own_pair, pairs, (pair_send, pair_recv), grp, seq, begin=False)
    low = jnp.bfloat16
    rows = normed_ref.shape[0]
    wide = 2 * HD
    couples = NH // 2
    attend_at = 1 + couples
    out_at = attend_at + NH
    end = out_at + MODEL_WIDTH // wide

    @pl.when(step == 0)
    def _():
        barrier = pltpu.get_barrier_semaphore()
        devices = list(first.peers(grp, seq)) + list(pair_task.peers(grp, seq))
        for device in devices:
            pl.semaphore_signal(barrier, inc=1, device_id=device, device_id_type=MESH)
        pl.semaphore_wait(barrier, len(devices))
        first.begin()
        second.begin()

    @pl.when(step < attend_at)
    def _():
        made = jnp.dot(normed_ref[...], w_ref[...], preferred_element_type=jnp.float32)
        cosine, sine = cosine_ref[...], sine_ref[...]
        left = turn(made[:, :HD], cosine, sine).astype(low)
        right = made[:, HD:]

        @pl.when(step == 0)
        def _():
            own_pair[:, :HD] = left
            own_pair[:, HD:] = right.astype(low)
            pair_task.begin()
            projected_ref[:, NH * HD :] = own_pair[...]

        @pl.when(step > 0)
        def _():
            place = pl.multiple_of((step - 1) * wide, wide)
            projected_ref[:, pl.ds(place, HD)] = left
            projected_ref[:, pl.ds(pl.multiple_of(place + HD, HD), HD)] = turn(
                right, cosine, sine
            ).astype(low)

    @pl.when(step == attend_at)
    def _():
        pair_task.finish()
        for at in range(pairs.shape[0]):
            pairs_ref[at * rows : (at + 1) * rows, :] = pairs[at]

    @pl.when(step == attend_at + 2)
    def _():
        first.pass_on(1)
        first.pass_on(4)

    @pl.when(step == out_at)
    def _():
        first.pass_on(2)
        first.pass_on(5)

    @pl.when((step >= attend_at) & (step < out_at))
    def _():
        head = step - attend_at
        place = pl.ds(pl.multiple_of(head * HD, HD), HD)
        scale = HD ** (-0.5)
        for block in range(SEQLEN // rows):

            @pl.when(seq == block)
            def _():
                keys = (block + 1) * rows
                scores = dot_last(pairs_ref[:keys, :HD], projected_ref[:, place]) * scale
                scores = jnp.where(
                    score_mask(key_seg_ref, query_seg_ref, block, rows), scores, MASKED
                )
                highest = jnp.max(scores, axis=0, keepdims=True)
                exponent = jnp.exp(scores - highest)
                totals = jnp.sum(exponent, axis=0, keepdims=True)
                probs_low = (exponent * (1.0 / totals)).astype(low)
                context = dot_first(probs_low, pairs_ref[:keys, HD:])
                context_ref[:, place] = context.astype(low)
                total_ref[head] = highest + jnp.log(totals)

    @pl.when(step >= out_at)
    def _():
        place = pl.ds(pl.multiple_of((step - out_at) * wide, wide), wide)
        branch = jnp.dot(context_ref[...], w_ref[...], preferred_element_type=jnp.float32)
        hidden_ref[:, place] = tokens_ref[:, place].astype(jnp.float32) + branch

    @pl.when(step == end - 1)
    def _():
        chunk = 32
        gain = gain_ref[1:2, :]

        def some(at, _):
            part = pl.ds(pl.multiple_of(at * chunk, chunk), chunk)
            hidden = hidden_ref[part, :]
            inverse = lax.rsqrt(jnp.mean(hidden * hidden, axis=-1, keepdims=True) + NORM_EPS)
            inverse_ref[part, :] = inverse
            second_ref[part, :] = (hidden * inverse * gain).astype(low)
            return 0

        lax.fori_loop(0, rows // chunk, some, 0)
        first.pass_on(6)
        first.pass_on(3)
        for came in (1, 4, 2, 5, 6, 3):
            second.pass_on(came)
        first.finish()
        second.finish()


def attention_block(number, normed, tokens, gains, tables, key_segs, query_segs, cotangent, weights):
    rows, width = normed.shape
    low, wide = jnp.bfloat16, 2 * HD
    couples = NH // 2
    count = SEQLEN // rows
    first = gather_plane(cotangent.shape, placed=True)
    second = gather_plane(normed.shape, placed=True)
    pair_task = Exchange("seq", (count, rows, wide), whole, block_of)

    def weight_block(step):
        turned = step - NH
        return (0, jnp.where(step == 0, couples, jnp.where(step <= couples, step - 1, jnp.maximum(turned, couples + 1))))

    def full(shape):
        return pl.BlockSpec(shape, lambda step: (0,) * len(shape))

    hbm = pl.BlockSpec(memory_space=pl.ANY)
    steps = 1 + couples + NH + width // wide
    plane = jax.ShapeDtypeStruct((8, rows, width), low)
    shapes = [
        jax.ShapeDtypeStruct((rows, NH * HD + wide), low),
        jax.ShapeDtypeStruct((SEQLEN, wide), low),
        jax.ShapeDtypeStruct((rows, NH * HD), low),
        jax.ShapeDtypeStruct((NH, 1, rows), jnp.float32),
        jax.ShapeDtypeStruct((rows, width), jnp.float32),
        jax.ShapeDtypeStruct((rows, width), low),
        jax.ShapeDtypeStruct((rows, 1), jnp.float32),
    ]
    return pl.pallas_call(
        functools.partial(block_kernel, first, second, pair_task),
        grid=(steps,),
        in_specs=[
            full((SEQLEN, 1)),
            full((1, rows)),
            full((rows, width)),
            full((rows, width)),
            full((2, width)),
            full((rows, HD)),
            full((rows, HD)),
            hbm,
            hbm,
            pl.BlockSpec((width, wide), weight_block),
        ],
        out_specs=[full(shape.shape) for shape in shapes] + [hbm, hbm],
        out_shape=shapes + [plane, plane],
        scratch_shapes=[pltpu.VMEM((rows, wide), low), pltpu.VMEM((count, rows, wide), low)]
        + [pltpu.SemaphoreType.DMA((14,))] * 4
        + [pltpu.SemaphoreType.DMA((pair_task.sem_count,))] * 2,
        compiler_params=pltpu.CompilerParams(
            collective_id=number, has_side_effects=True, vmem_limit_bytes=56 * 2**20
        ),
        cost_estimate=SMALL_COST,
        name="attention_block",
    )(
        key_segs[:, None], query_segs[None, :], normed, tokens, gains, *tables, cotangent, normed,
        weights,
    )


def add_blocks(total, blocks):
    step = min(32, total.shape[0])

    def some(at, _):
        rows = pl.ds(pl.multiple_of(at * step, step), step)
        made = blocks[0, rows, :].astype(jnp.float32)
        for block in range(1, blocks.shape[0]):
            made = made + blocks[block, rows, :].astype(jnp.float32)
        total[rows, :] = made.astype(total.dtype)
        return 0

    lax.fori_loop(0, total.shape[0] // step, some, 0)


def norm_one_back(
    weights_hbm, query_grad_ref, pair_grad_ref, hidden_grad_ref, tokens_ref, inverse_ref, gain_ref,
    gain_two_ref, input_grad_ref, gain_terms, w_block, norm_grad, w_sems,
):
    width, query_columns = tokens_ref.shape[1], query_grad_ref.shape[1]
    rows, columns = w_block.shape[1:]
    count = width // rows

    def w_copy(at):
        view = weights_hbm.at[pl.ds(pl.multiple_of(at * rows, rows), rows), pl.ds(0, columns)]
        return pltpu.make_async_copy(view, w_block.at[at % 2], w_sems.at[at % 2])

    w_copy(0).start()

    def one(at, _):
        w_copy(at).wait()

        @pl.when(at + 1 < count)
        def _():
            w_copy(at + 1).start()

        made = dot_last(query_grad_ref[...], w_block[at % 2, :, :query_columns])
        made = made + dot_last(pair_grad_ref[...], w_block[at % 2, :, query_columns:])
        norm_grad[:, pl.ds(pl.multiple_of(at * rows, rows), rows)] = made
        return 0

    lax.fori_loop(0, count, one, 0)
    chunk = 32
    gain = gain_ref[0:1, :]

    def some(at, sums):
        part = pl.ds(pl.multiple_of(at * chunk, chunk), chunk)
        inverse, token = inverse_ref[part, :], tokens_ref[part, :].astype(jnp.float32)
        made = norm_grad[part, :]
        scaled = gain * made
        mean = jnp.mean(token * scaled, axis=-1, keepdims=True)
        input_grad_ref[part, :] = (
            hidden_grad_ref[part, :] + inverse * scaled - token * (inverse * inverse * inverse * mean)
        )
        return sums + jnp.sum(made * token * inverse, axis=0, keepdims=True)

    zeros = jnp.zeros((1, width), jnp.float32)
    gain_terms[0:1, :] = lax.fori_loop(0, tokens_ref.shape[0] // chunk, some, zeros)
    gain_terms[1:2, :] = gain_two_ref[...]


def tail_kernel(
    tasks, shares_hbm, pair_hbm, gating_hbm, weights_hbm, query_grad_ref, pair_grad_ref,
    hidden_grad_ref, tokens_ref, inverse_ref, gain_ref, gain_two_ref, gating_plane, share_plane,
    pair_plane, gain_plane, input_grad_ref, share_parts, share_sum, mine, core_in, halves, wholes,
    pair_parts, pair_sum, gain_terms, gain_parts, gain_sum, w_block, norm_grad, w_sems, *sems,
):
    gating, pair, gain_seq, gain_grp, pair_seq, pair_gather, *halves_of = tasks
    shares, share_gathers = halves_of[:2], halves_of[2:]
    grp, seq = lax.axis_index("grp"), lax.axis_index("seq")
    barrier = pltpu.get_barrier_semaphore()
    devices = list(gain_grp.peers(grp, seq)) + list(gain_seq.peers(grp, seq))
    for device in devices:
        pl.semaphore_signal(barrier, inc=1, device_id=device, device_id_type=MESH)
    pl.semaphore_wait(barrier, len(devices))
    sems = [(sems[2 * at], sems[2 * at + 1]) for at in range(len(tasks))]

    def share_part(at):
        shares[at].finish()
        add_blocks(share_sum.at[at], share_parts.at[at])
        share_gathers[at].start(share_sum.at[at], share_plane, sems[8 + at], grp, seq)

    shares[0].start(shares_hbm, share_parts.at[0], sems[6], grp, seq)
    pair.start(pair_hbm, None, sems[1], grp, seq, (mine, core_in, halves, wholes))
    gating.start(gating_hbm, gating_plane, sems[0], grp, seq, begin=False)
    gating.kept.start()
    for at in (1, 4, 7):
        gating.out[at].start()
    pair.first_sums()
    norm_one_back(
        weights_hbm, query_grad_ref, pair_grad_ref, hidden_grad_ref, tokens_ref, inverse_ref,
        gain_ref, gain_two_ref, input_grad_ref, gain_terms, w_block, norm_grad, w_sems,
    )
    gain_seq.start(gain_terms, gain_parts, sems[2], grp, seq)
    for _ in pair.forward():
        pass
    for at in (2, 5):
        gating.out[at].start()
    handing = gating.forward()
    next(handing)
    pair_seq.start(pair.total(), pair_parts, sems[4], grp, seq)
    shares[1].start(shares_hbm, share_parts.at[1], sems[7], grp, seq)
    gain_seq.finish()
    gain_sum[...] = jnp.sum(gain_parts[...], axis=0)
    gain_grp.start(gain_sum, gain_plane, sems[3], grp, seq)
    share_part(0)
    pair_seq.finish()
    add_blocks(pair_sum, pair_parts)
    pair_gather.start(pair_sum, pair_plane, sems[5], grp, seq)
    next(handing)
    share_part(1)
    next(handing)
    hand_on([share_gathers[0], pair_gather, share_gathers[1]])
    for copy in pair.copies:
        copy.wait_send()
    for task in (gain_grp, gating, pair_gather, *share_gathers):
        task.finish()


def gather_gating(shape):
    return gather_plane(
        shape,
        split=1,
        target_view=lambda ref, index: ref.at[:, index],
        out_shape=(shape[0], lax.axis_size("grp"), *shape[1:]),
    )


def tail_exchange(number, shares, pair, gating, weights, back):
    gain_terms = jax.ShapeDtypeStruct((2, back[3].shape[1]), jnp.float32)
    tokens_here = back[3].shape[0]
    seq_count = lax.axis_size("seq")
    low = jnp.bfloat16
    columns, rows_all = shares.shape
    rows = rows_all // seq_count
    _, pair_rows, pair_columns = pair.shape
    sub = pair_rows // seq_count
    half = columns // 2

    def share_task(at):
        return Exchange(
            "seq",
            (seq_count, half, rows),
            lambda ref, index: ref.at[
                pl.ds(at * half, half), pl.ds(pl.multiple_of(index * rows, rows), rows)
            ],
            block_of,
        )

    def share_gather(at):
        return gather_plane(
            (half, rows),
            target_view=lambda ref, index: ref.at[index, pl.ds(at * half, half)],
            out_shape=(8, columns, rows),
        )

    tasks = [
        gather_gating(gating.shape),
        PlaneSum(pair_rows, pair_columns, placed=False),
        gather_axis("seq", gain_terms)[0],
        gather_axis("grp", gain_terms)[0],
        Exchange(
            "seq",
            (seq_count, sub, pair_columns),
            lambda ref, index: rows_of(ref, index, sub),
            block_of,
        ),
        gather_plane((sub, pair_columns)),
        share_task(0),
        share_task(1),
        share_gather(0),
        share_gather(1),
    ]
    hbm = pl.BlockSpec(memory_space=pl.ANY)
    vmem = pl.BlockSpec(memory_space=pltpu.VMEM)
    scratch = [
        pltpu.VMEM((2, seq_count, half, rows), low),
        pltpu.VMEM((2, half, rows), low),
        *tasks[1].scratch(),
        pltpu.VMEM((seq_count, sub, pair_columns), low),
        pltpu.VMEM((sub, pair_columns), low),
        pltpu.VMEM(gain_terms.shape, jnp.float32),
        pltpu.VMEM((seq_count, *gain_terms.shape), jnp.float32),
        pltpu.VMEM(gain_terms.shape, jnp.float32),
        pltpu.VMEM((2, 2 * HD, (NH + 2) * HD), low),
        pltpu.VMEM((tokens_here, back[3].shape[1]), jnp.float32),
        pltpu.SemaphoreType.DMA((2,)),
    ]
    for task in tasks:
        scratch += [pltpu.SemaphoreType.DMA((task.sem_count,))] * 2
    return pl.pallas_call(
        functools.partial(tail_kernel, tasks),
        in_specs=[hbm] * 4 + [vmem] * len(back),
        out_specs=[hbm] * 4 + [vmem],
        out_shape=[
            jax.ShapeDtypeStruct(tasks[0].out_shape, low),
            jax.ShapeDtypeStruct((8, columns, rows), low),
            jax.ShapeDtypeStruct((8, sub, pair_columns), low),
            jax.ShapeDtypeStruct((8, *gain_terms.shape), jnp.float32),
            jax.ShapeDtypeStruct((tokens_here, back[3].shape[1]), jnp.float32),
        ],
        scratch_shapes=scratch,
        compiler_params=pltpu.CompilerParams(
            collective_id=number, has_side_effects=True, vmem_limit_bytes=60 * 2**20
        ),
        cost_estimate=SMALL_COST,
        name="tail_exchange",
    )(shares, pair, gating, weights, *back)


def half_rows(axis, height):
    def half_of(view, second):
        index = (slice(None),) * axis + (pl.ds(height if second else 0, height),)
        return view.at[index]

    return half_of


def whole(ref, index):
    return ref


def block_of(ref, index):
    return ref.at[index]


def gather_plane(
    shape, split=0, source_view=whole, target_view=block_of, out_shape=None, placed=False
):
    out_shape = out_shape or (lax.axis_size("grp"), *shape)
    if lax.axis_size("grp") == 8:
        halves = half_rows(split, shape[split] // 2)
        return PlaneGather(out_shape, source_view, target_view, halves, placed)
    return Exchange("grp", out_shape, source_view, target_view)


def hand_on(tasks):
    going = [task.forward() for task in tasks]
    while going:
        going = [steps for steps in going if next(steps, going) is not going]


def exchange_kernel(tasks, wires, arrays, outputs, *refs):
    sources, targets = refs[:arrays], refs[arrays : arrays + outputs]
    refs = list(refs[arrays + outputs :])
    sems, scratch = [], []
    for task in tasks:
        sems.append((refs.pop(0), refs.pop(0)))
        held = len(task.scratch()) if isinstance(task, PlaneSum) else 0
        scratch.append([refs.pop(0) for _ in range(held)])
    grp, seq = lax.axis_index("grp"), lax.axis_index("seq")
    barrier = pltpu.get_barrier_semaphore()
    axes = {"grp": [], "seq": []}
    for task in tasks:
        devices = list(task.peers(grp, seq))
        if len(devices) > len(axes[task.axis]):
            axes[task.axis] = devices
    devices = axes["grp"] + axes["seq"]
    for device in devices:
        pl.semaphore_signal(barrier, inc=1, device_id=device, device_id_type=MESH)
    pl.semaphore_wait(barrier, len(devices))

    def start(at):
        after, source, target = wires[at]
        source = targets[source] if after is not None else sources[source]
        more = (scratch[at],) if scratch[at] else ()
        tasks[at].start(source, targets[target], sems[at], grp, seq, *more)

    open_tasks = list(range(len(tasks)))
    first = [at for at in open_tasks if wires[at][0] is None]
    for at in first:
        start(at)
    for at in first:
        if isinstance(tasks[at], PlaneSum):
            tasks[at].first_sums()
    hand_on([tasks[at] for at in first])
    for at in open_tasks[:]:
        after = wires[at][0]
        if after is not None:
            tasks[after].finish()
            open_tasks.remove(after)
            start(at)
            hand_on([tasks[at]])
    for at in open_tasks:
        tasks[at].finish()


def exchange(number, work):
    tasks = [piece[0] for piece in work]
    arrays, shapes, wires = [], [], []
    for piece in work:
        if isinstance(piece[1], int):
            after, source = piece[1], wires[piece[1]][2]
            kind = shapes[source].dtype
        else:
            after, source = None, len(arrays)
            arrays.append(piece[1])
            kind = piece[1].dtype
        if len(piece) == 3:
            target = wires[piece[2]][2]
        else:
            target = len(shapes)
            shapes.append(jax.ShapeDtypeStruct(piece[0].out_shape, kind))
        wires.append((after, source, target))
    scratch = []
    for task in tasks:
        scratch += [pltpu.SemaphoreType.DMA((task.sem_count,))] * 2
        if isinstance(task, PlaneSum):
            scratch += task.scratch()
    return pl.pallas_call(
        functools.partial(exchange_kernel, tasks, wires, len(arrays), len(shapes)),
        in_specs=[pl.BlockSpec(memory_space=pl.ANY)] * len(arrays),
        out_specs=[pl.BlockSpec(memory_space=pl.ANY)] * len(shapes),
        out_shape=shapes,
        scratch_shapes=scratch,
        compiler_params=pltpu.CompilerParams(collective_id=number, has_side_effects=True),
        cost_estimate=SMALL_COST,
        name="exchange",
    )(*arrays)


def gather_axis(axis, array):
    task = Exchange(axis, (lax.axis_size(axis), *array.shape), whole, block_of)
    return task, array


def split_rows(axis, array):
    count = lax.axis_size(axis)
    rows, columns = array.shape
    height = rows // count
    task = Exchange(
        axis,
        (count, height, columns),
        lambda ref, index: rows_of(ref, index, height),
        block_of,
    )
    return task, array


def split_columns(axis, array, placed=False):
    count = lax.axis_size(axis)
    rows, columns = array.shape
    width = columns // count
    if placed and count == 8:
        task = PlacedExchange(
            (count, rows, width), lambda ref, index: columns_of(ref, index, width)
        )
        return task, array
    task = Exchange(
        axis,
        (count, rows, width),
        lambda ref, index: columns_of(ref, index, width),
        block_of,
    )
    return task, array


def plane_sum_kernel(
    own, part_ref, gate_ref, up_ref, x_ref, total_ref, grads_out, core_in, chip, half_x, half_y,
    whole_x, whole_y, x_block, stage, send_sems, recv_sems, x_sems, out_sems,
):
    grp, seq = lax.axis_index("grp"), lax.axis_index("seq")
    core, side_x, side_y = [flip(grp, bits) for bits in (1, 2, 4)]
    blocks = [PLACES[bits] for bits in (6, 2, 4, 0)]
    core_blocks = [PLACES[bits] for bits in (7, 3, 5, 1)]
    half = total_ref.shape[0] // 2
    low, high = pl.ds(0, half), pl.ds(half, half)
    rows = x_block.shape[2]
    count = x_ref.shape[1] // rows

    def x_copy(at):
        view = x_ref.at[:, pl.ds(pl.multiple_of(at * rows, rows), rows)]
        return pltpu.make_async_copy(view, x_block.at[at % 2], x_sems.at[at % 2])

    def out_copies(at):
        return [
            pltpu.make_async_copy(
                stage.at[which, at % 2, own_columns(grp, own)],
                grads_out.at[pl.ds(pl.multiple_of((2 * at + which) * own, own), own)],
                out_sems.at[which, at % 2],
            )
            for which in range(2)
        ]

    x_copy(0).start()
    barrier = pltpu.get_barrier_semaphore()
    for device in (core, side_x, side_y):
        pl.semaphore_signal(barrier, inc=1, device_id=(device, seq), device_id_type=MESH)
    pl.semaphore_wait(barrier, 3)

    sems = (send_sems, recv_sems)
    copies = [
        remote(part_ref.at[block], core_in.at[at], sems, at, (core, seq))
        for at, block in enumerate(core_blocks)
    ]
    copies += [
        remote(chip.at[0, low], half_x, sems, 4, (side_x, seq)),
        remote(chip.at[0, high], half_y, sems, 5, (side_y, seq)),
        remote(chip.at[1, low], whole_x.at[low], sems, 6, (side_x, seq)),
        remote(chip.at[2, high], whole_y.at[high], sems, 7, (side_y, seq)),
        remote(chip.at[1, high], whole_x.at[high], sems, 8, (side_x, seq)),
        remote(chip.at[2, low], whole_y.at[low], sems, 9, (side_y, seq)),
    ]
    for copy in copies[:4]:
        copy.start()

    def step(at, _):
        @pl.when(at == 1)
        def _():
            for came, then in ((0, (4, 5)), (1, (6,)), (2, (7,))):
                copies[came].wait_recv()
                add_rows(chip.at[came], part_ref.at[blocks[came]], core_in.at[came])
                for start in then:
                    copies[start].start()

        @pl.when(at == count - 1)
        def _():
            copies[5].wait_recv()
            add_rows(chip.at[1, high], chip.at[1, high], half_y)
            copies[8].start()
            copies[4].wait_recv()
            add_rows(chip.at[2, low], chip.at[2, low], half_x)
            copies[9].start()

        x_copy(at).wait()

        @pl.when(at + 1 < count)
        def _():
            x_copy(at + 1).start()

        @pl.when(at >= 2)
        def _():
            for copy in out_copies(at - 2):
                copy.wait()

        for which, ref in enumerate((gate_ref, up_ref)):
            stage[which, at % 2] = jnp.dot(
                ref[...], x_block[at % 2], preferred_element_type=jnp.float32
            ).astype(stage.dtype)
        for copy in out_copies(at):
            copy.start()
        return 0

    lax.fori_loop(0, count, step, 0)
    copies[3].wait_recv()
    add_rows(total_ref, part_ref.at[blocks[3]], core_in.at[3])
    for at, came, rows_at in (
        (6, whole_x, low),
        (7, whole_y, high),
        (8, whole_x, high),
        (9, whole_y, low),
    ):
        copies[at].wait_recv()
        add_rows(total_ref.at[rows_at], total_ref.at[rows_at], came.at[rows_at])
    for copy in copies:
        copy.wait_send()
    for at in (count - 2, count - 1):
        for copy in out_copies(at):
            copy.wait()


def plane_sum(number, own, part, gate_grad, up_grad, x, seq_count):
    count = lax.axis_size("grp")
    rows_all, columns = part.shape
    rows = rows_all // count
    if count != 8:
        total = lax.psum_scatter(part, "grp", scatter_dimension=0, tiled=True)
        begin = (lax.axis_index("grp") * own) % 128
        both = jnp.concatenate(
            [lax.dynamic_slice_in_dim(grad, begin, own) for grad in (gate_grad, up_grad)], axis=0
        )
        return total.astype(jnp.float32), weight_grad(both, x, seq_count)
    low = jnp.bfloat16
    cols, tokens_all = gate_grad.shape
    width = x.shape[1] // seq_count
    vmem = pl.BlockSpec(memory_space=pltpu.VMEM)
    hbm = pl.BlockSpec(memory_space=pl.ANY)
    grads = jax.ShapeDtypeStruct((2 * seq_count * own, width), low)
    return pl.pallas_call(
        functools.partial(plane_sum_kernel, own),
        in_specs=[vmem, vmem, vmem, hbm],
        out_specs=[vmem, hbm],
        out_shape=[jax.ShapeDtypeStruct((rows, columns), jnp.float32), grads],
        scratch_shapes=[
            pltpu.VMEM((4, rows, columns), low),
            pltpu.VMEM((3, rows, columns), low),
            pltpu.VMEM((rows // 2, columns), low),
            pltpu.VMEM((rows // 2, columns), low),
            pltpu.VMEM((rows, columns), low),
            pltpu.VMEM((rows, columns), low),
            pltpu.VMEM((2, tokens_all, width), low),
            pltpu.VMEM((2, 2, cols, width), low),
            pltpu.SemaphoreType.DMA((10,)),
            pltpu.SemaphoreType.DMA((10,)),
            pltpu.SemaphoreType.DMA((2,)),
            pltpu.SemaphoreType.DMA((2, 2)),
        ],
        compiler_params=pltpu.CompilerParams(
            collective_id=number, has_side_effects=True, vmem_limit_bytes=56 * 2**20
        ),
        cost_estimate=SMALL_COST,
        name="plane_sum",
    )(part.reshape(count, rows, columns), gate_grad, up_grad, x)


def local(
    tokens,
    cotangent,
    segment_ids,
    tile_owner_slots,
    weights_low,
    master,
    moment_one,
    moment_two,
    left_basis_set,
    right_basis_set,
    gains,
    gain_moment_one,
    gain_moment_two,
):
    grp_count = lax.axis_size("grp")
    seq_count = lax.axis_size("seq")
    grp_here, seq_here = lax.axis_index("grp"), lax.axis_index("seq")
    rows_here = tokens.shape[0]
    slots_here, rows_block, tile_width = weights_low.shape
    tile_count = tile_owner_slots.shape[0]
    query_cols = NH * HD
    value_end = query_cols + 2 * HD
    output_end = value_end + MODEL_WIDTH
    attn_tiles = output_end // tile_width
    query_tiles = query_cols // tile_width
    hidden_tiles = FF // tile_width
    own = FF // grp_count
    share = max(-(-((at * own) % tile_width + own) // tile_width) for at in range(grp_count))
    share_width = MODEL_WIDTH // grp_count
    sub_rows = rows_block // grp_count
    halves = 2 if sub_rows >= 32 else 1
    half_block, half_sub = rows_block // halves, sub_rows // halves
    first_place = (seq_here * rows_here) % SEQLEN
    key_tables = turn_tables(jnp.arange(SEQLEN, dtype=jnp.int32))
    tables = [lax.dynamic_slice_in_dim(table, first_place, rows_here) for table in key_tables]

    hidden_ids = grp_here * own // tile_width + jnp.arange(share, dtype=jnp.int32)
    hidden_ids = jnp.minimum(hidden_ids, hidden_tiles - 1)
    feed_ids = (
        attn_tiles
        + jnp.arange(3, dtype=jnp.int32)[:, None] * hidden_tiles
        + hidden_ids[None, :]
    ).reshape(-1)
    feed_slots, attn_slots = tile_owner_slots[feed_ids], tile_owner_slots[:attn_tiles]

    tok_float = tokens.astype(jnp.float32)
    inverse_one = lax.rsqrt(jnp.mean(tok_float * tok_float, axis=-1, keepdims=True) + NORM_EPS)
    normed = (tok_float * inverse_one * gains[0]).astype(jnp.bfloat16)

    def weight_half(at):
        return gather_plane(
            (slots_here, half_block, tile_width),
            split=1,
            source_view=lambda ref, index: ref.at[:, pl.ds(at * half_block, half_block)],
        )

    def attn_half(at):
        return gather_plane(
            (seq_count, half_sub, output_end),
            target_view=lambda ref, index: ref.at[:, at, index],
            out_shape=(seq_count, halves, grp_count, half_sub, output_end),
        )

    flat = (grp_count * slots_here, half_block, tile_width)
    tiles, segments = exchange(
        0,
        [(weight_half(0), weights_low), gather_axis("seq", segment_ids.reshape(-1, tile_width))],
    )
    feed_rows, attn_rows = pick(tiles.reshape(flat), feed_slots, attn_slots)
    feed_parts = [lax.all_gather(feed_rows, "seq", axis=0, tiled=False)]
    if halves == 2:
        tiles, attn_first = exchange(
            1, [(weight_half(1), weights_low), gather_axis("seq", attn_rows)]
        )
        feed_rows, attn_rows = pick(tiles.reshape(flat), feed_slots, attn_slots)
        feed_parts.append(lax.all_gather(feed_rows, "seq", axis=0, tiled=False))
        attn_weights, _ = exchange(
            2,
            [(attn_half(0), attn_first), gather_axis("seq", attn_rows), (attn_half(1), 1, 0)],
        )
    else:
        _, attn_weights = exchange(2, [gather_axis("seq", attn_rows), (attn_half(0), 0)])
    attn_weights = attn_weights.reshape(MODEL_WIDTH, output_end)

    first_key = seq_here * rows_here - first_place
    key_segs = lax.dynamic_slice_in_dim(segments.reshape(-1), first_key, SEQLEN)
    at = (first_place // rows_here).reshape(1)
    if grp_count == 8 and seq_count * rows_here == SEQLEN:
        (
            projected, pairs, context, log_totals, hidden, normed_two, inverse_two, cot_plane,
            normed_plane,
        ) = attention_block(
            3, normed, tokens, gains, tables, key_segs, segment_ids, cotangent, attn_weights
        )
    else:
        projected = project(normed, attn_weights, tables)
        pairs, cot_plane, normed_plane = exchange(
            3,
            [
                gather_axis("seq", projected[:, query_cols:]),
                (gather_plane(cotangent.shape, placed=True), cotangent),
                (gather_plane(normed.shape, placed=True), normed),
            ],
        )
        pairs = lax.dynamic_slice_in_dim(pairs.reshape(-1, 2 * HD), first_key, SEQLEN)
        context, log_totals = attend(at, projected, pairs, key_segs, segment_ids)
        branch = jnp.dot(
            context, attn_weights[:, value_end:], preferred_element_type=jnp.float32
        )
        hidden = tok_float + branch
        inverse_two = lax.rsqrt(jnp.mean(hidden * hidden, axis=-1, keepdims=True) + NORM_EPS)
        normed_two = (hidden * inverse_two * gains[1]).astype(jnp.bfloat16)

    cot_plane = cot_plane.reshape(-1, MODEL_WIDTH)
    normed_plane = normed_plane.reshape(-1, MODEL_WIDTH)
    real_cols = ((grp_here * own) % tile_width).reshape(1)
    if halves == 2:
        some = jnp.max(feed_parts[0][0, :8, :tile_width].astype(jnp.float32)) * 0.0
        real_cols = real_cols + some.astype(jnp.int32)
    if grp_count == 8:
        gate_grad, up_grad, two_part, feed_part, second_plane, context_plane, down_grad = (
            feed_gather(
                4, own, real_cols, normed_two, context, cot_plane, feed_parts, seq_count
            )
        )
        second_plane = second_plane.reshape(-1, MODEL_WIDTH)
    else:
        second_plane, context_plane = exchange(
            4,
            [
                (gather_plane(normed_two.shape), normed_two),
                (gather_plane(context.shape), context),
            ],
        )
        second_plane = second_plane.reshape(-1, MODEL_WIDTH)
        activated, gate_grad, up_grad, two_part, feed_part = feed_forward(
            own, real_cols, second_plane, cot_plane, feed_parts, seq_count
        )
        activated = lax.dynamic_slice_in_dim(activated, (grp_here * own) % tile_width, own)
        down_grad = weight_grad(activated, cot_plane, seq_count)
    context_plane = context_plane.reshape(-1, MODEL_WIDTH)
    down_grad, two_part = lax.optimization_barrier((down_grad, two_part))
    down_grad = lax.psum_scatter(down_grad, "seq", scatter_dimension=0, tiled=True)
    norm_two_grad, gating_grads = plane_sum(
        5, own, two_part, gate_grad, up_grad, second_plane, seq_count
    )
    gating_grads = lax.psum_scatter(gating_grads, "seq", scatter_dimension=0, tiled=True)
    gating_grads = gating_grads.reshape(2, own, rows_block)

    out_grad = cotangent.astype(jnp.float32)
    gain_two_term = jnp.sum(norm_two_grad * hidden * inverse_two, axis=0)
    hidden_grad = (
        out_grad
        + inverse_two * gains[1] * norm_two_grad
        - hidden
        * inverse_two**3
        * jnp.mean(hidden * gains[1] * norm_two_grad, axis=-1, keepdims=True)
    )
    branch_grad = hidden_grad.astype(jnp.bfloat16)
    fused = grp_count == 8 and seq_count * rows_here == SEQLEN
    if fused:
        feed_part = feed_part.reshape(grp_count, rows_here, MODEL_WIDTH)
        query_grad, pair_part, feed_out, down_plane = attend_back_sum(
            6, projected, pairs, branch_grad, log_totals, key_segs, segment_ids, key_tables,
            tables, feed_part, down_grad, attn_weights,
        )
    else:
        context_grad = times_transpose(branch_grad, attn_weights[:, value_end:]).astype(jnp.bfloat16)
        query_grad, pair_part = attend_back(
            at, projected, pairs, context_grad, log_totals, key_segs, segment_ids, key_tables, tables
        )
        feed_out = lax.psum_scatter(
            feed_part.reshape(-1, MODEL_WIDTH), "grp", scatter_dimension=0, tiled=True
        )
        (down_plane,) = exchange(10, [(gather_plane(down_grad.shape), down_grad)])
    block_out = (hidden + feed_out.astype(jnp.float32)).astype(jnp.bfloat16)
    if seq_count * rows_here > SEQLEN:
        pair_part = lax.dynamic_update_slice_in_dim(
            jnp.zeros((seq_count * rows_here, 2 * HD), pair_part.dtype), pair_part, first_key, 0
        )
    pair_parts, query_share, branch_share = exchange(
        7,
        [
            split_rows("seq", pair_part),
            split_columns("grp", query_grad, placed=True),
            split_columns("grp", branch_grad, placed=True),
        ],
    )
    pair_grad = jnp.sum(pair_parts.astype(jnp.float32), axis=0).astype(jnp.bfloat16)
    shares = share_grad(
        query_share.reshape(-1, share_width),
        branch_share.reshape(-1, share_width),
        normed_plane,
        context_plane,
    )
    pair_weight_grad = contract(normed, pair_grad).astype(jnp.bfloat16)
    pair_blocks = pair_weight_grad.reshape(seq_count, grp_count, sub_rows, 2 * HD)
    if grp_count == 8:
        pair_blocks = jnp.transpose(pair_blocks, (1, 0, 2, 3))
        gating_plane, share_plane, pair_plane, gain_parts, input_grad = tail_exchange(
            8,
            shares,
            pair_blocks.reshape(grp_count, seq_count * sub_rows, 2 * HD),
            gating_grads,
            attn_weights,
            (query_grad, pair_grad, hidden_grad, tokens, inverse_one, gains, gain_two_term[None, :]),
        )
    else:
        projected_grad = jnp.concatenate([query_grad, pair_grad], axis=1)
        norm_one_grad = times_transpose(projected_grad, attn_weights[:, :value_end])
        gain_one_term = jnp.sum(norm_one_grad * tok_float * inverse_one, axis=0)
        input_grad = (
            hidden_grad
            + inverse_one * gains[0] * norm_one_grad
            - tok_float
            * inverse_one**3
            * jnp.mean(tok_float * gains[0] * norm_one_grad, axis=-1, keepdims=True)
        )
        gain_terms = jnp.stack([gain_one_term, gain_two_term])
        pair_task = Exchange(
            "grp",
            (grp_count, seq_count, sub_rows, 2 * HD),
            lambda ref, index: ref.at[:, index],
            block_of,
        )
        work = [
            split_columns("seq", shares),
            (pair_task, pair_blocks),
            gather_axis("seq", gain_terms),
            (gather_gating(gating_grads.shape), gating_grads),
        ]
        share_parts, pair_parts, gain_parts, gating_plane = exchange(8, work)
        gain_seq = jnp.sum(gain_parts, axis=0)
        shares = jnp.sum(share_parts.astype(jnp.float32), axis=0).astype(jnp.bfloat16)
        pair_parts = jnp.sum(pair_parts.astype(jnp.float32), axis=0).astype(jnp.bfloat16)
        pair_task = Exchange("seq", pair_parts.shape, block_of, block_of)
        _, pair_plane, share_plane, gain_parts = exchange(
            9,
            [
                (pair_task, pair_parts),
                (gather_plane(pair_parts.shape), 0),
                (gather_plane(shares.shape), shares),
                gather_axis("grp", gain_seq),
            ],
        )
        pair_plane = jnp.sum(pair_plane.astype(jnp.float32), axis=1).astype(jnp.bfloat16)

    gain_grads = jnp.sum(gain_parts, axis=0)

    tile_of_slot = (
        jnp.full((grp_count * slots_here,), tile_count, jnp.int32)
        .at[tile_owner_slots]
        .set(jnp.arange(tile_count, dtype=jnp.int32))
    )
    tiles_here = lax.dynamic_slice_in_dim(tile_of_slot, grp_here * slots_here, slots_here)
    feed_at = jnp.clip(tiles_here - attn_tiles, 0, 3 * hidden_tiles - 1)
    which, column = feed_at // hidden_tiles, feed_at % hidden_tiles
    is_query = tiles_here < query_tiles
    is_pair = (tiles_here >= query_tiles) & (tiles_here < query_tiles + 2)
    is_feed = tiles_here >= attn_tiles
    kind = jnp.where(is_feed, jnp.where(which < 2, 0, 1), jnp.where(is_pair, 3, 2))
    kind = jnp.where(tiles_here == tile_count, 4, kind)
    out_at = jnp.clip(tiles_here - query_tiles - 2, 0, query_tiles - 1)
    per_share = share_width // tile_width
    share_at = jnp.where(is_query, jnp.minimum(tiles_here, query_tiles - 1), out_at)
    at = jnp.stack(
        [
            kind,
            jnp.minimum(which, 1) * hidden_tiles + column,
            column,
            share_at // per_share * 2 * per_share
            + share_at % per_share
            + jnp.where(is_query, 0, per_share),
            jnp.where(is_pair, tiles_here - query_tiles, 0),
        ]
    )
    new_master, new_one, new_two = adam(
        at,
        gating_plane.reshape(-1, rows_block),
        down_plane.reshape(-1, rows_block),
        share_plane.reshape(-1, rows_block),
        pair_plane,
        left_basis_set,
        right_basis_set,
        master,
        moment_one,
        moment_two,
    )
    gain_one = BETA_ONE * gain_moment_one + (1.0 - BETA_ONE) * gain_grads
    gain_two = BETA_TWO * gain_moment_two + (1.0 - BETA_TWO) * gain_grads * gain_grads
    new_gains = gains - GAIN_RATE * gain_one / (jnp.sqrt(gain_two) + ADAM_EPS)
    return (
        block_out,
        input_grad,
        new_master,
        new_one,
        new_two,
        gain_grads,
        new_gains,
        gain_one,
        gain_two,
    )


def solution(mesh):
    return jax.shard_map(
        local,
        mesh=mesh,
        in_specs=(
            P(("grp", "seq"), None),
            P(("grp", "seq"), None),
            P(("grp", "seq")),
            P(),
            P("grp", "seq", None),
            P("grp", "seq", None),
            P("grp", "seq", None),
            P("grp", "seq", None),
            P("grp", "seq", None),
            P("grp", "seq", None),
            P(),
            P(),
            P(),
        ),
        out_specs=(
            P(("grp", "seq"), None),
            P(("grp", "seq"), None),
            P("grp", "seq", None),
            P("grp", "seq", None),
            P("grp", "seq", None),
            P(),
            P(),
            P(),
            P(),
        ),
        check_vma=False,
    )
```

```python
import functools
import math

import jax
import jax.numpy as jnp
from jax import lax
from jax.experimental import pallas as pl
from jax.experimental.pallas import tpu as pltpu
from jax.sharding import PartitionSpec as P

MODEL_WIDTH = 2048
NH = 16
HD = 128
FF = 5632
SEQLEN = 1024


NORM_EPS = 1e-05
BETA_ONE = 0.95
BETA_TWO = 0.95
ADAM_EPS = 1e-08
WEIGHT_DECAY = 0.01
LEARN_RATE = 0.03
GAIN_RATE = 1.5
ROPE_BASE = 10000.0
MASKED = -1e30
PRECISE = lax.Precision.HIGHEST


def contract(left_side, right_side):
    return lax.dot_general(
        left_side, right_side, (((0,), (0,)), ((), ())), preferred_element_type=jnp.float32
    )


def times_transpose(left_side, right_side):
    return lax.dot_general(
        left_side, right_side, (((1,), (1,)), ((), ())), preferred_element_type=jnp.float32
    )


def turn_tables(places):
    half_width = HD // 2
    frequency = ROPE_BASE ** (-(jnp.arange(half_width, dtype=jnp.float32) * 2.0) / HD)
    angles = places.astype(jnp.float32)[:, None] * frequency[None, :]
    return jnp.cos(angles), jnp.sin(angles)


def turn(rows, cosine, sine):
    cosine = jnp.concatenate([cosine, cosine], axis=1)
    sine = jnp.concatenate([-sine, sine], axis=1)
    return rows * cosine + pltpu.roll(rows, HD // 2, 1) * sine


def turn_back(rows, cosine, sine):
    return turn(rows, cosine, -sine)


def dot_last(left_side, right_side):
    return lax.dot_general(
        left_side, right_side, (((1,), (1,)), ((), ())), preferred_element_type=jnp.float32
    )


def dot_first(left_side, right_side):
    return lax.dot_general(
        left_side, right_side, (((0,), (0,)), ((), ())), preferred_element_type=jnp.float32
    )


SMALL_COST = pl.CostEstimate(flops=1, bytes_accessed=1, transcendentals=0)


def project_kernel(x_ref, w_ref, cosine_ref, sine_ref, out_ref):
    made = jnp.dot(x_ref[...], w_ref[...], preferred_element_type=jnp.float32)
    cosine, sine = cosine_ref[...], sine_ref[...]
    first, second = made[:, :HD], made[:, HD:]
    last = pl.program_id(0) == pl.num_programs(0) - 1
    out_ref[:, :HD] = turn(first, cosine, sine).astype(out_ref.dtype)
    out_ref[:, HD:] = jnp.where(last, second, turn(second, cosine, sine)).astype(out_ref.dtype)


def project(normed, weights, tables):
    rows, width = normed.shape
    steps = NH // 2 + 1
    return pl.pallas_call(
        project_kernel,
        grid=(steps,),
        in_specs=[
            pl.BlockSpec((rows, width), lambda j: (0, 0)),
            pl.BlockSpec((width, 2 * HD), lambda j: (0, j)),
            pl.BlockSpec((rows, HD // 2), lambda j: (0, 0)),
            pl.BlockSpec((rows, HD // 2), lambda j: (0, 0)),
        ],
        out_specs=pl.BlockSpec((rows, 2 * HD), lambda j: (0, j)),
        out_shape=jax.ShapeDtypeStruct((rows, steps * 2 * HD), jnp.bfloat16),
        compiler_params=pltpu.CompilerParams(vmem_limit_bytes=56 * 2**20),
        cost_estimate=SMALL_COST,
        name="project",
    )(normed, weights, *tables)


def score_mask(key_seg_ref, query_seg_ref, block, rows):
    keys = (block + 1) * rows
    same = key_seg_ref[:keys, :] == query_seg_ref[...]
    key_at = lax.broadcasted_iota(jnp.int32, (keys, rows), 0)
    query_at = lax.broadcasted_iota(jnp.int32, (keys, rows), 1) + block * rows
    return same & (key_at <= query_at)


def attend_kernel(at_ref, q_ref, k_ref, v_ref, key_seg_ref, query_seg_ref, context_ref, total_ref):
    scale = HD ** (-0.5)
    rows = q_ref.shape[0]
    for block in range(SEQLEN // rows):

        @pl.when(at_ref[0] == block)
        def _():
            keys = (block + 1) * rows
            scores = dot_last(k_ref[:keys, :], q_ref[...]) * scale
            scores = jnp.where(
                score_mask(key_seg_ref, query_seg_ref, block, rows), scores, MASKED
            )
            highest = jnp.max(scores, axis=0, keepdims=True)
            exponent = jnp.exp(scores - highest)
            totals = jnp.sum(exponent, axis=0, keepdims=True)
            probs_low = (exponent * (1.0 / totals)).astype(jnp.bfloat16)
            context = dot_first(probs_low, v_ref[:keys, :])
            context_ref[...] = context.astype(jnp.bfloat16)
            total_ref[0] = highest + jnp.log(totals)


def attend_back_head(
    place, q_ref, k_ref, v_ref, grad_ref, total_ref, key_seg_ref, query_seg_ref, key_cosine_ref,
    key_sine_ref, cosine_ref, sine_ref, query_grad_ref, pair_grad_ref, key_sum, value_sum,
):
    scale = HD ** (-0.5)
    rows = q_ref.shape[0]
    head = pl.program_id(0)

    @pl.when(head == 0)
    def _():
        key_sum[...] = jnp.zeros_like(key_sum)
        value_sum[...] = jnp.zeros_like(value_sum)

    for block in range(SEQLEN // rows):

        @pl.when(place == block)
        def _():
            keys = (block + 1) * rows
            queries, grads = q_ref[...], grad_ref[...]
            shifted = dot_last(k_ref[:keys, :], queries) * scale - total_ref[0]
            allowed = score_mask(key_seg_ref, query_seg_ref, block, rows)
            probs = jnp.where(allowed, jnp.exp(shifted), 0.0)
            prob_grad = dot_last(v_ref[:keys, :], grads)
            centre = jnp.sum(probs * prob_grad, axis=0, keepdims=True)
            score_grad = (probs * (prob_grad - centre) * scale).astype(jnp.bfloat16)
            value_sum[:keys, :] += jnp.dot(
                probs.astype(jnp.bfloat16), grads, preferred_element_type=jnp.float32
            )
            key_sum[:keys, :] += jnp.dot(score_grad, queries, preferred_element_type=jnp.float32)
            query_grad = dot_first(score_grad, k_ref[:keys, :])
            query_grad_ref[...] = turn_back(query_grad, cosine_ref[...], sine_ref[...]).astype(
                jnp.bfloat16
            )

    @pl.when(head == pl.num_programs(0) - 1)
    def _():
        pair_grad_ref[:, :HD] = turn_back(
            key_sum[...], key_cosine_ref[...], key_sine_ref[...]
        ).astype(jnp.bfloat16)
        pair_grad_ref[:, HD:] = value_sum[...].astype(jnp.bfloat16)


def attend_back_kernel(at_ref, *refs):
    attend_back_head(at_ref[0], *refs)


def attention_specs(kinds, rows):
    specs = {
        "at": pl.BlockSpec(memory_space=pltpu.SMEM),
        "head": pl.BlockSpec((rows, HD), lambda h: (0, h)),
        "branch": pl.BlockSpec((rows, MODEL_WIDTH), lambda h: (0, 0)),
        "keys": pl.BlockSpec((SEQLEN, HD), lambda h: (0, 0)),
        "values": pl.BlockSpec((SEQLEN, HD), lambda h: (0, 1)),
        "pair": pl.BlockSpec((SEQLEN, 2 * HD), lambda h: (0, 0)),
        "total": pl.BlockSpec((1, 1, rows), lambda h: (h, 0, 0)),
        "key_seg": pl.BlockSpec((SEQLEN, 1), lambda h: (0, 0)),
        "query_seg": pl.BlockSpec((1, rows), lambda h: (0, 0)),
        "key_table": pl.BlockSpec((SEQLEN, HD // 2), lambda h: (0, 0)),
        "table": pl.BlockSpec((rows, HD // 2), lambda h: (0, 0)),
    }
    return [specs[kind] for kind in kinds]


def attend(at, projected, pairs, key_segs, query_segs):
    rows = projected.shape[0]
    columns = NH * HD
    return pl.pallas_call(
        attend_kernel,
        grid=(NH,),
        in_specs=attention_specs(["at", "head", "keys", "values", "key_seg", "query_seg"], rows),
        out_specs=attention_specs(["head", "total"], rows),
        out_shape=(
            jax.ShapeDtypeStruct((rows, columns), jnp.bfloat16),
            jax.ShapeDtypeStruct((NH, 1, rows), jnp.float32),
        ),
        compiler_params=pltpu.CompilerParams(vmem_limit_bytes=32 * 2**20),
        cost_estimate=SMALL_COST,
        name="attend",
    )(at, projected, pairs, pairs, key_segs[:, None], query_segs[None, :])


def attend_back(at, projected, pairs, grads, totals, key_segs, query_segs, key_tables, tables):
    rows = projected.shape[0]
    columns = NH * HD
    return pl.pallas_call(
        attend_back_kernel,
        grid=(NH,),
        in_specs=attention_specs(
            ["at", "head", "keys", "values", "head", "total", "key_seg", "query_seg"]
            + ["key_table", "key_table", "table", "table"],
            rows,
        ),
        out_specs=attention_specs(["head", "pair"], rows),
        out_shape=(
            jax.ShapeDtypeStruct((rows, columns), jnp.bfloat16),
            jax.ShapeDtypeStruct((SEQLEN, 2 * HD), jnp.bfloat16),
        ),
        scratch_shapes=[pltpu.VMEM((SEQLEN, HD), jnp.float32)] * 2,
        compiler_params=pltpu.CompilerParams(vmem_limit_bytes=32 * 2**20),
        cost_estimate=SMALL_COST,
        name="attend_back",
    )(
        at, projected, pairs, pairs, grads, totals, key_segs[:, None], query_segs[None, :],
        *key_tables, *tables,
    )


def own_columns(grp, own):
    return pl.ds(pl.multiple_of((grp * own) % 128, math.gcd(own, 128)), own)


def load_weights(parts, weights, sems):
    count, rows, _ = parts[0].shape
    halves = len(parts)
    return [
        pltpu.make_async_copy(
            parts[half].at[block],
            weights.at[pl.ds((block * halves + half) * rows, rows)],
            sems.at[block * halves + half],
        )
        for half in range(halves)
        for block in range(count)
    ]


def feed_block(own, first, x, cot, weights, act_ref, gate_grad_ref, up_grad_ref, two_ref, out_ref):
    low = jnp.bfloat16
    wide = jnp.float32
    cols = act_ref.shape[0]
    gate = jnp.dot(x, weights[:, :cols], preferred_element_type=wide)
    upper = jnp.dot(x, weights[:, cols : 2 * cols], preferred_element_type=wide)
    act_grad = jnp.dot(cot, weights[:, 2 * cols :], preferred_element_type=wide)
    column = lax.broadcasted_iota(jnp.int32, gate.shape, 1)
    real = (column >= first) & (column < first + own)
    sigmoid = 1.0 / (1.0 + jnp.exp(-gate))
    silu = gate * sigmoid
    activated = jnp.where(real, silu * upper, 0.0).astype(low)
    act_grad = jnp.where(real, act_grad, 0.0)
    gate_grad = (act_grad * upper * sigmoid * (1.0 + gate * (1.0 - sigmoid))).astype(low)
    up_grad = (act_grad * silu).astype(low)
    act_ref[...] = jnp.transpose(activated)
    gate_grad_ref[...] = jnp.transpose(gate_grad)
    up_grad_ref[...] = jnp.transpose(up_grad)
    two = dot_last(gate_grad, weights[:, :cols]) + dot_last(up_grad, weights[:, cols : 2 * cols])
    two_ref[...] = two.astype(low)
    out_ref[...] = dot_last(activated, weights[:, 2 * cols :]).astype(low)


def feed_kernel(own, real_ref, x_ref, cot_ref, *refs):
    parts, refs = refs[:-7], refs[-7:]
    weights, sems = refs[5:]

    @pl.when(pl.program_id(0) == 0)
    def _():
        copies = load_weights(parts, weights, sems)
        for copy in copies:
            copy.start()
        for copy in copies:
            copy.wait()

    feed_block(own, real_ref[0], x_ref[...], cot_ref[...], weights, *refs[:5])


def feed_forward(own, real_cols, x, cot, parts, seq_count):
    tokens_all, width = x.shape
    _, rows, cols = parts[0].shape
    cols = cols // 3
    step = 256
    low = jnp.bfloat16
    block = pl.BlockSpec((step, width), lambda i: (i, 0))
    narrow = pl.BlockSpec((cols, step), lambda i: (0, i))
    return pl.pallas_call(
        functools.partial(feed_kernel, own),
        grid=(tokens_all // step,),
        in_specs=[pl.BlockSpec(memory_space=pltpu.SMEM), block, block]
        + [pl.BlockSpec(memory_space=pl.ANY)] * len(parts),
        out_specs=[narrow, narrow, narrow, block, block],
        out_shape=[jax.ShapeDtypeStruct((cols, tokens_all), low)] * 3
        + [jax.ShapeDtypeStruct((tokens_all, width), low)] * 2,
        scratch_shapes=[
            pltpu.VMEM((width, 3 * cols), low),
            pltpu.SemaphoreType.DMA((len(parts) * seq_count,)),
        ],
        compiler_params=pltpu.CompilerParams(vmem_limit_bytes=52 * 2**20),
        cost_estimate=SMALL_COST,
        name="feed_forward",
    )(real_cols, x, cot, *parts)


def feed_gather_kernel(
    own, first, second, halves, real_ref, own_ref, context_ref, cot_ref, cot_all_ref, *refs
):
    parts, refs = refs[:halves], refs[halves:]
    (
        gate_grad_ref, up_grad_ref, two_ref, out_ref, second_ref, context_plane_ref, down_out,
        blocks, weights, act_block, act, x_block, stage, load_sems, keep_sems, x_sems, out_sems,
        first_send, first_recv, second_send, second_recv,
    ) = refs
    step = pl.program_id(0)
    grp, seq = lax.axis_index("grp"), lax.axis_index("seq")
    first.start(own_ref, blocks, (first_send, first_recv), grp, seq, begin=False)
    second.start(context_ref, context_plane_ref, (second_send, second_recv), grp, seq, begin=False)
    loads = load_weights(parts, weights, load_sems)
    cols = act.shape[0]
    step_rows = act_block.shape[1]
    rows = x_block.shape[2]
    count = cot_all_ref.shape[1] // rows

    @pl.when(step == 0)
    def _():
        for copy in loads:
            copy.start()
        barrier = pltpu.get_barrier_semaphore()
        for device in first.peers(grp, seq):
            pl.semaphore_signal(barrier, inc=1, device_id=device, device_id_type=MESH)
        pl.semaphore_wait(barrier, 3)
        first.begin()
        first.kept.wait()
        for copy in loads:
            copy.wait()

    @pl.when(step == 1)
    def _():
        first.due[7].wait_recv()

    @pl.when(step == 2)
    def _():
        for came in (1, 4, 2):
            first.pass_on(came)

    @pl.when(step == 3)
    def _():
        first.pass_on(5)
        second.begin()

    @pl.when(step == 4)
    def _():
        first.due[8].wait_recv()
        first.due[9].wait_recv()
        first.pass_on(6)
        first.pass_on(3)

    @pl.when(step == 5)
    def _():
        first.due[10].wait_recv()
        first.due[11].wait_recv()

    @pl.when(step == 7)
    def _():
        first.due[12].wait_recv()
        first.due[13].wait_recv()
        second.pass_on(1)
        second.pass_on(4)

    keep = pltpu.make_async_copy(blocks.at[step], second_ref.at[step], keep_sems.at[step])
    keep.start()
    feed_block(
        own, real_ref[0], blocks[step], cot_ref[...], weights, act_block, gate_grad_ref, up_grad_ref,
        two_ref, out_ref,
    )
    act[:, pl.ds(pl.multiple_of(step * step_rows, step_rows), step_rows)] = act_block[...]

    def x_copy(at):
        view = cot_all_ref.at[:, pl.ds(pl.multiple_of(at * rows, rows), rows)]
        return pltpu.make_async_copy(view, x_block.at[at % 2], x_sems.at[at % 2])

    def out_copy(at):
        place = pl.ds(pl.multiple_of(at * own, own), own)
        mine = stage.at[at % 2, own_columns(grp, own)]
        return pltpu.make_async_copy(mine, down_out.at[place], out_sems.at[at % 2])

    @pl.when(step == 7)
    def _():
        x_copy(0).start()
        second.pass_on(2)
        second.pass_on(5)

        def one(at, _):
            x_copy(at).wait()

            @pl.when(at + 1 < count)
            def _():
                x_copy(at + 1).start()

            @pl.when(at >= 2)
            def _():
                out_copy(at - 2).wait()

            stage[at % 2] = jnp.dot(
                act[...], x_block[at % 2], preferred_element_type=jnp.float32
            ).astype(stage.dtype)
            out_copy(at).start()
            return 0

        lax.fori_loop(0, count, one, 0)
        second.pass_on(6)
        second.pass_on(3)
        out_copy(count - 2).wait()
        out_copy(count - 1).wait()
        second.finish()
        for copy in first.out[1:]:
            copy.wait_send()
        for at in range(8):
            pltpu.make_async_copy(blocks.at[at], second_ref.at[at], keep_sems.at[at]).wait()


def feed_gather(number, own, real_cols, normed, context, cot, parts, seq_count):
    rows, width = normed.shape
    cols = parts[0].shape[2] // 3
    low = jnp.bfloat16
    block = pl.BlockSpec((rows, width), lambda i: (i, 0))
    narrow = pl.BlockSpec((cols, rows), lambda i: (0, i))
    first = gather_plane(normed.shape, placed=True)
    second = gather_plane(context.shape, placed=True)
    hbm = pl.BlockSpec(memory_space=pl.ANY)
    plane = jax.ShapeDtypeStruct((8, rows, width), low)
    model_rows = width // seq_count
    return pl.pallas_call(
        functools.partial(feed_gather_kernel, own, first, second, len(parts)),
        grid=(8,),
        in_specs=[pl.BlockSpec(memory_space=pltpu.SMEM), hbm, hbm, block, hbm]
        + [hbm] * len(parts),
        out_specs=[narrow, narrow, block, block, hbm, hbm, hbm],
        out_shape=[jax.ShapeDtypeStruct((cols, 8 * rows), low)] * 2
        + [jax.ShapeDtypeStruct((8 * rows, width), low)] * 2
        + [plane, plane, jax.ShapeDtypeStruct((seq_count * own, model_rows), low)],
        scratch_shapes=[
            pltpu.VMEM((8, rows, width), low),
            pltpu.VMEM((width, 3 * cols), low),
            pltpu.VMEM((cols, rows), low),
            pltpu.VMEM((cols, 8 * rows), low),
            pltpu.VMEM((2, 8 * rows, model_rows), low),
            pltpu.VMEM((2, cols, model_rows), low),
            pltpu.SemaphoreType.DMA((seq_count * len(parts),)),
            pltpu.SemaphoreType.DMA((8,)),
            pltpu.SemaphoreType.DMA((2,)),
            pltpu.SemaphoreType.DMA((2,)),
        ]
        + [pltpu.SemaphoreType.DMA((14,))] * 4,
        compiler_params=pltpu.CompilerParams(
            collective_id=number, has_side_effects=True, vmem_limit_bytes=60 * 2**20
        ),
        cost_estimate=SMALL_COST,
        name="feed_gather",
    )(real_cols, normed, context, cot, cot, *parts)


def weight_grad_kernel(left_ref, x_ref, out_ref):
    out_ref[...] = jnp.dot(
        left_ref[...], x_ref[...], preferred_element_type=jnp.float32
    ).astype(out_ref.dtype)


def weight_grad(left, x, seq_count):
    cols, tokens_all = left.shape
    rows = x.shape[1] // seq_count
    return pl.pallas_call(
        weight_grad_kernel,
        grid=(seq_count,),
        in_specs=[
            pl.BlockSpec((cols, tokens_all), lambda i: (0, 0)),
            pl.BlockSpec((tokens_all, rows), lambda i: (0, i)),
        ],
        out_specs=pl.BlockSpec((cols, rows), lambda i: (i, 0)),
        out_shape=jax.ShapeDtypeStruct((seq_count * cols, rows), jnp.bfloat16),
        compiler_params=pltpu.CompilerParams(vmem_limit_bytes=40 * 2**20),
        cost_estimate=SMALL_COST,
        name="weight_grad",
    )(left, x)


def share_grad_kernel(query_ref, out_ref, normed_ref, context_ref, grads_ref, turned):
    half = query_ref.shape[1]

    @pl.when(pl.program_id(0) == 0)
    def _():
        turned[0], turned[1] = jnp.transpose(query_ref[...]), jnp.transpose(out_ref[...])

    for at, right in enumerate((normed_ref, context_ref)):
        made = jnp.dot(turned[at], right[...], preferred_element_type=jnp.float32)
        grads_ref[at * half : (at + 1) * half, :] = made.astype(grads_ref.dtype)


def share_grad(query_share, out_share, normed, context):
    tokens_all, width = normed.shape
    columns = query_share.shape[1]
    step = 512
    narrow = pl.BlockSpec((tokens_all, columns), lambda i: (0, 0))
    block = pl.BlockSpec((tokens_all, step), lambda i: (0, i))
    return pl.pallas_call(
        share_grad_kernel,
        grid=(width // step,),
        in_specs=[narrow, narrow, block, block],
        out_specs=pl.BlockSpec((2 * columns, step), lambda i: (0, i)),
        out_shape=jax.ShapeDtypeStruct((2 * columns, width), jnp.bfloat16),
        scratch_shapes=[pltpu.VMEM((2, columns, tokens_all), jnp.bfloat16)],
        compiler_params=pltpu.CompilerParams(vmem_limit_bytes=60 * 2**20),
        cost_estimate=SMALL_COST,
        name="share_grad",
    )(query_share, out_share, normed, context)


def pick_kernel(rows, feed_ref, attn_ref, tiles_ref, feed_out, attn_out, sems):
    grp = lax.axis_index("grp")
    width = tiles_ref.shape[2]
    copies = []
    for at in range(feed_ref.shape[0]):
        copies.append(
            (tiles_ref.at[feed_ref[at]], feed_out.at[:, at * width : (at + 1) * width])
        )
    share = pl.ds(pl.multiple_of(grp * rows, rows), rows)
    for at in range(attn_ref.shape[0]):
        copies.append(
            (tiles_ref.at[attn_ref[at], share], attn_out.at[:, at * width : (at + 1) * width])
        )
    copies = [
        pltpu.make_async_copy(source, target, sems.at[at])
        for at, (source, target) in enumerate(copies)
    ]
    for copy in copies:
        copy.start()
    for copy in copies:
        copy.wait()


def pick(tiles, feed_slots, attn_slots):
    _, rows, width = tiles.shape
    share = rows // lax.axis_size("grp")
    feed, attn = feed_slots.shape[0], attn_slots.shape[0]
    return pl.pallas_call(
        functools.partial(pick_kernel, share),
        in_specs=[pl.BlockSpec(memory_space=pltpu.SMEM)] * 2 + [pl.BlockSpec(memory_space=pl.ANY)],
        out_specs=[pl.BlockSpec(memory_space=pltpu.VMEM)] * 2,
        out_shape=[
            jax.ShapeDtypeStruct((rows, feed * width), tiles.dtype),
            jax.ShapeDtypeStruct((share, attn * width), tiles.dtype),
        ],
        scratch_shapes=[pltpu.SemaphoreType.DMA((feed + attn,))],
        cost_estimate=SMALL_COST,
        name="pick",
    )(feed_slots, attn_slots, tiles)


def adam_kernel(group, at_ref, *refs):
    feeds = [refs[at * group : (at + 1) * group] for at in range(4)]
    left_ref, right_ref, master_ref, one_ref, two_ref = refs[4 * group : 4 * group + 5]
    new_master_ref, new_one_ref, new_two_ref, grad = refs[4 * group + 5 :]
    low = jnp.bfloat16
    for slot in range(group):
        kind = at_ref[0, pl.program_id(0) * group + slot]
        for number in range(3):

            @pl.when(kind == number)
            def _():
                grad[slot] = feeds[number][slot][...]

        @pl.when(kind == 3)
        def _():
            pair = feeds[3][slot][...].reshape(grad.shape[2], grad.shape[1])
            grad[slot] = jnp.transpose(pair.astype(jnp.float32)).astype(grad.dtype)

        @pl.when(kind == 4)
        def _():
            grad[slot] = jnp.zeros(grad.shape[1:], grad.dtype)

    slots = range(group)
    left = [left_ref[slot].astype(low) for slot in slots]
    right = [right_ref[slot].astype(low) for slot in slots]
    turned = [
        jnp.dot(grad[slot], left[slot], preferred_element_type=jnp.float32) for slot in slots
    ]
    turned = [dot_first(turned[slot].astype(low), right[slot]) for slot in slots]
    scaled = []
    for slot in slots:
        new_one = BETA_ONE * one_ref[slot] + (1.0 - BETA_ONE) * turned[slot]
        new_two = BETA_TWO * two_ref[slot] + (1.0 - BETA_TWO) * turned[slot] * turned[slot]
        new_one_ref[slot], new_two_ref[slot] = new_one, new_two
        scaled.append((new_one / (jnp.sqrt(new_two) + ADAM_EPS)).astype(low))
    restored = [dot_last(scaled[slot], right[slot]).astype(low) for slot in slots]
    restored = [
        jnp.dot(left[slot], restored[slot], preferred_element_type=jnp.float32) for slot in slots
    ]
    for slot in slots:
        new_master_ref[slot] = (
            master_ref[slot] * (1.0 - LEARN_RATE * WEIGHT_DECAY) - LEARN_RATE * restored[slot]
        )


def adam(at, gating, down, shares, pairs, left, right, master, one, two):
    slots, rows, width = master.shape
    group = 3 if slots % 3 == 0 else 1
    tile = pl.BlockSpec((group, rows, width), lambda i, at: (i, 0, 0))
    shape = jax.ShapeDtypeStruct(master.shape, jnp.float32)

    def feed(row):
        return [
            pl.BlockSpec((width, rows), lambda i, at, slot=slot: (at[row, i * group + slot], 0))
            for slot in range(group)
        ]

    pair = [
        pl.BlockSpec(
            (*pairs.shape[:2], width), lambda i, at, slot=slot: (0, 0, at[4, i * group + slot])
        )
        for slot in range(group)
    ]
    return pl.pallas_call(
        functools.partial(adam_kernel, group),
        grid_spec=pltpu.PrefetchScalarGridSpec(
            num_scalar_prefetch=1,
            grid=(slots // group,),
            in_specs=feed(1)
            + feed(2)
            + feed(3)
            + pair
            + [
                pl.BlockSpec((group, rows, rows), lambda i, at: (i, 0, 0)),
                pl.BlockSpec((group, width, width), lambda i, at: (i, 0, 0)),
                tile,
                tile,
                tile,
            ],
            out_specs=[tile] * 3,
            scratch_shapes=[pltpu.VMEM((group, width, rows), jnp.bfloat16)],
        ),
        out_shape=[shape] * 3,
        compiler_params=pltpu.CompilerParams(vmem_limit_bytes=60 * 2**20),
        cost_estimate=SMALL_COST,
        name="adam",
    )(
        at, *[gating] * group, *[down] * group, *[shares] * group, *[pairs] * group,
        left, right, master, one, two,
    )


MESH = pl.DeviceIdType.MESH


def remote(source, target, sems, at, device):
    return pltpu.make_async_remote_copy(
        src_ref=source,
        dst_ref=target,
        send_sem=sems[0].at[at],
        recv_sem=sems[1].at[at],
        device_id=device,
        device_id_type=MESH,
    )


def columns_of(ref, index, width):
    return ref.at[:, pl.ds(pl.multiple_of(index * width, width), width)]


def rows_of(ref, index, height):
    return ref.at[pl.ds(pl.multiple_of(index * height, height), height), :]


PLACES = {0: 0, 1: 1, 2: 2, 4: 3, 3: 4, 5: 5, 6: 6, 7: 7}


def flip(device, bits):
    core, side_x, side_y = device % 2, (device // 2) % 2, device // 4
    for bit, there in ((1, 1 - 2 * core), (2, 2 - 4 * side_x), (4, 4 - 8 * side_y)):
        if bits & bit:
            device = device + there
    return device


class PlacedExchange:
    axis = "grp"
    sem_count = 8

    def __init__(self, out_shape, source_view):
        self.out_shape, self.source_view = out_shape, source_view

    def peers(self, grp, seq):
        for bits in range(1, 8):
            yield flip(grp, bits), seq

    def start(self, source, target, sems, grp, seq):
        self.own = pltpu.make_async_copy(
            self.source_view(source, grp), target.at[0], sems[0].at[0]
        )
        self.own.start()
        self.copies = []
        for bits in range(1, 8):
            there = flip(grp, bits)
            copy = remote(
                self.source_view(source, there), target.at[PLACES[bits]], sems, bits, (there, seq)
            )
            copy.start()
            self.copies.append(copy)

    def forward(self):
        return iter(())

    def finish(self):
        for copy in self.copies:
            copy.wait()
        self.own.wait()


class Exchange:
    def __init__(self, axis, out_shape, source_view, target_view):
        self.axis, self.out_shape = axis, out_shape
        self.source_view, self.target_view = source_view, target_view
        self.count = lax.axis_size(axis)
        self.sem_count = self.count

    def peers(self, grp, seq):
        me = grp if self.axis == "grp" else seq
        for step in range(1, self.count):
            there = (me + step) % self.count
            yield (there, seq) if self.axis == "grp" else (grp, there)

    def start(self, source, target, sems, grp, seq, begin=True):
        me = grp if self.axis == "grp" else seq
        self.own = pltpu.make_async_copy(
            self.source_view(source, me), self.target_view(target, me), sems[0].at[0]
        )
        self.sent, self.due = [], []
        for step, device in enumerate(self.peers(grp, seq), 1):
            there = (me + step) % self.count
            back = (me + self.count - step) % self.count
            self.sent.append(
                remote(
                    self.source_view(source, there), self.target_view(target, me), sems, step, device
                )
            )
            self.due.append(
                remote(
                    self.source_view(source, back), self.target_view(target, back), sems, step, device
                )
            )
        if begin:
            self.begin()

    def begin(self):
        for copy in [self.own] + self.sent:
            copy.start()

    def forward(self):
        return iter(())

    def finish(self):
        for copy in self.due:
            copy.wait_recv()
        for copy in self.sent:
            copy.wait_send()
        self.own.wait()


class PlaneGather:
    axis = "grp"
    sem_count = 14

    def __init__(self, out_shape, source_view, target_view, half_of, placed):
        self.out_shape, self.placed = out_shape, placed
        self.source_view, self.target_view, self.half_of = source_view, target_view, half_of

    def peers(self, grp, seq):
        for bits in (1, 2, 4):
            yield flip(grp, bits), seq

    def start(self, source, target, sems, grp, seq, begin=True):
        def part(device, bits, piece):
            view = self.target_view(target, PLACES[bits] if self.placed else flip(device, bits))
            return view if piece == "all" else self.half_of(view, piece == "b")

        def own(piece):
            view = self.source_view(source, grp)
            return view if piece == "all" else self.half_of(view, piece == "b")

        self.out, self.due = [None], [None]
        for via, here, there, piece in (
            (2, 0, 2, "a"),
            (2, 0, 2, "b"),
            (2, 4, 6, "b"),
            (4, 0, 4, "b"),
            (4, 0, 4, "a"),
            (4, 2, 6, "a"),
            (1, 0, 1, "all"),
            (1, 2, 3, "a"),
            (1, 2, 3, "b"),
            (1, 4, 5, "b"),
            (1, 4, 5, "a"),
            (1, 6, 7, "a"),
            (1, 6, 7, "b"),
        ):
            device = flip(grp, via)
            view = own(piece) if here == 0 else part(grp, here, piece)
            at = len(self.out)
            self.out.append(remote(view, part(device, there, piece), sems, at, (device, seq)))
            self.due.append(remote(view, part(grp, there, piece), sems, at, (device, seq)))
        self.kept = pltpu.make_async_copy(own("all"), part(grp, 0, "all"), sems[0].at[0])
        if begin:
            self.begin()

    def begin(self):
        self.kept.start()
        for at in (1, 4, 2, 5, 7):
            self.out[at].start()

    def pass_on(self, came):
        self.due[came].wait_recv()
        for at in {1: (6, 8), 4: (3, 10), 2: (9,), 5: (11,), 6: (12,), 3: (13,)}[came]:
            self.out[at].start()

    def forward(self):
        for pair in ((1, 4), (2, 5), (6, 3)):
            for came in pair:
                self.pass_on(came)
            yield

    def finish(self):
        for copy in self.due[7:]:
            copy.wait_recv()
        for copy in self.out[1:]:
            copy.wait_send()
        self.kept.wait()


def add_rows(total, first, second):
    step = 32

    def some(at, _):
        rows = pl.ds(pl.multiple_of(at * step, step), step)
        total[rows, :] = (
            first[rows, :].astype(jnp.float32) + second[rows, :].astype(jnp.float32)
        ).astype(total.dtype)
        return 0

    lax.fori_loop(0, total.shape[0] // step, some, 0)


class PlaneSum:
    axis = "grp"
    sem_count = 15

    def __init__(self, rows, columns, placed=True):
        self.rows, self.columns, self.placed = rows, columns, placed
        self.out_shape = (rows, columns)

    def scratch(self):
        low = jnp.bfloat16
        shape = (self.rows, self.columns)
        half = (self.rows // 2, self.columns)
        return [
            pltpu.VMEM((4, *shape), low),
            pltpu.VMEM((4, *shape), low),
            pltpu.VMEM((2, *half), low),
            pltpu.VMEM((2, *shape), low),
        ]

    def peers(self, grp, seq):
        for bits in (1, 2, 4):
            yield flip(grp, bits), seq

    def start(self, source, target, sems, grp, seq, scratch, begin=True):
        self.mine, self.core_in, self.halves, self.wholes = scratch
        core, side_x, side_y = [(flip(grp, bits), seq) for bits in (1, 2, 4)]
        half = self.rows // 2
        self.low, self.high = low, high = pl.ds(0, half), pl.ds(half, half)
        mine, halves, wholes = self.mine, self.halves, self.wholes

        def block(bits):
            return source.at[PLACES[bits] if self.placed else flip(grp, bits)]

        self.copies = [
            remote(block(bits), self.core_in.at[at], sems, at, core)
            for at, bits in enumerate((7, 3, 5, 1))
        ] + [
            remote(mine.at[0, low], halves.at[0], sems, 4, side_x),
            remote(mine.at[0, high], halves.at[1], sems, 5, side_y),
            remote(mine.at[1, low], wholes.at[0, low], sems, 6, side_x),
            remote(mine.at[2, high], wholes.at[1, high], sems, 7, side_y),
            remote(mine.at[1, high], wholes.at[0, high], sems, 8, side_x),
            remote(mine.at[2, low], wholes.at[1, low], sems, 9, side_y),
        ]
        self.loads = [
            pltpu.make_async_copy(block(bits), mine.at[at], sems[0].at[10 + at])
            for at, bits in enumerate((6, 2, 4, 0))
        ]
        if target is not None:
            self.store = pltpu.make_async_copy(mine.at[3], target, sems[0].at[14])
        if begin:
            self.begin()

    def begin(self):
        for copy in self.copies[:4] + self.loads:
            copy.start()

    def first_sums(self):
        for came, then in ((0, (4, 5)), (1, (6,)), (2, (7,)), (3, ())):
            self.copies[came].wait_recv()
            self.loads[came].wait()
            add_rows(self.mine.at[came], self.mine.at[came], self.core_in.at[came])
            for at in then:
                self.copies[at].start()

    def forward(self):
        mine, low, high = self.mine, self.low, self.high
        yield
        self.copies[5].wait_recv()
        add_rows(mine.at[1, high], mine.at[1, high], self.halves.at[1])
        self.copies[8].start()
        self.copies[4].wait_recv()
        add_rows(mine.at[2, low], mine.at[2, low], self.halves.at[0])
        self.copies[9].start()

    def total(self):
        mine = self.mine
        for at, side, rows in ((6, 0, self.low), (7, 1, self.high), (8, 0, self.high), (9, 1, self.low)):
            self.copies[at].wait_recv()
            add_rows(mine.at[3, rows], mine.at[3, rows], self.wholes.at[side, rows])
        return mine.at[3]

    def finish(self):
        self.total()
        self.store.start()
        for copy in self.copies:
            copy.wait_send()
        self.store.wait()


class LineGather:
    axis = "seq"

    def __init__(self, shape):
        self.count = lax.axis_size("seq")
        self.out_shape = (self.count, *shape)
        self.sem_count = 2 * self.count

    def peers(self, grp, seq):
        for step in range(1, self.count):
            yield grp, (seq + step) % self.count

    def start(self, source, target, sems, grp, seq):
        self.seq, self.sems = seq, sems
        self.own = pltpu.make_async_copy(source, target.at[seq], sems[0].at[0])
        self.own.start()

        def make(away, up):
            there = (seq + (1 if up else self.count - 1)) % self.count
            block = (seq + (self.count - away if up else away)) % self.count
            view = source if away == 0 else target.at[block]
            at = 1 + away if up else self.count + away
            return remote(view, target.at[block], sems, at, (grp, there))

        def came(away, up):
            block = (seq + (self.count - away if up else away)) % self.count
            at = away if up else self.count + away - 1
            side = (seq + (self.count - 1 if up else 1)) % self.count
            return remote(target.at[block], target.at[block], sems, at, (grp, side))

        self.make, self.came = make, came
        self.has = lambda away, up: (seq - away >= 0) if up else (seq + away < self.count)
        self.last = lambda up: (seq + 1 < self.count) if up else (seq >= 1)
        for up in (True, False):

            @pl.when(self.last(up))
            def _():
                make(0, up).start()

    def forward(self):
        for away in range(1, self.count):
            for up in (True, False):

                @pl.when(self.has(away, up))
                def _():
                    self.came(away, up).wait_recv()
                    if away < self.count - 1:

                        @pl.when(self.last(up))
                        def _():
                            self.make(away, up).start()

            yield

    def finish(self):
        for away in range(self.count - 1):
            for up in (True, False):

                @pl.when(self.has(away, up) & self.last(up))
                def _():
                    self.make(away, up).wait_send()
        self.own.wait()


def attend_back_sum_kernel(
    sum_task, gather_task, q_ref, k_ref, v_ref, branch_ref, total_ref, key_seg_ref, query_seg_ref,
    key_cosine_ref, key_sine_ref, cosine_ref, sine_ref, part_hbm, down_hbm, weights_hbm,
    query_grad_ref, pair_grad_ref, sum_hbm, down_plane, key_sum, value_sum, grad_ref, w_block,
    w_sems, mine, core_in, halves, wholes, sum_send, sum_recv, gather_send, gather_recv,
):
    step = pl.program_id(0)
    grp, seq = lax.axis_index("grp"), lax.axis_index("seq")
    scratch = (mine, core_in, halves, wholes)
    sum_task.start(part_hbm, sum_hbm, (sum_send, sum_recv), grp, seq, scratch, begin=False)
    gather_task.start(down_hbm, down_plane, (gather_send, gather_recv), grp, seq, begin=False)

    def w_copy(at):
        rows = pl.ds(pl.multiple_of(at * HD, HD), HD)
        view = weights_hbm.at[rows, pl.ds((NH + 2) * HD, MODEL_WIDTH)]
        return pltpu.make_async_copy(view, w_block.at[at % 2], w_sems.at[at % 2])

    @pl.when(step == 0)
    def _():
        w_copy(step).start()
        barrier = pltpu.get_barrier_semaphore()
        for device in sum_task.peers(grp, seq):
            pl.semaphore_signal(barrier, inc=1, device_id=device, device_id_type=MESH)
        pl.semaphore_wait(barrier, 3)
        sum_task.begin()
        gather_task.begin()

    @pl.when(step == 6)
    def _():
        sum_task.first_sums()

    w_copy(step).wait()

    @pl.when(step + 1 < pl.num_programs(0))
    def _():
        w_copy(step + 1).start()

    grad_ref[...] = dot_last(branch_ref[...], w_block[step % 2]).astype(grad_ref.dtype)
    attend_back_head(
        seq, q_ref, k_ref, v_ref, grad_ref, total_ref, key_seg_ref, query_seg_ref, key_cosine_ref,
        key_sine_ref, cosine_ref, sine_ref, query_grad_ref, pair_grad_ref, key_sum, value_sum,
    )

    @pl.when(step == pl.num_programs(0) - 1)
    def _():
        hand_on([gather_task, sum_task])
        gather_task.finish()
        sum_task.finish()


def attend_back_sum(
    number, projected, pairs, branch_grad, totals, key_segs, query_segs, key_tables, tables, part,
    down, weights,
):
    rows = projected.shape[0]
    columns = NH * HD
    low = jnp.bfloat16
    sum_task = PlaneSum(*part.shape[1:])
    gather_task = gather_plane(down.shape)
    hbm = pl.BlockSpec(memory_space=pl.ANY)
    return pl.pallas_call(
        functools.partial(attend_back_sum_kernel, sum_task, gather_task),
        grid=(NH,),
        in_specs=attention_specs(
            ["head", "keys", "values", "branch", "total", "key_seg", "query_seg"]
            + ["key_table", "key_table", "table", "table"],
            rows,
        )
        + [hbm, hbm, hbm],
        out_specs=attention_specs(["head", "pair"], rows) + [hbm, hbm],
        out_shape=[
            jax.ShapeDtypeStruct((rows, columns), low),
            jax.ShapeDtypeStruct((SEQLEN, 2 * HD), low),
            jax.ShapeDtypeStruct(sum_task.out_shape, low),
            jax.ShapeDtypeStruct(gather_task.out_shape, low),
        ],
        scratch_shapes=[pltpu.VMEM((SEQLEN, HD), jnp.float32)] * 2
        + [
            pltpu.VMEM((rows, HD), low),
            pltpu.VMEM((2, HD, MODEL_WIDTH), low),
            pltpu.SemaphoreType.DMA((2,)),
        ]
        + sum_task.scratch()
        + [pltpu.SemaphoreType.DMA((sum_task.sem_count,))] * 2
        + [pltpu.SemaphoreType.DMA((gather_task.sem_count,))] * 2,
        compiler_params=pltpu.CompilerParams(
            collective_id=number, has_side_effects=True, vmem_limit_bytes=48 * 2**20
        ),
        cost_estimate=SMALL_COST,
        name="attend_back_sum",
    )(
        projected, pairs, pairs, branch_grad, totals, key_segs[:, None], query_segs[None, :],
        *key_tables, *tables, part, down, weights,
    )


def block_kernel(
    first, second, pair_task, key_seg_ref, query_seg_ref, normed_ref, tokens_ref, gain_ref,
    cosine_ref, sine_ref, cot_hbm, normed_hbm, w_ref, projected_ref, pairs_ref, context_ref,
    total_ref, hidden_ref, second_ref, inverse_ref, cot_plane, normed_plane, own_pair, pairs,
    first_send, first_recv, second_send, second_recv, pair_send, pair_recv,
):
    step = pl.program_id(0)
    grp, seq = lax.axis_index("grp"), lax.axis_index("seq")
    first.start(cot_hbm, cot_plane, (first_send, first_recv), grp, seq, begin=False)
    second.start(normed_hbm, normed_plane, (second_send, second_recv), grp, seq, begin=False)
    pair_task.start(own_pair, pairs, (pair_send, pair_recv), grp, seq, begin=False)
    low = jnp.bfloat16
    rows = normed_ref.shape[0]
    wide = 2 * HD
    couples = NH // 2
    attend_at = 1 + couples
    out_at = attend_at + NH
    end = out_at + MODEL_WIDTH // wide

    @pl.when(step == 0)
    def _():
        barrier = pltpu.get_barrier_semaphore()
        devices = list(first.peers(grp, seq)) + list(pair_task.peers(grp, seq))
        for device in devices:
            pl.semaphore_signal(barrier, inc=1, device_id=device, device_id_type=MESH)
        pl.semaphore_wait(barrier, len(devices))
        first.begin()
        second.begin()

    @pl.when(step < attend_at)
    def _():
        made = jnp.dot(normed_ref[...], w_ref[...], preferred_element_type=jnp.float32)
        cosine, sine = cosine_ref[...], sine_ref[...]
        left = turn(made[:, :HD], cosine, sine).astype(low)
        right = made[:, HD:]

        @pl.when(step == 0)
        def _():
            own_pair[:, :HD] = left
            own_pair[:, HD:] = right.astype(low)
            pair_task.begin()
            projected_ref[:, NH * HD :] = own_pair[...]

        @pl.when(step > 0)
        def _():
            place = pl.multiple_of((step - 1) * wide, wide)
            projected_ref[:, pl.ds(place, HD)] = left
            projected_ref[:, pl.ds(pl.multiple_of(place + HD, HD), HD)] = turn(
                right, cosine, sine
            ).astype(low)

    @pl.when(step == attend_at)
    def _():
        pair_task.finish()
        for at in range(pairs.shape[0]):
            pairs_ref[at * rows : (at + 1) * rows, :] = pairs[at]

    @pl.when(step == attend_at + 2)
    def _():
        first.pass_on(1)
        first.pass_on(4)

    @pl.when(step == out_at)
    def _():
        first.pass_on(2)
        first.pass_on(5)

    @pl.when((step >= attend_at) & (step < out_at))
    def _():
        head = step - attend_at
        place = pl.ds(pl.multiple_of(head * HD, HD), HD)
        scale = HD ** (-0.5)
        for block in range(SEQLEN // rows):

            @pl.when(seq == block)
            def _():
                keys = (block + 1) * rows
                scores = dot_last(pairs_ref[:keys, :HD], projected_ref[:, place]) * scale
                scores = jnp.where(
                    score_mask(key_seg_ref, query_seg_ref, block, rows), scores, MASKED
                )
                highest = jnp.max(scores, axis=0, keepdims=True)
                exponent = jnp.exp(scores - highest)
                totals = jnp.sum(exponent, axis=0, keepdims=True)
                probs_low = (exponent * (1.0 / totals)).astype(low)
                context = dot_first(probs_low, pairs_ref[:keys, HD:])
                context_ref[:, place] = context.astype(low)
                total_ref[head] = highest + jnp.log(totals)

    @pl.when(step >= out_at)
    def _():
        place = pl.ds(pl.multiple_of((step - out_at) * wide, wide), wide)
        branch = jnp.dot(context_ref[...], w_ref[...], preferred_element_type=jnp.float32)
        hidden_ref[:, place] = tokens_ref[:, place].astype(jnp.float32) + branch

    @pl.when(step == end - 1)
    def _():
        chunk = 32
        gain = gain_ref[1:2, :]

        def some(at, _):
            part = pl.ds(pl.multiple_of(at * chunk, chunk), chunk)
            hidden = hidden_ref[part, :]
            inverse = lax.rsqrt(jnp.mean(hidden * hidden, axis=-1, keepdims=True) + NORM_EPS)
            inverse_ref[part, :] = inverse
            second_ref[part, :] = (hidden * inverse * gain).astype(low)
            return 0

        lax.fori_loop(0, rows // chunk, some, 0)
        first.pass_on(6)
        first.pass_on(3)
        for came in (1, 4, 2, 5, 6, 3):
            second.pass_on(came)
        first.finish()
        second.finish()


def attention_block(number, normed, tokens, gains, tables, key_segs, query_segs, cotangent, weights):
    rows, width = normed.shape
    low, wide = jnp.bfloat16, 2 * HD
    couples = NH // 2
    count = SEQLEN // rows
    first = gather_plane(cotangent.shape, placed=True)
    second = gather_plane(normed.shape, placed=True)
    pair_task = Exchange("seq", (count, rows, wide), whole, block_of)

    def weight_block(step):
        turned = step - NH
        return (0, jnp.where(step == 0, couples, jnp.where(step <= couples, step - 1, jnp.maximum(turned, couples + 1))))

    def full(shape):
        return pl.BlockSpec(shape, lambda step: (0,) * len(shape))

    hbm = pl.BlockSpec(memory_space=pl.ANY)
    steps = 1 + couples + NH + width // wide
    plane = jax.ShapeDtypeStruct((8, rows, width), low)
    shapes = [
        jax.ShapeDtypeStruct((rows, NH * HD + wide), low),
        jax.ShapeDtypeStruct((SEQLEN, wide), low),
        jax.ShapeDtypeStruct((rows, NH * HD), low),
        jax.ShapeDtypeStruct((NH, 1, rows), jnp.float32),
        jax.ShapeDtypeStruct((rows, width), jnp.float32),
        jax.ShapeDtypeStruct((rows, width), low),
        jax.ShapeDtypeStruct((rows, 1), jnp.float32),
    ]
    return pl.pallas_call(
        functools.partial(block_kernel, first, second, pair_task),
        grid=(steps,),
        in_specs=[
            full((SEQLEN, 1)),
            full((1, rows)),
            full((rows, width)),
            full((rows, width)),
            full((2, width)),
            full((rows, HD // 2)),
            full((rows, HD // 2)),
            hbm,
            hbm,
            pl.BlockSpec((width, wide), weight_block),
        ],
        out_specs=[full(shape.shape) for shape in shapes] + [hbm, hbm],
        out_shape=shapes + [plane, plane],
        scratch_shapes=[pltpu.VMEM((rows, wide), low), pltpu.VMEM((count, rows, wide), low)]
        + [pltpu.SemaphoreType.DMA((14,))] * 4
        + [pltpu.SemaphoreType.DMA((pair_task.sem_count,))] * 2,
        compiler_params=pltpu.CompilerParams(
            collective_id=number, has_side_effects=True, vmem_limit_bytes=56 * 2**20
        ),
        cost_estimate=SMALL_COST,
        name="attention_block",
    )(
        key_segs[:, None], query_segs[None, :], normed, tokens, gains, *tables, cotangent, normed,
        weights,
    )


def add_blocks(total, blocks):
    step = min(32, total.shape[0])

    def some(at, _):
        rows = pl.ds(pl.multiple_of(at * step, step), step)
        made = blocks[0, rows, :].astype(jnp.float32)
        for block in range(1, blocks.shape[0]):
            made = made + blocks[block, rows, :].astype(jnp.float32)
        total[rows, :] = made.astype(total.dtype)
        return 0

    lax.fori_loop(0, total.shape[0] // step, some, 0)


def norm_one_back(
    weights_hbm, query_grad_ref, pair_grad_ref, hidden_grad_ref, tokens_ref, inverse_ref, gain_ref,
    gain_two_ref, input_grad_ref, gain_terms, w_block, norm_grad, w_sems,
):
    width, query_columns = tokens_ref.shape[1], query_grad_ref.shape[1]
    rows, columns = w_block.shape[1:]
    count = width // rows

    def w_copy(at):
        view = weights_hbm.at[pl.ds(pl.multiple_of(at * rows, rows), rows), pl.ds(0, columns)]
        return pltpu.make_async_copy(view, w_block.at[at % 2], w_sems.at[at % 2])

    w_copy(0).start()

    def one(at, _):
        w_copy(at).wait()

        @pl.when(at + 1 < count)
        def _():
            w_copy(at + 1).start()

        made = dot_last(query_grad_ref[...], w_block[at % 2, :, :query_columns])
        made = made + dot_last(pair_grad_ref[...], w_block[at % 2, :, query_columns:])
        norm_grad[:, pl.ds(pl.multiple_of(at * rows, rows), rows)] = made
        return 0

    lax.fori_loop(0, count, one, 0)
    chunk = 32
    gain = gain_ref[0:1, :]

    def some(at, sums):
        part = pl.ds(pl.multiple_of(at * chunk, chunk), chunk)
        inverse, token = inverse_ref[part, :], tokens_ref[part, :].astype(jnp.float32)
        made = norm_grad[part, :]
        scaled = gain * made
        mean = jnp.mean(token * scaled, axis=-1, keepdims=True)
        input_grad_ref[part, :] = (
            hidden_grad_ref[part, :] + inverse * scaled - token * (inverse * inverse * inverse * mean)
        )
        return sums + jnp.sum(made * token * inverse, axis=0, keepdims=True)

    zeros = jnp.zeros((1, width), jnp.float32)
    gain_terms[0:1, :] = lax.fori_loop(0, tokens_ref.shape[0] // chunk, some, zeros)
    gain_terms[1:2, :] = gain_two_ref[...]


def tail_kernel(
    tasks, shares_hbm, pair_hbm, gating_hbm, weights_hbm, query_grad_ref, pair_grad_ref,
    hidden_grad_ref, tokens_ref, inverse_ref, gain_ref, gain_two_ref, gating_plane, share_plane,
    pair_plane, gain_plane, input_grad_ref, share_parts, share_sum, mine, core_in, halves, wholes,
    pair_parts, pair_sum, gain_terms, gain_parts, gain_sum, w_block, norm_grad, w_sems, *sems,
):
    gating, pair, gain_seq, gain_grp, pair_seq, pair_gather, *halves_of = tasks
    shares, share_gathers = halves_of[:2], halves_of[2:]
    grp, seq = lax.axis_index("grp"), lax.axis_index("seq")
    barrier = pltpu.get_barrier_semaphore()
    devices = list(gain_grp.peers(grp, seq)) + list(gain_seq.peers(grp, seq))
    for device in devices:
        pl.semaphore_signal(barrier, inc=1, device_id=device, device_id_type=MESH)
    pl.semaphore_wait(barrier, len(devices))
    sems = [(sems[2 * at], sems[2 * at + 1]) for at in range(len(tasks))]

    def share_part(at):
        shares[at].finish()
        add_blocks(share_sum.at[at], share_parts.at[at])
        share_gathers[at].start(share_sum.at[at], share_plane, sems[8 + at], grp, seq)

    shares[0].start(shares_hbm, share_parts.at[0], sems[6], grp, seq)
    pair.start(pair_hbm, None, sems[1], grp, seq, (mine, core_in, halves, wholes))
    gating.start(gating_hbm, gating_plane, sems[0], grp, seq, begin=False)
    gating.kept.start()
    for at in (1, 4, 7):
        gating.out[at].start()
    pair.first_sums()
    norm_one_back(
        weights_hbm, query_grad_ref, pair_grad_ref, hidden_grad_ref, tokens_ref, inverse_ref,
        gain_ref, gain_two_ref, input_grad_ref, gain_terms, w_block, norm_grad, w_sems,
    )
    gain_seq.start(gain_terms, gain_parts, sems[2], grp, seq)
    for _ in pair.forward():
        pass
    for at in (2, 5):
        gating.out[at].start()
    handing = gating.forward()
    next(handing)
    pair_seq.start(pair.total(), pair_parts, sems[4], grp, seq)
    shares[1].start(shares_hbm, share_parts.at[1], sems[7], grp, seq)
    gain_seq.finish()
    gain_sum[...] = jnp.sum(gain_parts[...], axis=0)
    gain_grp.start(gain_sum, gain_plane, sems[3], grp, seq)
    share_part(0)
    pair_seq.finish()
    add_blocks(pair_sum, pair_parts)
    pair_gather.start(pair_sum, pair_plane, sems[5], grp, seq)
    next(handing)
    share_part(1)
    next(handing)
    hand_on([share_gathers[0], pair_gather, share_gathers[1]])
    for copy in pair.copies:
        copy.wait_send()
    for task in (gain_grp, gating, pair_gather, *share_gathers):
        task.finish()


def gather_gating(shape):
    return gather_plane(
        shape,
        split=1,
        target_view=lambda ref, index: ref.at[:, index],
        out_shape=(shape[0], lax.axis_size("grp"), *shape[1:]),
    )


def tail_exchange(number, shares, pair, gating, weights, back):
    gain_terms = jax.ShapeDtypeStruct((2, back[3].shape[1]), jnp.float32)
    tokens_here = back[3].shape[0]
    seq_count = lax.axis_size("seq")
    low = jnp.bfloat16
    columns, rows_all = shares.shape
    rows = rows_all // seq_count
    _, pair_rows, pair_columns = pair.shape
    sub = pair_rows // seq_count
    half = columns // 2

    def share_task(at):
        return Exchange(
            "seq",
            (seq_count, half, rows),
            lambda ref, index: ref.at[
                pl.ds(at * half, half), pl.ds(pl.multiple_of(index * rows, rows), rows)
            ],
            block_of,
        )

    def share_gather(at):
        return gather_plane(
            (half, rows),
            target_view=lambda ref, index: ref.at[index, pl.ds(at * half, half)],
            out_shape=(8, columns, rows),
        )

    tasks = [
        gather_gating(gating.shape),
        PlaneSum(pair_rows, pair_columns, placed=False),
        gather_axis("seq", gain_terms)[0],
        gather_axis("grp", gain_terms)[0],
        Exchange(
            "seq",
            (seq_count, sub, pair_columns),
            lambda ref, index: rows_of(ref, index, sub),
            block_of,
        ),
        gather_plane((sub, pair_columns)),
        share_task(0),
        share_task(1),
        share_gather(0),
        share_gather(1),
    ]
    hbm = pl.BlockSpec(memory_space=pl.ANY)
    vmem = pl.BlockSpec(memory_space=pltpu.VMEM)
    scratch = [
        pltpu.VMEM((2, seq_count, half, rows), low),
        pltpu.VMEM((2, half, rows), low),
        *tasks[1].scratch(),
        pltpu.VMEM((seq_count, sub, pair_columns), low),
        pltpu.VMEM((sub, pair_columns), low),
        pltpu.VMEM(gain_terms.shape, jnp.float32),
        pltpu.VMEM((seq_count, *gain_terms.shape), jnp.float32),
        pltpu.VMEM(gain_terms.shape, jnp.float32),
        pltpu.VMEM((2, 2 * HD, (NH + 2) * HD), low),
        pltpu.VMEM((tokens_here, back[3].shape[1]), jnp.float32),
        pltpu.SemaphoreType.DMA((2,)),
    ]
    for task in tasks:
        scratch += [pltpu.SemaphoreType.DMA((task.sem_count,))] * 2
    return pl.pallas_call(
        functools.partial(tail_kernel, tasks),
        in_specs=[hbm] * 4 + [vmem] * len(back),
        out_specs=[hbm] * 4 + [vmem],
        out_shape=[
            jax.ShapeDtypeStruct(tasks[0].out_shape, low),
            jax.ShapeDtypeStruct((8, columns, rows), low),
            jax.ShapeDtypeStruct((8, sub, pair_columns), low),
            jax.ShapeDtypeStruct((8, *gain_terms.shape), jnp.float32),
            jax.ShapeDtypeStruct((tokens_here, back[3].shape[1]), jnp.float32),
        ],
        scratch_shapes=scratch,
        compiler_params=pltpu.CompilerParams(
            collective_id=number, has_side_effects=True, vmem_limit_bytes=60 * 2**20
        ),
        cost_estimate=SMALL_COST,
        name="tail_exchange",
    )(shares, pair, gating, weights, *back)


def half_rows(axis, height):
    def half_of(view, second):
        index = (slice(None),) * axis + (pl.ds(height if second else 0, height),)
        return view.at[index]

    return half_of


def whole(ref, index):
    return ref


def block_of(ref, index):
    return ref.at[index]


def gather_plane(
    shape, split=0, source_view=whole, target_view=block_of, out_shape=None, placed=False
):
    out_shape = out_shape or (lax.axis_size("grp"), *shape)
    if lax.axis_size("grp") == 8:
        halves = half_rows(split, shape[split] // 2)
        return PlaneGather(out_shape, source_view, target_view, halves, placed)
    return Exchange("grp", out_shape, source_view, target_view)


def hand_on(tasks):
    going = [task.forward() for task in tasks]
    while going:
        going = [steps for steps in going if next(steps, going) is not going]


def exchange_kernel(tasks, wires, arrays, outputs, *refs):
    sources, targets = refs[:arrays], refs[arrays : arrays + outputs]
    refs = list(refs[arrays + outputs :])
    sems, scratch = [], []
    for task in tasks:
        sems.append((refs.pop(0), refs.pop(0)))
        held = len(task.scratch()) if isinstance(task, PlaneSum) else 0
        scratch.append([refs.pop(0) for _ in range(held)])
    grp, seq = lax.axis_index("grp"), lax.axis_index("seq")
    barrier = pltpu.get_barrier_semaphore()
    axes = {"grp": [], "seq": []}
    for task in tasks:
        devices = list(task.peers(grp, seq))
        if len(devices) > len(axes[task.axis]):
            axes[task.axis] = devices
    devices = axes["grp"] + axes["seq"]
    for device in devices:
        pl.semaphore_signal(barrier, inc=1, device_id=device, device_id_type=MESH)
    pl.semaphore_wait(barrier, len(devices))

    def start(at):
        after, source, target = wires[at]
        source = targets[source] if after is not None else sources[source]
        more = (scratch[at],) if scratch[at] else ()
        tasks[at].start(source, targets[target], sems[at], grp, seq, *more)

    open_tasks = list(range(len(tasks)))
    first = [at for at in open_tasks if wires[at][0] is None]
    for at in first:
        start(at)
    for at in first:
        if isinstance(tasks[at], PlaneSum):
            tasks[at].first_sums()
    hand_on([tasks[at] for at in first])
    for at in open_tasks[:]:
        after = wires[at][0]
        if after is not None:
            tasks[after].finish()
            open_tasks.remove(after)
            start(at)
            hand_on([tasks[at]])
    for at in open_tasks:
        tasks[at].finish()


def exchange(number, work):
    tasks = [piece[0] for piece in work]
    arrays, shapes, wires = [], [], []
    for piece in work:
        if isinstance(piece[1], int):
            after, source = piece[1], wires[piece[1]][2]
            kind = shapes[source].dtype
        else:
            after, source = None, len(arrays)
            arrays.append(piece[1])
            kind = piece[1].dtype
        if len(piece) == 3:
            target = wires[piece[2]][2]
        else:
            target = len(shapes)
            shapes.append(jax.ShapeDtypeStruct(piece[0].out_shape, kind))
        wires.append((after, source, target))
    scratch = []
    for task in tasks:
        scratch += [pltpu.SemaphoreType.DMA((task.sem_count,))] * 2
        if isinstance(task, PlaneSum):
            scratch += task.scratch()
    return pl.pallas_call(
        functools.partial(exchange_kernel, tasks, wires, len(arrays), len(shapes)),
        in_specs=[pl.BlockSpec(memory_space=pl.ANY)] * len(arrays),
        out_specs=[pl.BlockSpec(memory_space=pl.ANY)] * len(shapes),
        out_shape=shapes,
        scratch_shapes=scratch,
        compiler_params=pltpu.CompilerParams(collective_id=number, has_side_effects=True),
        cost_estimate=SMALL_COST,
        name="exchange",
    )(*arrays)


def gather_axis(axis, array):
    task = Exchange(axis, (lax.axis_size(axis), *array.shape), whole, block_of)
    return task, array


def split_rows(axis, array):
    count = lax.axis_size(axis)
    rows, columns = array.shape
    height = rows // count
    task = Exchange(
        axis,
        (count, height, columns),
        lambda ref, index: rows_of(ref, index, height),
        block_of,
    )
    return task, array


def split_columns(axis, array, placed=False):
    count = lax.axis_size(axis)
    rows, columns = array.shape
    width = columns // count
    if placed and count == 8:
        task = PlacedExchange(
            (count, rows, width), lambda ref, index: columns_of(ref, index, width)
        )
        return task, array
    task = Exchange(
        axis,
        (count, rows, width),
        lambda ref, index: columns_of(ref, index, width),
        block_of,
    )
    return task, array


def plane_sum_kernel(
    own, part_ref, gate_ref, up_ref, x_ref, total_ref, grads_out, core_in, chip, half_x, half_y,
    whole_x, whole_y, x_block, stage, send_sems, recv_sems, x_sems, out_sems,
):
    grp, seq = lax.axis_index("grp"), lax.axis_index("seq")
    core, side_x, side_y = [flip(grp, bits) for bits in (1, 2, 4)]
    blocks = [PLACES[bits] for bits in (6, 2, 4, 0)]
    core_blocks = [PLACES[bits] for bits in (7, 3, 5, 1)]
    half = total_ref.shape[0] // 2
    low, high = pl.ds(0, half), pl.ds(half, half)
    rows = x_block.shape[2]
    count = x_ref.shape[1] // rows

    def x_copy(at):
        view = x_ref.at[:, pl.ds(pl.multiple_of(at * rows, rows), rows)]
        return pltpu.make_async_copy(view, x_block.at[at % 2], x_sems.at[at % 2])

    def out_copies(at):
        return [
            pltpu.make_async_copy(
                stage.at[which, at % 2, own_columns(grp, own)],
                grads_out.at[pl.ds(pl.multiple_of((2 * at + which) * own, own), own)],
                out_sems.at[which, at % 2],
            )
            for which in range(2)
        ]

    x_copy(0).start()
    barrier = pltpu.get_barrier_semaphore()
    for device in (core, side_x, side_y):
        pl.semaphore_signal(barrier, inc=1, device_id=(device, seq), device_id_type=MESH)
    pl.semaphore_wait(barrier, 3)

    sems = (send_sems, recv_sems)
    copies = [
        remote(part_ref.at[block], core_in.at[at], sems, at, (core, seq))
        for at, block in enumerate(core_blocks)
    ]
    copies += [
        remote(chip.at[0, low], half_x, sems, 4, (side_x, seq)),
        remote(chip.at[0, high], half_y, sems, 5, (side_y, seq)),
        remote(chip.at[1, low], whole_x.at[low], sems, 6, (side_x, seq)),
        remote(chip.at[2, high], whole_y.at[high], sems, 7, (side_y, seq)),
        remote(chip.at[1, high], whole_x.at[high], sems, 8, (side_x, seq)),
        remote(chip.at[2, low], whole_y.at[low], sems, 9, (side_y, seq)),
    ]
    for copy in copies[:4]:
        copy.start()

    def step(at, _):
        @pl.when(at == 1)
        def _():
            for came, then in ((0, (4, 5)), (1, (6,)), (2, (7,))):
                copies[came].wait_recv()
                add_rows(chip.at[came], part_ref.at[blocks[came]], core_in.at[came])
                for start in then:
                    copies[start].start()

        @pl.when(at == count - 1)
        def _():
            copies[5].wait_recv()
            add_rows(chip.at[1, high], chip.at[1, high], half_y)
            copies[8].start()
            copies[4].wait_recv()
            add_rows(chip.at[2, low], chip.at[2, low], half_x)
            copies[9].start()

        x_copy(at).wait()

        @pl.when(at + 1 < count)
        def _():
            x_copy(at + 1).start()

        @pl.when(at >= 2)
        def _():
            for copy in out_copies(at - 2):
                copy.wait()

        for which, ref in enumerate((gate_ref, up_ref)):
            stage[which, at % 2] = jnp.dot(
                ref[...], x_block[at % 2], preferred_element_type=jnp.float32
            ).astype(stage.dtype)
        for copy in out_copies(at):
            copy.start()
        return 0

    lax.fori_loop(0, count, step, 0)
    copies[3].wait_recv()
    add_rows(total_ref, part_ref.at[blocks[3]], core_in.at[3])
    for at, came, rows_at in (
        (6, whole_x, low),
        (7, whole_y, high),
        (8, whole_x, high),
        (9, whole_y, low),
    ):
        copies[at].wait_recv()
        add_rows(total_ref.at[rows_at], total_ref.at[rows_at], came.at[rows_at])
    for copy in copies:
        copy.wait_send()
    for at in (count - 2, count - 1):
        for copy in out_copies(at):
            copy.wait()


def plane_sum(number, own, part, gate_grad, up_grad, x, seq_count):
    count = lax.axis_size("grp")
    rows_all, columns = part.shape
    rows = rows_all // count
    if count != 8:
        total = lax.psum_scatter(part, "grp", scatter_dimension=0, tiled=True)
        begin = (lax.axis_index("grp") * own) % 128
        both = jnp.concatenate(
            [lax.dynamic_slice_in_dim(grad, begin, own) for grad in (gate_grad, up_grad)], axis=0
        )
        return total.astype(jnp.float32), weight_grad(both, x, seq_count)
    low = jnp.bfloat16
    cols, tokens_all = gate_grad.shape
    width = x.shape[1] // seq_count
    vmem = pl.BlockSpec(memory_space=pltpu.VMEM)
    hbm = pl.BlockSpec(memory_space=pl.ANY)
    grads = jax.ShapeDtypeStruct((2 * seq_count * own, width), low)
    return pl.pallas_call(
        functools.partial(plane_sum_kernel, own),
        in_specs=[vmem, vmem, vmem, hbm],
        out_specs=[vmem, hbm],
        out_shape=[jax.ShapeDtypeStruct((rows, columns), jnp.float32), grads],
        scratch_shapes=[
            pltpu.VMEM((4, rows, columns), low),
            pltpu.VMEM((3, rows, columns), low),
            pltpu.VMEM((rows // 2, columns), low),
            pltpu.VMEM((rows // 2, columns), low),
            pltpu.VMEM((rows, columns), low),
            pltpu.VMEM((rows, columns), low),
            pltpu.VMEM((2, tokens_all, width), low),
            pltpu.VMEM((2, 2, cols, width), low),
            pltpu.SemaphoreType.DMA((10,)),
            pltpu.SemaphoreType.DMA((10,)),
            pltpu.SemaphoreType.DMA((2,)),
            pltpu.SemaphoreType.DMA((2, 2)),
        ],
        compiler_params=pltpu.CompilerParams(
            collective_id=number, has_side_effects=True, vmem_limit_bytes=56 * 2**20
        ),
        cost_estimate=SMALL_COST,
        name="plane_sum",
    )(part.reshape(count, rows, columns), gate_grad, up_grad, x)


def local(
    tokens,
    cotangent,
    segment_ids,
    tile_owner_slots,
    weights_low,
    master,
    moment_one,
    moment_two,
    left_basis_set,
    right_basis_set,
    gains,
    gain_moment_one,
    gain_moment_two,
):
    grp_count = lax.axis_size("grp")
    seq_count = lax.axis_size("seq")
    grp_here, seq_here = lax.axis_index("grp"), lax.axis_index("seq")
    rows_here = tokens.shape[0]
    slots_here, rows_block, tile_width = weights_low.shape
    tile_count = tile_owner_slots.shape[0]
    query_cols = NH * HD
    value_end = query_cols + 2 * HD
    output_end = value_end + MODEL_WIDTH
    attn_tiles = output_end // tile_width
    query_tiles = query_cols // tile_width
    hidden_tiles = FF // tile_width
    own = FF // grp_count
    share = max(-(-((at * own) % tile_width + own) // tile_width) for at in range(grp_count))
    share_width = MODEL_WIDTH // grp_count
    sub_rows = rows_block // grp_count
    halves = 2 if sub_rows >= 32 else 1
    half_block, half_sub = rows_block // halves, sub_rows // halves
    first_place = (seq_here * rows_here) % SEQLEN
    key_tables = turn_tables(jnp.arange(SEQLEN, dtype=jnp.int32))
    tables = [lax.dynamic_slice_in_dim(table, first_place, rows_here) for table in key_tables]

    hidden_ids = grp_here * own // tile_width + jnp.arange(share, dtype=jnp.int32)
    hidden_ids = jnp.minimum(hidden_ids, hidden_tiles - 1)
    feed_ids = (
        attn_tiles
        + jnp.arange(3, dtype=jnp.int32)[:, None] * hidden_tiles
        + hidden_ids[None, :]
    ).reshape(-1)
    feed_slots, attn_slots = tile_owner_slots[feed_ids], tile_owner_slots[:attn_tiles]

    tok_float = tokens.astype(jnp.float32)
    inverse_one = lax.rsqrt(jnp.mean(tok_float * tok_float, axis=-1, keepdims=True) + NORM_EPS)
    normed = (tok_float * inverse_one * gains[0]).astype(jnp.bfloat16)

    def weight_half(at):
        return gather_plane(
            (slots_here, half_block, tile_width),
            split=1,
            source_view=lambda ref, index: ref.at[:, pl.ds(at * half_block, half_block)],
        )

    def attn_half(at):
        return gather_plane(
            (seq_count, half_sub, output_end),
            target_view=lambda ref, index: ref.at[:, at, index],
            out_shape=(seq_count, halves, grp_count, half_sub, output_end),
        )

    flat = (grp_count * slots_here, half_block, tile_width)
    tiles, segments = exchange(
        0,
        [(weight_half(0), weights_low), gather_axis("seq", segment_ids.reshape(-1, tile_width))],
    )
    feed_rows, attn_rows = pick(tiles.reshape(flat), feed_slots, attn_slots)
    feed_parts = [lax.all_gather(feed_rows, "seq", axis=0, tiled=False)]
    if halves == 2:
        tiles, attn_first = exchange(
            1, [(weight_half(1), weights_low), gather_axis("seq", attn_rows)]
        )
        feed_rows, attn_rows = pick(tiles.reshape(flat), feed_slots, attn_slots)
        feed_parts.append(lax.all_gather(feed_rows, "seq", axis=0, tiled=False))
        attn_weights, _ = exchange(
            2,
            [(attn_half(0), attn_first), gather_axis("seq", attn_rows), (attn_half(1), 1, 0)],
        )
    else:
        _, attn_weights = exchange(2, [gather_axis("seq", attn_rows), (attn_half(0), 0)])
    attn_weights = attn_weights.reshape(MODEL_WIDTH, output_end)

    first_key = seq_here * rows_here - first_place
    key_segs = lax.dynamic_slice_in_dim(segments.reshape(-1), first_key, SEQLEN)
    at = (first_place // rows_here).reshape(1)
    if grp_count == 8 and seq_count * rows_here == SEQLEN:
        (
            projected, pairs, context, log_totals, hidden, normed_two, inverse_two, cot_plane,
            normed_plane,
        ) = attention_block(
            3, normed, tokens, gains, tables, key_segs, segment_ids, cotangent, attn_weights
        )
    else:
        projected = project(normed, attn_weights, tables)
        pairs, cot_plane, normed_plane = exchange(
            3,
            [
                gather_axis("seq", projected[:, query_cols:]),
                (gather_plane(cotangent.shape, placed=True), cotangent),
                (gather_plane(normed.shape, placed=True), normed),
            ],
        )
        pairs = lax.dynamic_slice_in_dim(pairs.reshape(-1, 2 * HD), first_key, SEQLEN)
        context, log_totals = attend(at, projected, pairs, key_segs, segment_ids)
        branch = jnp.dot(
            context, attn_weights[:, value_end:], preferred_element_type=jnp.float32
        )
        hidden = tok_float + branch
        inverse_two = lax.rsqrt(jnp.mean(hidden * hidden, axis=-1, keepdims=True) + NORM_EPS)
        normed_two = (hidden * inverse_two * gains[1]).astype(jnp.bfloat16)

    cot_plane = cot_plane.reshape(-1, MODEL_WIDTH)
    normed_plane = normed_plane.reshape(-1, MODEL_WIDTH)
    real_cols = ((grp_here * own) % tile_width).reshape(1)
    if halves == 2:
        some = jnp.max(feed_parts[0][0, :8, :tile_width].astype(jnp.float32)) * 0.0
        real_cols = real_cols + some.astype(jnp.int32)
    if grp_count == 8:
        gate_grad, up_grad, two_part, feed_part, second_plane, context_plane, down_grad = (
            feed_gather(
                4, own, real_cols, normed_two, context, cot_plane, feed_parts, seq_count
            )
        )
        second_plane = second_plane.reshape(-1, MODEL_WIDTH)
    else:
        second_plane, context_plane = exchange(
            4,
            [
                (gather_plane(normed_two.shape), normed_two),
                (gather_plane(context.shape), context),
            ],
        )
        second_plane = second_plane.reshape(-1, MODEL_WIDTH)
        activated, gate_grad, up_grad, two_part, feed_part = feed_forward(
            own, real_cols, second_plane, cot_plane, feed_parts, seq_count
        )
        activated = lax.dynamic_slice_in_dim(activated, (grp_here * own) % tile_width, own)
        down_grad = weight_grad(activated, cot_plane, seq_count)
    context_plane = context_plane.reshape(-1, MODEL_WIDTH)
    down_grad, two_part = lax.optimization_barrier((down_grad, two_part))
    down_grad = lax.psum_scatter(down_grad, "seq", scatter_dimension=0, tiled=True)
    norm_two_grad, gating_grads = plane_sum(
        5, own, two_part, gate_grad, up_grad, second_plane, seq_count
    )
    gating_grads = lax.psum_scatter(gating_grads, "seq", scatter_dimension=0, tiled=True)
    gating_grads = gating_grads.reshape(2, own, rows_block)

    out_grad = cotangent.astype(jnp.float32)
    gain_two_term = jnp.sum(norm_two_grad * hidden * inverse_two, axis=0)
    hidden_grad = (
        out_grad
        + inverse_two * gains[1] * norm_two_grad
        - hidden
        * inverse_two**3
        * jnp.mean(hidden * gains[1] * norm_two_grad, axis=-1, keepdims=True)
    )
    branch_grad = hidden_grad.astype(jnp.bfloat16)
    fused = grp_count == 8 and seq_count * rows_here == SEQLEN
    if fused:
        feed_part = feed_part.reshape(grp_count, rows_here, MODEL_WIDTH)
        query_grad, pair_part, feed_out, down_plane = attend_back_sum(
            6, projected, pairs, branch_grad, log_totals, key_segs, segment_ids, key_tables,
            tables, feed_part, down_grad, attn_weights,
        )
    else:
        context_grad = times_transpose(branch_grad, attn_weights[:, value_end:]).astype(jnp.bfloat16)
        query_grad, pair_part = attend_back(
            at, projected, pairs, context_grad, log_totals, key_segs, segment_ids, key_tables, tables
        )
        feed_out = lax.psum_scatter(
            feed_part.reshape(-1, MODEL_WIDTH), "grp", scatter_dimension=0, tiled=True
        )
        (down_plane,) = exchange(10, [(gather_plane(down_grad.shape), down_grad)])
    block_out = (hidden + feed_out.astype(jnp.float32)).astype(jnp.bfloat16)
    if seq_count * rows_here > SEQLEN:
        pair_part = lax.dynamic_update_slice_in_dim(
            jnp.zeros((seq_count * rows_here, 2 * HD), pair_part.dtype), pair_part, first_key, 0
        )
    pair_parts, query_share, branch_share = exchange(
        7,
        [
            split_rows("seq", pair_part),
            split_columns("grp", query_grad, placed=True),
            split_columns("grp", branch_grad, placed=True),
        ],
    )
    pair_grad = jnp.sum(pair_parts.astype(jnp.float32), axis=0).astype(jnp.bfloat16)
    shares = share_grad(
        query_share.reshape(-1, share_width),
        branch_share.reshape(-1, share_width),
        normed_plane,
        context_plane,
    )
    pair_weight_grad = contract(normed, pair_grad).astype(jnp.bfloat16)
    pair_blocks = pair_weight_grad.reshape(seq_count, grp_count, sub_rows, 2 * HD)
    if grp_count == 8:
        pair_blocks = jnp.transpose(pair_blocks, (1, 0, 2, 3))
        gating_plane, share_plane, pair_plane, gain_parts, input_grad = tail_exchange(
            8,
            shares,
            pair_blocks.reshape(grp_count, seq_count * sub_rows, 2 * HD),
            gating_grads,
            attn_weights,
            (query_grad, pair_grad, hidden_grad, tokens, inverse_one, gains, gain_two_term[None, :]),
        )
    else:
        projected_grad = jnp.concatenate([query_grad, pair_grad], axis=1)
        norm_one_grad = times_transpose(projected_grad, attn_weights[:, :value_end])
        gain_one_term = jnp.sum(norm_one_grad * tok_float * inverse_one, axis=0)
        input_grad = (
            hidden_grad
            + inverse_one * gains[0] * norm_one_grad
            - tok_float
            * inverse_one**3
            * jnp.mean(tok_float * gains[0] * norm_one_grad, axis=-1, keepdims=True)
        )
        gain_terms = jnp.stack([gain_one_term, gain_two_term])
        pair_task = Exchange(
            "grp",
            (grp_count, seq_count, sub_rows, 2 * HD),
            lambda ref, index: ref.at[:, index],
            block_of,
        )
        work = [
            split_columns("seq", shares),
            (pair_task, pair_blocks),
            gather_axis("seq", gain_terms),
            (gather_gating(gating_grads.shape), gating_grads),
        ]
        share_parts, pair_parts, gain_parts, gating_plane = exchange(8, work)
        gain_seq = jnp.sum(gain_parts, axis=0)
        shares = jnp.sum(share_parts.astype(jnp.float32), axis=0).astype(jnp.bfloat16)
        pair_parts = jnp.sum(pair_parts.astype(jnp.float32), axis=0).astype(jnp.bfloat16)
        pair_task = Exchange("seq", pair_parts.shape, block_of, block_of)
        _, pair_plane, share_plane, gain_parts = exchange(
            9,
            [
                (pair_task, pair_parts),
                (gather_plane(pair_parts.shape), 0),
                (gather_plane(shares.shape), shares),
                gather_axis("grp", gain_seq),
            ],
        )
        pair_plane = jnp.sum(pair_plane.astype(jnp.float32), axis=1).astype(jnp.bfloat16)

    gain_grads = jnp.sum(gain_parts, axis=0)

    owner_slots, _ = lax.optimization_barrier((tile_owner_slots, pair_grad))
    tile_of_slot = (
        jnp.full((grp_count * slots_here,), tile_count, jnp.int32)
        .at[owner_slots]
        .set(jnp.arange(tile_count, dtype=jnp.int32))
    )
    tiles_here = lax.dynamic_slice_in_dim(tile_of_slot, grp_here * slots_here, slots_here)
    feed_at = jnp.clip(tiles_here - attn_tiles, 0, 3 * hidden_tiles - 1)
    which, column = feed_at // hidden_tiles, feed_at % hidden_tiles
    is_query = tiles_here < query_tiles
    is_pair = (tiles_here >= query_tiles) & (tiles_here < query_tiles + 2)
    is_feed = tiles_here >= attn_tiles
    kind = jnp.where(is_feed, jnp.where(which < 2, 0, 1), jnp.where(is_pair, 3, 2))
    kind = jnp.where(tiles_here == tile_count, 4, kind)
    out_at = jnp.clip(tiles_here - query_tiles - 2, 0, query_tiles - 1)
    per_share = share_width // tile_width
    share_at = jnp.where(is_query, jnp.minimum(tiles_here, query_tiles - 1), out_at)
    at = jnp.stack(
        [
            kind,
            jnp.minimum(which, 1) * hidden_tiles + column,
            column,
            share_at // per_share * 2 * per_share
            + share_at % per_share
            + jnp.where(is_query, 0, per_share),
            jnp.where(is_pair, tiles_here - query_tiles, 0),
        ]
    )
    new_master, new_one, new_two = adam(
        at,
        gating_plane.reshape(-1, rows_block),
        down_plane.reshape(-1, rows_block),
        share_plane.reshape(-1, rows_block),
        pair_plane,
        left_basis_set,
        right_basis_set,
        master,
        moment_one,
        moment_two,
    )
    gain_one = BETA_ONE * gain_moment_one + (1.0 - BETA_ONE) * gain_grads
    gain_two = BETA_TWO * gain_moment_two + (1.0 - BETA_TWO) * gain_grads * gain_grads
    new_gains = gains - GAIN_RATE * gain_one / (jnp.sqrt(gain_two) + ADAM_EPS)
    return (
        block_out,
        input_grad,
        new_master,
        new_one,
        new_two,
        gain_grads,
        new_gains,
        gain_one,
        gain_two,
    )


def solution(mesh):
    return jax.shard_map(
        local,
        mesh=mesh,
        in_specs=(
            P(("grp", "seq"), None),
            P(("grp", "seq"), None),
            P(("grp", "seq")),
            P(),
            P("grp", "seq", None),
            P("grp", "seq", None),
            P("grp", "seq", None),
            P("grp", "seq", None),
            P("grp", "seq", None),
            P("grp", "seq", None),
            P(),
            P(),
            P(),
        ),
        out_specs=(
            P(("grp", "seq"), None),
            P(("grp", "seq"), None),
            P("grp", "seq", None),
            P("grp", "seq", None),
            P("grp", "seq", None),
            P(),
            P(),
            P(),
            P(),
        ),
        check_vma=False,
    )
```

```python
import functools
import math

import jax
import jax.numpy as jnp
from jax import lax
from jax.experimental import pallas as pl
from jax.experimental.pallas import tpu as pltpu
from jax.sharding import PartitionSpec as P

MODEL_WIDTH = 2048
NH = 16
HD = 128
FF = 5632
SEQLEN = 1024


NORM_EPS = 1e-05
BETA_ONE = 0.95
BETA_TWO = 0.95
ADAM_EPS = 1e-08
WEIGHT_DECAY = 0.01
LEARN_RATE = 0.03
GAIN_RATE = 1.5
ROPE_BASE = 10000.0
MASKED = -1e30
PRECISE = lax.Precision.HIGHEST


def contract(left_side, right_side):
    return lax.dot_general(
        left_side, right_side, (((0,), (0,)), ((), ())), preferred_element_type=jnp.float32
    )


def times_transpose(left_side, right_side):
    return lax.dot_general(
        left_side, right_side, (((1,), (1,)), ((), ())), preferred_element_type=jnp.float32
    )


def turn_tables(places):
    half_width = HD // 2
    frequency = ROPE_BASE ** (-(jnp.arange(half_width, dtype=jnp.float32) * 2.0) / HD)
    angles = places.astype(jnp.float32)[:, None] * frequency[None, :]
    return jnp.cos(angles), jnp.sin(angles)


def turn(rows, cosine, sine):
    cosine = jnp.concatenate([cosine, cosine], axis=1)
    sine = jnp.concatenate([-sine, sine], axis=1)
    return rows * cosine + pltpu.roll(rows, HD // 2, 1) * sine


def turn_back(rows, cosine, sine):
    return turn(rows, cosine, -sine)


def dot_last(left_side, right_side):
    return lax.dot_general(
        left_side, right_side, (((1,), (1,)), ((), ())), preferred_element_type=jnp.float32
    )


def dot_first(left_side, right_side):
    return lax.dot_general(
        left_side, right_side, (((0,), (0,)), ((), ())), preferred_element_type=jnp.float32
    )


SMALL_COST = pl.CostEstimate(flops=1, bytes_accessed=1, transcendentals=0)


def project_kernel(x_ref, w_ref, cosine_ref, sine_ref, out_ref):
    made = jnp.dot(x_ref[...], w_ref[...], preferred_element_type=jnp.float32)
    cosine, sine = cosine_ref[...], sine_ref[...]
    first, second = made[:, :HD], made[:, HD:]
    last = pl.program_id(0) == pl.num_programs(0) - 1
    out_ref[:, :HD] = turn(first, cosine, sine).astype(out_ref.dtype)
    out_ref[:, HD:] = jnp.where(last, second, turn(second, cosine, sine)).astype(out_ref.dtype)


def project(normed, weights, tables):
    rows, width = normed.shape
    steps = NH // 2 + 1
    return pl.pallas_call(
        project_kernel,
        grid=(steps,),
        in_specs=[
            pl.BlockSpec((rows, width), lambda j: (0, 0)),
            pl.BlockSpec((width, 2 * HD), lambda j: (0, j)),
            pl.BlockSpec((rows, HD // 2), lambda j: (0, 0)),
            pl.BlockSpec((rows, HD // 2), lambda j: (0, 0)),
        ],
        out_specs=pl.BlockSpec((rows, 2 * HD), lambda j: (0, j)),
        out_shape=jax.ShapeDtypeStruct((rows, steps * 2 * HD), jnp.bfloat16),
        compiler_params=pltpu.CompilerParams(vmem_limit_bytes=56 * 2**20),
        cost_estimate=SMALL_COST,
        name="project",
    )(normed, weights, *tables)


def score_mask(key_seg_ref, query_seg_ref, block, rows):
    keys = (block + 1) * rows
    same = key_seg_ref[:keys, :] == query_seg_ref[...]
    key_at = lax.broadcasted_iota(jnp.int32, (keys, rows), 0)
    query_at = lax.broadcasted_iota(jnp.int32, (keys, rows), 1) + block * rows
    return same & (key_at <= query_at)


def attend_kernel(at_ref, q_ref, k_ref, v_ref, key_seg_ref, query_seg_ref, context_ref, total_ref):
    scale = HD ** (-0.5)
    rows = q_ref.shape[0]
    for block in range(SEQLEN // rows):

        @pl.when(at_ref[0] == block)
        def _():
            keys = (block + 1) * rows
            scores = dot_last(k_ref[:keys, :], q_ref[...]) * scale
            scores = jnp.where(
                score_mask(key_seg_ref, query_seg_ref, block, rows), scores, MASKED
            )
            highest = jnp.max(scores, axis=0, keepdims=True)
            exponent = jnp.exp(scores - highest)
            totals = jnp.sum(exponent, axis=0, keepdims=True)
            probs_low = (exponent * (1.0 / totals)).astype(jnp.bfloat16)
            context = dot_first(probs_low, v_ref[:keys, :])
            context_ref[...] = context.astype(jnp.bfloat16)
            total_ref[0] = highest + jnp.log(totals)


def attend_back_head(
    place, q_ref, k_ref, v_ref, grad_ref, total_ref, key_seg_ref, query_seg_ref, key_cosine_ref,
    key_sine_ref, cosine_ref, sine_ref, query_grad_ref, pair_grad_ref, key_sum, value_sum,
):
    scale = HD ** (-0.5)
    rows = q_ref.shape[0]
    head = pl.program_id(0)

    @pl.when(head == 0)
    def _():
        key_sum[...] = jnp.zeros_like(key_sum)
        value_sum[...] = jnp.zeros_like(value_sum)

    for block in range(SEQLEN // rows):

        @pl.when(place == block)
        def _():
            keys = (block + 1) * rows
            queries, grads = q_ref[...], grad_ref[...]
            shifted = dot_last(k_ref[:keys, :], queries) * scale - total_ref[0]
            allowed = score_mask(key_seg_ref, query_seg_ref, block, rows)
            probs = jnp.where(allowed, jnp.exp(shifted), 0.0)
            prob_grad = dot_last(v_ref[:keys, :], grads)
            centre = jnp.sum(probs * prob_grad, axis=0, keepdims=True)
            score_grad = (probs * (prob_grad - centre) * scale).astype(jnp.bfloat16)
            value_sum[:keys, :] += jnp.dot(
                probs.astype(jnp.bfloat16), grads, preferred_element_type=jnp.float32
            )
            key_sum[:keys, :] += jnp.dot(score_grad, queries, preferred_element_type=jnp.float32)
            query_grad = dot_first(score_grad, k_ref[:keys, :])
            query_grad_ref[...] = turn_back(query_grad, cosine_ref[...], sine_ref[...]).astype(
                jnp.bfloat16
            )

    @pl.when(head == pl.num_programs(0) - 1)
    def _():
        pair_grad_ref[:, :HD] = turn_back(
            key_sum[...], key_cosine_ref[...], key_sine_ref[...]
        ).astype(jnp.bfloat16)
        pair_grad_ref[:, HD:] = value_sum[...].astype(jnp.bfloat16)


def attend_back_kernel(at_ref, *refs):
    attend_back_head(at_ref[0], *refs)


def attention_specs(kinds, rows):
    specs = {
        "at": pl.BlockSpec(memory_space=pltpu.SMEM),
        "head": pl.BlockSpec((rows, HD), lambda h: (0, h)),
        "branch": pl.BlockSpec((rows, MODEL_WIDTH), lambda h: (0, 0)),
        "keys": pl.BlockSpec((SEQLEN, HD), lambda h: (0, 0)),
        "values": pl.BlockSpec((SEQLEN, HD), lambda h: (0, 1)),
        "pair": pl.BlockSpec((SEQLEN, 2 * HD), lambda h: (0, 0)),
        "total": pl.BlockSpec((1, 1, rows), lambda h: (h, 0, 0)),
        "key_seg": pl.BlockSpec((SEQLEN, 1), lambda h: (0, 0)),
        "query_seg": pl.BlockSpec((1, rows), lambda h: (0, 0)),
        "key_table": pl.BlockSpec((SEQLEN, HD // 2), lambda h: (0, 0)),
        "table": pl.BlockSpec((rows, HD // 2), lambda h: (0, 0)),
    }
    return [specs[kind] for kind in kinds]


def attend(at, projected, pairs, key_segs, query_segs):
    rows = projected.shape[0]
    columns = NH * HD
    return pl.pallas_call(
        attend_kernel,
        grid=(NH,),
        in_specs=attention_specs(["at", "head", "keys", "values", "key_seg", "query_seg"], rows),
        out_specs=attention_specs(["head", "total"], rows),
        out_shape=(
            jax.ShapeDtypeStruct((rows, columns), jnp.bfloat16),
            jax.ShapeDtypeStruct((NH, 1, rows), jnp.float32),
        ),
        compiler_params=pltpu.CompilerParams(vmem_limit_bytes=32 * 2**20),
        cost_estimate=SMALL_COST,
        name="attend",
    )(at, projected, pairs, pairs, key_segs[:, None], query_segs[None, :])


def attend_back(at, projected, pairs, grads, totals, key_segs, query_segs, key_tables, tables):
    rows = projected.shape[0]
    columns = NH * HD
    return pl.pallas_call(
        attend_back_kernel,
        grid=(NH,),
        in_specs=attention_specs(
            ["at", "head", "keys", "values", "head", "total", "key_seg", "query_seg"]
            + ["key_table", "key_table", "table", "table"],
            rows,
        ),
        out_specs=attention_specs(["head", "pair"], rows),
        out_shape=(
            jax.ShapeDtypeStruct((rows, columns), jnp.bfloat16),
            jax.ShapeDtypeStruct((SEQLEN, 2 * HD), jnp.bfloat16),
        ),
        scratch_shapes=[pltpu.VMEM((SEQLEN, HD), jnp.float32)] * 2,
        compiler_params=pltpu.CompilerParams(vmem_limit_bytes=32 * 2**20),
        cost_estimate=SMALL_COST,
        name="attend_back",
    )(
        at, projected, pairs, pairs, grads, totals, key_segs[:, None], query_segs[None, :],
        *key_tables, *tables,
    )


def own_columns(grp, own):
    return pl.ds(pl.multiple_of((grp * own) % 128, math.gcd(own, 128)), own)


def load_weights(parts, weights, sems):
    count, rows, _ = parts[0].shape
    halves = len(parts)
    return [
        pltpu.make_async_copy(
            parts[half].at[block],
            weights.at[pl.ds((block * halves + half) * rows, rows)],
            sems.at[block * halves + half],
        )
        for half in range(halves)
        for block in range(count)
    ]


def feed_block(own, first, x, cot, weights, act_ref, gate_grad_ref, up_grad_ref, two_ref, out_ref):
    low = jnp.bfloat16
    wide = jnp.float32
    cols = act_ref.shape[0]
    gate = jnp.dot(x, weights[:, :cols], preferred_element_type=wide)
    upper = jnp.dot(x, weights[:, cols : 2 * cols], preferred_element_type=wide)
    act_grad = jnp.dot(cot, weights[:, 2 * cols :], preferred_element_type=wide)
    column = lax.broadcasted_iota(jnp.int32, gate.shape, 1)
    real = (column >= first) & (column < first + own)
    sigmoid = 1.0 / (1.0 + jnp.exp(-gate))
    silu = gate * sigmoid
    activated = jnp.where(real, silu * upper, 0.0).astype(low)
    act_grad = jnp.where(real, act_grad, 0.0)
    gate_grad = (act_grad * upper * sigmoid * (1.0 + gate * (1.0 - sigmoid))).astype(low)
    up_grad = (act_grad * silu).astype(low)
    act_ref[...] = jnp.transpose(activated)
    gate_grad_ref[...] = jnp.transpose(gate_grad)
    up_grad_ref[...] = jnp.transpose(up_grad)
    two = dot_last(gate_grad, weights[:, :cols]) + dot_last(up_grad, weights[:, cols : 2 * cols])
    two_ref[...] = two.astype(low)
    out_ref[...] = dot_last(activated, weights[:, 2 * cols :]).astype(low)


def feed_kernel(own, real_ref, x_ref, cot_ref, *refs):
    parts, refs = refs[:-7], refs[-7:]
    weights, sems = refs[5:]

    @pl.when(pl.program_id(0) == 0)
    def _():
        copies = load_weights(parts, weights, sems)
        for copy in copies:
            copy.start()
        for copy in copies:
            copy.wait()

    feed_block(own, real_ref[0], x_ref[...], cot_ref[...], weights, *refs[:5])


def feed_forward(own, real_cols, x, cot, parts, seq_count):
    tokens_all, width = x.shape
    _, rows, cols = parts[0].shape
    cols = cols // 3
    step = 256
    low = jnp.bfloat16
    block = pl.BlockSpec((step, width), lambda i: (i, 0))
    narrow = pl.BlockSpec((cols, step), lambda i: (0, i))
    return pl.pallas_call(
        functools.partial(feed_kernel, own),
        grid=(tokens_all // step,),
        in_specs=[pl.BlockSpec(memory_space=pltpu.SMEM), block, block]
        + [pl.BlockSpec(memory_space=pl.ANY)] * len(parts),
        out_specs=[narrow, narrow, narrow, block, block],
        out_shape=[jax.ShapeDtypeStruct((cols, tokens_all), low)] * 3
        + [jax.ShapeDtypeStruct((tokens_all, width), low)] * 2,
        scratch_shapes=[
            pltpu.VMEM((width, 3 * cols), low),
            pltpu.SemaphoreType.DMA((len(parts) * seq_count,)),
        ],
        compiler_params=pltpu.CompilerParams(vmem_limit_bytes=52 * 2**20),
        cost_estimate=SMALL_COST,
        name="feed_forward",
    )(real_cols, x, cot, *parts)


def feed_gather_kernel(
    own, first, second, halves, real_ref, own_ref, context_ref, cot_ref, cot_all_ref, *refs
):
    parts, refs = refs[:halves], refs[halves:]
    (
        gate_grad_ref, up_grad_ref, two_ref, out_ref, second_ref, context_plane_ref, down_out,
        blocks, weights, act_block, act, x_block, stage, load_sems, keep_sems, x_sems, out_sems,
        first_send, first_recv, second_send, second_recv,
    ) = refs
    step = pl.program_id(0)
    grp, seq = lax.axis_index("grp"), lax.axis_index("seq")
    first.start(own_ref, blocks, (first_send, first_recv), grp, seq, begin=False)
    second.start(context_ref, context_plane_ref, (second_send, second_recv), grp, seq, begin=False)
    loads = load_weights(parts, weights, load_sems)
    cols = act.shape[0]
    step_rows = act_block.shape[1]
    rows = x_block.shape[2]
    count = cot_all_ref.shape[1] // rows

    @pl.when(step == 0)
    def _():
        for copy in loads:
            copy.start()
        barrier = pltpu.get_barrier_semaphore()
        for device in first.peers(grp, seq):
            pl.semaphore_signal(barrier, inc=1, device_id=device, device_id_type=MESH)
        pl.semaphore_wait(barrier, 3)
        first.begin()
        first.kept.wait()
        for copy in loads:
            copy.wait()

    @pl.when(step == 1)
    def _():
        first.due[7].wait_recv()

    @pl.when(step == 2)
    def _():
        for came in (1, 4, 2):
            first.pass_on(came)

    @pl.when(step == 3)
    def _():
        first.pass_on(5)
        second.begin()

    @pl.when(step == 4)
    def _():
        first.due[8].wait_recv()
        first.due[9].wait_recv()
        first.pass_on(6)
        first.pass_on(3)

    @pl.when(step == 5)
    def _():
        first.due[10].wait_recv()
        first.due[11].wait_recv()

    @pl.when(step == 7)
    def _():
        first.due[12].wait_recv()
        first.due[13].wait_recv()
        second.pass_on(1)
        second.pass_on(4)

    keep = pltpu.make_async_copy(blocks.at[step], second_ref.at[step], keep_sems.at[step])
    keep.start()
    feed_block(
        own, real_ref[0], blocks[step], cot_ref[...], weights, act_block, gate_grad_ref, up_grad_ref,
        two_ref, out_ref,
    )
    act[:, pl.ds(pl.multiple_of(step * step_rows, step_rows), step_rows)] = act_block[...]

    def x_copy(at):
        view = cot_all_ref.at[:, pl.ds(pl.multiple_of(at * rows, rows), rows)]
        return pltpu.make_async_copy(view, x_block.at[at % 2], x_sems.at[at % 2])

    def out_copy(at):
        place = pl.ds(pl.multiple_of(at * own, own), own)
        mine = stage.at[at % 2, own_columns(grp, own)]
        return pltpu.make_async_copy(mine, down_out.at[place], out_sems.at[at % 2])

    @pl.when(step == 7)
    def _():
        x_copy(0).start()
        second.pass_on(2)
        second.pass_on(5)

        def one(at, _):
            x_copy(at).wait()

            @pl.when(at + 1 < count)
            def _():
                x_copy(at + 1).start()

            @pl.when(at >= 2)
            def _():
                out_copy(at - 2).wait()

            stage[at % 2] = jnp.dot(
                act[...], x_block[at % 2], preferred_element_type=jnp.float32
            ).astype(stage.dtype)
            out_copy(at).start()
            return 0

        lax.fori_loop(0, count, one, 0)
        second.pass_on(6)
        second.pass_on(3)
        out_copy(count - 2).wait()
        out_copy(count - 1).wait()
        second.finish()
        for copy in first.out[1:]:
            copy.wait_send()
        for at in range(8):
            pltpu.make_async_copy(blocks.at[at], second_ref.at[at], keep_sems.at[at]).wait()


def feed_gather(number, own, real_cols, normed, context, cot, parts, seq_count):
    rows, width = normed.shape
    cols = parts[0].shape[2] // 3
    low = jnp.bfloat16
    block = pl.BlockSpec((rows, width), lambda i: (i, 0))
    narrow = pl.BlockSpec((cols, rows), lambda i: (0, i))
    first = gather_plane(normed.shape, placed=True)
    second = gather_plane(context.shape, placed=True)
    hbm = pl.BlockSpec(memory_space=pl.ANY)
    plane = jax.ShapeDtypeStruct((8, rows, width), low)
    model_rows = width // seq_count
    return pl.pallas_call(
        functools.partial(feed_gather_kernel, own, first, second, len(parts)),
        grid=(8,),
        in_specs=[pl.BlockSpec(memory_space=pltpu.SMEM), hbm, hbm, block, hbm]
        + [hbm] * len(parts),
        out_specs=[narrow, narrow, block, block, hbm, hbm, hbm],
        out_shape=[jax.ShapeDtypeStruct((cols, 8 * rows), low)] * 2
        + [jax.ShapeDtypeStruct((8 * rows, width), low)] * 2
        + [plane, plane, jax.ShapeDtypeStruct((seq_count * own, model_rows), low)],
        scratch_shapes=[
            pltpu.VMEM((8, rows, width), low),
            pltpu.VMEM((width, 3 * cols), low),
            pltpu.VMEM((cols, rows), low),
            pltpu.VMEM((cols, 8 * rows), low),
            pltpu.VMEM((2, 8 * rows, model_rows), low),
            pltpu.VMEM((2, cols, model_rows), low),
            pltpu.SemaphoreType.DMA((seq_count * len(parts),)),
            pltpu.SemaphoreType.DMA((8,)),
            pltpu.SemaphoreType.DMA((2,)),
            pltpu.SemaphoreType.DMA((2,)),
        ]
        + [pltpu.SemaphoreType.DMA((14,))] * 4,
        compiler_params=pltpu.CompilerParams(
            collective_id=number, has_side_effects=True, vmem_limit_bytes=60 * 2**20
        ),
        cost_estimate=SMALL_COST,
        name="feed_gather",
    )(real_cols, normed, context, cot, cot, *parts)


def weight_grad_kernel(left_ref, x_ref, out_ref):
    out_ref[...] = jnp.dot(
        left_ref[...], x_ref[...], preferred_element_type=jnp.float32
    ).astype(out_ref.dtype)


def weight_grad(left, x, seq_count):
    cols, tokens_all = left.shape
    rows = x.shape[1] // seq_count
    return pl.pallas_call(
        weight_grad_kernel,
        grid=(seq_count,),
        in_specs=[
            pl.BlockSpec((cols, tokens_all), lambda i: (0, 0)),
            pl.BlockSpec((tokens_all, rows), lambda i: (0, i)),
        ],
        out_specs=pl.BlockSpec((cols, rows), lambda i: (i, 0)),
        out_shape=jax.ShapeDtypeStruct((seq_count * cols, rows), jnp.bfloat16),
        compiler_params=pltpu.CompilerParams(vmem_limit_bytes=40 * 2**20),
        cost_estimate=SMALL_COST,
        name="weight_grad",
    )(left, x)


def share_grad_kernel(query_ref, out_ref, normed_ref, context_ref, grads_ref, turned):
    half = query_ref.shape[1]

    @pl.when(pl.program_id(0) == 0)
    def _():
        turned[0], turned[1] = jnp.transpose(query_ref[...]), jnp.transpose(out_ref[...])

    for at, right in enumerate((normed_ref, context_ref)):
        made = jnp.dot(turned[at], right[...], preferred_element_type=jnp.float32)
        grads_ref[at * half : (at + 1) * half, :] = made.astype(grads_ref.dtype)


def share_grad(query_share, out_share, normed, context):
    tokens_all, width = normed.shape
    columns = query_share.shape[1]
    step = 512
    narrow = pl.BlockSpec((tokens_all, columns), lambda i: (0, 0))
    block = pl.BlockSpec((tokens_all, step), lambda i: (0, i))
    return pl.pallas_call(
        share_grad_kernel,
        grid=(width // step,),
        in_specs=[narrow, narrow, block, block],
        out_specs=pl.BlockSpec((2 * columns, step), lambda i: (0, i)),
        out_shape=jax.ShapeDtypeStruct((2 * columns, width), jnp.bfloat16),
        scratch_shapes=[pltpu.VMEM((2, columns, tokens_all), jnp.bfloat16)],
        compiler_params=pltpu.CompilerParams(vmem_limit_bytes=60 * 2**20),
        cost_estimate=SMALL_COST,
        name="share_grad",
    )(query_share, out_share, normed, context)


def pick_kernel(rows, feed_ref, attn_ref, tiles_ref, feed_out, attn_out, sems):
    grp = lax.axis_index("grp")
    width = tiles_ref.shape[2]
    copies = []
    for at in range(feed_ref.shape[0]):
        copies.append(
            (tiles_ref.at[feed_ref[at]], feed_out.at[:, at * width : (at + 1) * width])
        )
    share = pl.ds(pl.multiple_of(grp * rows, rows), rows)
    for at in range(attn_ref.shape[0]):
        copies.append(
            (tiles_ref.at[attn_ref[at], share], attn_out.at[:, at * width : (at + 1) * width])
        )
    copies = [
        pltpu.make_async_copy(source, target, sems.at[at])
        for at, (source, target) in enumerate(copies)
    ]
    for copy in copies:
        copy.start()
    for copy in copies:
        copy.wait()


def pick(tiles, feed_slots, attn_slots):
    _, rows, width = tiles.shape
    share = rows // lax.axis_size("grp")
    feed, attn = feed_slots.shape[0], attn_slots.shape[0]
    return pl.pallas_call(
        functools.partial(pick_kernel, share),
        in_specs=[pl.BlockSpec(memory_space=pltpu.SMEM)] * 2 + [pl.BlockSpec(memory_space=pl.ANY)],
        out_specs=[pl.BlockSpec(memory_space=pltpu.VMEM)] * 2,
        out_shape=[
            jax.ShapeDtypeStruct((rows, feed * width), tiles.dtype),
            jax.ShapeDtypeStruct((share, attn * width), tiles.dtype),
        ],
        scratch_shapes=[pltpu.SemaphoreType.DMA((feed + attn,))],
        cost_estimate=SMALL_COST,
        name="pick",
    )(feed_slots, attn_slots, tiles)


def adam_kernel(group, at_ref, *refs):
    feeds = [refs[at * group : (at + 1) * group] for at in range(4)]
    left_ref, right_ref, master_ref, one_ref, two_ref = refs[4 * group : 4 * group + 5]
    new_master_ref, new_one_ref, new_two_ref, grad = refs[4 * group + 5 :]
    low = jnp.bfloat16
    for slot in range(group):
        kind = at_ref[0, pl.program_id(0) * group + slot]
        for number in range(3):

            @pl.when(kind == number)
            def _():
                grad[slot] = feeds[number][slot][...]

        @pl.when(kind == 3)
        def _():
            pair = feeds[3][slot][...].reshape(grad.shape[2], grad.shape[1])
            grad[slot] = jnp.transpose(pair.astype(jnp.float32)).astype(grad.dtype)

        @pl.when(kind == 4)
        def _():
            grad[slot] = jnp.zeros(grad.shape[1:], grad.dtype)

    slots = range(group)
    left = [left_ref[slot].astype(low) for slot in slots]
    right = [right_ref[slot].astype(low) for slot in slots]
    turned = [
        jnp.dot(grad[slot], left[slot], preferred_element_type=jnp.float32) for slot in slots
    ]
    turned = [dot_first(turned[slot].astype(low), right[slot]) for slot in slots]
    scaled = []
    for slot in slots:
        new_one = BETA_ONE * one_ref[slot] + (1.0 - BETA_ONE) * turned[slot]
        new_two = BETA_TWO * two_ref[slot] + (1.0 - BETA_TWO) * turned[slot] * turned[slot]
        new_one_ref[slot], new_two_ref[slot] = new_one, new_two
        scaled.append((new_one / (jnp.sqrt(new_two) + ADAM_EPS)).astype(low))
    restored = [dot_last(scaled[slot], right[slot]).astype(low) for slot in slots]
    restored = [
        jnp.dot(left[slot], restored[slot], preferred_element_type=jnp.float32) for slot in slots
    ]
    for slot in slots:
        new_master_ref[slot] = (
            master_ref[slot] * (1.0 - LEARN_RATE * WEIGHT_DECAY) - LEARN_RATE * restored[slot]
        )


def adam(at, gating, down, shares, pairs, left, right, master, one, two):
    slots, rows, width = master.shape
    group = 3 if slots % 3 == 0 else 1
    tile = pl.BlockSpec((group, rows, width), lambda i, at: (i, 0, 0))
    shape = jax.ShapeDtypeStruct(master.shape, jnp.float32)

    def feed(row):
        return [
            pl.BlockSpec((width, rows), lambda i, at, slot=slot: (at[row, i * group + slot], 0))
            for slot in range(group)
        ]

    pair = [
        pl.BlockSpec(
            (*pairs.shape[:2], width), lambda i, at, slot=slot: (0, 0, at[4, i * group + slot])
        )
        for slot in range(group)
    ]
    return pl.pallas_call(
        functools.partial(adam_kernel, group),
        grid_spec=pltpu.PrefetchScalarGridSpec(
            num_scalar_prefetch=1,
            grid=(slots // group,),
            in_specs=feed(1)
            + feed(2)
            + feed(3)
            + pair
            + [
                pl.BlockSpec((group, rows, rows), lambda i, at: (i, 0, 0)),
                pl.BlockSpec((group, width, width), lambda i, at: (i, 0, 0)),
                tile,
                tile,
                tile,
            ],
            out_specs=[tile] * 3,
            scratch_shapes=[pltpu.VMEM((group, width, rows), jnp.bfloat16)],
        ),
        out_shape=[shape] * 3,
        compiler_params=pltpu.CompilerParams(vmem_limit_bytes=60 * 2**20),
        cost_estimate=SMALL_COST,
        name="adam",
    )(
        at, *[gating] * group, *[down] * group, *[shares] * group, *[pairs] * group,
        left, right, master, one, two,
    )


MESH = pl.DeviceIdType.MESH


def remote(source, target, sems, at, device):
    return pltpu.make_async_remote_copy(
        src_ref=source,
        dst_ref=target,
        send_sem=sems[0].at[at],
        recv_sem=sems[1].at[at],
        device_id=device,
        device_id_type=MESH,
    )


def columns_of(ref, index, width):
    return ref.at[:, pl.ds(pl.multiple_of(index * width, width), width)]


def rows_of(ref, index, height):
    return ref.at[pl.ds(pl.multiple_of(index * height, height), height), :]


PLACES = {0: 0, 1: 1, 2: 2, 4: 3, 3: 4, 5: 5, 6: 6, 7: 7}


def flip(device, bits):
    core, side_x, side_y = device % 2, (device // 2) % 2, device // 4
    for bit, there in ((1, 1 - 2 * core), (2, 2 - 4 * side_x), (4, 4 - 8 * side_y)):
        if bits & bit:
            device = device + there
    return device


class PlacedExchange:
    axis = "grp"
    sem_count = 8

    def __init__(self, out_shape, source_view):
        self.out_shape, self.source_view = out_shape, source_view

    def peers(self, grp, seq):
        for bits in range(1, 8):
            yield flip(grp, bits), seq

    def start(self, source, target, sems, grp, seq):
        self.own = pltpu.make_async_copy(
            self.source_view(source, grp), target.at[0], sems[0].at[0]
        )
        self.own.start()
        self.copies = []
        for bits in range(1, 8):
            there = flip(grp, bits)
            copy = remote(
                self.source_view(source, there), target.at[PLACES[bits]], sems, bits, (there, seq)
            )
            copy.start()
            self.copies.append(copy)

    def forward(self):
        return iter(())

    def finish(self):
        for copy in self.copies:
            copy.wait()
        self.own.wait()


class Exchange:
    def __init__(self, axis, out_shape, source_view, target_view):
        self.axis, self.out_shape = axis, out_shape
        self.source_view, self.target_view = source_view, target_view
        self.count = lax.axis_size(axis)
        self.sem_count = self.count

    def peers(self, grp, seq):
        me = grp if self.axis == "grp" else seq
        for step in range(1, self.count):
            there = (me + step) % self.count
            yield (there, seq) if self.axis == "grp" else (grp, there)

    def start(self, source, target, sems, grp, seq, begin=True):
        me = grp if self.axis == "grp" else seq
        self.own = pltpu.make_async_copy(
            self.source_view(source, me), self.target_view(target, me), sems[0].at[0]
        )
        self.sent, self.due = [], []
        for step, device in enumerate(self.peers(grp, seq), 1):
            there = (me + step) % self.count
            back = (me + self.count - step) % self.count
            self.sent.append(
                remote(
                    self.source_view(source, there), self.target_view(target, me), sems, step, device
                )
            )
            self.due.append(
                remote(
                    self.source_view(source, back), self.target_view(target, back), sems, step, device
                )
            )
        if begin:
            self.begin()

    def begin(self):
        for copy in [self.own] + self.sent:
            copy.start()

    def forward(self):
        return iter(())

    def finish(self):
        for copy in self.due:
            copy.wait_recv()
        for copy in self.sent:
            copy.wait_send()
        self.own.wait()


class PlaneGather:
    axis = "grp"
    sem_count = 14

    def __init__(self, out_shape, source_view, target_view, half_of, placed):
        self.out_shape, self.placed = out_shape, placed
        self.source_view, self.target_view, self.half_of = source_view, target_view, half_of

    def peers(self, grp, seq):
        for bits in (1, 2, 4):
            yield flip(grp, bits), seq

    def start(self, source, target, sems, grp, seq, begin=True):
        def part(device, bits, piece):
            view = self.target_view(target, PLACES[bits] if self.placed else flip(device, bits))
            return view if piece == "all" else self.half_of(view, piece == "b")

        def own(piece):
            view = self.source_view(source, grp)
            return view if piece == "all" else self.half_of(view, piece == "b")

        self.out, self.due = [None], [None]
        for via, here, there, piece in (
            (2, 0, 2, "a"),
            (2, 0, 2, "b"),
            (2, 4, 6, "b"),
            (4, 0, 4, "b"),
            (4, 0, 4, "a"),
            (4, 2, 6, "a"),
            (1, 0, 1, "all"),
            (1, 2, 3, "a"),
            (1, 2, 3, "b"),
            (1, 4, 5, "b"),
            (1, 4, 5, "a"),
            (1, 6, 7, "a"),
            (1, 6, 7, "b"),
        ):
            device = flip(grp, via)
            view = own(piece) if here == 0 else part(grp, here, piece)
            at = len(self.out)
            self.out.append(remote(view, part(device, there, piece), sems, at, (device, seq)))
            self.due.append(remote(view, part(grp, there, piece), sems, at, (device, seq)))
        self.kept = pltpu.make_async_copy(own("all"), part(grp, 0, "all"), sems[0].at[0])
        if begin:
            self.begin()

    def begin(self):
        self.kept.start()
        for at in (1, 4, 2, 5, 7):
            self.out[at].start()

    def pass_on(self, came):
        self.due[came].wait_recv()
        for at in {1: (6, 8), 4: (3, 10), 2: (9,), 5: (11,), 6: (12,), 3: (13,)}[came]:
            self.out[at].start()

    def forward(self):
        for pair in ((1, 4), (2, 5), (6, 3)):
            for came in pair:
                self.pass_on(came)
            yield

    def finish(self):
        for copy in self.due[7:]:
            copy.wait_recv()
        for copy in self.out[1:]:
            copy.wait_send()
        self.kept.wait()


def add_rows(total, first, second):
    step = 32

    def some(at, _):
        rows = pl.ds(pl.multiple_of(at * step, step), step)
        total[rows, :] = (
            first[rows, :].astype(jnp.float32) + second[rows, :].astype(jnp.float32)
        ).astype(total.dtype)
        return 0

    lax.fori_loop(0, total.shape[0] // step, some, 0)


class PlaneSum:
    axis = "grp"
    sem_count = 15

    def __init__(self, rows, columns, placed=True):
        self.rows, self.columns, self.placed = rows, columns, placed
        self.out_shape = (rows, columns)

    def scratch(self):
        low = jnp.bfloat16
        shape = (self.rows, self.columns)
        half = (self.rows // 2, self.columns)
        return [
            pltpu.VMEM((4, *shape), low),
            pltpu.VMEM((4, *shape), low),
            pltpu.VMEM((2, *half), low),
            pltpu.VMEM((2, *shape), low),
        ]

    def peers(self, grp, seq):
        for bits in (1, 2, 4):
            yield flip(grp, bits), seq

    def start(self, source, target, sems, grp, seq, scratch, begin=True):
        self.mine, self.core_in, self.halves, self.wholes = scratch
        core, side_x, side_y = [(flip(grp, bits), seq) for bits in (1, 2, 4)]
        half = self.rows // 2
        self.low, self.high = low, high = pl.ds(0, half), pl.ds(half, half)
        mine, halves, wholes = self.mine, self.halves, self.wholes

        def block(bits):
            return source.at[PLACES[bits] if self.placed else flip(grp, bits)]

        self.copies = [
            remote(block(bits), self.core_in.at[at], sems, at, core)
            for at, bits in enumerate((7, 3, 5, 1))
        ] + [
            remote(mine.at[0, low], halves.at[0], sems, 4, side_x),
            remote(mine.at[0, high], halves.at[1], sems, 5, side_y),
            remote(mine.at[1, low], wholes.at[0, low], sems, 6, side_x),
            remote(mine.at[2, high], wholes.at[1, high], sems, 7, side_y),
            remote(mine.at[1, high], wholes.at[0, high], sems, 8, side_x),
            remote(mine.at[2, low], wholes.at[1, low], sems, 9, side_y),
        ]
        self.loads = [
            pltpu.make_async_copy(block(bits), mine.at[at], sems[0].at[10 + at])
            for at, bits in enumerate((6, 2, 4, 0))
        ]
        if target is not None:
            self.store = pltpu.make_async_copy(mine.at[3], target, sems[0].at[14])
        if begin:
            self.begin()

    def begin(self):
        for copy in self.copies[:4] + self.loads:
            copy.start()

    def first_sums(self):
        for came, then in ((0, (4, 5)), (1, (6,)), (2, (7,)), (3, ())):
            self.copies[came].wait_recv()
            self.loads[came].wait()
            add_rows(self.mine.at[came], self.mine.at[came], self.core_in.at[came])
            for at in then:
                self.copies[at].start()

    def forward(self):
        mine, low, high = self.mine, self.low, self.high
        yield
        self.copies[5].wait_recv()
        add_rows(mine.at[1, high], mine.at[1, high], self.halves.at[1])
        self.copies[8].start()
        self.copies[4].wait_recv()
        add_rows(mine.at[2, low], mine.at[2, low], self.halves.at[0])
        self.copies[9].start()

    def total(self):
        mine = self.mine
        for at, side, rows in ((6, 0, self.low), (7, 1, self.high), (8, 0, self.high), (9, 1, self.low)):
            self.copies[at].wait_recv()
            add_rows(mine.at[3, rows], mine.at[3, rows], self.wholes.at[side, rows])
        return mine.at[3]

    def finish(self):
        self.total()
        self.store.start()
        for copy in self.copies:
            copy.wait_send()
        self.store.wait()


class LineGather:
    axis = "seq"

    def __init__(self, shape):
        self.count = lax.axis_size("seq")
        self.out_shape = (self.count, *shape)
        self.sem_count = 2 * self.count

    def peers(self, grp, seq):
        for step in range(1, self.count):
            yield grp, (seq + step) % self.count

    def start(self, source, target, sems, grp, seq):
        self.seq, self.sems = seq, sems
        self.own = pltpu.make_async_copy(source, target.at[seq], sems[0].at[0])
        self.own.start()

        def make(away, up):
            there = (seq + (1 if up else self.count - 1)) % self.count
            block = (seq + (self.count - away if up else away)) % self.count
            view = source if away == 0 else target.at[block]
            at = 1 + away if up else self.count + away
            return remote(view, target.at[block], sems, at, (grp, there))

        def came(away, up):
            block = (seq + (self.count - away if up else away)) % self.count
            at = away if up else self.count + away - 1
            side = (seq + (self.count - 1 if up else 1)) % self.count
            return remote(target.at[block], target.at[block], sems, at, (grp, side))

        self.make, self.came = make, came
        self.has = lambda away, up: (seq - away >= 0) if up else (seq + away < self.count)
        self.last = lambda up: (seq + 1 < self.count) if up else (seq >= 1)
        for up in (True, False):

            @pl.when(self.last(up))
            def _():
                make(0, up).start()

    def forward(self):
        for away in range(1, self.count):
            for up in (True, False):

                @pl.when(self.has(away, up))
                def _():
                    self.came(away, up).wait_recv()
                    if away < self.count - 1:

                        @pl.when(self.last(up))
                        def _():
                            self.make(away, up).start()

            yield

    def finish(self):
        for away in range(self.count - 1):
            for up in (True, False):

                @pl.when(self.has(away, up) & self.last(up))
                def _():
                    self.make(away, up).wait_send()
        self.own.wait()


def attend_back_sum_kernel(
    sum_task, gather_task, q_ref, k_ref, v_ref, branch_ref, total_ref, key_seg_ref, query_seg_ref,
    key_cosine_ref, key_sine_ref, cosine_ref, sine_ref, part_hbm, down_hbm, weights_hbm,
    query_grad_ref, pair_grad_ref, sum_hbm, down_plane, key_sum, value_sum, grad_ref, w_block,
    w_sems, mine, core_in, halves, wholes, sum_send, sum_recv, gather_send, gather_recv,
):
    step = pl.program_id(0)
    grp, seq = lax.axis_index("grp"), lax.axis_index("seq")
    scratch = (mine, core_in, halves, wholes)
    sum_task.start(part_hbm, sum_hbm, (sum_send, sum_recv), grp, seq, scratch, begin=False)
    gather_task.start(down_hbm, down_plane, (gather_send, gather_recv), grp, seq, begin=False)

    def w_copy(at):
        rows = pl.ds(pl.multiple_of(at * HD, HD), HD)
        view = weights_hbm.at[rows, pl.ds((NH + 2) * HD, MODEL_WIDTH)]
        return pltpu.make_async_copy(view, w_block.at[at % 2], w_sems.at[at % 2])

    @pl.when(step == 0)
    def _():
        w_copy(step).start()
        barrier = pltpu.get_barrier_semaphore()
        for device in sum_task.peers(grp, seq):
            pl.semaphore_signal(barrier, inc=1, device_id=device, device_id_type=MESH)
        pl.semaphore_wait(barrier, 3)
        sum_task.begin()
        gather_task.begin()

    @pl.when(step == 6)
    def _():
        sum_task.first_sums()

    w_copy(step).wait()

    @pl.when(step + 1 < pl.num_programs(0))
    def _():
        w_copy(step + 1).start()

    grad_ref[...] = dot_last(branch_ref[...], w_block[step % 2]).astype(grad_ref.dtype)
    attend_back_head(
        seq, q_ref, k_ref, v_ref, grad_ref, total_ref, key_seg_ref, query_seg_ref, key_cosine_ref,
        key_sine_ref, cosine_ref, sine_ref, query_grad_ref, pair_grad_ref, key_sum, value_sum,
    )

    @pl.when(step == pl.num_programs(0) - 1)
    def _():
        hand_on([gather_task, sum_task])
        gather_task.finish()
        sum_task.finish()


def attend_back_sum(
    number, projected, pairs, branch_grad, totals, key_segs, query_segs, key_tables, tables, part,
    down, weights,
):
    rows = projected.shape[0]
    columns = NH * HD
    low = jnp.bfloat16
    sum_task = PlaneSum(*part.shape[1:])
    gather_task = gather_plane(down.shape)
    hbm = pl.BlockSpec(memory_space=pl.ANY)
    return pl.pallas_call(
        functools.partial(attend_back_sum_kernel, sum_task, gather_task),
        grid=(NH,),
        in_specs=attention_specs(
            ["head", "keys", "values", "branch", "total", "key_seg", "query_seg"]
            + ["key_table", "key_table", "table", "table"],
            rows,
        )
        + [hbm, hbm, hbm],
        out_specs=attention_specs(["head", "pair"], rows) + [hbm, hbm],
        out_shape=[
            jax.ShapeDtypeStruct((rows, columns), low),
            jax.ShapeDtypeStruct((SEQLEN, 2 * HD), low),
            jax.ShapeDtypeStruct(sum_task.out_shape, low),
            jax.ShapeDtypeStruct(gather_task.out_shape, low),
        ],
        scratch_shapes=[pltpu.VMEM((SEQLEN, HD), jnp.float32)] * 2
        + [
            pltpu.VMEM((rows, HD), low),
            pltpu.VMEM((2, HD, MODEL_WIDTH), low),
            pltpu.SemaphoreType.DMA((2,)),
        ]
        + sum_task.scratch()
        + [pltpu.SemaphoreType.DMA((sum_task.sem_count,))] * 2
        + [pltpu.SemaphoreType.DMA((gather_task.sem_count,))] * 2,
        compiler_params=pltpu.CompilerParams(
            collective_id=number, has_side_effects=True, vmem_limit_bytes=48 * 2**20
        ),
        cost_estimate=SMALL_COST,
        name="attend_back_sum",
    )(
        projected, pairs, pairs, branch_grad, totals, key_segs[:, None], query_segs[None, :],
        *key_tables, *tables, part, down, weights,
    )


def block_kernel(
    first, second, pair_task, key_seg_ref, query_seg_ref, normed_ref, tokens_ref, gain_ref,
    cosine_ref, sine_ref, cot_hbm, normed_hbm, w_ref, projected_ref, pairs_ref, context_ref,
    total_ref, hidden_ref, second_ref, inverse_ref, cot_plane, normed_plane, own_pair, pairs,
    first_send, first_recv, second_send, second_recv, pair_send, pair_recv,
):
    step = pl.program_id(0)
    grp, seq = lax.axis_index("grp"), lax.axis_index("seq")
    first.start(cot_hbm, cot_plane, (first_send, first_recv), grp, seq, begin=False)
    second.start(normed_hbm, normed_plane, (second_send, second_recv), grp, seq, begin=False)
    pair_task.start(own_pair, pairs, (pair_send, pair_recv), grp, seq, begin=False)
    low = jnp.bfloat16
    rows = normed_ref.shape[0]
    wide = 2 * HD
    couples = NH // 2
    attend_at = 1 + couples
    out_at = attend_at + NH
    end = out_at + MODEL_WIDTH // wide

    @pl.when(step == 0)
    def _():
        barrier = pltpu.get_barrier_semaphore()
        devices = list(first.peers(grp, seq)) + list(pair_task.peers(grp, seq))
        for device in devices:
            pl.semaphore_signal(barrier, inc=1, device_id=device, device_id_type=MESH)
        pl.semaphore_wait(barrier, len(devices))
        first.begin()
        second.begin()

    @pl.when(step < attend_at)
    def _():
        made = jnp.dot(normed_ref[...], w_ref[...], preferred_element_type=jnp.float32)
        cosine, sine = cosine_ref[...], sine_ref[...]
        left = turn(made[:, :HD], cosine, sine).astype(low)
        right = made[:, HD:]

        @pl.when(step == 0)
        def _():
            own_pair[:, :HD] = left
            own_pair[:, HD:] = right.astype(low)
            pair_task.begin()
            projected_ref[:, NH * HD :] = own_pair[...]

        @pl.when(step > 0)
        def _():
            place = pl.multiple_of((step - 1) * wide, wide)
            projected_ref[:, pl.ds(place, HD)] = left
            projected_ref[:, pl.ds(pl.multiple_of(place + HD, HD), HD)] = turn(
                right, cosine, sine
            ).astype(low)

    @pl.when(step == attend_at)
    def _():
        pair_task.finish()
        for at in range(pairs.shape[0]):
            pairs_ref[at * rows : (at + 1) * rows, :] = pairs[at]

    @pl.when(step == attend_at + 2)
    def _():
        first.pass_on(1)
        first.pass_on(4)

    @pl.when(step == out_at)
    def _():
        first.pass_on(2)
        first.pass_on(5)

    @pl.when(step == out_at + 2)
    def _():
        second.pass_on(1)
        second.pass_on(4)

    @pl.when((step >= attend_at) & (step < out_at))
    def _():
        head = step - attend_at
        place = pl.ds(pl.multiple_of(head * HD, HD), HD)
        scale = HD ** (-0.5)
        for block in range(SEQLEN // rows):

            @pl.when(seq == block)
            def _():
                keys = (block + 1) * rows
                scores = dot_last(pairs_ref[:keys, :HD], projected_ref[:, place]) * scale
                scores = jnp.where(
                    score_mask(key_seg_ref, query_seg_ref, block, rows), scores, MASKED
                )
                highest = jnp.max(scores, axis=0, keepdims=True)
                exponent = jnp.exp(scores - highest)
                totals = jnp.sum(exponent, axis=0, keepdims=True)
                probs_low = (exponent * (1.0 / totals)).astype(low)
                context = dot_first(probs_low, pairs_ref[:keys, HD:])
                context_ref[:, place] = context.astype(low)
                total_ref[head] = highest + jnp.log(totals)

    @pl.when(step >= out_at)
    def _():
        place = pl.ds(pl.multiple_of((step - out_at) * wide, wide), wide)
        branch = jnp.dot(context_ref[...], w_ref[...], preferred_element_type=jnp.float32)
        hidden_ref[:, place] = tokens_ref[:, place].astype(jnp.float32) + branch

    @pl.when(step == end - 1)
    def _():
        chunk = 32
        gain = gain_ref[1:2, :]

        def some(at, _):
            part = pl.ds(pl.multiple_of(at * chunk, chunk), chunk)
            hidden = hidden_ref[part, :]
            inverse = lax.rsqrt(jnp.mean(hidden * hidden, axis=-1, keepdims=True) + NORM_EPS)
            inverse_ref[part, :] = inverse
            second_ref[part, :] = (hidden * inverse * gain).astype(low)
            return 0

        lax.fori_loop(0, rows // chunk, some, 0)
        first.pass_on(6)
        first.pass_on(3)
        for came in (2, 5, 6, 3):
            second.pass_on(came)
        first.finish()
        second.finish()


def attention_block(number, normed, tokens, gains, tables, key_segs, query_segs, cotangent, weights):
    rows, width = normed.shape
    low, wide = jnp.bfloat16, 2 * HD
    couples = NH // 2
    count = SEQLEN // rows
    first = gather_plane(cotangent.shape, placed=True)
    second = gather_plane(normed.shape, placed=True)
    pair_task = Exchange("seq", (count, rows, wide), whole, block_of)

    def weight_block(step):
        turned = step - NH
        return (0, jnp.where(step == 0, couples, jnp.where(step <= couples, step - 1, jnp.maximum(turned, couples + 1))))

    def full(shape):
        return pl.BlockSpec(shape, lambda step: (0,) * len(shape))

    hbm = pl.BlockSpec(memory_space=pl.ANY)
    steps = 1 + couples + NH + width // wide
    plane = jax.ShapeDtypeStruct((8, rows, width), low)
    shapes = [
        jax.ShapeDtypeStruct((rows, NH * HD + wide), low),
        jax.ShapeDtypeStruct((SEQLEN, wide), low),
        jax.ShapeDtypeStruct((rows, NH * HD), low),
        jax.ShapeDtypeStruct((NH, 1, rows), jnp.float32),
        jax.ShapeDtypeStruct((rows, width), jnp.float32),
        jax.ShapeDtypeStruct((rows, width), low),
        jax.ShapeDtypeStruct((rows, 1), jnp.float32),
    ]
    return pl.pallas_call(
        functools.partial(block_kernel, first, second, pair_task),
        grid=(steps,),
        in_specs=[
            full((SEQLEN, 1)),
            full((1, rows)),
            full((rows, width)),
            full((rows, width)),
            full((2, width)),
            full((rows, HD // 2)),
            full((rows, HD // 2)),
            hbm,
            hbm,
            pl.BlockSpec((width, wide), weight_block),
        ],
        out_specs=[full(shape.shape) for shape in shapes] + [hbm, hbm],
        out_shape=shapes + [plane, plane],
        scratch_shapes=[pltpu.VMEM((rows, wide), low), pltpu.VMEM((count, rows, wide), low)]
        + [pltpu.SemaphoreType.DMA((14,))] * 4
        + [pltpu.SemaphoreType.DMA((pair_task.sem_count,))] * 2,
        compiler_params=pltpu.CompilerParams(
            collective_id=number, has_side_effects=True, vmem_limit_bytes=56 * 2**20
        ),
        cost_estimate=SMALL_COST,
        name="attention_block",
    )(
        key_segs[:, None], query_segs[None, :], normed, tokens, gains, *tables, cotangent, normed,
        weights,
    )


def add_blocks(total, blocks):
    step = min(32, total.shape[0])

    def some(at, _):
        rows = pl.ds(pl.multiple_of(at * step, step), step)
        made = blocks[0, rows, :].astype(jnp.float32)
        for block in range(1, blocks.shape[0]):
            made = made + blocks[block, rows, :].astype(jnp.float32)
        total[rows, :] = made.astype(total.dtype)
        return 0

    lax.fori_loop(0, total.shape[0] // step, some, 0)


def norm_one_back(
    weights_hbm, query_grad_ref, pair_grad_ref, hidden_grad_ref, tokens_ref, inverse_ref, gain_ref,
    gain_two_ref, input_grad_ref, gain_terms, w_block, norm_grad, w_sems,
):
    width, query_columns = tokens_ref.shape[1], query_grad_ref.shape[1]
    rows, columns = w_block.shape[1:]
    count = width // rows

    def w_copy(at):
        view = weights_hbm.at[pl.ds(pl.multiple_of(at * rows, rows), rows), pl.ds(0, columns)]
        return pltpu.make_async_copy(view, w_block.at[at % 2], w_sems.at[at % 2])

    w_copy(0).start()

    def one(at, _):
        w_copy(at).wait()

        @pl.when(at + 1 < count)
        def _():
            w_copy(at + 1).start()

        made = dot_last(query_grad_ref[...], w_block[at % 2, :, :query_columns])
        made = made + dot_last(pair_grad_ref[...], w_block[at % 2, :, query_columns:])
        norm_grad[:, pl.ds(pl.multiple_of(at * rows, rows), rows)] = made
        return 0

    lax.fori_loop(0, count, one, 0)
    chunk = 32
    gain = gain_ref[0:1, :]

    def some(at, sums):
        part = pl.ds(pl.multiple_of(at * chunk, chunk), chunk)
        inverse, token = inverse_ref[part, :], tokens_ref[part, :].astype(jnp.float32)
        made = norm_grad[part, :]
        scaled = gain * made
        mean = jnp.mean(token * scaled, axis=-1, keepdims=True)
        input_grad_ref[part, :] = (
            hidden_grad_ref[part, :] + inverse * scaled - token * (inverse * inverse * inverse * mean)
        )
        return sums + jnp.sum(made * token * inverse, axis=0, keepdims=True)

    zeros = jnp.zeros((1, width), jnp.float32)
    gain_terms[0:1, :] = lax.fori_loop(0, tokens_ref.shape[0] // chunk, some, zeros)
    gain_terms[1:2, :] = gain_two_ref[...]


def tail_kernel(
    tasks, shares_hbm, pair_hbm, gating_hbm, weights_hbm, query_grad_ref, pair_grad_ref,
    hidden_grad_ref, tokens_ref, inverse_ref, gain_ref, gain_two_ref, gating_plane, share_plane,
    pair_plane, gain_plane, input_grad_ref, share_parts, share_sum, mine, core_in, halves, wholes,
    pair_parts, pair_sum, gain_terms, gain_parts, gain_sum, w_block, norm_grad, w_sems, *sems,
):
    gating, pair, gain_seq, gain_grp, pair_seq, pair_gather, *halves_of = tasks
    shares, share_gathers = halves_of[:2], halves_of[2:]
    grp, seq = lax.axis_index("grp"), lax.axis_index("seq")
    barrier = pltpu.get_barrier_semaphore()
    devices = list(gain_grp.peers(grp, seq)) + list(gain_seq.peers(grp, seq))
    for device in devices:
        pl.semaphore_signal(barrier, inc=1, device_id=device, device_id_type=MESH)
    pl.semaphore_wait(barrier, len(devices))
    sems = [(sems[2 * at], sems[2 * at + 1]) for at in range(len(tasks))]

    def share_part(at):
        shares[at].finish()
        add_blocks(share_sum.at[at], share_parts.at[at])
        share_gathers[at].start(share_sum.at[at], share_plane, sems[8 + at], grp, seq)

    shares[0].start(shares_hbm, share_parts.at[0], sems[6], grp, seq)
    pair.start(pair_hbm, None, sems[1], grp, seq, (mine, core_in, halves, wholes))
    gating.start(gating_hbm, gating_plane, sems[0], grp, seq, begin=False)
    gating.kept.start()
    for at in (1, 4, 7):
        gating.out[at].start()
    pair.first_sums()
    norm_one_back(
        weights_hbm, query_grad_ref, pair_grad_ref, hidden_grad_ref, tokens_ref, inverse_ref,
        gain_ref, gain_two_ref, input_grad_ref, gain_terms, w_block, norm_grad, w_sems,
    )
    gain_seq.start(gain_terms, gain_parts, sems[2], grp, seq)
    for _ in pair.forward():
        pass
    for at in (2, 5):
        gating.out[at].start()
    handing = gating.forward()
    next(handing)
    pair_seq.start(pair.total(), pair_parts, sems[4], grp, seq)
    shares[1].start(shares_hbm, share_parts.at[1], sems[7], grp, seq)
    gain_seq.finish()
    gain_sum[...] = jnp.sum(gain_parts[...], axis=0)
    gain_grp.start(gain_sum, gain_plane, sems[3], grp, seq)
    share_part(0)
    pair_seq.finish()
    add_blocks(pair_sum, pair_parts)
    pair_gather.start(pair_sum, pair_plane, sems[5], grp, seq)
    next(handing)
    share_part(1)
    next(handing)
    hand_on([share_gathers[0], pair_gather, share_gathers[1]])
    for copy in pair.copies:
        copy.wait_send()
    for task in (gain_grp, gating, pair_gather, *share_gathers):
        task.finish()


def gather_gating(shape):
    return gather_plane(
        shape,
        split=1,
        target_view=lambda ref, index: ref.at[:, index],
        out_shape=(shape[0], lax.axis_size("grp"), *shape[1:]),
    )


def tail_exchange(number, shares, pair, gating, weights, back):
    gain_terms = jax.ShapeDtypeStruct((2, back[3].shape[1]), jnp.float32)
    tokens_here = back[3].shape[0]
    seq_count = lax.axis_size("seq")
    low = jnp.bfloat16
    columns, rows_all = shares.shape
    rows = rows_all // seq_count
    _, pair_rows, pair_columns = pair.shape
    sub = pair_rows // seq_count
    half = columns // 2

    def share_task(at):
        return Exchange(
            "seq",
            (seq_count, half, rows),
            lambda ref, index: ref.at[
                pl.ds(at * half, half), pl.ds(pl.multiple_of(index * rows, rows), rows)
            ],
            block_of,
        )

    def share_gather(at):
        return gather_plane(
            (half, rows),
            target_view=lambda ref, index: ref.at[index, pl.ds(at * half, half)],
            out_shape=(8, columns, rows),
        )

    tasks = [
        gather_gating(gating.shape),
        PlaneSum(pair_rows, pair_columns, placed=False),
        gather_axis("seq", gain_terms)[0],
        gather_axis("grp", gain_terms)[0],
        Exchange(
            "seq",
            (seq_count, sub, pair_columns),
            lambda ref, index: rows_of(ref, index, sub),
            block_of,
        ),
        gather_plane((sub, pair_columns)),
        share_task(0),
        share_task(1),
        share_gather(0),
        share_gather(1),
    ]
    hbm = pl.BlockSpec(memory_space=pl.ANY)
    vmem = pl.BlockSpec(memory_space=pltpu.VMEM)
    scratch = [
        pltpu.VMEM((2, seq_count, half, rows), low),
        pltpu.VMEM((2, half, rows), low),
        *tasks[1].scratch(),
        pltpu.VMEM((seq_count, sub, pair_columns), low),
        pltpu.VMEM((sub, pair_columns), low),
        pltpu.VMEM(gain_terms.shape, jnp.float32),
        pltpu.VMEM((seq_count, *gain_terms.shape), jnp.float32),
        pltpu.VMEM(gain_terms.shape, jnp.float32),
        pltpu.VMEM((2, 2 * HD, (NH + 2) * HD), low),
        pltpu.VMEM((tokens_here, back[3].shape[1]), jnp.float32),
        pltpu.SemaphoreType.DMA((2,)),
    ]
    for task in tasks:
        scratch += [pltpu.SemaphoreType.DMA((task.sem_count,))] * 2
    return pl.pallas_call(
        functools.partial(tail_kernel, tasks),
        in_specs=[hbm] * 4 + [vmem] * len(back),
        out_specs=[hbm] * 4 + [vmem],
        out_shape=[
            jax.ShapeDtypeStruct(tasks[0].out_shape, low),
            jax.ShapeDtypeStruct((8, columns, rows), low),
            jax.ShapeDtypeStruct((8, sub, pair_columns), low),
            jax.ShapeDtypeStruct((8, *gain_terms.shape), jnp.float32),
            jax.ShapeDtypeStruct((tokens_here, back[3].shape[1]), jnp.float32),
        ],
        scratch_shapes=scratch,
        compiler_params=pltpu.CompilerParams(
            collective_id=number, has_side_effects=True, vmem_limit_bytes=60 * 2**20
        ),
        cost_estimate=SMALL_COST,
        name="tail_exchange",
    )(shares, pair, gating, weights, *back)


def half_rows(axis, height):
    def half_of(view, second):
        index = (slice(None),) * axis + (pl.ds(height if second else 0, height),)
        return view.at[index]

    return half_of


def whole(ref, index):
    return ref


def block_of(ref, index):
    return ref.at[index]


def gather_plane(
    shape, split=0, source_view=whole, target_view=block_of, out_shape=None, placed=False
):
    out_shape = out_shape or (lax.axis_size("grp"), *shape)
    if lax.axis_size("grp") == 8:
        halves = half_rows(split, shape[split] // 2)
        return PlaneGather(out_shape, source_view, target_view, halves, placed)
    return Exchange("grp", out_shape, source_view, target_view)


def hand_on(tasks):
    going = [task.forward() for task in tasks]
    while going:
        going = [steps for steps in going if next(steps, going) is not going]


def exchange_kernel(tasks, wires, arrays, outputs, *refs):
    sources, targets = refs[:arrays], refs[arrays : arrays + outputs]
    refs = list(refs[arrays + outputs :])
    sems, scratch = [], []
    for task in tasks:
        sems.append((refs.pop(0), refs.pop(0)))
        held = len(task.scratch()) if isinstance(task, PlaneSum) else 0
        scratch.append([refs.pop(0) for _ in range(held)])
    grp, seq = lax.axis_index("grp"), lax.axis_index("seq")
    barrier = pltpu.get_barrier_semaphore()
    axes = {"grp": [], "seq": []}
    for task in tasks:
        devices = list(task.peers(grp, seq))
        if len(devices) > len(axes[task.axis]):
            axes[task.axis] = devices
    devices = axes["grp"] + axes["seq"]
    for device in devices:
        pl.semaphore_signal(barrier, inc=1, device_id=device, device_id_type=MESH)
    pl.semaphore_wait(barrier, len(devices))

    def start(at):
        after, source, target = wires[at]
        source = targets[source] if after is not None else sources[source]
        more = (scratch[at],) if scratch[at] else ()
        tasks[at].start(source, targets[target], sems[at], grp, seq, *more)

    open_tasks = list(range(len(tasks)))
    first = [at for at in open_tasks if wires[at][0] is None]
    for at in first:
        start(at)
    for at in first:
        if isinstance(tasks[at], PlaneSum):
            tasks[at].first_sums()
    hand_on([tasks[at] for at in first])
    for at in open_tasks[:]:
        after = wires[at][0]
        if after is not None:
            tasks[after].finish()
            open_tasks.remove(after)
            start(at)
            hand_on([tasks[at]])
    for at in open_tasks:
        tasks[at].finish()


def exchange(number, work):
    tasks = [piece[0] for piece in work]
    arrays, shapes, wires = [], [], []
    for piece in work:
        if isinstance(piece[1], int):
            after, source = piece[1], wires[piece[1]][2]
            kind = shapes[source].dtype
        else:
            after, source = None, len(arrays)
            arrays.append(piece[1])
            kind = piece[1].dtype
        if len(piece) == 3:
            target = wires[piece[2]][2]
        else:
            target = len(shapes)
            shapes.append(jax.ShapeDtypeStruct(piece[0].out_shape, kind))
        wires.append((after, source, target))
    scratch = []
    for task in tasks:
        scratch += [pltpu.SemaphoreType.DMA((task.sem_count,))] * 2
        if isinstance(task, PlaneSum):
            scratch += task.scratch()
    return pl.pallas_call(
        functools.partial(exchange_kernel, tasks, wires, len(arrays), len(shapes)),
        in_specs=[pl.BlockSpec(memory_space=pl.ANY)] * len(arrays),
        out_specs=[pl.BlockSpec(memory_space=pl.ANY)] * len(shapes),
        out_shape=shapes,
        scratch_shapes=scratch,
        compiler_params=pltpu.CompilerParams(collective_id=number, has_side_effects=True),
        cost_estimate=SMALL_COST,
        name="exchange",
    )(*arrays)


def gather_axis(axis, array):
    task = Exchange(axis, (lax.axis_size(axis), *array.shape), whole, block_of)
    return task, array


def split_rows(axis, array):
    count = lax.axis_size(axis)
    rows, columns = array.shape
    height = rows // count
    task = Exchange(
        axis,
        (count, height, columns),
        lambda ref, index: rows_of(ref, index, height),
        block_of,
    )
    return task, array


def split_columns(axis, array, placed=False):
    count = lax.axis_size(axis)
    rows, columns = array.shape
    width = columns // count
    if placed and count == 8:
        task = PlacedExchange(
            (count, rows, width), lambda ref, index: columns_of(ref, index, width)
        )
        return task, array
    task = Exchange(
        axis,
        (count, rows, width),
        lambda ref, index: columns_of(ref, index, width),
        block_of,
    )
    return task, array


def plane_sum_kernel(
    own, part_ref, gate_ref, up_ref, x_ref, total_ref, grads_out, core_in, chip, half_x, half_y,
    whole_x, whole_y, x_block, stage, send_sems, recv_sems, x_sems, out_sems,
):
    grp, seq = lax.axis_index("grp"), lax.axis_index("seq")
    core, side_x, side_y = [flip(grp, bits) for bits in (1, 2, 4)]
    blocks = [PLACES[bits] for bits in (6, 2, 4, 0)]
    core_blocks = [PLACES[bits] for bits in (7, 3, 5, 1)]
    half = total_ref.shape[0] // 2
    low, high = pl.ds(0, half), pl.ds(half, half)
    rows = x_block.shape[2]
    count = x_ref.shape[1] // rows

    def x_copy(at):
        view = x_ref.at[:, pl.ds(pl.multiple_of(at * rows, rows), rows)]
        return pltpu.make_async_copy(view, x_block.at[at % 2], x_sems.at[at % 2])

    def out_copies(at):
        return [
            pltpu.make_async_copy(
                stage.at[which, at % 2, own_columns(grp, own)],
                grads_out.at[pl.ds(pl.multiple_of((2 * at + which) * own, own), own)],
                out_sems.at[which, at % 2],
            )
            for which in range(2)
        ]

    x_copy(0).start()
    barrier = pltpu.get_barrier_semaphore()
    for device in (core, side_x, side_y):
        pl.semaphore_signal(barrier, inc=1, device_id=(device, seq), device_id_type=MESH)
    pl.semaphore_wait(barrier, 3)

    sems = (send_sems, recv_sems)
    copies = [
        remote(part_ref.at[block], core_in.at[at], sems, at, (core, seq))
        for at, block in enumerate(core_blocks)
    ]
    copies += [
        remote(chip.at[0, low], half_x, sems, 4, (side_x, seq)),
        remote(chip.at[0, high], half_y, sems, 5, (side_y, seq)),
        remote(chip.at[1, low], whole_x.at[low], sems, 6, (side_x, seq)),
        remote(chip.at[2, high], whole_y.at[high], sems, 7, (side_y, seq)),
        remote(chip.at[1, high], whole_x.at[high], sems, 8, (side_x, seq)),
        remote(chip.at[2, low], whole_y.at[low], sems, 9, (side_y, seq)),
    ]
    for copy in copies[:4]:
        copy.start()

    def step(at, _):
        @pl.when(at == 1)
        def _():
            for came, then in ((0, (4, 5)), (1, (6,)), (2, (7,))):
                copies[came].wait_recv()
                add_rows(chip.at[came], part_ref.at[blocks[came]], core_in.at[came])
                for start in then:
                    copies[start].start()

        @pl.when(at == count - 1)
        def _():
            copies[5].wait_recv()
            add_rows(chip.at[1, high], chip.at[1, high], half_y)
            copies[8].start()
            copies[4].wait_recv()
            add_rows(chip.at[2, low], chip.at[2, low], half_x)
            copies[9].start()

        x_copy(at).wait()

        @pl.when(at + 1 < count)
        def _():
            x_copy(at + 1).start()

        @pl.when(at >= 2)
        def _():
            for copy in out_copies(at - 2):
                copy.wait()

        for which, ref in enumerate((gate_ref, up_ref)):
            stage[which, at % 2] = jnp.dot(
                ref[...], x_block[at % 2], preferred_element_type=jnp.float32
            ).astype(stage.dtype)
        for copy in out_copies(at):
            copy.start()
        return 0

    lax.fori_loop(0, count, step, 0)
    copies[3].wait_recv()
    add_rows(total_ref, part_ref.at[blocks[3]], core_in.at[3])
    for at, came, rows_at in (
        (6, whole_x, low),
        (7, whole_y, high),
        (8, whole_x, high),
        (9, whole_y, low),
    ):
        copies[at].wait_recv()
        add_rows(total_ref.at[rows_at], total_ref.at[rows_at], came.at[rows_at])
    for copy in copies:
        copy.wait_send()
    for at in (count - 2, count - 1):
        for copy in out_copies(at):
            copy.wait()


def plane_sum(number, own, part, gate_grad, up_grad, x, seq_count):
    count = lax.axis_size("grp")
    rows_all, columns = part.shape
    rows = rows_all // count
    if count != 8:
        total = lax.psum_scatter(part, "grp", scatter_dimension=0, tiled=True)
        begin = (lax.axis_index("grp") * own) % 128
        both = jnp.concatenate(
            [lax.dynamic_slice_in_dim(grad, begin, own) for grad in (gate_grad, up_grad)], axis=0
        )
        return total.astype(jnp.float32), weight_grad(both, x, seq_count)
    low = jnp.bfloat16
    cols, tokens_all = gate_grad.shape
    width = x.shape[1] // seq_count
    vmem = pl.BlockSpec(memory_space=pltpu.VMEM)
    hbm = pl.BlockSpec(memory_space=pl.ANY)
    grads = jax.ShapeDtypeStruct((2 * seq_count * own, width), low)
    return pl.pallas_call(
        functools.partial(plane_sum_kernel, own),
        in_specs=[vmem, vmem, vmem, hbm],
        out_specs=[vmem, hbm],
        out_shape=[jax.ShapeDtypeStruct((rows, columns), jnp.float32), grads],
        scratch_shapes=[
            pltpu.VMEM((4, rows, columns), low),
            pltpu.VMEM((3, rows, columns), low),
            pltpu.VMEM((rows // 2, columns), low),
            pltpu.VMEM((rows // 2, columns), low),
            pltpu.VMEM((rows, columns), low),
            pltpu.VMEM((rows, columns), low),
            pltpu.VMEM((2, tokens_all, width), low),
            pltpu.VMEM((2, 2, cols, width), low),
            pltpu.SemaphoreType.DMA((10,)),
            pltpu.SemaphoreType.DMA((10,)),
            pltpu.SemaphoreType.DMA((2,)),
            pltpu.SemaphoreType.DMA((2, 2)),
        ],
        compiler_params=pltpu.CompilerParams(
            collective_id=number, has_side_effects=True, vmem_limit_bytes=56 * 2**20
        ),
        cost_estimate=SMALL_COST,
        name="plane_sum",
    )(part.reshape(count, rows, columns), gate_grad, up_grad, x)


def local(
    tokens,
    cotangent,
    segment_ids,
    tile_owner_slots,
    weights_low,
    master,
    moment_one,
    moment_two,
    left_basis_set,
    right_basis_set,
    gains,
    gain_moment_one,
    gain_moment_two,
):
    grp_count = lax.axis_size("grp")
    seq_count = lax.axis_size("seq")
    grp_here, seq_here = lax.axis_index("grp"), lax.axis_index("seq")
    rows_here = tokens.shape[0]
    slots_here, rows_block, tile_width = weights_low.shape
    tile_count = tile_owner_slots.shape[0]
    query_cols = NH * HD
    value_end = query_cols + 2 * HD
    output_end = value_end + MODEL_WIDTH
    attn_tiles = output_end // tile_width
    query_tiles = query_cols // tile_width
    hidden_tiles = FF // tile_width
    own = FF // grp_count
    share = max(-(-((at * own) % tile_width + own) // tile_width) for at in range(grp_count))
    share_width = MODEL_WIDTH // grp_count
    sub_rows = rows_block // grp_count
    halves = 2 if sub_rows >= 32 else 1
    half_block, half_sub = rows_block // halves, sub_rows // halves
    first_place = (seq_here * rows_here) % SEQLEN
    key_tables = turn_tables(jnp.arange(SEQLEN, dtype=jnp.int32))
    tables = [lax.dynamic_slice_in_dim(table, first_place, rows_here) for table in key_tables]

    hidden_ids = grp_here * own // tile_width + jnp.arange(share, dtype=jnp.int32)
    hidden_ids = jnp.minimum(hidden_ids, hidden_tiles - 1)
    feed_ids = (
        attn_tiles
        + jnp.arange(3, dtype=jnp.int32)[:, None] * hidden_tiles
        + hidden_ids[None, :]
    ).reshape(-1)
    feed_slots, attn_slots = tile_owner_slots[feed_ids], tile_owner_slots[:attn_tiles]

    tok_float = tokens.astype(jnp.float32)
    inverse_one = lax.rsqrt(jnp.mean(tok_float * tok_float, axis=-1, keepdims=True) + NORM_EPS)
    normed = (tok_float * inverse_one * gains[0]).astype(jnp.bfloat16)

    def weight_half(at):
        return gather_plane(
            (slots_here, half_block, tile_width),
            split=1,
            source_view=lambda ref, index: ref.at[:, pl.ds(at * half_block, half_block)],
        )

    def attn_half(at):
        return gather_plane(
            (seq_count, half_sub, output_end),
            target_view=lambda ref, index: ref.at[:, at, index],
            out_shape=(seq_count, halves, grp_count, half_sub, output_end),
        )

    flat = (grp_count * slots_here, half_block, tile_width)
    tiles, segments = exchange(
        0,
        [(weight_half(0), weights_low), gather_axis("seq", segment_ids.reshape(-1, tile_width))],
    )
    feed_rows, attn_rows = pick(tiles.reshape(flat), feed_slots, attn_slots)
    feed_parts = [lax.all_gather(feed_rows, "seq", axis=0, tiled=False)]
    if halves == 2:
        tiles, attn_first = exchange(
            1, [(weight_half(1), weights_low), gather_axis("seq", attn_rows)]
        )
        feed_rows, attn_rows = pick(tiles.reshape(flat), feed_slots, attn_slots)
        feed_parts.append(lax.all_gather(feed_rows, "seq", axis=0, tiled=False))
        attn_weights, _ = exchange(
            2,
            [(attn_half(0), attn_first), gather_axis("seq", attn_rows), (attn_half(1), 1, 0)],
        )
    else:
        _, attn_weights = exchange(2, [gather_axis("seq", attn_rows), (attn_half(0), 0)])
    attn_weights = attn_weights.reshape(MODEL_WIDTH, output_end)

    first_key = seq_here * rows_here - first_place
    key_segs = lax.dynamic_slice_in_dim(segments.reshape(-1), first_key, SEQLEN)
    at = (first_place // rows_here).reshape(1)
    if grp_count == 8 and seq_count * rows_here == SEQLEN:
        (
            projected, pairs, context, log_totals, hidden, normed_two, inverse_two, cot_plane,
            normed_plane,
        ) = attention_block(
            3, normed, tokens, gains, tables, key_segs, segment_ids, cotangent, attn_weights
        )
    else:
        projected = project(normed, attn_weights, tables)
        pairs, cot_plane, normed_plane = exchange(
            3,
            [
                gather_axis("seq", projected[:, query_cols:]),
                (gather_plane(cotangent.shape, placed=True), cotangent),
                (gather_plane(normed.shape, placed=True), normed),
            ],
        )
        pairs = lax.dynamic_slice_in_dim(pairs.reshape(-1, 2 * HD), first_key, SEQLEN)
        context, log_totals = attend(at, projected, pairs, key_segs, segment_ids)
        branch = jnp.dot(
            context, attn_weights[:, value_end:], preferred_element_type=jnp.float32
        )
        hidden = tok_float + branch
        inverse_two = lax.rsqrt(jnp.mean(hidden * hidden, axis=-1, keepdims=True) + NORM_EPS)
        normed_two = (hidden * inverse_two * gains[1]).astype(jnp.bfloat16)

    cot_plane = cot_plane.reshape(-1, MODEL_WIDTH)
    normed_plane = normed_plane.reshape(-1, MODEL_WIDTH)
    real_cols = ((grp_here * own) % tile_width).reshape(1)
    if halves == 2:
        some = jnp.max(feed_parts[0][0, :8, :tile_width].astype(jnp.float32)) * 0.0
        real_cols = real_cols + some.astype(jnp.int32)
    if grp_count == 8:
        gate_grad, up_grad, two_part, feed_part, second_plane, context_plane, down_grad = (
            feed_gather(
                4, own, real_cols, normed_two, context, cot_plane, feed_parts, seq_count
            )
        )
        second_plane = second_plane.reshape(-1, MODEL_WIDTH)
    else:
        second_plane, context_plane = exchange(
            4,
            [
                (gather_plane(normed_two.shape), normed_two),
                (gather_plane(context.shape), context),
            ],
        )
        second_plane = second_plane.reshape(-1, MODEL_WIDTH)
        activated, gate_grad, up_grad, two_part, feed_part = feed_forward(
            own, real_cols, second_plane, cot_plane, feed_parts, seq_count
        )
        activated = lax.dynamic_slice_in_dim(activated, (grp_here * own) % tile_width, own)
        down_grad = weight_grad(activated, cot_plane, seq_count)
    context_plane = context_plane.reshape(-1, MODEL_WIDTH)
    down_grad, two_part = lax.optimization_barrier((down_grad, two_part))
    down_grad = lax.psum_scatter(down_grad, "seq", scatter_dimension=0, tiled=True)
    norm_two_grad, gating_grads = plane_sum(
        5, own, two_part, gate_grad, up_grad, second_plane, seq_count
    )
    gating_grads = lax.psum_scatter(gating_grads, "seq", scatter_dimension=0, tiled=True)
    gating_grads = gating_grads.reshape(2, own, rows_block)

    out_grad = cotangent.astype(jnp.float32)
    gain_two_term = jnp.sum(norm_two_grad * hidden * inverse_two, axis=0)
    hidden_grad = (
        out_grad
        + inverse_two * gains[1] * norm_two_grad
        - hidden
        * inverse_two**3
        * jnp.mean(hidden * gains[1] * norm_two_grad, axis=-1, keepdims=True)
    )
    branch_grad = hidden_grad.astype(jnp.bfloat16)
    fused = grp_count == 8 and seq_count * rows_here == SEQLEN
    if fused:
        feed_part = feed_part.reshape(grp_count, rows_here, MODEL_WIDTH)
        query_grad, pair_part, feed_out, down_plane = attend_back_sum(
            6, projected, pairs, branch_grad, log_totals, key_segs, segment_ids, key_tables,
            tables, feed_part, down_grad, attn_weights,
        )
    else:
        context_grad = times_transpose(branch_grad, attn_weights[:, value_end:]).astype(jnp.bfloat16)
        query_grad, pair_part = attend_back(
            at, projected, pairs, context_grad, log_totals, key_segs, segment_ids, key_tables, tables
        )
        feed_out = lax.psum_scatter(
            feed_part.reshape(-1, MODEL_WIDTH), "grp", scatter_dimension=0, tiled=True
        )
        (down_plane,) = exchange(10, [(gather_plane(down_grad.shape), down_grad)])
    block_out = (hidden + feed_out.astype(jnp.float32)).astype(jnp.bfloat16)
    if seq_count * rows_here > SEQLEN:
        pair_part = lax.dynamic_update_slice_in_dim(
            jnp.zeros((seq_count * rows_here, 2 * HD), pair_part.dtype), pair_part, first_key, 0
        )
    pair_parts, query_share, branch_share = exchange(
        7,
        [
            split_rows("seq", pair_part),
            split_columns("grp", query_grad, placed=True),
            split_columns("grp", branch_grad, placed=True),
        ],
    )
    pair_grad = jnp.sum(pair_parts.astype(jnp.float32), axis=0).astype(jnp.bfloat16)
    shares = share_grad(
        query_share.reshape(-1, share_width),
        branch_share.reshape(-1, share_width),
        normed_plane,
        context_plane,
    )
    pair_weight_grad = contract(normed, pair_grad).astype(jnp.bfloat16)
    pair_blocks = pair_weight_grad.reshape(seq_count, grp_count, sub_rows, 2 * HD)
    if grp_count == 8:
        pair_blocks = jnp.transpose(pair_blocks, (1, 0, 2, 3))
        gating_plane, share_plane, pair_plane, gain_parts, input_grad = tail_exchange(
            8,
            shares,
            pair_blocks.reshape(grp_count, seq_count * sub_rows, 2 * HD),
            gating_grads,
            attn_weights,
            (query_grad, pair_grad, hidden_grad, tokens, inverse_one, gains, gain_two_term[None, :]),
        )
    else:
        projected_grad = jnp.concatenate([query_grad, pair_grad], axis=1)
        norm_one_grad = times_transpose(projected_grad, attn_weights[:, :value_end])
        gain_one_term = jnp.sum(norm_one_grad * tok_float * inverse_one, axis=0)
        input_grad = (
            hidden_grad
            + inverse_one * gains[0] * norm_one_grad
            - tok_float
            * inverse_one**3
            * jnp.mean(tok_float * gains[0] * norm_one_grad, axis=-1, keepdims=True)
        )
        gain_terms = jnp.stack([gain_one_term, gain_two_term])
        pair_task = Exchange(
            "grp",
            (grp_count, seq_count, sub_rows, 2 * HD),
            lambda ref, index: ref.at[:, index],
            block_of,
        )
        work = [
            split_columns("seq", shares),
            (pair_task, pair_blocks),
            gather_axis("seq", gain_terms),
            (gather_gating(gating_grads.shape), gating_grads),
        ]
        share_parts, pair_parts, gain_parts, gating_plane = exchange(8, work)
        gain_seq = jnp.sum(gain_parts, axis=0)
        shares = jnp.sum(share_parts.astype(jnp.float32), axis=0).astype(jnp.bfloat16)
        pair_parts = jnp.sum(pair_parts.astype(jnp.float32), axis=0).astype(jnp.bfloat16)
        pair_task = Exchange("seq", pair_parts.shape, block_of, block_of)
        _, pair_plane, share_plane, gain_parts = exchange(
            9,
            [
                (pair_task, pair_parts),
                (gather_plane(pair_parts.shape), 0),
                (gather_plane(shares.shape), shares),
                gather_axis("grp", gain_seq),
            ],
        )
        pair_plane = jnp.sum(pair_plane.astype(jnp.float32), axis=1).astype(jnp.bfloat16)

    gain_grads = jnp.sum(gain_parts, axis=0)

    owner_slots, _ = lax.optimization_barrier((tile_owner_slots, pair_grad))
    tile_of_slot = (
        jnp.full((grp_count * slots_here,), tile_count, jnp.int32)
        .at[owner_slots]
        .set(jnp.arange(tile_count, dtype=jnp.int32))
    )
    tiles_here = lax.dynamic_slice_in_dim(tile_of_slot, grp_here * slots_here, slots_here)
    feed_at = jnp.clip(tiles_here - attn_tiles, 0, 3 * hidden_tiles - 1)
    which, column = feed_at // hidden_tiles, feed_at % hidden_tiles
    is_query = tiles_here < query_tiles
    is_pair = (tiles_here >= query_tiles) & (tiles_here < query_tiles + 2)
    is_feed = tiles_here >= attn_tiles
    kind = jnp.where(is_feed, jnp.where(which < 2, 0, 1), jnp.where(is_pair, 3, 2))
    kind = jnp.where(tiles_here == tile_count, 4, kind)
    out_at = jnp.clip(tiles_here - query_tiles - 2, 0, query_tiles - 1)
    per_share = share_width // tile_width
    share_at = jnp.where(is_query, jnp.minimum(tiles_here, query_tiles - 1), out_at)
    at = jnp.stack(
        [
            kind,
            jnp.minimum(which, 1) * hidden_tiles + column,
            column,
            share_at // per_share * 2 * per_share
            + share_at % per_share
            + jnp.where(is_query, 0, per_share),
            jnp.where(is_pair, tiles_here - query_tiles, 0),
        ]
    )
    new_master, new_one, new_two = adam(
        at,
        gating_plane.reshape(-1, rows_block),
        down_plane.reshape(-1, rows_block),
        share_plane.reshape(-1, rows_block),
        pair_plane,
        left_basis_set,
        right_basis_set,
        master,
        moment_one,
        moment_two,
    )
    gain_one = BETA_ONE * gain_moment_one + (1.0 - BETA_ONE) * gain_grads
    gain_two = BETA_TWO * gain_moment_two + (1.0 - BETA_TWO) * gain_grads * gain_grads
    new_gains = gains - GAIN_RATE * gain_one / (jnp.sqrt(gain_two) + ADAM_EPS)
    return (
        block_out,
        input_grad,
        new_master,
        new_one,
        new_two,
        gain_grads,
        new_gains,
        gain_one,
        gain_two,
    )


def solution(mesh):
    return jax.shard_map(
        local,
        mesh=mesh,
        in_specs=(
            P(("grp", "seq"), None),
            P(("grp", "seq"), None),
            P(("grp", "seq")),
            P(),
            P("grp", "seq", None),
            P("grp", "seq", None),
            P("grp", "seq", None),
            P("grp", "seq", None),
            P("grp", "seq", None),
            P("grp", "seq", None),
            P(),
            P(),
            P(),
        ),
        out_specs=(
            P(("grp", "seq"), None),
            P(("grp", "seq"), None),
            P("grp", "seq", None),
            P("grp", "seq", None),
            P("grp", "seq", None),
            P(),
            P(),
            P(),
            P(),
        ),
        check_vma=False,
    )
```
